32 devices in a mesh: grp: 4 (over z), seq: 8 (over y, x, core).
Axes of the slice: x: 2, y: 2, z: 4, core: 2. Of those that a mesh axis runs over, the one named last changes fastest.
Arguments:
- tokens: bfloat16 [16384, 1024], P(('grp', 'seq')), may hold values from -6 to 6
- lengths: int32 [4], replicated, may hold values from 1024 to 4096, as said below
- mixer_gain: bfloat16 [1024], P('seq'), may hold values from 0.5 to 1.5
- gelu_weight: bfloat16 [1024, 1536], P('seq'), may hold values from -0.1875 to 0.1875
- input_weight: bfloat16 [1024, 1536], P('seq'), may hold values from -0.1875 to 0.1875
- conv_taps: bfloat16 [1536, 4], P('seq'), may hold values from -3 to 3
- conv_bias: bfloat16 [1536], P('seq'), may hold values from -2 to 2
- rgate_weight: bfloat16 [1536, 128], P('seq'), may hold values from -0.5 to 0.5
- rgate_bias: bfloat16 [1536], P('seq'), may hold values from -3 to 3
- igate_weight: bfloat16 [1536, 128], P('seq'), may hold values from -0.5 to 0.5
- igate_bias: bfloat16 [1536], P('seq'), may hold values from -3 to 3
- decay_param: bfloat16 [1536], P('seq')
- output_weight: bfloat16 [1536, 1024], P('seq'), may hold values from -0.625 to 0.625
- mlp_gain: bfloat16 [1024], P('seq'), may hold values from 0.5 to 1.5
- mlp_gate: bfloat16 [1024, 3072], P('seq'), may hold values from -0.1875 to 0.1875
- mlp_value: bfloat16 [1024, 3072], P('seq'), may hold values from -0.1875 to 0.1875
- mlp_down: bfloat16 [3072, 1024], P('seq'), may hold values from -0.21875 to 0.21875
- cotangent: bfloat16 [16384, 1024], P(('grp', 'seq')), may hold values from -6 to 6
Outputs:
- mixed: bfloat16 [16384, 1024], P(('grp', 'seq'))
- tokens_grad: float32 [16384, 1024], P(('grp', 'seq'))
- mixer_grad: float32 [1024], P('seq')
- gelu_grad: float32 [1024, 1536], P('seq')
- input_grad: float32 [1024, 1536], P('seq')
- taps_grad: float32 [1536, 4], P('seq')
- cbias_grad: float32 [1536], P('seq')
- rgate_grad: float32 [1536, 128], P('seq')
- rbias_grad: float32 [1536], P('seq')
- igate_grad: float32 [1536, 128], P('seq')
- ibias_grad: float32 [1536], P('seq')
- decay_grad: float32 [1536], P('seq')
- output_grad: float32 [1536, 1024], P('seq')
- mlpgain_grad: float32 [1024], P('seq')
- mlpgate_grad: float32 [1024, 3072], P('seq')
- mlpvalue_grad: float32 [1024, 3072], P('seq')
- mlpdown_grad: float32 [3072, 1024], P('seq')
The draws below stay inside these ranges and needn't reach their ends.
Inputs may be any that keep to these rules, and one draw needn't show every extreme that they name: `lengths`: valid tokens of each slot, from its start; the rest of the slot is padding. Some slot has exactly 4096 and some exactly 1024.
All inputs are finite; a program needn't handle non-finite values.
Results may differ from the reference program's by a relative error of at most 0.0091.
Values may be sent and summed in bfloat16 or wider, within the bound.
A program may use at most 192 MiB of HBM per device.

```python
import math
import jax
import jax.numpy as jnp
from jax import lax

D = 1024
LRU = 1536
FF = 3072
HEADS = 12
BLK = 128
CONV = 4
SEQ_LEN = 4096
LEN_MIN = 1024
ROWS = 16384
SLOTS = 4


def draw_lengths(key, part):
    first_key, second_key = jax.random.split(jax.random.fold_in(key, 11))
    values = jax.random.randint(first_key, (SLOTS,), LEN_MIN, SEQ_LEN + 1)
    picked = jax.random.permutation(second_key, SLOTS)
    values = values.at[picked[0]].set(SEQ_LEN)
    values = values.at[picked[1]].set(LEN_MIN)
    return values.astype(jnp.int32)


def draw_decay_param(key, part):
    slowest = 0.25
    fastest = 8.0
    unit = jax.random.uniform(jax.random.fold_in(key, 23), (LRU,), jnp.float32)
    rate = slowest / SEQ_LEN * (fastest / slowest) ** unit
    return (-jnp.log(jnp.expm1(rate))).astype(jnp.bfloat16)


def strengthened(drawn, rng, source, target, shards_of, factor):
    def block_of(axis_at):
        return (jnp.arange(drawn.shape[axis_at]) // (drawn.shape[axis_at] // shards_of)).reshape((-1,) + (1,) * (drawn.ndim - 1 - axis_at))

    near = jax.random.permutation(rng, shards_of)[block_of(target)]
    far = (block_of(target) + shards_of // 2) % shards_of
    return jnp.where((block_of(source) == near) | (block_of(source) == far), factor * drawn, drawn)


def block_scale(own_key, extent, shards, smallest, largest):
    def one(dim, shards_of):
        steps = jax.random.uniform(jax.random.fold_in(jax.random.fold_in(own_key, 6), dim), (shards_of,), jnp.float32, smallest / len(shards), largest / len(shards))
        return jnp.repeat(jnp.exp(steps), extent[dim] // shards_of).reshape((-1,) + (1,) * (len(extent) - dim - 1))

    factor_of = one(*shards[0])
    for cut in shards[1:]:
        factor_of = factor_of * one(*cut)
    return factor_of


def bell_draw(rng, dims, scale, most, cuts=(), kind=jnp.bfloat16):
    values = scale * jax.random.normal(rng, dims, jnp.float32)
    if cuts:
        values = values * block_scale(rng, dims, cuts, -0.22, 0.18)
    return jnp.clip(values, -most, most).astype(kind)


def noise_with(rng, dims, width, bound, cuts, heavy, kind=jnp.bfloat16):
    entries = width * jax.random.normal(rng, dims, jnp.float32)
    if cuts:
        entries = entries * block_scale(rng, dims, cuts, -0.22, 0.18)
    return jnp.clip(strengthened(entries, jax.random.fold_in(rng, 3), *heavy), -bound, bound).astype(kind)


def setup_inputs(seed: int = 0) -> dict:
    arg_keys = jax.random.split(jax.random.key(seed), 19)
    return {
        "tokens": noise_with(arg_keys[0], (ROWS, D), 1.0, 6.0, ((0, 32),), (0, 1, 32, 2.75)),
        "lengths": draw_lengths(jax.random.fold_in(arg_keys[18], 71), 0),
        "mixer_gain": jnp.clip(1.0 + 0.1 * jax.random.normal(arg_keys[2], (D,), jnp.float32), 0.5, 1.5).astype(jnp.bfloat16),
        "gelu_weight": bell_draw(arg_keys[3], (D, LRU), D ** -0.5, 0.1875, ((0, 8),)),
        "input_weight": bell_draw(arg_keys[4], (D, LRU), D ** -0.5, 0.1875, ((0, 8),)),
        "conv_taps": bell_draw(arg_keys[5], (LRU, CONV), 0.5, 3.0, ((0, 8),)),
        "conv_bias": bell_draw(arg_keys[6], (LRU,), 0.3, 2.0, ((0, 8),)),
        "rgate_weight": bell_draw(arg_keys[7], (LRU, BLK), BLK ** -0.5, 0.5, ((0, 8),)),
        "rgate_bias": bell_draw(arg_keys[8], (LRU,), 1.0, 3.0, ((0, 8),)),
        "igate_weight": bell_draw(arg_keys[9], (LRU, BLK), BLK ** -0.5, 0.5, ((0, 8),)),
        "igate_bias": bell_draw(arg_keys[10], (LRU,), 1.0, 3.0, ((0, 8),)),
        "decay_param": draw_decay_param(jax.random.fold_in(arg_keys[18], 71), 0),
        "output_weight": bell_draw(arg_keys[12], (LRU, D), (LRU // 16) ** -0.5, 0.625, ((0, 8),)),
        "mlp_gain": jnp.clip(1.0 + 0.1 * jax.random.normal(arg_keys[13], (D,), jnp.float32), 0.5, 1.5).astype(jnp.bfloat16),
        "mlp_gate": bell_draw(arg_keys[14], (D, FF), D ** -0.5, 0.1875, ((0, 8),)),
        "mlp_value": bell_draw(arg_keys[15], (D, FF), D ** -0.5, 0.1875, ((0, 8),)),
        "mlp_down": bell_draw(arg_keys[16], (FF, D), (FF // 4) ** -0.5, 0.21875, ((0, 8),)),
        "cotangent": bell_draw(arg_keys[17], (ROWS, D), 1.0, 6.0, ((0, 32),)),
    }


@jax.custom_vjp
def low(v):
    return lax.optimization_barrier(v.astype(jnp.bfloat16)).astype(jnp.float32)

@jax.custom_vjp
def low_back(v):
    return v

def low_keep(v):
    return (low(v), None)

def low_pass(kept, grad):
    return (grad,)

def back_keep(v):
    return (v, None)

def back_low(kept, grad):
    return (low(grad),)
low.defvjp(low_keep, low_pass)
low_back.defvjp(back_keep, back_low)
epsilon = 1e-06
cfactor = 8.0

def highest(spec, left, right):
    return jnp.einsum(spec, left, right, precision=lax.Precision.HIGHEST)

def chain_combine(earlier, later):
    return (earlier[0] * later[0], later[0] * earlier[1] + later[1])

def block_apply(values, weight):
    split = values.reshape(values.shape[0], values.shape[1], HEADS, BLK)
    blocks = weight.reshape(HEADS, BLK, BLK)
    return highest('glhi,hij->glhj', split, blocks).reshape(values.shape)

def forward(weights, inputs, valid):
    mixer_gain, gelu_weight, input_weight, conv_taps, conv_bias, rgate_weight, rgate_bias, igate_weight, igate_bias, decay_param, output_weight, mlp_gain, mlp_gate, mlp_value, mlp_down = weights
    normed_one = low(inputs * lax.rsqrt(lax.optimization_barrier(jnp.mean(inputs * inputs, axis=-1, keepdims=True)) + epsilon) * mixer_gain)
    gate_pre = low_back(highest('gld,de->gle', normed_one, gelu_weight))
    gate_act = jax.nn.gelu(gate_pre, approximate=True)
    linear = low_back(highest('gld,de->gle', normed_one, input_weight))
    conv = conv_bias + conv_taps[:, 0] * linear
    for lag in range(1, CONV):
        moved = jnp.pad(linear, ((0, 0), (lag, 0), (0, 0)))[:, :-lag, :]
        conv = conv + conv_taps[:, lag] * moved
    conv = low(conv)
    rgate = jax.nn.sigmoid(low_back(block_apply(conv, rgate_weight)) + rgate_bias)
    igate = jax.nn.sigmoid(low_back(block_apply(conv, igate_weight)) + igate_bias)
    log_decay = -cfactor * jax.nn.softplus(-decay_param) * rgate
    decay = jnp.exp(log_decay)
    inject = jnp.sqrt(-jnp.expm1(2.0 * log_decay)) * igate * conv
    _, state = lax.associative_scan(chain_combine, (decay, inject), axis=1)
    mixed_rec = low(state * gate_act)
    resid = inputs + low_back(highest('gle,ed->gld', mixed_rec, output_weight))
    normed_two = low(resid * lax.rsqrt(lax.optimization_barrier(jnp.mean(resid * resid, axis=-1, keepdims=True)) + epsilon) * mlp_gain)
    mgate_pre = low_back(highest('gld,df->glf', normed_two, mlp_gate))
    mvalue_pre = low_back(highest('gld,df->glf', normed_two, mlp_value))
    hidden = low(jax.nn.gelu(mgate_pre, approximate=True) * mvalue_pre)
    return (resid + highest('glf,fd->gld', hidden, mlp_down)) * valid[:, :, None]

def reference(tokens, lengths, mixer_gain, gelu_weight, input_weight, conv_taps, conv_bias, rgate_weight, rgate_bias, igate_weight, igate_bias, decay_param, output_weight, mlp_gain, mlp_gate, mlp_value, mlp_down, cotangent):
    params = tuple((item.astype(jnp.float32) for item in (mixer_gain, gelu_weight, input_weight, conv_taps, conv_bias, rgate_weight, rgate_bias, igate_weight, igate_bias, decay_param, output_weight, mlp_gain, mlp_gate, mlp_value, mlp_down)))
    group_size = math.gcd(SLOTS, max(1, 4096 // SEQ_LEN))
    batches = SLOTS // group_size
    inputs_all = tokens.astype(jnp.float32).reshape(batches, group_size, SEQ_LEN, D)
    cot_all = cotangent.astype(jnp.float32).reshape(batches, group_size, SEQ_LEN, D)
    lengths_all = lengths.astype(jnp.int32).reshape(batches, group_size)
    position = jnp.arange(SEQ_LEN, dtype=jnp.int32)

    def one_batch(totals, pieces):
        inputs_part, cot_part, length_part = pieces
        valid = (position[None, :] < length_part[:, None]).astype(jnp.float32)

        def run(inputs_in, weights):
            return forward(weights, inputs_in, valid)
        result, backward = jax.vjp(run, inputs_part, params)
        inputs_grad, weights_grad = backward(cot_part)
        totals = jax.tree.map(jnp.add, totals, weights_grad)
        return (totals, (result.astype(jnp.bfloat16), inputs_grad))
    zeros = jax.tree.map(jnp.zeros_like, params)
    totals, (results, grads) = lax.scan(one_batch, zeros, (inputs_all, cot_all, lengths_all))
    mixed = results.reshape(ROWS, D)
    tokens_grad = grads.reshape(ROWS, D)
    return (mixed, tokens_grad, totals[0], totals[1], totals[2], totals[3], totals[4], totals[5], totals[6], totals[7], totals[8], totals[9], totals[10], totals[11], totals[12], totals[13], totals[14])
```

```python
import functools

import jax
import jax.numpy as jnp
from jax import lax
from jax.experimental import pallas as pl
from jax.experimental.pallas import tpu as pltpu
from jax.sharding import PartitionSpec as P

epsilon = 1e-06
cfactor = 8.0


def passed_along(value, axis, steps):
    count = lax.axis_size(axis)
    leading, last = (max(0, -steps), min(count, count - steps))
    return lax.ppermute(value, axis, [(source, source + steps) for source in range(leading, last)])


def carried_in(value, axis, join, neutral, backward):
    count, mine = (lax.axis_size(axis), lax.axis_index(axis))
    pieces = jax.tree.map(lambda part: lax.all_gather(part, axis), value)
    if backward:
        pieces = jax.tree.map(lambda part: part[::-1], pieces)
        mine = count - 1 - mine
    so_far = jax.tree.map(
        lambda part, zero: jnp.full_like(part, 0) + jnp.asarray(zero, part.dtype), value, neutral
    )

    def step(position, so_far):
        longer = join(so_far, jax.tree.map(lambda part: part[position], pieces))
        return jax.tree.map(lambda new, old: jnp.where(position < mine, new, old), longer, so_far)

    return lax.fori_loop(0, count - 1, step, so_far)


def rms_norm(rows_in, gain):
    return rows_in * lax.rsqrt(jnp.mean(rows_in * rows_in, axis=-1, keepdims=True) + epsilon) * gain


def gelu_tanh(values):
    return jax.nn.gelu(values, approximate=True)


def matmul(left, right):
    return jnp.dot(left, right, preferred_element_type=jnp.float32)


def inner_rows(left, right):
    return lax.dot_general(
        left, right, (((0,), (0,)), ((), ())), preferred_element_type=jnp.float32
    )


def outer_cols(left, right):
    return lax.dot_general(
        left, right, (((1,), (1,)), ((), ())), preferred_element_type=jnp.float32
    )


def block_apply(values, weight, heads):
    count = values.shape[0]
    width = weight.shape[1]
    parts = values.reshape(count, heads, width)
    blocks = weight.reshape(heads, width, width)
    return jnp.einsum("rhi,hij->rhj", parts, blocks, preferred_element_type=jnp.float32).reshape(
        count, heads * width
    )


def block_back(grads, weight, heads):
    count = grads.shape[0]
    width = weight.shape[1]
    parts = grads.reshape(count, heads, width)
    blocks = weight.reshape(heads, width, width)
    return jnp.einsum("rhj,hij->rhi", parts, blocks, preferred_element_type=jnp.float32).reshape(
        count, heads * width
    )


def block_grad(values, grads, heads):
    count = values.shape[0]
    width = values.shape[1] // heads
    left = values.reshape(count, heads, width)
    right = grads.reshape(count, heads, width)
    return jnp.einsum("rhi,rhj->hij", left, right, preferred_element_type=jnp.float32).reshape(
        heads * width, width
    )


def chain_combine(earlier, later):
    return (earlier[0] * later[0], later[0] * earlier[1] + later[1])


def recurrence_gates(rgate_pre, igate_pre, conv_in, decay_in):
    rgate = jax.nn.sigmoid(rgate_pre)
    igate = jax.nn.sigmoid(igate_pre)
    log_decay = -cfactor * jax.nn.softplus(-decay_in) * rgate
    return (jnp.exp(log_decay), jnp.sqrt(-jnp.expm1(2.0 * log_decay)) * igate * conv_in)


MESH = pl.DeviceIdType.MESH


class Place:
    def __init__(self):
        self.z = lax.axis_index("grp")
        seq = lax.axis_index("seq")
        self.core = seq % 2
        self.x = (seq // 2) % 2
        self.y = seq // 4
        self.seq = seq
        self.sib = (self.z, self.at(self.y, self.x, 1 - self.core))
        self.xnb = (self.z, self.at(self.y, 1 - self.x, self.core))
        self.ynb = (self.z, self.at(1 - self.y, self.x, self.core))

    def at(self, y, x, core):
        return (y * 2 + x) * 2 + core

    def level(self, z):
        return (z, self.seq)


def meet(peers):
    barrier = pltpu.get_barrier_semaphore()
    for peer in peers:
        pl.semaphore_signal(barrier, inc=1, device_id=peer, device_id_type=MESH)
    pl.semaphore_wait(barrier, len(peers))


def when(cond, body):
    if cond is None:
        body()
    else:
        pl.when(cond)(body)


GOT = ("X", "Y", "D1", "D2", "SO", "SX", "SY", "S1", "S2")
SENT = ("ox", "oy", "os", "fy", "fx", "zX", "zY", "zD1", "zD2", "SX", "SY", "S1", "S2")


class Gather:
    def __init__(self, place, shards, fulls, kinds, send, recv, own):
        self.p, self.shards, self.fulls = place, shards, fulls
        self.send, self.recv, self.own = send, recv, own
        even = place.z % 2 == 0
        odd = place.z % 2 == 1
        self.fetch = [(None, even, odd)[kind] for kind in kinds]
        self.shared = [kind > 0 for kind in kinds]
        self.znb = place.level(place.z + 1 - 2 * (place.z % 2))

    def part(self, i, name):
        p = self.p
        n = self.shards[i].shape[0]
        spot = {
            "O": (p.y, p.x, p.core), "X": (p.y, 1 - p.x, p.core), "Y": (1 - p.y, p.x, p.core),
            "D1": (1 - p.y, 1 - p.x, p.core), "D2": (1 - p.y, 1 - p.x, p.core),
            "SO": (p.y, p.x, 1 - p.core), "SX": (p.y, 1 - p.x, 1 - p.core), "SY": (1 - p.y, p.x, 1 - p.core),
            "S1": (1 - p.y, 1 - p.x, 1 - p.core), "S2": (1 - p.y, 1 - p.x, 1 - p.core),
        }[name]
        first = pl.multiple_of(p.at(*spot) * n, n)
        if name in ("D1", "S1"):
            return pl.ds(first, n // 2)
        if name in ("D2", "S2"):
            return pl.ds(pl.multiple_of(first + n // 2, n // 2), n // 2)
        return pl.ds(first, n)

    def half(self, i, name, which):
        n = self.shards[i].shape[0]
        first = self.part(i, name).start
        return pl.ds(pl.multiple_of(first + which * (n // 2), n // 2), n // 2)

    def copy(self, i, how, got, peer, rows, src=None):
        full = self.fulls[i]
        return pltpu.make_async_remote_copy(
            src_ref=full.at[rows] if src is None else src,
            dst_ref=full.at[rows],
            send_sem=self.send.at[i, SENT.index(how)],
            recv_sem=self.recv.at[i, GOT.index(got)],
            device_id=peer,
            device_id_type=MESH,
        )

    def wait(self, i, name):
        self.copy(i, "ox", name, self.p.sib, self.part(i, name)).wait_recv()

    def own_far(self, i):
        p, mine = self.p, self.part(i, "O")
        return [self.copy(i, "ox", "X", p.xnb, mine, self.shards[i]), self.copy(i, "oy", "Y", p.ynb, mine, self.shards[i])]

    def own_near(self, i):
        return self.copy(i, "os", "SO", self.p.sib, self.part(i, "O"), self.shards[i])

    def own_kept(self, i):
        return pltpu.make_async_copy(self.shards[i], self.fulls[i].at[self.part(i, "O")], self.own.at[i])

    def start(self, i):
        def far():
            for c in self.own_far(i):
                c.start()

        when(self.fetch[i], far)
        self.own_near(i).start()
        self.own_kept(i).start()

    def onward_far(self, i, name):
        p = self.p
        far = []
        if name == "X":
            far.append(self.copy(i, "fy", "D1", p.ynb, self.half(i, "X", 0)))
        if name == "Y":
            far.append(self.copy(i, "fx", "D2", p.xnb, self.half(i, "Y", 1)))
        if self.shared[i]:
            far.append(self.copy(i, "z" + name, name, self.znb, self.part(i, name)))
        return far

    def onward_near(self, i, name):
        to_sib = {"X": "SX", "Y": "SY", "D1": "S1", "D2": "S2"}[name]
        return self.copy(i, to_sib, to_sib, self.p.sib, self.part(i, name))

    def relay(self, i, names):
        for name in names:
            self.wait(i, name)

            def far(name=name):
                for c in self.onward_far(i, name):
                    c.start()

            if name in ("X", "Y") or self.shared[i]:
                when(self.fetch[i], far)
            self.onward_near(i, name).start()

    def arrive(self, i):
        for name in ("SO", "SX", "SY", "S1", "S2"):
            self.wait(i, name)
        self.own_kept(i).wait()

    def drain(self, i):
        self.own_near(i).wait_send()
        for name in ("X", "Y", "D1", "D2"):
            self.onward_near(i, name).wait_send()

        def far():
            for c in self.own_far(i):
                c.wait_send()
            for name in ("X", "Y", "D1", "D2"):
                for c in self.onward_far(i, name):
                    c.wait_send()

        when(self.fetch[i], far)

    def peers(self):
        return [self.p.sib, self.p.xnb, self.p.ynb, self.znb]


def rows_loop(total, body, step=16):
    @pl.loop(0, total // step)
    def _(k):
        body(pl.ds(pl.multiple_of(k * step, step), step))


def wide(value):
    return value.astype(jnp.float32)


class Reduce:
    def __init__(self, place, slots, sems):
        self.p = place
        self.slots = slots
        self.send, self.recv = sems
        z = place.z
        self.inner = (z == 1) | (z == 2)
        self.outer = (z == 0) | (z == 3)
        self.mine = jnp.where(z == 2, 1, 0)
        self.peer = place.level(jnp.where(self.inner, 3 - z, z))
        self.out = place.level(jnp.where(z < 2, 1 - z, 5 - z))

    def copy(self, i, tag, src, dst, peer, got=None):
        return pltpu.make_async_remote_copy(
            src_ref=src,
            dst_ref=dst,
            send_sem=self.send.at[i, tag],
            recv_sem=self.recv.at[i, tag if got is None else got],
            device_id=peer,
            device_id_type=MESH,
        )

    def to_sib(self, i, j, src, dst):
        return self.copy(i, j, src, dst, self.p.sib)

    def first(self, i):
        p, s = self.p, self.slots[i]
        return [
            self.copy(i, 4, s["a"].at[1 - p.x], s["xr"].at[0], p.xnb),
            self.copy(i, 5, s["a"].at[2 + 1 - p.x], s["xr"].at[1], p.xnb),
            self.copy(i, 6, s["b"].at[2 * (1 - p.y)], s["yr"].at[0], p.ynb),
            self.copy(i, 7, s["b"].at[2 * (1 - p.y) + 1], s["yr"].at[1], p.ynb),
        ]

    def second(self, i):
        p, s = self.p, self.slots[i]
        return [
            self.copy(i, 8, s["a"].at[2 * (1 - p.y) + p.x], s["yr2"], p.ynb),
            self.copy(i, 9, s["b"].at[2 * p.y + 1 - p.x], s["xr2"], p.xnb),
        ]

    def add_first(self, i):
        p, s = self.p, self.slots[i]
        n = s["n"]
        for k, cp in enumerate(self.first(i)):
            cp.wait_recv()
        for q in range(2):
            ja, jb = 2 * q + p.x, 2 * p.y + q

            def body(rows, q=q, ja=ja, jb=jb):
                s["a"][ja, rows, :] = (wide(s["a"][ja, rows, :]) + wide(s["xr"][q, rows, :])).astype(jnp.bfloat16)
                s["b"][jb, rows, :] = (wide(s["b"][jb, rows, :]) + wide(s["yr"][q, rows, :])).astype(jnp.bfloat16)

            rows_loop(n, body)
        for cp in self.second(i):
            cp.start()

    def up(self, i):
        s = self.slots[i]
        return [self.copy(i, 10 + k, s["u"].at[k], s["zo"].at[k], self.out) for k in range(2)]

    def across(self, i):
        s = self.slots[i]
        return self.copy(i, 12, s["u"].at[1 - self.mine], s["zp"], self.peer)

    def total_out(self, i):
        s = self.slots[i]
        res = s["res"].at[self.mine]
        return [self.copy(i, 13, res, res, self.out), self.copy(i, 14, res, res, self.peer)]

    def total_on(self, i):
        s = self.slots[i]
        res = s["res"].at[1 - self.mine]
        return self.copy(i, 15, res, res, self.out)

    def add_second(self, i):
        p, s = self.p, self.slots[i]
        me = 2 * p.y + p.x
        for cp in self.second(i):
            cp.wait_recv()

        def body(rows):
            s["u"][0, rows, :] = (wide(s["a"][me, rows, :]) + wide(s["yr2"][rows, :])).astype(jnp.bfloat16)
            s["u"][1, rows, :] = (wide(s["b"][me, rows, :]) + wide(s["xr2"][rows, :])).astype(jnp.bfloat16)

        rows_loop(s["n"], body)

        @pl.when(self.outer)
        def _():
            for cp in self.up(i):
                cp.start()

    def add_outer(self, i):
        s = self.slots[i]

        @pl.when(self.inner)
        def _():
            for cp in self.up(i):
                cp.wait_recv()

            def body(rows):
                for k in range(2):
                    s["u"][k, rows, :] = (wide(s["u"][k, rows, :]) + wide(s["zo"][k, rows, :])).astype(jnp.bfloat16)

            rows_loop(s["n"], body)
            self.across(i).start()

    def add_peer(self, i):
        s = self.slots[i]

        @pl.when(self.inner)
        def _():
            self.across(i).wait_recv()
            mine = self.mine

            def body(rows):
                s["res"][mine, rows, :] = (wide(s["u"][mine, rows, :]) + wide(s["zp"][rows, :])).astype(jnp.bfloat16)

            rows_loop(s["n"], body)
            for cp in self.total_out(i):
                cp.start()

    def pass_on(self, i):
        @pl.when(self.inner)
        def _():
            s = self.slots[i]
            other = s["res"].at[1 - self.mine]
            self.copy(i, 14, other, other, self.peer).wait_recv()
            self.total_on(i).start()

    def finish(self, i):
        s = self.slots[i]

        @pl.when(self.outer)
        def _():
            near = jnp.where(self.p.z == 3, 1, 0)
            self.copy(i, 13, s["res"].at[near], s["res"].at[near], self.out).wait_recv()
            self.copy(i, 15, s["res"].at[1 - near], s["res"].at[1 - near], self.out).wait_recv()
            for cp in self.up(i):
                cp.wait_send()

        @pl.when(self.inner)
        def _():
            for cp in [self.across(i), self.total_on(i)] + self.total_out(i):
                cp.wait_send()

        for cp in self.first(i) + self.second(i):
            cp.wait_send()

    def peers(self):
        p = self.p
        return [p.sib, p.xnb, p.ynb] + [p.level((p.z + d) % 4) for d in (1, 2, 3)]


class Small:
    def __init__(self, place, total, slots, sems):
        p = place
        self.total, self.slots = total, slots
        self.send, self.recv = sems
        z = p.z
        self.order = [p.sib, p.xnb, p.ynb, p.level(z + 1 - 2 * (z % 2)), p.level((z + 2) % 4)]

    def copy(self, k):
        return pltpu.make_async_remote_copy(
            src_ref=self.slots.at[0, k],
            dst_ref=self.slots.at[1, k],
            send_sem=self.send.at[k],
            recv_sem=self.recv.at[k],
            device_id=self.order[k],
            device_id_type=MESH,
        )

    def begin(self):
        self.slots[0, 0] = self.total[...]
        self.copy(0).start()

    def step(self, k):
        self.copy(k).wait_recv()
        both = self.slots[0, k] + self.slots[1, k]
        if k < 4:
            self.slots[0, k + 1] = both
            self.copy(k + 1).start()
        else:
            self.total[...] = both

    def drain(self):
        for k in range(5):
            self.copy(k).wait_send()


def gather_call(shards):
    kinds = (0, 2, 1, 0, 0, 1, 2, 0)
    count = len(shards)

    def kernel(*refs):
        ins, outs = refs[:count], refs[count : 2 * count]
        send, recv, own = refs[2 * count :]
        place = Place()
        gather = Gather(place, ins, outs, kinds, send, recv, own)
        meet(gather.peers())
        for i in range(3):
            gather.start(i)
        for i in range(count):
            gather.relay(i, ("X", "Y"))
            if i + 3 < count:
                gather.start(i + 3)
            if i >= 1:
                gather.relay(i - 1, ("D1", "D2"))
        gather.relay(count - 1, ("D1", "D2"))
        for i in range(count):
            gather.arrive(i)
            gather.drain(i)

    return pl.pallas_call(
        kernel,
        out_shape=[jax.ShapeDtypeStruct((8 * s.shape[0], s.shape[1]), s.dtype) for s in shards],
        in_specs=[pl.BlockSpec(memory_space=pl.ANY)] * count,
        out_specs=[pl.BlockSpec(memory_space=pl.ANY)] * count,
        scratch_shapes=[
            pltpu.SemaphoreType.DMA((count, len(SENT))),
            pltpu.SemaphoreType.DMA((count, len(GOT))),
            pltpu.SemaphoreType.DMA((count,)),
        ],
        compiler_params=pltpu.CompilerParams(collective_id=1, has_side_effects=True),
        name="gather_weights",
    )(*shards)


def slot_shapes(rows, columns):
    n, h = rows // 8, columns // 2
    bf = jnp.bfloat16
    return [
        ("a", pltpu.VMEM((4, n, h), bf)), ("b", pltpu.VMEM((4, n, h), bf)),
        ("xr", pltpu.VMEM((2, n, h), bf)), ("yr", pltpu.VMEM((2, n, h), bf)),
        ("yr2", pltpu.VMEM((n, h), bf)), ("xr2", pltpu.VMEM((n, h), bf)),
        ("u", pltpu.VMEM((2, n, h), bf)), ("zo", pltpu.VMEM((2, n, h), bf)),
        ("zp", pltpu.VMEM((n, h), bf)), ("res", pltpu.VMEM((2, n, h), bf)),
    ]


def reduce_call(partials, small):
    count = len(partials)
    shapes = [part.shape for part in partials]
    names = [name for name, _ in slot_shapes(*shapes[0])]

    def kernel(*refs):
        refs = list(refs)
        parts = refs[:count]
        small_in = refs[count]
        outs = refs[count + 1 : 2 * count + 1]
        small_out = refs[2 * count + 1]
        landed = refs[2 * count + 2 : 3 * count + 2]
        rest = refs[3 * count + 2 :]
        slots = []
        for i in range(count):
            s = dict(zip(names, rest[i * len(names) : (i + 1) * len(names)]))
            s["n"], s["h"] = shapes[i][0] // 8, shapes[i][1] // 2
            slots.append(s)
        send, recv, small_slots, small_send, small_recv, done = rest[count * len(names) :]
        place = Place()
        red = Reduce(place, slots, (send, recv))
        tot = Small(place, small_out, small_slots, (small_send, small_recv))
        meet(red.peers())
        small_out[...] = small_in[...]
        tot.begin()

        def block(i, j, core):
            n = slots[i]["n"]
            return pl.ds(pl.multiple_of((2 * j + core) * n, n), n)

        def sib(i, j):
            return red.to_sib(i, j, parts[i].at[block(i, j, 1 - place.core)], landed[i].at[j])

        for i in range(count):
            for j in range(4):
                sib(i, j).start()

        def fold(i):
            s = slots[i]
            n, h = s["n"], s["h"]
            for j in range(4):
                sib(i, j).wait_recv()

            def body(own, came):
                j = pl.program_id(0)

                def add(rows):
                    both = wide(own[rows, :]) + wide(came[rows, :])
                    s["a"][j, rows, :] = both[:, :h].astype(jnp.bfloat16)
                    s["b"][j, rows, :] = both[:, h:].astype(jnp.bfloat16)

                rows_loop(n, add)

            pltpu.emit_pipeline(
                body,
                grid=(4,),
                in_specs=[
                    pl.BlockSpec((n, 2 * h), lambda j: (2 * j + place.core, 0)),
                    pl.BlockSpec((None, n, 2 * h), lambda j: (j, 0, 0)),
                ],
            )(parts[i], landed[i])
            for cp in red.first(i):
                cp.start()

        def keep(i):
            red.finish(i)
            s = slots[i]
            return [
                pltpu.make_async_copy(s["res"].at[k], outs[i].at[:, pl.ds(k * s["h"], s["h"])], done.at[i, k]) for k in range(2)
            ]

        stages = [fold, red.add_first, red.add_second, red.add_outer, red.add_peer, red.pass_on]
        for t in range(count + len(stages) - 1):
            for k, stage in enumerate(stages):
                if 0 <= t - k < count:
                    stage(t - k)
            if t < 5:
                tot.step(t)
        copies = []
        for i in range(count):
            more = keep(i)
            for cp in more:
                cp.start()
            copies += more
            for j in range(4):
                sib(i, j).wait_send()
        for cp in copies:
            cp.wait()
        tot.drain()

    hbm = pl.BlockSpec(memory_space=pl.ANY)
    vmem = pl.BlockSpec(memory_space=pltpu.VMEM)
    bf = jnp.bfloat16
    result = pl.pallas_call(
        kernel,
        out_shape=[jax.ShapeDtypeStruct((r // 8, c), bf) for r, c in shapes]
        + [jax.ShapeDtypeStruct(small.shape, jnp.float32)]
        + [jax.ShapeDtypeStruct((4, r // 8, c), bf) for r, c in shapes],
        in_specs=[hbm] * count + [vmem],
        out_specs=[hbm] * count + [vmem] + [hbm] * count,
        scratch_shapes=[shape for r, c in shapes for _, shape in slot_shapes(r, c)]
        + [
            pltpu.SemaphoreType.DMA((count, 16)),
            pltpu.SemaphoreType.DMA((count, 16)),
            pltpu.VMEM((2, 5) + small.shape, jnp.float32),
            pltpu.SemaphoreType.DMA((5,)),
            pltpu.SemaphoreType.DMA((5,)),
            pltpu.SemaphoreType.DMA((count, 2)),
        ],
        compiler_params=pltpu.CompilerParams(collective_id=2, has_side_effects=True, vmem_limit_bytes=60 << 20),
        name="reduce_gradients",
    )(*partials, small)
    return result[:count], result[count]


def scan_call(decay, value, backward):
    rows, width = decay.shape
    lanes = 128
    segments, span, tiles = 8, rows // 8, width // lanes

    def kernel(decay_ref, value_ref, prod_ref, sum_ref):
        def step(k, carry):
            prod, total = carry
            t = span - 1 - k if backward else k
            spot = pl.ds(t, segments, stride=span)
            new_prod, new_total = [], []
            for c in range(tiles):
                d = decay_ref[c, spot, :]
                new_prod.append(prod[c] * d)
                new_total.append(total[c] * d + value_ref[c, spot, :])
                prod_ref[c, spot, :] = new_prod[c]
                sum_ref[c, spot, :] = new_total[c]
            return new_prod, new_total

        ones = [jnp.ones((segments, lanes), jnp.float32)] * tiles
        zeros = [jnp.zeros((segments, lanes), jnp.float32)] * tiles
        lax.fori_loop(0, span, step, (ones, zeros), unroll=2)
        order = list(range(segments))[::-1] if backward else list(range(segments))
        edge = order[0] * span + (0 if backward else span - 1)
        for seg in order[1:]:
            base = seg * span
            for c in range(tiles):
                prod, total = prod_ref[c, edge : edge + 1, :], sum_ref[c, edge : edge + 1, :]
                here = prod_ref[c, base : base + span, :]
                sum_ref[c, base : base + span, :] = sum_ref[c, base : base + span, :] + here * total
                prod_ref[c, base : base + span, :] = here * prod
            edge = base + (0 if backward else span - 1)

    shape = jax.ShapeDtypeStruct((tiles, rows, lanes), jnp.float32)
    fold = lambda v: v.reshape(rows, tiles, lanes).transpose(1, 0, 2)
    out = pl.pallas_call(
        kernel,
        out_shape=[shape, shape],
        compiler_params=pltpu.CompilerParams(vmem_limit_bytes=48 << 20),
        name="scan_rows",
    )(fold(decay), fold(value))
    return [v.transpose(1, 0, 2).reshape(rows, width) for v in out]


def local(
    tokens,
    lengths,
    mixer_gain,
    gelu_weight,
    input_weight,
    conv_taps,
    conv_bias,
    rgate_weight,
    rgate_bias,
    igate_weight,
    igate_bias,
    decay_param,
    output_weight,
    mlp_gain,
    mlp_gate,
    mlp_value,
    mlp_down,
    cotangent,
):
    count = tokens.shape[0]
    width_lru = input_weight.shape[1]
    block = rgate_weight.shape[1]
    heads = width_lru // block
    taps_count = conv_taps.shape[1]
    rim = taps_count - 1
    seq_count = lax.axis_size("seq")
    slot_length = count * seq_count
    first_row = (lax.axis_index("grp") * seq_count + lax.axis_index("seq")) * count
    global_row = first_row + jnp.arange(count, dtype=jnp.int32)
    position = global_row % slot_length
    slot_of = global_row // slot_length
    slot_ids = jnp.arange(lengths.shape[0], dtype=jnp.int32)
    slot_len = jnp.sum(
        jnp.where(slot_of[:, None] == slot_ids[None, :], lengths[None, :], 0), axis=1
    )
    valid = (position < slot_len).astype(jnp.float32)[:, None]
    starts = (position > 0).astype(jnp.float32)[:, None]
    lag_masks = [(position >= lag).astype(jnp.float32)[:, None] for lag in range(taps_count)]
    zeros_lru = jnp.zeros((width_lru,), jnp.float32)
    ones_lru = jnp.ones((width_lru,), jnp.float32)
    (
        gain_one,
        gelu_full,
        input_full,
        taps_full,
        cbias_full,
        rgate_full,
        rbias_full,
        igate_full,
        ibias_full,
        decay_full,
        output_full,
        gain_two,
        mgate_full,
        mvalue_full,
        mdown_full,
    ) = (
        lax.all_gather(mixer_gain, "seq", axis=0, tiled=True),
        lax.all_gather(gelu_weight, "seq", axis=0, tiled=True),
        lax.all_gather(input_weight, "seq", axis=0, tiled=True),
        lax.all_gather(conv_taps, "seq", axis=0, tiled=True),
        lax.all_gather(conv_bias, "seq", axis=0, tiled=True),
        lax.all_gather(rgate_weight, "seq", axis=0, tiled=True),
        lax.all_gather(rgate_bias, "seq", axis=0, tiled=True),
        lax.all_gather(igate_weight, "seq", axis=0, tiled=True),
        lax.all_gather(igate_bias, "seq", axis=0, tiled=True),
        lax.all_gather(decay_param, "seq", axis=0, tiled=True),
        lax.all_gather(output_weight, "seq", axis=0, tiled=True),
        lax.all_gather(mlp_gain, "seq", axis=0, tiled=True),
        lax.all_gather(mlp_gate, "seq", axis=0, tiled=True),
        lax.all_gather(mlp_value, "seq", axis=0, tiled=True),
        lax.all_gather(mlp_down, "seq", axis=0, tiled=True),
    )
    inputs = tokens.astype(jnp.float32)
    normed_one, norm_one_back = jax.vjp(rms_norm, inputs, gain_one.astype(jnp.float32))
    normed_one = normed_one.astype(jnp.bfloat16)
    gate_pre = matmul(normed_one, gelu_full)
    gate_act, gate_back = jax.vjp(gelu_tanh, gate_pre)
    linear = matmul(normed_one, input_full)
    rim_in = passed_along(linear[count - rim :], "seq", 1)
    extended = jnp.concatenate([rim_in, linear], axis=0)
    taps_fwd = taps_full.astype(jnp.float32)
    conv = cbias_full.astype(jnp.float32) + taps_fwd[:, 0] * linear
    for lag in range(1, taps_count):
        conv = conv + taps_fwd[:, lag] * (extended[rim - lag : rim - lag + count] * lag_masks[lag])
    conv_low = conv.astype(jnp.bfloat16)
    conv_value = conv_low.astype(jnp.float32)
    rgate_pre = block_apply(conv_low, rgate_full, heads) + rbias_full.astype(jnp.float32)
    igate_pre = block_apply(conv_low, igate_full, heads) + ibias_full.astype(jnp.float32)
    (decay, inject), gates_back = jax.vjp(
        recurrence_gates, rgate_pre, igate_pre, conv_value, decay_full.astype(jnp.float32)
    )
    decay_used = decay * starts
    cum_decay, state_zero = lax.associative_scan(chain_combine, (decay_used, inject), axis=0)
    scanned = carried_in(
        (cum_decay[-1], state_zero[-1]), "seq", chain_combine, (ones_lru, zeros_lru), False
    )
    carry_in = scanned[1]
    state = state_zero + cum_decay * carry_in
    mixed_rec = (state * gate_act).astype(jnp.bfloat16)
    resid = inputs + matmul(mixed_rec, output_full)
    normed_two, norm_two_back = jax.vjp(rms_norm, resid, gain_two.astype(jnp.float32))
    normed_two = normed_two.astype(jnp.bfloat16)
    mgate_pre = matmul(normed_two, mgate_full)
    mvalue_pre = matmul(normed_two, mvalue_full)
    mgate_act, mgate_back = jax.vjp(gelu_tanh, mgate_pre)
    hidden = (mgate_act * mvalue_pre).astype(jnp.bfloat16)
    mixed = ((resid + matmul(hidden, mdown_full)) * valid).astype(jnp.bfloat16)
    (
        gain_one,
        gelu_full,
        input_full,
        taps_full,
        cbias_full,
        rgate_full,
        rbias_full,
        igate_full,
        ibias_full,
        decay_full,
        output_full,
        gain_two,
        mgate_full,
        mvalue_full,
        mdown_full,
    ) = (
        lax.all_gather(mixer_gain, "seq", axis=0, tiled=True),
        lax.all_gather(gelu_weight, "seq", axis=0, tiled=True),
        lax.all_gather(input_weight, "seq", axis=0, tiled=True),
        lax.all_gather(conv_taps, "seq", axis=0, tiled=True),
        lax.all_gather(conv_bias, "seq", axis=0, tiled=True),
        lax.all_gather(rgate_weight, "seq", axis=0, tiled=True),
        lax.all_gather(rgate_bias, "seq", axis=0, tiled=True),
        lax.all_gather(igate_weight, "seq", axis=0, tiled=True),
        lax.all_gather(igate_bias, "seq", axis=0, tiled=True),
        lax.all_gather(decay_param, "seq", axis=0, tiled=True),
        lax.all_gather(output_weight, "seq", axis=0, tiled=True),
        lax.all_gather(mlp_gain, "seq", axis=0, tiled=True),
        lax.all_gather(mlp_gate, "seq", axis=0, tiled=True),
        lax.all_gather(mlp_value, "seq", axis=0, tiled=True),
        lax.all_gather(mlp_down, "seq", axis=0, tiled=True),
    )
    taps_back = taps_full.astype(jnp.float32)
    grad_out = cotangent.astype(jnp.float32) * valid
    grad_out_low = grad_out.astype(jnp.bfloat16)
    down_grad = inner_rows(hidden, grad_out_low)
    grad_hidden = outer_cols(grad_out_low, mdown_full)
    grad_mgate = mgate_back(grad_hidden * mvalue_pre)[0].astype(jnp.bfloat16)
    grad_mvalue = (grad_hidden * mgate_act).astype(jnp.bfloat16)
    mgate_grad = inner_rows(normed_two, grad_mgate)
    mvalue_grad = inner_rows(normed_two, grad_mvalue)
    grad_ntwo = outer_cols(grad_mgate, mgate_full) + outer_cols(grad_mvalue, mvalue_full)
    grad_resid_norm, gain_two_grad = norm_two_back(grad_ntwo)
    grad_resid = grad_out + grad_resid_norm
    grad_mix = grad_resid.astype(jnp.bfloat16)
    output_grad = inner_rows(mixed_rec, grad_mix)
    grad_rec = outer_cols(grad_mix, output_full)
    grad_state = grad_rec * gate_act
    grad_gate = gate_back(grad_rec * state)[0].astype(jnp.bfloat16)
    decay_next = jnp.concatenate([decay_used[1:], jnp.ones((1, width_lru), jnp.float32)], axis=0)
    rev_prod, rev_adjoint = lax.associative_scan(
        chain_combine, (jnp.flip(decay_next, 0), jnp.flip(grad_state, 0)), axis=0
    )
    tail_prod = jnp.flip(rev_prod, 0)
    adjoint_zero = jnp.flip(rev_adjoint, 0)
    summary_decay = decay_used[0] * tail_prod[0]
    summary_adjoint = decay_used[0] * adjoint_zero[0]
    scanned_back = carried_in(
        (summary_decay, summary_adjoint), "seq", chain_combine, (ones_lru, zeros_lru), True
    )
    incoming = scanned_back[1]
    adjoint = adjoint_zero + tail_prod * incoming
    state_prev = jnp.concatenate([carry_in[None, :], state[:-1]], axis=0)
    grad_decay = adjoint * state_prev * starts
    grad_rpre, grad_ipre, grad_direct, decay_grad = gates_back((grad_decay, adjoint))
    rbias_grad = jnp.sum(grad_rpre, axis=0)
    ibias_grad = jnp.sum(grad_ipre, axis=0)
    grad_rlow = grad_rpre.astype(jnp.bfloat16)
    grad_ilow = grad_ipre.astype(jnp.bfloat16)
    rgate_grad = block_grad(conv_low, grad_rlow, heads)
    igate_grad = block_grad(conv_low, grad_ilow, heads)
    grad_conv = (
        grad_direct
        + block_back(grad_rlow, rgate_full, heads)
        + block_back(grad_ilow, igate_full, heads)
    )
    cbias_grad = jnp.sum(grad_conv, axis=0)
    taps_columns = []
    grad_extended = jnp.zeros((count + rim, width_lru), jnp.float32)
    for lag in range(taps_count):
        masked_term = grad_conv * lag_masks[lag]
        taps_columns.append(jnp.sum(masked_term * extended[rim - lag : rim - lag + count], axis=0))
        grad_extended = grad_extended + jnp.pad(
            taps_back[:, lag] * masked_term, ((rim - lag, lag), (0, 0))
        )
    taps_grad = jnp.stack(taps_columns, axis=1)
    rim_back = passed_along(grad_extended[:rim], "seq", -1)
    grad_linear = grad_extended[rim:] + jnp.pad(rim_back, ((count - rim, 0), (0, 0)))
    grad_lin = grad_linear.astype(jnp.bfloat16)
    input_grad = inner_rows(normed_one, grad_lin)
    gelu_grad = inner_rows(normed_one, grad_gate)
    grad_none = outer_cols(grad_lin, input_full) + outer_cols(grad_gate, gelu_full)
    grad_inputs_norm, gain_one_grad = norm_one_back(grad_none)
    tokens_grad = grad_resid + grad_inputs_norm
    partials = (
        gain_one_grad,
        gelu_grad,
        input_grad,
        taps_grad,
        cbias_grad,
        rgate_grad,
        rbias_grad,
        igate_grad,
        ibias_grad,
        decay_grad,
        output_grad,
        gain_two_grad,
        mgate_grad,
        mvalue_grad,
        down_grad,
    )
    summed_seq = (
        lax.psum_scatter(partials[0], "seq", scatter_dimension=0, tiled=True),
        lax.psum_scatter(partials[1], "seq", scatter_dimension=0, tiled=True),
        lax.psum_scatter(partials[2], "seq", scatter_dimension=0, tiled=True),
        lax.psum_scatter(partials[3], "seq", scatter_dimension=0, tiled=True),
        lax.psum_scatter(partials[4], "seq", scatter_dimension=0, tiled=True),
        lax.psum_scatter(partials[5], "seq", scatter_dimension=0, tiled=True),
        lax.psum_scatter(partials[6], "seq", scatter_dimension=0, tiled=True),
        lax.psum_scatter(partials[7], "seq", scatter_dimension=0, tiled=True),
        lax.psum_scatter(partials[8], "seq", scatter_dimension=0, tiled=True),
        lax.psum_scatter(partials[9], "seq", scatter_dimension=0, tiled=True),
        lax.psum_scatter(partials[10], "seq", scatter_dimension=0, tiled=True),
        lax.psum_scatter(partials[11], "seq", scatter_dimension=0, tiled=True),
        lax.psum_scatter(partials[12], "seq", scatter_dimension=0, tiled=True),
        lax.psum_scatter(partials[13], "seq", scatter_dimension=0, tiled=True),
        lax.psum_scatter(partials[14], "seq", scatter_dimension=0, tiled=True),
    )
    totals = lax.psum(tuple(summed_seq), "grp")
    return (
        mixed,
        tokens_grad,
        totals[0],
        totals[1],
        totals[2],
        totals[3],
        totals[4],
        totals[5],
        totals[6],
        totals[7],
        totals[8],
        totals[9],
        totals[10],
        totals[11],
        totals[12],
        totals[13],
        totals[14],
    )


def local_fast(
    tokens,
    lengths,
    mixer_gain,
    gelu_weight,
    input_weight,
    conv_taps,
    conv_bias,
    rgate_weight,
    rgate_bias,
    igate_weight,
    igate_bias,
    decay_param,
    output_weight,
    mlp_gain,
    mlp_gate,
    mlp_value,
    mlp_down,
    cotangent,
):
    count = tokens.shape[0]
    width_lru = input_weight.shape[1]
    block = rgate_weight.shape[1]
    heads = width_lru // block
    taps_count = conv_taps.shape[1]
    rim = taps_count - 1
    seq_count = lax.axis_size("seq")
    slot_length = count * seq_count
    first_row = (lax.axis_index("grp") * seq_count + lax.axis_index("seq")) * count
    global_row = first_row + jnp.arange(count, dtype=jnp.int32)
    position = global_row % slot_length
    slot_of = global_row // slot_length
    slot_ids = jnp.arange(lengths.shape[0], dtype=jnp.int32)
    slot_len = jnp.sum(
        jnp.where(slot_of[:, None] == slot_ids[None, :], lengths[None, :], 0), axis=1
    )
    valid = (position < slot_len).astype(jnp.float32)[:, None]
    starts = (position > 0).astype(jnp.float32)[:, None]
    lag_masks = [(position >= lag).astype(jnp.float32)[:, None] for lag in range(taps_count)]
    zeros_lru = jnp.zeros((width_lru,), jnp.float32)
    ones_lru = jnp.ones((width_lru,), jnp.float32)
    lru_rows = jnp.concatenate(
        [conv_taps.T, conv_bias[None], rgate_bias[None], igate_bias[None], decay_param[None]], axis=0
    ).astype(jnp.float32)
    model_rows = jnp.stack([mixer_gain, mlp_gain]).astype(jnp.float32)
    mine = lax.axis_index("seq")
    small = jnp.zeros((16, width_lru), jnp.float32)
    small = lax.dynamic_update_slice(small, lru_rows, (0, mine * lru_rows.shape[1]))
    small = lax.dynamic_update_slice(small, model_rows, (8, mine * model_rows.shape[1]))
    gathered = gather_call(
        [small, gelu_weight, input_weight, jnp.concatenate([rgate_weight, igate_weight], axis=1), output_weight, mlp_gate, mlp_value, mlp_down]
    )
    small_full = gathered[0].reshape(seq_count, 16, width_lru).sum(axis=0)
    gelu_full, input_full, gates_full, output_full, mgate_full, mvalue_full, mdown_full = gathered[1:]
    rgate_full, igate_full = gates_full[:, :block], gates_full[:, block:]
    taps_full = small_full[:4].T
    cbias_full, rbias_full, ibias_full, decay_full = small_full[4], small_full[5], small_full[6], small_full[7]
    gain_one, gain_two = small_full[8, : tokens.shape[1]], small_full[9, : tokens.shape[1]]
    inputs = tokens.astype(jnp.float32)
    normed_one, norm_one_back = jax.vjp(rms_norm, inputs, gain_one.astype(jnp.float32))
    normed_one = normed_one.astype(jnp.bfloat16)
    gate_pre = matmul(normed_one, gelu_full)
    gate_act, gate_back = jax.vjp(gelu_tanh, gate_pre)
    linear = matmul(normed_one, input_full)
    rim_in = passed_along(linear[count - rim :], "seq", 1)
    extended = jnp.concatenate([rim_in, linear], axis=0)
    taps_fwd = taps_full.astype(jnp.float32)
    conv = cbias_full.astype(jnp.float32) + taps_fwd[:, 0] * linear
    for lag in range(1, taps_count):
        conv = conv + taps_fwd[:, lag] * (extended[rim - lag : rim - lag + count] * lag_masks[lag])
    conv_low = conv.astype(jnp.bfloat16)
    conv_value = conv_low.astype(jnp.float32)
    rgate_pre = block_apply(conv_low, rgate_full, heads) + rbias_full.astype(jnp.float32)
    igate_pre = block_apply(conv_low, igate_full, heads) + ibias_full.astype(jnp.float32)
    (decay, inject), gates_back = jax.vjp(
        recurrence_gates, rgate_pre, igate_pre, conv_value, decay_full.astype(jnp.float32)
    )
    decay_used = decay * starts
    cum_decay, state_zero = scan_call(decay_used, inject, False)
    scanned = carried_in(
        (cum_decay[-1], state_zero[-1]), "seq", chain_combine, (ones_lru, zeros_lru), False
    )
    carry_in = scanned[1]
    state = state_zero + cum_decay * carry_in
    mixed_rec = (state * gate_act).astype(jnp.bfloat16)
    resid = inputs + matmul(mixed_rec, output_full)
    normed_two, norm_two_back = jax.vjp(rms_norm, resid, gain_two.astype(jnp.float32))
    normed_two = normed_two.astype(jnp.bfloat16)
    mgate_pre = matmul(normed_two, mgate_full)
    mvalue_pre = matmul(normed_two, mvalue_full)
    mgate_act, mgate_back = jax.vjp(gelu_tanh, mgate_pre)
    hidden = (mgate_act * mvalue_pre).astype(jnp.bfloat16)
    mixed = ((resid + matmul(hidden, mdown_full)) * valid).astype(jnp.bfloat16)
    taps_back = taps_full.astype(jnp.float32)
    grad_out = cotangent.astype(jnp.float32) * valid
    grad_out_low = grad_out.astype(jnp.bfloat16)
    down_grad = inner_rows(hidden, grad_out_low)
    grad_hidden = outer_cols(grad_out_low, mdown_full)
    grad_mgate = mgate_back(grad_hidden * mvalue_pre)[0].astype(jnp.bfloat16)
    grad_mvalue = (grad_hidden * mgate_act).astype(jnp.bfloat16)
    mgate_grad = inner_rows(normed_two, grad_mgate)
    mvalue_grad = inner_rows(normed_two, grad_mvalue)
    grad_ntwo = outer_cols(grad_mgate, mgate_full) + outer_cols(grad_mvalue, mvalue_full)
    grad_resid_norm, gain_two_grad = norm_two_back(grad_ntwo)
    grad_resid = grad_out + grad_resid_norm
    grad_mix = grad_resid.astype(jnp.bfloat16)
    output_grad = inner_rows(mixed_rec, grad_mix)
    grad_rec = outer_cols(grad_mix, output_full)
    grad_state = grad_rec * gate_act
    grad_gate = gate_back(grad_rec * state)[0].astype(jnp.bfloat16)
    decay_next = jnp.concatenate([decay_used[1:], jnp.ones((1, width_lru), jnp.float32)], axis=0)
    tail_prod, adjoint_zero = scan_call(decay_next, grad_state, True)
    summary_decay = decay_used[0] * tail_prod[0]
    summary_adjoint = decay_used[0] * adjoint_zero[0]
    scanned_back = carried_in(
        (summary_decay, summary_adjoint), "seq", chain_combine, (ones_lru, zeros_lru), True
    )
    incoming = scanned_back[1]
    adjoint = adjoint_zero + tail_prod * incoming
    state_prev = jnp.concatenate([carry_in[None, :], state[:-1]], axis=0)
    grad_decay = adjoint * state_prev * starts
    grad_rpre, grad_ipre, grad_direct, decay_grad = gates_back((grad_decay, adjoint))
    rbias_grad = jnp.sum(grad_rpre, axis=0)
    ibias_grad = jnp.sum(grad_ipre, axis=0)
    grad_rlow = grad_rpre.astype(jnp.bfloat16)
    grad_ilow = grad_ipre.astype(jnp.bfloat16)
    rgate_grad = block_grad(conv_low, grad_rlow, heads)
    igate_grad = block_grad(conv_low, grad_ilow, heads)
    grad_conv = (
        grad_direct
        + block_back(grad_rlow, rgate_full, heads)
        + block_back(grad_ilow, igate_full, heads)
    )
    cbias_grad = jnp.sum(grad_conv, axis=0)
    taps_columns = []
    grad_extended = jnp.zeros((count + rim, width_lru), jnp.float32)
    for lag in range(taps_count):
        masked_term = grad_conv * lag_masks[lag]
        taps_columns.append(jnp.sum(masked_term * extended[rim - lag : rim - lag + count], axis=0))
        grad_extended = grad_extended + jnp.pad(
            taps_back[:, lag] * masked_term, ((rim - lag, lag), (0, 0))
        )
    taps_grad = jnp.stack(taps_columns, axis=1)
    rim_back = passed_along(grad_extended[:rim], "seq", -1)
    grad_linear = grad_extended[rim:] + jnp.pad(rim_back, ((count - rim, 0), (0, 0)))
    grad_lin = grad_linear.astype(jnp.bfloat16)
    input_grad = inner_rows(normed_one, grad_lin)
    gelu_grad = inner_rows(normed_one, grad_gate)
    grad_none = outer_cols(grad_lin, input_full) + outer_cols(grad_gate, gelu_full)
    grad_inputs_norm, gain_one_grad = norm_one_back(grad_none)
    tokens_grad = grad_resid + grad_inputs_norm
    low = lambda value: value.astype(jnp.bfloat16)
    lru_out = jnp.concatenate([taps_grad.T, cbias_grad[None], rbias_grad[None], ibias_grad[None], decay_grad[None]], axis=0)
    model_out = jnp.stack([gain_one_grad, gain_two_grad])
    small_part = jnp.concatenate(
        [lru_out, jnp.pad(model_out, ((0, 6), (0, width_lru - model_out.shape[1])))], axis=0
    )
    big, small_sum = reduce_call(
        [
            low(down_grad), low(mgate_grad), low(mvalue_grad), low(output_grad),
            jnp.concatenate([low(rgate_grad), low(igate_grad)], axis=1), low(input_grad), low(gelu_grad),
        ],
        small_part,
    )
    down, mgate, mvalue, out_w, gates, input_w, gelu_w = [value.astype(jnp.float32) for value in big]
    lru_own = lax.dynamic_slice(small_sum, (0, mine * conv_bias.shape[0]), (8, conv_bias.shape[0]))
    model_own = lax.dynamic_slice(small_sum, (8, mine * mixer_gain.shape[0]), (2, mixer_gain.shape[0]))
    return (
        mixed,
        tokens_grad,
        model_own[0],
        gelu_w,
        input_w,
        lru_own[:4].T,
        lru_own[4],
        gates[:, :block],
        lru_own[5],
        gates[:, block:],
        lru_own[6],
        lru_own[7],
        out_w,
        model_own[1],
        mgate,
        mvalue,
        down,
    )


def solution(mesh):
    placed = (
        P(("grp", "seq"), None),
        P(),
        P("seq"),
        P("seq", None),
        P("seq", None),
        P("seq", None),
        P("seq"),
        P("seq", None),
        P("seq"),
        P("seq", None),
        P("seq"),
        P("seq"),
        P("seq", None),
        P("seq"),
        P("seq", None),
        P("seq", None),
        P("seq", None),
        P(("grp", "seq"), None),
    )
    fits = mesh.shape["grp"] == 4 and mesh.shape["seq"] == 8
    return jax.shard_map(
        local_fast if fits else local,
        mesh=mesh,
        in_specs=placed,
        out_specs=(
            P(("grp", "seq"), None),
            P(("grp", "seq"), None),
            P("seq"),
            P("seq", None),
            P("seq", None),
            P("seq", None),
            P("seq"),
            P("seq", None),
            P("seq"),
            P("seq", None),
            P("seq"),
            P("seq"),
            P("seq", None),
            P("seq"),
            P("seq", None),
            P("seq", None),
            P("seq", None),
        ),
        check_vma=False,
    )
```

```python
import math
from types import SimpleNamespace

import jax
import jax.numpy as jnp
from jax import lax
from jax.experimental import pallas as pl
from jax.experimental.pallas import tpu as pltpu
from jax.sharding import PartitionSpec as P

epsilon = 1e-06
cfactor = 8.0


def passed_along(value, axis, steps):
    count = lax.axis_size(axis)
    leading, last = (max(0, -steps), min(count, count - steps))
    return lax.ppermute(value, axis, [(source, source + steps) for source in range(leading, last)])


def carried_in(value, axis, join, neutral, backward):
    count, mine = (lax.axis_size(axis), lax.axis_index(axis))
    pieces = jax.tree.map(lambda part: lax.all_gather(part, axis), value)
    if backward:
        pieces = jax.tree.map(lambda part: part[::-1], pieces)
        mine = count - 1 - mine
    so_far = jax.tree.map(
        lambda part, zero: jnp.full_like(part, 0) + jnp.asarray(zero, part.dtype), value, neutral
    )

    def step(position, so_far):
        longer = join(so_far, jax.tree.map(lambda part: part[position], pieces))
        return jax.tree.map(lambda new, old: jnp.where(position < mine, new, old), longer, so_far)

    return lax.fori_loop(0, count - 1, step, so_far)


def rms_norm(rows_in, gain):
    return rows_in * lax.rsqrt(jnp.mean(rows_in * rows_in, axis=-1, keepdims=True) + epsilon) * gain


def gelu_tanh(values):
    return jax.nn.gelu(values, approximate=True)


def matmul(left, right):
    return jnp.dot(left, right, preferred_element_type=jnp.float32)


def inner_rows(left, right):
    return lax.dot_general(
        left, right, (((0,), (0,)), ((), ())), preferred_element_type=jnp.float32
    )


def outer_cols(left, right):
    return lax.dot_general(
        left, right, (((1,), (1,)), ((), ())), preferred_element_type=jnp.float32
    )


def block_apply(values, weight, heads):
    count = values.shape[0]
    width = weight.shape[1]
    parts = values.reshape(count, heads, width)
    blocks = weight.reshape(heads, width, width)
    return jnp.einsum("rhi,hij->rhj", parts, blocks, preferred_element_type=jnp.float32).reshape(
        count, heads * width
    )


def block_back(grads, weight, heads):
    count = grads.shape[0]
    width = weight.shape[1]
    parts = grads.reshape(count, heads, width)
    blocks = weight.reshape(heads, width, width)
    return jnp.einsum("rhj,hij->rhi", parts, blocks, preferred_element_type=jnp.float32).reshape(
        count, heads * width
    )


def block_grad(values, grads, heads):
    count = values.shape[0]
    width = values.shape[1] // heads
    left = values.reshape(count, heads, width)
    right = grads.reshape(count, heads, width)
    return jnp.einsum("rhi,rhj->hij", left, right, preferred_element_type=jnp.float32).reshape(
        heads * width, width
    )


def chain_combine(earlier, later):
    return (earlier[0] * later[0], later[0] * earlier[1] + later[1])


def recurrence_gates(rgate_pre, igate_pre, conv_in, decay_in):
    rgate = jax.nn.sigmoid(rgate_pre)
    igate = jax.nn.sigmoid(igate_pre)
    log_decay = -cfactor * jax.nn.softplus(-decay_in) * rgate
    return (jnp.exp(log_decay), jnp.sqrt(-jnp.expm1(2.0 * log_decay)) * igate * conv_in)


MESH = pl.DeviceIdType.MESH


class Place:
    def __init__(self):
        self.z = lax.axis_index("grp")
        seq = lax.axis_index("seq")
        self.core = seq % 2
        self.x = (seq // 2) % 2
        self.y = seq // 4
        self.seq = seq
        self.sib = (self.z, self.at(self.y, self.x, 1 - self.core))
        self.xnb = (self.z, self.at(self.y, 1 - self.x, self.core))
        self.ynb = (self.z, self.at(1 - self.y, self.x, self.core))

    def at(self, y, x, core):
        return (y * 2 + x) * 2 + core

    def level(self, z):
        return (z, self.seq)


def meet(peers):
    barrier = pltpu.get_barrier_semaphore()
    for peer in peers:
        pl.semaphore_signal(barrier, inc=1, device_id=peer, device_id_type=MESH)
    pl.semaphore_wait(barrier, len(peers))


def when(cond, body):
    if cond is None:
        body()
    else:
        pl.when(cond)(body)


GOT = ("X", "Y", "D1", "D2", "SO", "SX", "SY", "S1", "S2")
SENT = ("ox", "oy", "os", "fy", "fx", "zX", "zY", "zD1", "zD2", "SX", "SY", "S1", "S2")


class Gather:
    def __init__(self, place, shards, fulls, kinds, send, recv, own):
        self.p, self.shards, self.fulls = place, shards, fulls
        self.send, self.recv, self.own = send, recv, own
        even = place.z % 2 == 0
        odd = place.z % 2 == 1
        self.fetch = [(None, even, odd)[kind] for kind in kinds]
        self.shared = [kind > 0 for kind in kinds]
        self.znb = place.level(place.z + 1 - 2 * (place.z % 2))

    def part(self, i, name):
        p = self.p
        n = self.shards[i].shape[0]
        spot = {
            "O": (p.y, p.x, p.core), "X": (p.y, 1 - p.x, p.core), "Y": (1 - p.y, p.x, p.core),
            "D1": (1 - p.y, 1 - p.x, p.core), "D2": (1 - p.y, 1 - p.x, p.core),
            "SO": (p.y, p.x, 1 - p.core), "SX": (p.y, 1 - p.x, 1 - p.core), "SY": (1 - p.y, p.x, 1 - p.core),
            "S1": (1 - p.y, 1 - p.x, 1 - p.core), "S2": (1 - p.y, 1 - p.x, 1 - p.core),
        }[name]
        first = pl.multiple_of(p.at(*spot) * n, n)
        if name in ("D1", "S1"):
            return pl.ds(first, n // 2)
        if name in ("D2", "S2"):
            return pl.ds(pl.multiple_of(first + n // 2, n // 2), n // 2)
        return pl.ds(first, n)

    def half(self, i, name, which):
        n = self.shards[i].shape[0]
        first = self.part(i, name).start
        return pl.ds(pl.multiple_of(first + which * (n // 2), n // 2), n // 2)

    def copy(self, i, how, got, peer, rows, src=None):
        full = self.fulls[i]
        return pltpu.make_async_remote_copy(
            src_ref=full.at[rows] if src is None else src,
            dst_ref=full.at[rows],
            send_sem=self.send.at[i, SENT.index(how)],
            recv_sem=self.recv.at[i, GOT.index(got)],
            device_id=peer,
            device_id_type=MESH,
        )

    def wait(self, i, name):
        self.copy(i, "ox", name, self.p.sib, self.part(i, name)).wait_recv()

    def own_far(self, i):
        p, mine = self.p, self.part(i, "O")
        return [self.copy(i, "ox", "X", p.xnb, mine, self.shards[i]), self.copy(i, "oy", "Y", p.ynb, mine, self.shards[i])]

    def own_near(self, i):
        return self.copy(i, "os", "SO", self.p.sib, self.part(i, "O"), self.shards[i])

    def own_kept(self, i):
        return pltpu.make_async_copy(self.shards[i], self.fulls[i].at[self.part(i, "O")], self.own.at[i])

    def start(self, i):
        def far():
            for c in self.own_far(i):
                c.start()

        when(self.fetch[i], far)
        self.own_near(i).start()
        self.own_kept(i).start()

    def onward_far(self, i, name):
        p = self.p
        far = []
        if name == "X":
            far.append(self.copy(i, "fy", "D1", p.ynb, self.half(i, "X", 0)))
        if name == "Y":
            far.append(self.copy(i, "fx", "D2", p.xnb, self.half(i, "Y", 1)))
        if self.shared[i]:
            far.append(self.copy(i, "z" + name, name, self.znb, self.part(i, name)))
        return far

    def onward_near(self, i, name):
        to_sib = {"X": "SX", "Y": "SY", "D1": "S1", "D2": "S2"}[name]
        return self.copy(i, to_sib, to_sib, self.p.sib, self.part(i, name))

    def relay(self, i, names):
        for name in names:
            self.wait(i, name)

            def far(name=name):
                for c in self.onward_far(i, name):
                    c.start()

            if name in ("X", "Y") or self.shared[i]:
                when(self.fetch[i], far)
            self.onward_near(i, name).start()

    def arrive(self, i):
        for name in ("SO", "SX", "SY", "S1", "S2"):
            self.wait(i, name)
        self.own_kept(i).wait()

    def drain(self, i):
        self.own_near(i).wait_send()
        for name in ("X", "Y", "D1", "D2"):
            self.onward_near(i, name).wait_send()

        def far():
            for c in self.own_far(i):
                c.wait_send()
            for name in ("X", "Y", "D1", "D2"):
                for c in self.onward_far(i, name):
                    c.wait_send()

        when(self.fetch[i], far)

    def peers(self):
        return [self.p.sib, self.p.xnb, self.p.ynb, self.znb]


def rows_loop(total, body, step=16):
    @pl.loop(0, total // step)
    def _(k):
        body(pl.ds(pl.multiple_of(k * step, step), step))


def wide(value):
    return value.astype(jnp.float32)

class Reduce:
    def __init__(self, place, slots, sems):
        self.p = place
        self.slots = slots
        self.send, self.recv = sems
        z = place.z
        self.inner = (z == 1) | (z == 2)
        self.outer = (z == 0) | (z == 3)
        self.mine = jnp.where(z == 2, 1, 0)
        self.peer = place.level(jnp.where(self.inner, 3 - z, z))
        self.out = place.level(jnp.where(z < 2, 1 - z, 5 - z))
        self.me = 2 * place.y + place.x

    def copy(self, i, tag, src, dst, peer):
        return pltpu.make_async_remote_copy(
            src_ref=src, dst_ref=dst, send_sem=self.send.at[i, tag], recv_sem=self.recv.at[i, tag], device_id=peer, device_id_type=MESH
        )

    def to_sib(self, i):
        s = self.slots[i]
        return self.copy(i, 0, s.stage, s.landed, self.p.sib)

    def first(self, i):
        p, s = self.p, self.slots[i]
        return [
            self.copy(i, 4, s.ab.at[0, 1 - p.x], s.xr.at[0], p.xnb),
            self.copy(i, 5, s.ab.at[0, 2 + 1 - p.x], s.xr.at[1], p.xnb),
            self.copy(i, 6, s.ab.at[1, 2 * (1 - p.y)], s.yr.at[0], p.ynb),
            self.copy(i, 7, s.ab.at[1, 2 * (1 - p.y) + 1], s.yr.at[1], p.ynb),
        ]

    def second(self, i):
        p, s = self.p, self.slots[i]
        return [
            self.copy(i, 8, s.ab.at[0, 2 * (1 - p.y) + p.x], s.yr2, p.ynb),
            self.copy(i, 9, s.ab.at[1, 2 * p.y + 1 - p.x], s.xr2, p.xnb),
        ]

    def start_first(self, i):
        for cp in self.first(i):
            cp.start()

    def add_first(self, i):
        p, s = self.p, self.slots[i]
        for cp in self.first(i):
            cp.wait_recv()
        for q in range(2):
            ja, jb = 2 * q + p.x, 2 * p.y + q

            def body(rows, q=q, ja=ja, jb=jb):
                s.ab[0, ja, rows, :] = low(wide(s.ab[0, ja, rows, :]) + wide(s.xr[q, rows, :]))
                s.ab[1, jb, rows, :] = low(wide(s.ab[1, jb, rows, :]) + wide(s.yr[q, rows, :]))

            rows_loop(s.n, body)
        for cp in self.second(i):
            cp.start()

    def up(self, i):
        s = self.slots[i]
        return [self.copy(i, 10 + k, s.ab.at[k, self.me], s.zo.at[k], self.out) for k in range(2)]

    def across(self, i):
        s = self.slots[i]
        return self.copy(i, 12, s.ab.at[1 - self.mine, self.me], s.zp, self.peer)

    def total_out(self, i):
        res = self.slots[i].res.at[self.mine]
        return [self.copy(i, 13, res, res, self.out), self.copy(i, 14, res, res, self.peer)]

    def total_on(self, i):
        res = self.slots[i].res.at[1 - self.mine]
        return self.copy(i, 15, res, res, self.out)

    def add_second(self, i):
        s, me = self.slots[i], self.me
        for cp in self.second(i):
            cp.wait_recv()

        def body(rows):
            s.ab[0, me, rows, :] = low(wide(s.ab[0, me, rows, :]) + wide(s.yr2[rows, :]))
            s.ab[1, me, rows, :] = low(wide(s.ab[1, me, rows, :]) + wide(s.xr2[rows, :]))

        rows_loop(s.n, body)

        @pl.when(self.outer)
        def _():
            for cp in self.up(i):
                cp.start()

    def add_outer(self, i):
        s, me = self.slots[i], self.me

        @pl.when(self.inner)
        def _():
            for cp in self.up(i):
                cp.wait_recv()

            def body(rows):
                for k in range(2):
                    s.ab[k, me, rows, :] = low(wide(s.ab[k, me, rows, :]) + wide(s.zo[k, rows, :]))

            rows_loop(s.n, body)
            self.across(i).start()

    def add_peer(self, i):
        s, me, mine = self.slots[i], self.me, self.mine

        @pl.when(self.inner)
        def _():
            self.across(i).wait_recv()

            def body(rows):
                s.res[mine, rows, :] = low(wide(s.ab[mine, me, rows, :]) + wide(s.zp[rows, :]))

            rows_loop(s.n, body)
            for cp in self.total_out(i):
                cp.start()

    def pass_on(self, i):
        @pl.when(self.inner)
        def _():
            other = self.slots[i].res.at[1 - self.mine]
            self.copy(i, 14, other, other, self.peer).wait_recv()
            self.total_on(i).start()

    def arrive(self, i):
        res = self.slots[i].res

        @pl.when(self.outer)
        def _():
            near = jnp.where(self.p.z == 3, 1, 0)
            self.copy(i, 13, res.at[near], res.at[near], self.out).wait_recv()
            self.copy(i, 15, res.at[1 - near], res.at[1 - near], self.out).wait_recv()

    def drain(self, i):
        @pl.when(self.outer)
        def _():
            for cp in self.up(i):
                cp.wait_send()

        @pl.when(self.inner)
        def _():
            for cp in [self.across(i), self.total_on(i)] + self.total_out(i):
                cp.wait_send()

        for cp in [self.to_sib(i)] + self.first(i) + self.second(i):
            cp.wait_send()


class Small:
    def __init__(self, place, total, slots, sems):
        p = place
        self.total, self.slots = total, slots
        self.send, self.recv = sems
        z = p.z
        self.order = [p.sib, p.xnb, p.ynb, p.level(z + 1 - 2 * (z % 2)), p.level((z + 2) % 4)]

    def copy(self, k):
        return pltpu.make_async_remote_copy(
            src_ref=self.slots.at[0, k],
            dst_ref=self.slots.at[1, k],
            send_sem=self.send.at[k],
            recv_sem=self.recv.at[k],
            device_id=self.order[k],
            device_id_type=MESH,
        )

    def begin(self):
        self.slots[0, 0] = self.total[...]
        self.copy(0).start()

    def step(self, k):
        self.copy(k).wait_recv()
        both = self.slots[0, k] + self.slots[1, k]
        if k < 4:
            self.slots[0, k + 1] = both
            self.copy(k + 1).start()
        else:
            self.total[...] = both

    def drain(self):
        for k in range(5):
            self.copy(k).wait_send()

ROOT = math.sqrt(2.0 / math.pi)
CUBE = 0.044715
LANES = 128


def low(value):
    return value.astype(jnp.bfloat16)


def gelu_parts(v):
    square = v * v
    t = jnp.tanh(ROOT * (v + CUBE * v * square))
    half = 0.5 * (1.0 + t)
    return v * half, half + 0.5 * v * (1.0 - t * t) * (ROOT * (1.0 + 3.0 * CUBE * square))


def gelu_value(v):
    return 0.5 * v * (1.0 + jnp.tanh(ROOT * (v + CUBE * v * (v * v))))


def dot(left, right):
    return jnp.dot(left, right, preferred_element_type=jnp.float32)


def dot_t(left, right):
    return lax.dot_general(left, right, (((1,), (1,)), ((), ())), preferred_element_type=jnp.float32)


def sigmoid(v):
    return 1.0 / (1.0 + jnp.exp(-v))


def minus_expm1(twice, half_of):
    t = jnp.tanh(half_of)
    return -2.0 * t / (1.0 - t)


def softplus_minus(v):
    return jnp.maximum(-v, 0.0) + jnp.log1p(jnp.exp(-jnp.abs(v)))


def strided_scan(decay_ref, value_ref, prod_ref, sum_ref, backward, rows):
    tiles, _, lanes = sum_ref.shape
    span = rows // 8

    def step(k, carry):
        prod, total = carry
        t = span - 1 - k if backward else k
        spot = pl.ds(t, 8, stride=span)
        new_prod, new_total = [], []
        for c in range(tiles):
            d, v = decay_ref[c, spot, :], value_ref[c, spot, :]
            if backward:
                seen = total[c] + v
                sum_ref[c, spot, :] = seen
                prod_ref[c, spot, :] = prod[c]
                new_prod.append(prod[c] * d)
                new_total.append(seen * d)
            else:
                new_prod.append(prod[c] * d)
                new_total.append(total[c] * d + v)
                prod_ref[c, spot, :] = new_prod[c]
                sum_ref[c, spot, :] = new_total[c]
        return new_prod, new_total

    ones = [jnp.ones((8, lanes), jnp.float32)] * tiles
    zeros = [jnp.zeros((8, lanes), jnp.float32)] * tiles
    return lax.fori_loop(0, span, step, (ones, zeros), unroll=2)


def segment_ends(ends, backward):
    before, whole = [], []
    order = range(7, -1, -1) if backward else range(8)
    for prod, total in zip(*ends):
        p = jnp.ones((1, prod.shape[1]), jnp.float32)
        s = jnp.zeros((1, prod.shape[1]), jnp.float32)
        ps, ss = [None] * 8, [None] * 8
        for k in order:
            ps[k], ss[k] = p, s
            d, v = prod[k : k + 1], total[k : k + 1]
            p, s = p * d, s * d + v
        before.append((jnp.concatenate(ps, axis=0), jnp.concatenate(ss, axis=0)))
        whole.append((p, s))
    return before, whole


class Ends:
    def __init__(self, place, slots, sems, backward):
        self.p, self.slots, self.backward = place, slots, backward
        self.send, self.recv = sems

    def copy(self, d):
        to = (self.p.seq + d) % 8
        return pltpu.make_async_remote_copy(
            src_ref=self.slots.at[self.p.seq], dst_ref=self.slots.at[self.p.seq], send_sem=self.send.at[d - 1],
            recv_sem=self.recv.at[d - 1], device_id=(self.p.z, to), device_id_type=MESH,
        )

    def come(self, d):
        src = (self.p.seq + 8 - d) % 8
        return pltpu.make_async_remote_copy(
            src_ref=self.slots.at[src], dst_ref=self.slots.at[src], send_sem=self.send.at[d - 1],
            recv_sem=self.recv.at[d - 1], device_id=(self.p.z, src), device_id_type=MESH,
        )

    def tell(self, whole):
        for c, (prod, total) in enumerate(whole):
            self.slots[self.p.seq, 0, c : c + 1, :] = prod
            self.slots[self.p.seq, 1, c : c + 1, :] = total
        for d in range(1, 8):
            self.copy(d).start()

    def joined(self):
        for d in range(1, 8):
            self.come(d).wait_recv()
        carry = jnp.zeros(self.slots.shape[2:], jnp.float32)
        for k in range(7, 0, -1) if self.backward else range(7):
            further = self.slots[k, 0] * carry + self.slots[k, 1]
            counts = k > self.p.seq if self.backward else k < self.p.seq
            carry = jnp.where(counts, further, carry)
        return carry

    def drain(self):
        for d in range(1, 8):
            self.copy(d).wait_send()


def named(keys, refs):
    return SimpleNamespace(**dict(zip(keys, refs)))


HBM = pl.BlockSpec(memory_space=pl.ANY)
VMEM = pl.BlockSpec(memory_space=pltpu.VMEM)


def forward_call(lengths, tokens, shards):
    rows, width = tokens.shape
    lru = shards[1].shape[1]
    ff = shards[5].shape[1]
    tiles = lru // LANES
    kinds = (0,) * 8
    count = len(shards)
    f32, bf = jnp.float32, jnp.bfloat16
    shape = jax.ShapeDtypeStruct
    wholes = [shape((8 * s.shape[0], s.shape[1]), s.dtype) for s in shards]
    saved = dict(
        mixed=shape((rows, width), bf),
        small=shape((16, lru), f32),
        n1t=shape((width, rows), bf),
        pre=shape((tiles, rows, LANES), f32),
        lin=shape((tiles, rows + 8, LANES), f32),
        conv=shape((tiles, rows, LANES), bf),
        convt=shape((tiles, LANES, rows), bf),
        rgate=shape((tiles, rows, LANES), f32),
        igate=shape((tiles, rows, LANES), f32),
        state=shape((tiles, rows + 8, LANES), f32),
        rect=shape((lru, rows), bf),
        resid=shape((rows, width), f32),
        n2t=shape((width, rows), bf),
        mg=shape((rows, ff), f32),
        mv=shape((rows, ff), f32),
        hidt=shape((ff, rows), bf),
    )
    names = list(saved)
    scratch = dict(
        x=pltpu.VMEM((rows, width), bf),
        n1=pltpu.VMEM((rows, width), bf),
        n1t=pltpu.VMEM((width, rows), bf),
        parts=pltpu.VMEM((8 * 16, lru), f32),
        small=pltpu.VMEM((16, lru), f32),
        pre=pltpu.VMEM((tiles, rows, LANES), f32),
        lin=pltpu.VMEM((tiles, rows + 8, LANES), f32),
        conv=pltpu.VMEM((tiles, rows, LANES), bf),
        convt=pltpu.VMEM((tiles, LANES, rows), bf),
        rgate=pltpu.VMEM((tiles, rows, LANES), f32),
        igate=pltpu.VMEM((tiles, rows, LANES), f32),
        prod=pltpu.VMEM((tiles, rows, LANES), f32),
        state=pltpu.VMEM((tiles, rows + 8, LANES), f32),
        total=pltpu.VMEM((tiles, rows, LANES), f32),
        rec=pltpu.VMEM((rows, lru), bf),
        rect=pltpu.VMEM((lru, rows), bf),
        resid=pltpu.VMEM((rows, width), f32),
        n2=pltpu.VMEM((rows, width), bf),
        n2t=pltpu.VMEM((width, rows), bf),
        hidden=pltpu.VMEM((rows, ff), bf),
        ends=pltpu.VMEM((8, 2, tiles, LANES), f32),
        gsend=pltpu.SemaphoreType.DMA((count, len(SENT))),
        grecv=pltpu.SemaphoreType.DMA((count, len(GOT))),
        gown=pltpu.SemaphoreType.DMA((count,)),
        esend=pltpu.SemaphoreType.DMA((7,)),
        erecv=pltpu.SemaphoreType.DMA((7,)),
        hsend=pltpu.SemaphoreType.DMA(()),
        hrecv=pltpu.SemaphoreType.DMA(()),
        load=pltpu.SemaphoreType.DMA((2,)),
        keep=pltpu.SemaphoreType.DMA((len(names),)),
    )
    keys = list(scratch)
    R = 128

    def kernel(lengths_ref, tokens_ref, *refs):
        ins, outs = refs[:count], refs[count : 2 * count]
        out = named(names, refs[2 * count : 2 * count + len(names)])
        v = named(keys, refs[2 * count + len(names) :])
        gelu_w, input_w, gates_w, output_w, mgate_w, mvalue_w, mdown_w = outs[1:]
        place = Place()
        gather = Gather(place, ins, outs, kinds, v.gsend, v.grecv, v.gown)
        ends = Ends(place, v.ends, (v.esend, v.erecv), False)
        z, seq = place.z, place.seq
        meet([(z, (seq + d) % 8) for d in range(1, 8)])
        kept = []

        def keep(src, dst):
            cp = pltpu.make_async_copy(src, dst, v.keep.at[len(kept)])
            cp.start()
            kept.append(cp)

        load = pltpu.make_async_copy(tokens_ref, v.x, v.load.at[0])
        load.start()
        for i in range(4):
            gather.start(i)
        load.wait()
        gather.relay(0, ("X", "Y"))
        gather.start(4)
        gather.relay(0, ("D1", "D2"))
        gather.arrive(0)
        load = pltpu.make_async_copy(outs[0], v.parts, v.load.at[1])
        load.start()
        gather.relay(1, ("X", "Y"))
        load.wait()
        small = v.small
        total = v.parts[0:16, :]
        for k in range(1, 8):
            total = total + v.parts[16 * k : 16 * (k + 1), :]
        small[...] = total
        keep(v.small, out.small)

        def norm_one(at):
            x = wide(v.x[at, :])
            scale = lax.rsqrt(jnp.mean(x * x, axis=-1, keepdims=True) + epsilon)
            v.n1[at, :] = low(x * scale * small[8:9, :width])

        rows_loop(rows, norm_one, 64)
        gather.relay(2, ("X", "Y"))
        gather.start(5)
        gather.relay(1, ("D1", "D2"))

        def turn(src, dst, at):
            dst[at, :] = src[:, at].T

        @pl.loop(0, width // 256)
        def _(k):
            turn(v.n1, v.n1t, pl.ds(pl.multiple_of(k * 256, 256), 256))

        keep(v.n1t, out.n1t)
        gather.relay(3, ("X", "Y"))
        gather.relay(2, ("D1", "D2"))
        gather.arrive(1)

        def project(weight, dst, first):
            def body(w):
                t = pl.program_id(0)
                both = dot(v.n1[...], w[...])
                dst[2 * t, pl.ds(first, rows), :] = both[:, :LANES]
                dst[2 * t + 1, pl.ds(first, rows), :] = both[:, LANES:]

            pltpu.emit_pipeline(body, grid=(tiles // 2,), in_specs=[pl.BlockSpec((width, 2 * LANES), lambda t: (0, t))])(weight)

        project(gelu_w, v.pre, 0)
        keep(v.pre, out.pre)
        gather.relay(4, ("X", "Y"))
        gather.start(6)
        gather.relay(3, ("D1", "D2"))
        gather.arrive(2)
        project(input_w, v.lin, 8)

        def halo():
            return pltpu.make_async_remote_copy(
                src_ref=v.lin.at[:, pl.ds(rows, 8)], dst_ref=v.lin.at[:, pl.ds(0, 8)], send_sem=v.hsend, recv_sem=v.hrecv,
                device_id=(z, (seq + 1) % 8), device_id_type=MESH,
            )

        @pl.when(seq < 7)
        def _():
            halo().start()

        gather.relay(5, ("X", "Y"))
        gather.relay(4, ("D1", "D2"))
        gather.start(7)
        gather.arrive(3)

        @pl.when(seq == 0)
        def _():
            v.lin[:, 0:8, :] = jnp.zeros((tiles, 8, LANES), f32)

        @pl.when(seq > 0)
        def _():
            halo().wait_recv()

        keep(v.lin, out.lin)

        def gates(w):
            h = pl.program_id(0)
            lane = pl.ds(pl.multiple_of(h * LANES, LANES), LANES)
            taps = [small[k : k + 1, lane] for k in range(4)]
            cb, rb, ib, dp = [small[k : k + 1, lane] for k in range(4, 8)]
            rate = -cfactor * softplus_minus(dp)
            for r in range(0, rows, R):
                acc = cb + taps[0] * v.lin[h, 8 + r : 8 + r + R, :]
                for k in range(1, 4):
                    acc = acc + taps[k] * v.lin[h, 8 + r - k : 8 + r - k + R, :]
                cl = low(acc)
                v.conv[h, r : r + R, :] = cl
                v.convt[h, :, r : r + R] = cl.T
                both = dot(cl, w[...])
                rg = sigmoid(both[:, :LANES] + rb)
                ig = sigmoid(both[:, LANES:] + ib)
                v.rgate[h, r : r + R, :] = rg
                v.igate[h, r : r + R, :] = ig
                log_decay = rate * rg
                v.prod[h, r : r + R, :] = jnp.exp(log_decay)
                v.total[h, r : r + R, :] = jnp.sqrt(minus_expm1(2.0 * log_decay, log_decay)) * ig * wide(cl)

        pltpu.emit_pipeline(gates, grid=(tiles,), in_specs=[pl.BlockSpec((LANES, 2 * LANES), lambda h: (h, 0))])(gates_w)
        for src, dst in ((v.conv, out.conv), (v.convt, out.convt), (v.rgate, out.rgate), (v.igate, out.igate)):
            keep(src, dst)
        gather.relay(6, ("X", "Y"))
        gather.relay(5, ("D1", "D2"))
        tails = strided_scan(v.prod, v.total, v.prod, v.total, False, rows)
        before, whole = segment_ends(tails, False)
        ends.tell(whole)
        gather.relay(7, ("X", "Y"))
        gather.relay(6, ("D1", "D2"))
        carry = ends.joined()
        span = rows // 8
        for c in range(tiles):
            v.state[c, 0:8, :] = jnp.broadcast_to(carry[c : c + 1, :], (8, LANES))
            into = before[c][0] * carry[c : c + 1, :] + before[c][1]
            v.parts[8 * c : 8 * c + 8, 0:LANES] = into

        @pl.loop(0, tiles)
        def _(c):
            lane = pl.ds(pl.multiple_of(c * LANES, LANES), LANES)
            into = v.parts[pl.ds(pl.multiple_of(c * 8, 8), 8), 0:LANES]
            for s in range(8):
                at = slice(s * span, (s + 1) * span)
                state = v.total[c, at, :] + v.prod[c, at, :] * into[s : s + 1, :]
                v.state[c, 8 + s * span : 8 + (s + 1) * span, :] = state
                v.rec[at, lane] = low(state * gelu_value(v.pre[c, at, :]))
            v.rect[lane, :] = v.rec[:, lane].T

        keep(v.state, out.state)
        keep(v.rect, out.rect)
        gather.arrive(4)

        def back_to_width(w):
            t = pl.program_id(0)
            at = pl.ds(pl.multiple_of(t * 256, 256), 256)
            v.resid[:, at] = wide(v.x[:, at]) + dot(v.rec[...], w[...])

        pltpu.emit_pipeline(back_to_width, grid=(width // 256,), in_specs=[pl.BlockSpec((lru, 256), lambda t: (0, t))])(output_w)
        keep(v.resid, out.resid)
        gather.relay(7, ("D1", "D2"))

        def norm_two(at):
            x = v.resid[at, :]
            scale = lax.rsqrt(jnp.mean(x * x, axis=-1, keepdims=True) + epsilon)
            v.n2[at, :] = low(x * scale * small[9:10, :width])

        rows_loop(rows, norm_two, 64)

        @pl.loop(0, width // 256)
        def _(k):
            turn(v.n2, v.n2t, pl.ds(pl.multiple_of(k * 256, 256), 256))

        keep(v.n2t, out.n2t)
        gather.arrive(5)
        gather.arrive(6)

        def mlp(wg, wv, mg, mv, hidt):
            t = pl.program_id(0)
            at = pl.ds(pl.multiple_of(t * 256, 256), 256)
            mg[...] = dot(v.n2[...], wg[...])
            mv[...] = dot(v.n2[...], wv[...])

            def act(rs):
                v.hidden[rs, at] = low(gelu_value(mg[rs, :]) * mv[rs, :])

            rows_loop(rows, act, 64)
            hidt[...] = v.hidden[:, at].T

        wide_tile = pl.BlockSpec((width, 256), lambda t: (0, t))
        pltpu.emit_pipeline(
            mlp,
            grid=(ff // 256,),
            in_specs=[wide_tile, wide_tile],
            out_specs=[pl.BlockSpec((rows, 256), lambda t: (0, t))] * 2 + [pl.BlockSpec((256, rows), lambda t: (t, 0))],
        )(mgate_w, mvalue_w, out.mg, out.mv, out.hidt)
        gather.arrive(7)
        valid_rows = lengths_ref[z] - seq * rows

        def down(w, mixed):
            t = pl.program_id(0)
            at = pl.ds(pl.multiple_of(t * 256, 256), 256)
            valid = (lax.broadcasted_iota(jnp.int32, (rows, 256), 0) < valid_rows).astype(f32)
            mixed[...] = low((v.resid[:, at] + dot(v.hidden[...], w[...])) * valid)

        pltpu.emit_pipeline(
            down,
            grid=(width // 256,),
            in_specs=[pl.BlockSpec((ff, 256), lambda t: (0, t))],
            out_specs=[pl.BlockSpec((rows, 256), lambda t: (0, t))],
        )(mdown_w, out.mixed)
        for cp in kept:
            cp.wait()
        for i in range(count):
            gather.drain(i)
        ends.drain()

        @pl.when(seq < 7)
        def _():
            halo().wait_send()

    result = pl.pallas_call(
        kernel,
        out_shape=wholes + [saved[name] for name in names],
        in_specs=[pl.BlockSpec(memory_space=pltpu.SMEM), HBM] + [HBM] * count,
        out_specs=[HBM] * (count + len(names)),
        scratch_shapes=[scratch[key] for key in keys],
        compiler_params=pltpu.CompilerParams(collective_id=1, has_side_effects=True, vmem_limit_bytes=60 << 20),
        name="forward",
    )(lengths, tokens, *shards)
    return result[:count], named(names, result[count:])

def slot_scratch(rows, columns):
    n, h = rows // 8, columns // 2
    bf = jnp.bfloat16
    return dict(
        ab=pltpu.VMEM((2, 4, n, h), bf),
        xr=pltpu.VMEM((2, n, h), bf),
        yr=pltpu.VMEM((2, n, h), bf),
        yr2=pltpu.VMEM((n, h), bf),
        xr2=pltpu.VMEM((n, h), bf),
        zo=pltpu.VMEM((2, n, h), bf),
        zp=pltpu.VMEM((n, h), bf),
        res=pltpu.VMEM((2, n, h), bf),
    )


def backward_call(lengths, tokens, cotangent, weights, saved):
    rows, width = tokens.shape
    gelu_full, input_full, gates_full, output_full, mgate_full, mvalue_full, mdown_full = weights
    lru, ff = gelu_full.shape[1], mgate_full.shape[1]
    tiles = lru // LANES
    f32, bf = jnp.float32, jnp.bfloat16
    shape = jax.ShapeDtypeStruct
    DOWN, MGATE, MVALUE, OUTPUT, GELU, INPUT, GATES = range(7)
    full = [mdown_full, mgate_full, mvalue_full, output_full, gelu_full, input_full, gates_full]
    extents = [w.shape for w in full]
    tile_of = [256, 512, 512, 256, 256, 256, None]
    count = len(full)
    split = lambda v: v.reshape(4, 2, v.shape[0] // 8, v.shape[1])
    inputs = dict(
        tokens=tokens, cot=cotangent, gelu_w=gelu_full, input_w=input_full, gates_w=gates_full, output_w=output_full, mgate_w=mgate_full,
        mvalue_w=mvalue_full, mdown_w=mdown_full, small=saved.small, n1t=split(saved.n1t), pre=saved.pre, lin=saved.lin, conv=saved.conv,
        convt=saved.convt, rgate=saved.rgate, igate=saved.igate, state=saved.state, rect=split(saved.rect), resid=saved.resid,
        n2t=split(saved.n2t), mg=saved.mg, mv=saved.mv, hidt=split(saved.hidt),
    )
    slot_keys = list(slot_scratch(8, 256))
    scratch = dict(
        go=pltpu.VMEM((rows, width), bf),
        gm=pltpu.VMEM((rows, width), bf),
        gn=pltpu.VMEM((rows, width), f32),
        x=pltpu.VMEM((rows, width), bf),
        resid=pltpu.VMEM((rows, width), f32),
        gh=pltpu.VMEM((rows, 256), f32),
        small=pltpu.VMEM((16, lru), f32),
        part=pltpu.VMEM((16, lru), f32),
        gain=pltpu.VMEM((8, width), f32),
        adj=pltpu.VMEM((tiles, rows + 8, LANES), f32),
        prod=pltpu.VMEM((tiles, rows, LANES), f32),
        into=pltpu.VMEM((tiles, 8, LANES), f32),
        gg=pltpu.VMEM((rows, lru), bf),
        gl=pltpu.VMEM((rows, lru), bf),
        gri=pltpu.VMEM((rows, 2 * LANES), bf),
        direct=pltpu.VMEM((rows, LANES), f32),
        gstage=pltpu.VMEM((4, 2, lru // 8, 2 * LANES), bf),
        glanded=pltpu.VMEM((4, lru // 8, 2 * LANES), bf),
        ends=pltpu.VMEM((8, 2, tiles, LANES), f32),
        sslots=pltpu.VMEM((2, 5, 16, lru), f32),
        rsend=pltpu.SemaphoreType.DMA((count, 16)),
        rrecv=pltpu.SemaphoreType.DMA((count, 16)),
        esend=pltpu.SemaphoreType.DMA((7,)),
        erecv=pltpu.SemaphoreType.DMA((7,)),
        hsend=pltpu.SemaphoreType.DMA(()),
        hrecv=pltpu.SemaphoreType.DMA(()),
        ssend=pltpu.SemaphoreType.DMA((5,)),
        srecv=pltpu.SemaphoreType.DMA((5,)),
        load=pltpu.SemaphoreType.DMA((4,)),
        keep=pltpu.SemaphoreType.DMA((count + 1, 2)),
    )
    keys = list(scratch)
    outs = dict(
        tokens_grad=shape((rows, width), f32),
        small_sum=shape((16, lru), f32),
        gmg=shape((rows, ff), bf),
        gmv=shape((rows, ff), bf),
    )
    out_keys = list(outs)
    stages = [shape((4, r // 8, c), bf) for r, c in extents[:-1]]
    sums = [shape((r // 8, c), bf) for r, c in extents]

    def kernel(lengths_ref, *refs):
        refs = list(refs)

        def take(k):
            got = refs[:k]
            del refs[:k]
            return got

        w = named(inputs, take(len(inputs)))
        out = named(out_keys, take(len(out_keys)))
        sum_refs = take(count)
        staged, landed = take(count - 1), take(count - 1)
        v = named(keys, take(len(keys)))
        slots = []
        for i, (r, c) in enumerate(extents):
            s = named(slot_keys, take(len(slot_keys)))
            s.n, s.h, s.columns, s.tile = r // 8, c // 2, c, tile_of[i]
            slots.append(s)
        place = Place()
        z, seq, core = place.z, place.seq, place.core
        for i in range(count - 1):
            slots[i].stage, slots[i].landed = staged[i], landed[i]
        slots[GATES].stage, slots[GATES].landed = v.gstage.at[:, 1 - core], v.glanded
        red = Reduce(place, slots, (v.rsend, v.rrecv))
        ends = Ends(place, v.ends, (v.esend, v.erecv), True)
        tot = Small(place, v.part, v.sslots, (v.ssend, v.srecv))
        loads = [
            pltpu.make_async_copy(w.cot, v.go, v.load.at[0]),
            pltpu.make_async_copy(w.small, v.small, v.load.at[1]),
            pltpu.make_async_copy(w.resid, v.resid, v.load.at[2]),
            pltpu.make_async_copy(w.tokens, v.x, v.load.at[3]),
        ]
        for cp in loads:
            cp.start()
        meet([(z, (seq + d) % 8) for d in range(1, 8)] + [((z + d) % 4, seq) for d in range(1, 4)])
        loads[0].wait()
        valid_rows = lengths_ref[z] - seq * rows

        def mask(at):
            here = lax.broadcasted_iota(jnp.int32, (64, width), 0) + at.start < valid_rows
            v.go[at, :] = low(jnp.where(here, wide(v.go[at, :]), 0.0))

        rows_loop(rows, mask, 64)

        def spread(s, left, right):
            return dot(left[...].reshape(4 * s.n, rows), right).reshape(4, s.n, s.tile)

        def right_of(held, s):
            t = pl.program_id(0)
            return held[:, pl.ds(pl.multiple_of(t * s.tile, s.tile), s.tile)]

        def weight_pass(i, left, right, streamed, own):
            s = slots[i]
            steps = s.columns // s.tile
            in_specs = [pl.BlockSpec((4, None, s.n, rows), lambda t: (0, core if own else 1 - core, 0, 0))]
            operands = [left]
            if streamed:
                in_specs.append(pl.BlockSpec((rows, s.tile), lambda t: (0, t)))
                operands.append(right)
            block = pl.BlockSpec((4, s.n, s.tile), lambda t: (0, 0, t))

            def body(*args):
                value = spread(s, args[0], args[1][...] if streamed else right_of(right, s))
                if own:
                    t = pl.program_id(0)
                    half = steps // 2
                    at = pl.ds(pl.multiple_of((t % half) * s.tile, s.tile), s.tile)
                    s.ab[t // half, :, :, at] = low(value + wide(args[-1][...]))
                else:
                    args[-1][...] = low(value)

            if own:
                red.to_sib(i).wait_recv()
                pltpu.emit_pipeline(body, grid=(steps,), in_specs=in_specs + [block])(*operands, s.landed)
                red.start_first(i)
            else:
                pltpu.emit_pipeline(body, grid=(steps,), in_specs=in_specs, out_specs=[block])(*operands, s.stage)
                red.to_sib(i).start()

        weight_pass(DOWN, w.hidt, v.go, False, False)

        def mlp(md, mg, mv, wg, wv, gmg, gmv):
            v.gh[...] = dot_t(v.go[...], md[...])

            def act(at):
                value, slope = gelu_parts(mg[at, :])
                gh = v.gh[at, :]
                gmg[at, :] = low(gh * mv[at, :] * slope)
                gmv[at, :] = low(gh * value)

            rows_loop(rows, act, 64)
            more = dot_t(gmg[...], wg[...]) + dot_t(gmv[...], wv[...])

            @pl.when(pl.program_id(0) == 0)
            def _():
                v.gn[...] = more

            @pl.when(pl.program_id(0) > 0)
            def _():
                v.gn[...] += more

        across = pl.BlockSpec((rows, 256), lambda t: (0, t))
        pltpu.emit_pipeline(
            mlp,
            grid=(ff // 256,),
            in_specs=[pl.BlockSpec((256, width), lambda t: (t, 0)), across, across]
            + [pl.BlockSpec((width, 256), lambda t: (0, t))] * 2,
            out_specs=[across, across],
        )(w.mdown_w, w.mg, w.mv, w.mgate_w, w.mvalue_w, out.gmg, out.gmv)
        weight_pass(DOWN, w.hidt, v.go, False, True)
        weight_pass(MGATE, w.n2t, out.gmg, True, False)
        weight_pass(MVALUE, w.n2t, out.gmv, True, False)
        for cp in loads[1:]:
            cp.wait()
        small, part = v.small, v.part
        part[...] = jnp.zeros_like(part)

        def eight(value):
            return value.reshape(value.shape[0] // 8, 8, value.shape[1]).sum(axis=0)

        def norm_back(read, gain, write):
            v.gain[...] = jnp.zeros_like(v.gain)

            def chunk(at):
                x, grad, add = read(at)
                scale = lax.rsqrt(jnp.mean(x * x, axis=-1, keepdims=True) + epsilon)
                v.gain[...] += eight(grad * x * scale)
                scaled = grad * gain
                m = jnp.mean(scaled * x, axis=-1, keepdims=True)
                write(at, add + scale * (scaled - x * (scale * scale * m)))

            rows_loop(rows, chunk, 64)
            return v.gain[...].sum(axis=0, keepdims=True)

        def keep_resid(at, value):
            v.gn[at, :] = value
            v.gm[at, :] = low(value)

        part[9:10, :width] = norm_back(lambda at: (v.resid[at, :], v.gn[at, :], wide(v.go[at, :])), small[9:10, :width], keep_resid)
        weight_pass(MGATE, w.n2t, out.gmg, True, True)
        weight_pass(MVALUE, w.n2t, out.gmv, True, True)
        red.add_first(DOWN)

        weight_pass(OUTPUT, w.rect, v.gm, False, False)

        def into_branch(wo, pre, state, rgate):
            t = pl.program_id(0)
            v.gh[...] = dot_t(v.gm[...], wo[...])
            for q in range(2):
                c = 2 * t + q
                lane = pl.ds(pl.multiple_of(c * LANES, LANES), LANES)
                rate = -cfactor * softplus_minus(small[7:8, lane])

                def chunk(at, q=q, c=c, lane=lane, rate=rate):
                    grad = v.gh[at, q * LANES : (q + 1) * LANES]
                    value, slope = gelu_parts(pre[q, at, :])
                    v.adj[c, at, :] = grad * value
                    v.gg[at, lane] = low(grad * state[q, pl.ds(pl.multiple_of(at.start + 8, 8), 64), :] * slope)
                    v.prod[c, at, :] = jnp.exp(rate * rgate[q, at, :])

                rows_loop(rows, chunk, 64)

        pair = lambda t: (t, 0, 0)
        pltpu.emit_pipeline(
            into_branch,
            grid=(tiles // 2,),
            in_specs=[
                pl.BlockSpec((256, width), lambda t: (t, 0)), pl.BlockSpec((2, rows, LANES), pair),
                pl.BlockSpec((2, rows + 8, LANES), pair), pl.BlockSpec((2, rows, LANES), pair),
            ],
        )(w.output_w, w.pre, w.state, w.rgate)
        weight_pass(OUTPUT, w.rect, v.gm, False, True)
        tails = strided_scan(v.prod, v.adj, v.prod, v.adj, True, rows)
        before, whole = segment_ends(tails, True)
        ends.tell(whole)
        weight_pass(GELU, w.n1t, v.gg, False, False)
        red.add_first(MGATE)
        carry = ends.joined()
        for c in range(tiles):
            v.into[c] = before[c][0] * carry[c : c + 1, :] + before[c][1]
        span = rows // 8

        def through_gates(rgate, igate, conv, convt, state, wg):
            c = pl.program_id(0)
            lane = pl.ds(pl.multiple_of(c * LANES, LANES), LANES)
            dp = small[7:8, lane]
            rate = -cfactor * softplus_minus(dp)
            sums = [jnp.zeros((8, LANES), f32) for _ in range(3)]
            for k in range(8):
                at = slice(k * span, (k + 1) * span)
                adj = v.adj[c, at, :] + v.prod[c, at, :] * v.into[c, k : k + 1, :]
                rg, ig, cv = rgate[at, :], igate[at, :], wide(conv[at, :])
                log_decay = rate * rg
                decay = jnp.exp(log_decay)
                mult = jnp.sqrt(minus_expm1(2.0 * log_decay, log_decay))
                grad_decay = adj * state[7 + k * span : 7 + (k + 1) * span, :]
                grad_log = grad_decay * decay - adj * ig * cv * (decay * decay) / mult
                grad_r = grad_log * rate * rg * (1.0 - rg)
                through = adj * mult
                grad_i = through * cv * ig * (1.0 - ig)
                v.direct[at, :] = through * ig
                v.gri[at, :LANES] = low(grad_r)
                v.gri[at, LANES:] = low(grad_i)
                for q, value in enumerate((grad_log * rg, grad_r, grad_i)):
                    sums[q] = sums[q] + eight(value)
            part[7:8, lane] = sums[0].sum(axis=0, keepdims=True) * (cfactor * sigmoid(-dp))
            part[5:6, lane] = sums[1].sum(axis=0, keepdims=True)
            part[6:7, lane] = sums[2].sum(axis=0, keepdims=True)
            product = low(dot(convt[...], v.gri[...]))
            for q in range(2):
                unit = 2 * c + q
                block = unit // 3
                at = pl.ds(pl.multiple_of((unit % 3) * 64, 64), 64)
                v.gstage[block // 2, block % 2, at, :] = product[64 * q : 64 * (q + 1), :]
            grad_conv = v.direct[...] + dot_t(v.gri[...], wg[...])
            v.adj[c, pl.ds(0, rows), :] = grad_conv
            part[4:5, lane] = eight(grad_conv).sum(axis=0, keepdims=True)

        one = lambda t: (t, 0, 0)
        pltpu.emit_pipeline(
            through_gates,
            grid=(tiles,),
            in_specs=[
                pl.BlockSpec((None, rows, LANES), one), pl.BlockSpec((None, rows, LANES), one), pl.BlockSpec((None, rows, LANES), one),
                pl.BlockSpec((None, LANES, rows), one), pl.BlockSpec((None, rows + 8, LANES), one),
                pl.BlockSpec((LANES, 2 * LANES), lambda t: (t, 0)),
            ],
        )(w.rgate, w.igate, w.conv, w.convt, w.state, w.gates_w)

        def halo():
            return pltpu.make_async_remote_copy(
                src_ref=v.adj.at[:, pl.ds(0, 8)], dst_ref=v.adj.at[:, pl.ds(rows, 8)], send_sem=v.hsend, recv_sem=v.hrecv,
                device_id=(z, (seq + 7) % 8), device_id_type=MESH,
            )

        @pl.when(seq > 0)
        def _():
            halo().start()

        red.to_sib(GATES).start()
        weight_pass(GELU, w.n1t, v.gg, False, True)
        red.add_first(MVALUE)
        red.add_second(DOWN)

        @pl.when(seq == 7)
        def _():
            v.adj[:, pl.ds(rows, 8), :] = jnp.zeros((tiles, 8, LANES), f32)

        @pl.when(seq < 7)
        def _():
            halo().wait_recv()

        def through_conv(lin):
            c = pl.program_id(0)
            lane = pl.ds(pl.multiple_of(c * LANES, LANES), LANES)
            taps = [small[k : k + 1, lane] for k in range(4)]
            sums = [jnp.zeros((8, LANES), f32) for _ in range(4)]
            for r in range(0, rows, 128):
                here = v.adj[c, r : r + 128, :]
                acc = taps[0] * here
                for k in range(4):
                    sums[k] = sums[k] + eight(here * lin[8 + r - k : 8 + r - k + 128, :])
                    if k:
                        acc = acc + taps[k] * v.adj[c, r + k : r + k + 128, :]
                v.gl[r : r + 128, lane] = low(acc)
            for k in range(4):
                part[k : k + 1, lane] = sums[k].sum(axis=0, keepdims=True)

        pltpu.emit_pipeline(through_conv, grid=(tiles,), in_specs=[pl.BlockSpec((None, rows + 8, LANES), one)])(w.lin)
        weight_pass(INPUT, w.n1t, v.gl, False, False)

        def gates_own():
            s = slots[GATES]
            red.to_sib(GATES).wait_recv()
            for j in range(4):

                def body(at, j=j):
                    both = low(wide(v.gstage[j, core, at, :]) + wide(v.glanded[j, at, :]))
                    s.ab[0, j, at, :] = both[:, : s.h]
                    s.ab[1, j, at, :] = both[:, s.h :]

                rows_loop(s.n, body)
            red.start_first(GATES)

        def into_norm(wi, wg):
            t = pl.program_id(0)
            at = pl.ds(pl.multiple_of(t * 256, 256), 256)
            v.resid[:, at] = dot_t(v.gl[...], wi[...]) + dot_t(v.gg[...], wg[...])

        pltpu.emit_pipeline(into_norm, grid=(width // 256,), in_specs=[pl.BlockSpec((256, lru), lambda t: (t, 0))] * 2)(w.input_w, w.gelu_w)
        weight_pass(INPUT, w.n1t, v.gl, False, True)
        gates_own()
        red.add_first(OUTPUT)
        red.add_second(MGATE)
        red.add_outer(DOWN)

        def keep_tokens(at, value):
            v.gn[at, :] = value

        part[8:9, :width] = norm_back(lambda at: (wide(v.x[at, :]), v.resid[at, :], v.gn[at, :]), small[8:9, :width], keep_tokens)
        tot.begin()
        kept = [pltpu.make_async_copy(v.gn, out.tokens_grad, v.keep.at[count, 0])]
        kept[0].start()

        def finish(i):
            s = slots[i]
            red.arrive(i)
            for k in range(2):
                cp = pltpu.make_async_copy(s.res.at[k], sum_refs[i].at[:, pl.ds(k * s.h, s.h)], v.keep.at[i, k])
                cp.start()
                kept.append(cp)

        steps = [
            (red.add_first, GELU), (red.add_second, MVALUE), (red.add_outer, MGATE), (red.add_peer, DOWN), (tot.step, 0),
            (red.add_first, INPUT), (red.add_second, OUTPUT), (red.add_outer, MVALUE), (red.add_peer, MGATE), (red.pass_on, DOWN), (tot.step, 1),
            (red.add_first, GATES), (red.add_second, GELU), (red.add_outer, OUTPUT), (red.add_peer, MVALUE), (red.pass_on, MGATE), (finish, DOWN),
            (tot.step, 2),
            (red.add_second, INPUT), (red.add_outer, GELU), (red.add_peer, OUTPUT), (red.pass_on, MVALUE), (finish, MGATE), (tot.step, 3),
            (red.add_second, GATES), (red.add_outer, INPUT), (red.add_peer, GELU), (red.pass_on, OUTPUT), (finish, MVALUE), (tot.step, 4),
            (red.add_outer, GATES), (red.add_peer, INPUT), (red.pass_on, GELU), (finish, OUTPUT),
            (red.add_peer, GATES), (red.pass_on, INPUT), (finish, GELU), (red.pass_on, GATES), (finish, INPUT), (finish, GATES),
        ]
        for act, i in steps:
            act(i)
        cp = pltpu.make_async_copy(part, out.small_sum, v.keep.at[count, 1])
        cp.start()
        kept.append(cp)
        for cp in kept:
            cp.wait()
        for i in range(count):
            red.drain(i)
        tot.drain()
        ends.drain()

        @pl.when(seq > 0)
        def _():
            halo().wait_send()

    slot_list = [value for r, c in extents for value in slot_scratch(r, c).values()]
    result = pl.pallas_call(
        kernel,
        out_shape=list(outs.values()) + sums + stages + stages,
        in_specs=[pl.BlockSpec(memory_space=pltpu.SMEM)] + [HBM] * len(inputs),
        out_specs=[HBM] * (len(outs) + count + 2 * (count - 1)),
        scratch_shapes=list(scratch.values()) + slot_list,
        compiler_params=pltpu.CompilerParams(collective_id=2, has_side_effects=True, vmem_limit_bytes=62 << 20),
        name="backward",
    )(lengths, *inputs.values())
    return result[0], result[1], result[len(outs) : len(outs) + count]


def local(
    tokens,
    lengths,
    mixer_gain,
    gelu_weight,
    input_weight,
    conv_taps,
    conv_bias,
    rgate_weight,
    rgate_bias,
    igate_weight,
    igate_bias,
    decay_param,
    output_weight,
    mlp_gain,
    mlp_gate,
    mlp_value,
    mlp_down,
    cotangent,
):
    count = tokens.shape[0]
    width_lru = input_weight.shape[1]
    block = rgate_weight.shape[1]
    heads = width_lru // block
    taps_count = conv_taps.shape[1]
    rim = taps_count - 1
    seq_count = lax.axis_size("seq")
    slot_length = count * seq_count
    first_row = (lax.axis_index("grp") * seq_count + lax.axis_index("seq")) * count
    global_row = first_row + jnp.arange(count, dtype=jnp.int32)
    position = global_row % slot_length
    slot_of = global_row // slot_length
    slot_ids = jnp.arange(lengths.shape[0], dtype=jnp.int32)
    slot_len = jnp.sum(
        jnp.where(slot_of[:, None] == slot_ids[None, :], lengths[None, :], 0), axis=1
    )
    valid = (position < slot_len).astype(jnp.float32)[:, None]
    starts = (position > 0).astype(jnp.float32)[:, None]
    lag_masks = [(position >= lag).astype(jnp.float32)[:, None] for lag in range(taps_count)]
    zeros_lru = jnp.zeros((width_lru,), jnp.float32)
    ones_lru = jnp.ones((width_lru,), jnp.float32)
    (
        gain_one,
        gelu_full,
        input_full,
        taps_full,
        cbias_full,
        rgate_full,
        rbias_full,
        igate_full,
        ibias_full,
        decay_full,
        output_full,
        gain_two,
        mgate_full,
        mvalue_full,
        mdown_full,
    ) = (
        lax.all_gather(mixer_gain, "seq", axis=0, tiled=True),
        lax.all_gather(gelu_weight, "seq", axis=0, tiled=True),
        lax.all_gather(input_weight, "seq", axis=0, tiled=True),
        lax.all_gather(conv_taps, "seq", axis=0, tiled=True),
        lax.all_gather(conv_bias, "seq", axis=0, tiled=True),
        lax.all_gather(rgate_weight, "seq", axis=0, tiled=True),
        lax.all_gather(rgate_bias, "seq", axis=0, tiled=True),
        lax.all_gather(igate_weight, "seq", axis=0, tiled=True),
        lax.all_gather(igate_bias, "seq", axis=0, tiled=True),
        lax.all_gather(decay_param, "seq", axis=0, tiled=True),
        lax.all_gather(output_weight, "seq", axis=0, tiled=True),
        lax.all_gather(mlp_gain, "seq", axis=0, tiled=True),
        lax.all_gather(mlp_gate, "seq", axis=0, tiled=True),
        lax.all_gather(mlp_value, "seq", axis=0, tiled=True),
        lax.all_gather(mlp_down, "seq", axis=0, tiled=True),
    )
    inputs = tokens.astype(jnp.float32)
    normed_one, norm_one_back = jax.vjp(rms_norm, inputs, gain_one.astype(jnp.float32))
    normed_one = normed_one.astype(jnp.bfloat16)
    gate_pre = matmul(normed_one, gelu_full)
    gate_act, gate_back = jax.vjp(gelu_tanh, gate_pre)
    linear = matmul(normed_one, input_full)
    rim_in = passed_along(linear[count - rim :], "seq", 1)
    extended = jnp.concatenate([rim_in, linear], axis=0)
    taps_fwd = taps_full.astype(jnp.float32)
    conv = cbias_full.astype(jnp.float32) + taps_fwd[:, 0] * linear
    for lag in range(1, taps_count):
        conv = conv + taps_fwd[:, lag] * (extended[rim - lag : rim - lag + count] * lag_masks[lag])
    conv_low = conv.astype(jnp.bfloat16)
    conv_value = conv_low.astype(jnp.float32)
    rgate_pre = block_apply(conv_low, rgate_full, heads) + rbias_full.astype(jnp.float32)
    igate_pre = block_apply(conv_low, igate_full, heads) + ibias_full.astype(jnp.float32)
    (decay, inject), gates_back = jax.vjp(
        recurrence_gates, rgate_pre, igate_pre, conv_value, decay_full.astype(jnp.float32)
    )
    decay_used = decay * starts
    cum_decay, state_zero = lax.associative_scan(chain_combine, (decay_used, inject), axis=0)
    scanned = carried_in(
        (cum_decay[-1], state_zero[-1]), "seq", chain_combine, (ones_lru, zeros_lru), False
    )
    carry_in = scanned[1]
    state = state_zero + cum_decay * carry_in
    mixed_rec = (state * gate_act).astype(jnp.bfloat16)
    resid = inputs + matmul(mixed_rec, output_full)
    normed_two, norm_two_back = jax.vjp(rms_norm, resid, gain_two.astype(jnp.float32))
    normed_two = normed_two.astype(jnp.bfloat16)
    mgate_pre = matmul(normed_two, mgate_full)
    mvalue_pre = matmul(normed_two, mvalue_full)
    mgate_act, mgate_back = jax.vjp(gelu_tanh, mgate_pre)
    hidden = (mgate_act * mvalue_pre).astype(jnp.bfloat16)
    mixed = ((resid + matmul(hidden, mdown_full)) * valid).astype(jnp.bfloat16)
    (
        gain_one,
        gelu_full,
        input_full,
        taps_full,
        cbias_full,
        rgate_full,
        rbias_full,
        igate_full,
        ibias_full,
        decay_full,
        output_full,
        gain_two,
        mgate_full,
        mvalue_full,
        mdown_full,
    ) = (
        lax.all_gather(mixer_gain, "seq", axis=0, tiled=True),
        lax.all_gather(gelu_weight, "seq", axis=0, tiled=True),
        lax.all_gather(input_weight, "seq", axis=0, tiled=True),
        lax.all_gather(conv_taps, "seq", axis=0, tiled=True),
        lax.all_gather(conv_bias, "seq", axis=0, tiled=True),
        lax.all_gather(rgate_weight, "seq", axis=0, tiled=True),
        lax.all_gather(rgate_bias, "seq", axis=0, tiled=True),
        lax.all_gather(igate_weight, "seq", axis=0, tiled=True),
        lax.all_gather(igate_bias, "seq", axis=0, tiled=True),
        lax.all_gather(decay_param, "seq", axis=0, tiled=True),
        lax.all_gather(output_weight, "seq", axis=0, tiled=True),
        lax.all_gather(mlp_gain, "seq", axis=0, tiled=True),
        lax.all_gather(mlp_gate, "seq", axis=0, tiled=True),
        lax.all_gather(mlp_value, "seq", axis=0, tiled=True),
        lax.all_gather(mlp_down, "seq", axis=0, tiled=True),
    )
    taps_back = taps_full.astype(jnp.float32)
    grad_out = cotangent.astype(jnp.float32) * valid
    grad_out_low = grad_out.astype(jnp.bfloat16)
    down_grad = inner_rows(hidden, grad_out_low)
    grad_hidden = outer_cols(grad_out_low, mdown_full)
    grad_mgate = mgate_back(grad_hidden * mvalue_pre)[0].astype(jnp.bfloat16)
    grad_mvalue = (grad_hidden * mgate_act).astype(jnp.bfloat16)
    mgate_grad = inner_rows(normed_two, grad_mgate)
    mvalue_grad = inner_rows(normed_two, grad_mvalue)
    grad_ntwo = outer_cols(grad_mgate, mgate_full) + outer_cols(grad_mvalue, mvalue_full)
    grad_resid_norm, gain_two_grad = norm_two_back(grad_ntwo)
    grad_resid = grad_out + grad_resid_norm
    grad_mix = grad_resid.astype(jnp.bfloat16)
    output_grad = inner_rows(mixed_rec, grad_mix)
    grad_rec = outer_cols(grad_mix, output_full)
    grad_state = grad_rec * gate_act
    grad_gate = gate_back(grad_rec * state)[0].astype(jnp.bfloat16)
    decay_next = jnp.concatenate([decay_used[1:], jnp.ones((1, width_lru), jnp.float32)], axis=0)
    rev_prod, rev_adjoint = lax.associative_scan(
        chain_combine, (jnp.flip(decay_next, 0), jnp.flip(grad_state, 0)), axis=0
    )
    tail_prod = jnp.flip(rev_prod, 0)
    adjoint_zero = jnp.flip(rev_adjoint, 0)
    summary_decay = decay_used[0] * tail_prod[0]
    summary_adjoint = decay_used[0] * adjoint_zero[0]
    scanned_back = carried_in(
        (summary_decay, summary_adjoint), "seq", chain_combine, (ones_lru, zeros_lru), True
    )
    incoming = scanned_back[1]
    adjoint = adjoint_zero + tail_prod * incoming
    state_prev = jnp.concatenate([carry_in[None, :], state[:-1]], axis=0)
    grad_decay = adjoint * state_prev * starts
    grad_rpre, grad_ipre, grad_direct, decay_grad = gates_back((grad_decay, adjoint))
    rbias_grad = jnp.sum(grad_rpre, axis=0)
    ibias_grad = jnp.sum(grad_ipre, axis=0)
    grad_rlow = grad_rpre.astype(jnp.bfloat16)
    grad_ilow = grad_ipre.astype(jnp.bfloat16)
    rgate_grad = block_grad(conv_low, grad_rlow, heads)
    igate_grad = block_grad(conv_low, grad_ilow, heads)
    grad_conv = (
        grad_direct
        + block_back(grad_rlow, rgate_full, heads)
        + block_back(grad_ilow, igate_full, heads)
    )
    cbias_grad = jnp.sum(grad_conv, axis=0)
    taps_columns = []
    grad_extended = jnp.zeros((count + rim, width_lru), jnp.float32)
    for lag in range(taps_count):
        masked_term = grad_conv * lag_masks[lag]
        taps_columns.append(jnp.sum(masked_term * extended[rim - lag : rim - lag + count], axis=0))
        grad_extended = grad_extended + jnp.pad(
            taps_back[:, lag] * masked_term, ((rim - lag, lag), (0, 0))
        )
    taps_grad = jnp.stack(taps_columns, axis=1)
    rim_back = passed_along(grad_extended[:rim], "seq", -1)
    grad_linear = grad_extended[rim:] + jnp.pad(rim_back, ((count - rim, 0), (0, 0)))
    grad_lin = grad_linear.astype(jnp.bfloat16)
    input_grad = inner_rows(normed_one, grad_lin)
    gelu_grad = inner_rows(normed_one, grad_gate)
    grad_none = outer_cols(grad_lin, input_full) + outer_cols(grad_gate, gelu_full)
    grad_inputs_norm, gain_one_grad = norm_one_back(grad_none)
    tokens_grad = grad_resid + grad_inputs_norm
    partials = (
        gain_one_grad,
        gelu_grad,
        input_grad,
        taps_grad,
        cbias_grad,
        rgate_grad,
        rbias_grad,
        igate_grad,
        ibias_grad,
        decay_grad,
        output_grad,
        gain_two_grad,
        mgate_grad,
        mvalue_grad,
        down_grad,
    )
    summed_seq = (
        lax.psum_scatter(partials[0], "seq", scatter_dimension=0, tiled=True),
        lax.psum_scatter(partials[1], "seq", scatter_dimension=0, tiled=True),
        lax.psum_scatter(partials[2], "seq", scatter_dimension=0, tiled=True),
        lax.psum_scatter(partials[3], "seq", scatter_dimension=0, tiled=True),
        lax.psum_scatter(partials[4], "seq", scatter_dimension=0, tiled=True),
        lax.psum_scatter(partials[5], "seq", scatter_dimension=0, tiled=True),
        lax.psum_scatter(partials[6], "seq", scatter_dimension=0, tiled=True),
        lax.psum_scatter(partials[7], "seq", scatter_dimension=0, tiled=True),
        lax.psum_scatter(partials[8], "seq", scatter_dimension=0, tiled=True),
        lax.psum_scatter(partials[9], "seq", scatter_dimension=0, tiled=True),
        lax.psum_scatter(partials[10], "seq", scatter_dimension=0, tiled=True),
        lax.psum_scatter(partials[11], "seq", scatter_dimension=0, tiled=True),
        lax.psum_scatter(partials[12], "seq", scatter_dimension=0, tiled=True),
        lax.psum_scatter(partials[13], "seq", scatter_dimension=0, tiled=True),
        lax.psum_scatter(partials[14], "seq", scatter_dimension=0, tiled=True),
    )
    totals = lax.psum(tuple(summed_seq), "grp")
    return (
        mixed,
        tokens_grad,
        totals[0],
        totals[1],
        totals[2],
        totals[3],
        totals[4],
        totals[5],
        totals[6],
        totals[7],
        totals[8],
        totals[9],
        totals[10],
        totals[11],
        totals[12],
        totals[13],
        totals[14],
    )


def local_fast(
    tokens,
    lengths,
    mixer_gain,
    gelu_weight,
    input_weight,
    conv_taps,
    conv_bias,
    rgate_weight,
    rgate_bias,
    igate_weight,
    igate_bias,
    decay_param,
    output_weight,
    mlp_gain,
    mlp_gate,
    mlp_value,
    mlp_down,
    cotangent,
):
    block = rgate_weight.shape[1]
    width_lru = input_weight.shape[1]
    lru_rows = jnp.concatenate(
        [conv_taps.T, conv_bias[None], rgate_bias[None], igate_bias[None], decay_param[None]], axis=0
    ).astype(jnp.float32)
    model_rows = jnp.stack([mixer_gain, mlp_gain]).astype(jnp.float32)
    mine = lax.axis_index("seq")
    small = jnp.zeros((16, width_lru), jnp.float32)
    small = lax.dynamic_update_slice(small, lru_rows, (0, mine * lru_rows.shape[1]))
    small = lax.dynamic_update_slice(small, model_rows, (8, mine * model_rows.shape[1]))
    gates = jnp.concatenate([rgate_weight, igate_weight], axis=1)
    weights, saved = forward_call(
        lengths, tokens, [small, gelu_weight, input_weight, gates, output_weight, mlp_gate, mlp_value, mlp_down]
    )
    tokens_grad, small_sum, big = backward_call(lengths, tokens, cotangent, weights[1:], saved)
    down, mgate, mvalue, out_w, gelu_w, input_w, gates = [value.astype(jnp.float32) for value in big]
    lru_own = lax.dynamic_slice(small_sum, (0, mine * conv_bias.shape[0]), (8, conv_bias.shape[0]))
    model_own = lax.dynamic_slice(small_sum, (8, mine * mixer_gain.shape[0]), (2, mixer_gain.shape[0]))
    return (
        saved.mixed,
        tokens_grad,
        model_own[0],
        gelu_w,
        input_w,
        lru_own[:4].T,
        lru_own[4],
        gates[:, :block],
        lru_own[5],
        gates[:, block:],
        lru_own[6],
        lru_own[7],
        out_w,
        model_own[1],
        mgate,
        mvalue,
        down,
    )


def solution(mesh):
    placed = (
        P(("grp", "seq"), None),
        P(),
        P("seq"),
        P("seq", None),
        P("seq", None),
        P("seq", None),
        P("seq"),
        P("seq", None),
        P("seq"),
        P("seq", None),
        P("seq"),
        P("seq"),
        P("seq", None),
        P("seq"),
        P("seq", None),
        P("seq", None),
        P("seq", None),
        P(("grp", "seq"), None),
    )
    fits = mesh.shape["grp"] == 4 and mesh.shape["seq"] == 8
    return jax.shard_map(
        local_fast if fits else local,
        mesh=mesh,
        in_specs=placed,
        out_specs=(
            P(("grp", "seq"), None),
            P(("grp", "seq"), None),
            P("seq"),
            P("seq", None),
            P("seq", None),
            P("seq", None),
            P("seq"),
            P("seq", None),
            P("seq"),
            P("seq", None),
            P("seq"),
            P("seq"),
            P("seq", None),
            P("seq"),
            P("seq", None),
            P("seq", None),
            P("seq", None),
        ),
        check_vma=False,
    )
```

```python
import math
from types import SimpleNamespace

import jax
import jax.numpy as jnp
from jax import lax
from jax.experimental import pallas as pl
from jax.experimental.pallas import tpu as pltpu
from jax.sharding import PartitionSpec as P

epsilon = 1e-06
cfactor = 8.0


def passed_along(value, axis, steps):
    count = lax.axis_size(axis)
    leading, last = (max(0, -steps), min(count, count - steps))
    return lax.ppermute(value, axis, [(source, source + steps) for source in range(leading, last)])


def carried_in(value, axis, join, neutral, backward):
    count, mine = (lax.axis_size(axis), lax.axis_index(axis))
    pieces = jax.tree.map(lambda part: lax.all_gather(part, axis), value)
    if backward:
        pieces = jax.tree.map(lambda part: part[::-1], pieces)
        mine = count - 1 - mine
    so_far = jax.tree.map(
        lambda part, zero: jnp.full_like(part, 0) + jnp.asarray(zero, part.dtype), value, neutral
    )

    def step(position, so_far):
        longer = join(so_far, jax.tree.map(lambda part: part[position], pieces))
        return jax.tree.map(lambda new, old: jnp.where(position < mine, new, old), longer, so_far)

    return lax.fori_loop(0, count - 1, step, so_far)


def rms_norm(rows_in, gain):
    return rows_in * lax.rsqrt(jnp.mean(rows_in * rows_in, axis=-1, keepdims=True) + epsilon) * gain


def gelu_tanh(values):
    return jax.nn.gelu(values, approximate=True)


def matmul(left, right):
    return jnp.dot(left, right, preferred_element_type=jnp.float32)


def inner_rows(left, right):
    return lax.dot_general(
        left, right, (((0,), (0,)), ((), ())), preferred_element_type=jnp.float32
    )


def outer_cols(left, right):
    return lax.dot_general(
        left, right, (((1,), (1,)), ((), ())), preferred_element_type=jnp.float32
    )


def block_apply(values, weight, heads):
    count = values.shape[0]
    width = weight.shape[1]
    parts = values.reshape(count, heads, width)
    blocks = weight.reshape(heads, width, width)
    return jnp.einsum("rhi,hij->rhj", parts, blocks, preferred_element_type=jnp.float32).reshape(
        count, heads * width
    )


def block_back(grads, weight, heads):
    count = grads.shape[0]
    width = weight.shape[1]
    parts = grads.reshape(count, heads, width)
    blocks = weight.reshape(heads, width, width)
    return jnp.einsum("rhj,hij->rhi", parts, blocks, preferred_element_type=jnp.float32).reshape(
        count, heads * width
    )


def block_grad(values, grads, heads):
    count = values.shape[0]
    width = values.shape[1] // heads
    left = values.reshape(count, heads, width)
    right = grads.reshape(count, heads, width)
    return jnp.einsum("rhi,rhj->hij", left, right, preferred_element_type=jnp.float32).reshape(
        heads * width, width
    )


def chain_combine(earlier, later):
    return (earlier[0] * later[0], later[0] * earlier[1] + later[1])


def recurrence_gates(rgate_pre, igate_pre, conv_in, decay_in):
    rgate = jax.nn.sigmoid(rgate_pre)
    igate = jax.nn.sigmoid(igate_pre)
    log_decay = -cfactor * jax.nn.softplus(-decay_in) * rgate
    return (jnp.exp(log_decay), jnp.sqrt(-jnp.expm1(2.0 * log_decay)) * igate * conv_in)


MESH = pl.DeviceIdType.MESH


class Place:
    def __init__(self):
        self.z = lax.axis_index("grp")
        seq = lax.axis_index("seq")
        self.core = seq % 2
        self.x = (seq // 2) % 2
        self.y = seq // 4
        self.seq = seq
        self.sib = (self.z, self.at(self.y, self.x, 1 - self.core))
        self.xnb = (self.z, self.at(self.y, 1 - self.x, self.core))
        self.ynb = (self.z, self.at(1 - self.y, self.x, self.core))

    def at(self, y, x, core):
        return (y * 2 + x) * 2 + core

    def level(self, z):
        return (z, self.seq)


def meet(peers):
    barrier = pltpu.get_barrier_semaphore()
    for peer in peers:
        pl.semaphore_signal(barrier, inc=1, device_id=peer, device_id_type=MESH)
    pl.semaphore_wait(barrier, len(peers))


def when(cond, body):
    if cond is None:
        body()
    else:
        pl.when(cond)(body)


GOT = ("X", "Y", "D1", "D2", "SO", "SX", "SY", "S1", "S2")
SENT = ("ox", "oy", "os", "fy", "fx", "zX", "zY", "zD1", "zD2", "SX", "SY", "S1", "S2")


class Gather:
    def __init__(self, place, shards, fulls, kinds, send, recv, own, bounce):
        self.p, self.shards, self.fulls, self.bounce = place, shards, fulls, bounce
        self.send, self.recv, self.own = send, recv, own
        even = place.z % 2 == 0
        odd = place.z % 2 == 1
        self.fetch = [(None, even, odd)[kind] for kind in kinds]
        self.shared = [kind > 0 for kind in kinds]
        self.znb = place.level(place.z + 1 - 2 * (place.z % 2))

    def part(self, i, name):
        p = self.p
        n = self.shards[i].shape[0]
        spot = {
            "O": (p.y, p.x, p.core), "X": (p.y, 1 - p.x, p.core), "Y": (1 - p.y, p.x, p.core),
            "D1": (1 - p.y, 1 - p.x, p.core), "D2": (1 - p.y, 1 - p.x, p.core),
            "SO": (p.y, p.x, 1 - p.core), "SX": (p.y, 1 - p.x, 1 - p.core), "SY": (1 - p.y, p.x, 1 - p.core),
            "S1": (1 - p.y, 1 - p.x, 1 - p.core), "S2": (1 - p.y, 1 - p.x, 1 - p.core),
        }[name]
        first = pl.multiple_of(p.at(*spot) * n, n)
        if name in ("D1", "S1"):
            return pl.ds(first, n // 2)
        if name in ("D2", "S2"):
            return pl.ds(pl.multiple_of(first + n // 2, n // 2), n // 2)
        return pl.ds(first, n)

    def half(self, i, name, which):
        n = self.shards[i].shape[0]
        first = self.part(i, name).start
        return pl.ds(pl.multiple_of(first + which * (n // 2), n // 2), n // 2)

    def copy(self, i, how, got, peer, rows, src=None):
        full = self.fulls[i]
        return pltpu.make_async_remote_copy(
            src_ref=full.at[rows] if src is None else src,
            dst_ref=full.at[rows],
            send_sem=self.send.at[i, SENT.index(how)],
            recv_sem=self.recv.at[i, GOT.index(got)],
            device_id=peer,
            device_id_type=MESH,
        )

    def wait(self, i, name):
        self.copy(i, "ox", name, self.p.sib, self.part(i, name)).wait_recv()

    def own_far(self, i):
        p, mine = self.p, self.part(i, "O")
        return [self.copy(i, "ox", "X", p.xnb, mine, self.shards[i]), self.copy(i, "oy", "Y", p.ynb, mine, self.shards[i])]

    def own_near(self, i):
        return self.copy(i, "os", "SO", self.p.sib, self.part(i, "O"), self.shards[i])

    def own_kept(self, i, leg):
        if leg == 0:
            return pltpu.make_async_copy(self.shards[i], self.bounce[i], self.own.at[i, 0])
        return pltpu.make_async_copy(self.bounce[i], self.fulls[i].at[self.part(i, "O")], self.own.at[i, 1])

    def start(self, i):
        def far():
            for c in self.own_far(i):
                c.start()

        when(self.fetch[i], far)
        self.own_near(i).start()
        self.own_kept(i, 0).start()

    def onward_far(self, i, name):
        p = self.p
        far = []
        if name == "X":
            far.append(self.copy(i, "fy", "D1", p.ynb, self.half(i, "X", 0)))
        if name == "Y":
            far.append(self.copy(i, "fx", "D2", p.xnb, self.half(i, "Y", 1)))
        if self.shared[i]:
            far.append(self.copy(i, "z" + name, name, self.znb, self.part(i, name)))
        return far

    def onward_near(self, i, name):
        to_sib = {"X": "SX", "Y": "SY", "D1": "S1", "D2": "S2"}[name]
        return self.copy(i, to_sib, to_sib, self.p.sib, self.part(i, name))

    def relay(self, i, names):
        for name in names:
            self.wait(i, name)

            def far(name=name):
                for c in self.onward_far(i, name):
                    c.start()

            if name in ("X", "Y") or self.shared[i]:
                when(self.fetch[i], far)
            self.onward_near(i, name).start()
            if name == "X":
                self.own_kept(i, 0).wait()
                self.own_kept(i, 1).start()

    def arrive(self, i):
        for name in ("SO", "SX", "SY", "S1", "S2"):
            self.wait(i, name)
        self.own_kept(i, 1).wait()

    def drain(self, i):
        self.own_near(i).wait_send()
        for name in ("X", "Y", "D1", "D2"):
            self.onward_near(i, name).wait_send()

        def far():
            for c in self.own_far(i):
                c.wait_send()
            for name in ("X", "Y", "D1", "D2"):
                for c in self.onward_far(i, name):
                    c.wait_send()

        when(self.fetch[i], far)

    def peers(self):
        return [self.p.sib, self.p.xnb, self.p.ynb, self.znb]


def rows_loop(total, body, step=16, start=0):
    @pl.loop(start // step, total // step)
    def _(k):
        body(pl.ds(pl.multiple_of(k * step, step), step))


def wide(value):
    return value.astype(jnp.float32)

class Reduce:
    def __init__(self, place, slots, sems):
        self.p = place
        self.slots = slots
        self.send, self.recv = sems
        z = place.z
        inner = (z == 1) | (z == 2)
        self.inner = inner
        self.outer = (z == 0) | (z == 3)
        self.peer = place.level(jnp.where(inner, 3 - z, z))
        self.out = place.level(jnp.where(z < 2, 1 - z, 5 - z))
        self.me = 2 * place.y + place.x

    def makes(self, h):
        return self.p.z == 1 + h

    def helps(self, h):
        return self.p.z == 2 - h

    def copy(self, i, tag, src, dst, peer):
        return pltpu.make_async_remote_copy(
            src_ref=src, dst_ref=dst, send_sem=self.send.at[i, tag], recv_sem=self.recv.at[i, tag], device_id=peer, device_id_type=MESH
        )

    def first(self, i, h):
        p, s = self.p, self.slots[i]
        if h == 0:
            return [self.copy(i, q, s.ab.at[0, 2 * q + 1 - p.x], s.fr.at[0, q], p.xnb) for q in range(2)]
        return [self.copy(i, 2 + q, s.ab.at[1, 2 * (1 - p.y) + q], s.fr.at[1, q], p.ynb) for q in range(2)]

    def second(self, i, h):
        p, s = self.p, self.slots[i]
        if h == 0:
            return self.copy(i, 4, s.ab.at[0, 2 * (1 - p.y) + p.x], s.se.at[0], p.ynb)
        return self.copy(i, 5, s.ab.at[1, 2 * p.y + 1 - p.x], s.se.at[1], p.xnb)

    def up(self, i, h):
        s = self.slots[i]
        return self.copy(i, 6 + h, s.ab.at[h, self.me], s.zo.at[h], self.out)

    def across(self, i, h):
        s = self.slots[i]
        return self.copy(i, 8 + h, s.ab.at[h, self.me], s.zp, self.peer)

    def down(self, i, h):
        res = self.slots[i].res.at[h]
        return self.copy(i, 10 + h, res, res, self.out)

    def over(self, i, h):
        res = self.slots[i].res.at[h]
        return self.copy(i, 12 + h, res, res, self.peer)

    def start_first(self, i, h):
        for cp in self.first(i, h):
            cp.start()

    def add_first(self, i, h):
        p, s = self.p, self.slots[i]
        for cp in self.first(i, h):
            cp.wait_recv()
        for q in range(2):
            j = 2 * q + p.x if h == 0 else 2 * p.y + q

            def body(rows, q=q, j=j):
                s.ab[h, j, rows, :] = low(wide(s.ab[h, j, rows, :]) + wide(s.fr[h, q, rows, :]))

            rows_loop(s.n, body)
        self.second(i, h).start()

    def add_second(self, i, h):
        s, me = self.slots[i], self.me
        self.second(i, h).wait_recv()

        def body(rows):
            s.ab[h, me, rows, :] = low(wide(s.ab[h, me, rows, :]) + wide(s.se[h, rows, :]))

        rows_loop(s.n, body)

        @pl.when(self.outer)
        def _():
            self.up(i, h).start()

    def add_outer(self, i, h):
        s, me = self.slots[i], self.me

        @pl.when(self.inner)
        def _():
            self.up(i, h).wait_recv()

            def body(rows):
                s.ab[h, me, rows, :] = low(wide(s.ab[h, me, rows, :]) + wide(s.zo[h, rows, :]))

            rows_loop(s.n, body)

        @pl.when(self.helps(h))
        def _():
            self.across(i, h).start()

    def add_peer(self, i, h):
        s, me = self.slots[i], self.me

        @pl.when(self.makes(h))
        def _():
            self.across(i, h).wait_recv()

            def body(rows):
                s.res[h, rows, :] = low(wide(s.ab[h, me, rows, :]) + wide(s.zp[rows, :]))

            rows_loop(s.n, body)
            self.down(i, h).start()
            self.over(i, h).start()

    def pass_on(self, i, h):
        @pl.when(self.helps(h))
        def _():
            self.over(i, h).wait_recv()
            self.down(i, h).start()

    def arrive(self, i, h):
        @pl.when(self.outer)
        def _():
            self.down(i, h).wait_recv()

    def drain(self, i):
        for h in range(2):

            @pl.when(self.outer)
            def _(h=h):
                self.up(i, h).wait_send()

            @pl.when(self.inner)
            def _(h=h):
                self.down(i, h).wait_send()

            @pl.when(self.makes(h))
            def _(h=h):
                self.over(i, h).wait_send()

            @pl.when(self.helps(h))
            def _(h=h):
                self.across(i, h).wait_send()

            for cp in self.first(i, h) + [self.second(i, h)]:
                cp.wait_send()


class Small:
    def __init__(self, place, total, slots, sems):
        p = place
        self.total, self.slots = total, slots
        self.send, self.recv = sems
        z = p.z
        self.order = [p.sib, p.xnb, p.ynb, p.level(z + 1 - 2 * (z % 2)), p.level((z + 2) % 4)]

    def copy(self, k):
        return pltpu.make_async_remote_copy(
            src_ref=self.slots.at[0, k],
            dst_ref=self.slots.at[1, k],
            send_sem=self.send.at[k],
            recv_sem=self.recv.at[k],
            device_id=self.order[k],
            device_id_type=MESH,
        )

    def begin(self):
        self.slots[0, 0] = self.total[...]
        self.copy(0).start()

    def step(self, k):
        self.copy(k).wait_recv()
        both = self.slots[0, k] + self.slots[1, k]
        if k < 4:
            self.slots[0, k + 1] = both
            self.copy(k + 1).start()
        else:
            self.total[...] = both

    def drain(self):
        for k in range(5):
            self.copy(k).wait_send()

ROOT = math.sqrt(2.0 / math.pi)
CUBE = 0.044715
LANES = 128


def low(value):
    return value.astype(jnp.bfloat16)


def gelu_parts(v):
    square = v * v
    t = jnp.tanh(ROOT * (v + CUBE * v * square))
    half = 0.5 * (1.0 + t)
    return v * half, half + 0.5 * v * (1.0 - t * t) * (ROOT * (1.0 + 3.0 * CUBE * square))


def dot(left, right):
    return jnp.dot(left, right, preferred_element_type=jnp.float32)


def dot_t(left, right):
    return lax.dot_general(left, right, (((1,), (1,)), ((), ())), preferred_element_type=jnp.float32)


def sigmoid(v):
    return 1.0 / (1.0 + jnp.exp(-v))


def minus_expm1(twice, half_of):
    t = jnp.tanh(half_of)
    return -2.0 * t / (1.0 - t)


def softplus_minus(v):
    return jnp.maximum(-v, 0.0) + jnp.log1p(jnp.exp(-jnp.abs(v)))


def strided_scan(decay_ref, value_ref, prod_ref, sum_ref, backward, rows, between):
    tiles, _, lanes = sum_ref.shape
    span = rows // 8

    def step(k, carry):
        prod, total = carry
        t = span - 1 - k if backward else k
        spot = pl.ds(t, 8, stride=span)
        new_prod, new_total = [], []
        for c in range(tiles):
            d, v = decay_ref[c, spot, :], value_ref[c, spot, :]
            if backward:
                seen = total[c] + v
                sum_ref[c, spot, :] = seen
                prod_ref[c, spot, :] = prod[c]
                new_prod.append(prod[c] * d)
                new_total.append(seen * d)
            else:
                new_prod.append(prod[c] * d)
                new_total.append(total[c] * d + v)
                prod_ref[c, spot, :] = new_prod[c]
                sum_ref[c, spot, :] = new_total[c]
        return new_prod, new_total

    ones = [jnp.ones((8, lanes), jnp.float32)] * tiles
    zeros = [jnp.zeros((8, lanes), jnp.float32)] * tiles
    half = lax.fori_loop(0, span // 2, step, (ones, zeros), unroll=2)
    between()
    return lax.fori_loop(span // 2, span, step, half, unroll=2)


def segment_ends(ends, backward):
    before, whole = [], []
    order = range(7, -1, -1) if backward else range(8)
    for prod, total in zip(*ends):
        p = jnp.ones((1, prod.shape[1]), jnp.float32)
        s = jnp.zeros((1, prod.shape[1]), jnp.float32)
        ps, ss = [None] * 8, [None] * 8
        for k in order:
            ps[k], ss[k] = p, s
            d, v = prod[k : k + 1], total[k : k + 1]
            p, s = p * d, s * d + v
        before.append((jnp.concatenate(ps, axis=0), jnp.concatenate(ss, axis=0)))
        whole.append((p, s))
    return before, whole


class Ends:
    def __init__(self, place, slots, sems, backward):
        self.p, self.slots, self.backward = place, slots, backward
        self.send, self.recv = sems

    def copy(self, d):
        to = (self.p.seq + d) % 8
        return pltpu.make_async_remote_copy(
            src_ref=self.slots.at[self.p.seq], dst_ref=self.slots.at[self.p.seq], send_sem=self.send.at[d - 1],
            recv_sem=self.recv.at[d - 1], device_id=(self.p.z, to), device_id_type=MESH,
        )

    def come(self, d):
        src = (self.p.seq + 8 - d) % 8
        return pltpu.make_async_remote_copy(
            src_ref=self.slots.at[src], dst_ref=self.slots.at[src], send_sem=self.send.at[d - 1],
            recv_sem=self.recv.at[d - 1], device_id=(self.p.z, src), device_id_type=MESH,
        )

    def tell(self, whole):
        for c, (prod, total) in enumerate(whole):
            self.slots[self.p.seq, 0, c : c + 1, :] = prod
            self.slots[self.p.seq, 1, c : c + 1, :] = total
        for d in range(1, 8):
            self.copy(d).start()

    def joined(self):
        for d in range(1, 8):
            self.come(d).wait_recv()
        carry = jnp.zeros(self.slots.shape[2:], jnp.float32)
        for k in range(7, 0, -1) if self.backward else range(7):
            further = self.slots[k, 0] * carry + self.slots[k, 1]
            counts = k > self.p.seq if self.backward else k < self.p.seq
            carry = jnp.where(counts, further, carry)
        return carry

    def drain(self):
        for d in range(1, 8):
            self.copy(d).wait_send()


def named(keys, refs):
    return SimpleNamespace(**dict(zip(keys, refs)))


HBM = pl.BlockSpec(memory_space=pl.ANY)
VMEM = pl.BlockSpec(memory_space=pltpu.VMEM)


def forward_call(lengths, tokens, shards):
    rows, width = tokens.shape
    lru = shards[1].shape[1]
    ff = shards[5].shape[1]
    tiles = lru // LANES
    kinds = (0,) * 8
    count = len(shards)
    f32, bf = jnp.float32, jnp.bfloat16
    shape = jax.ShapeDtypeStruct
    wholes = [shape((8 * s.shape[0], s.shape[1]), s.dtype) for s in shards]
    saved = dict(
        mixed=shape((rows, width), bf),
        small=shape((16, lru), f32),
        n1t=shape((width, rows), bf),
        pre=shape((tiles, rows, LANES), f32),
        lin=shape((tiles, rows + 8, LANES), f32),
        convt=shape((tiles, LANES, rows), bf),
        decay=shape((tiles, rows, LANES), f32),
        k2=shape((tiles, rows, LANES), f32),
        k3=shape((tiles, rows, LANES), f32),
        k6=shape((tiles, rows, LANES), f32),
        k7=shape((tiles, rows, LANES), f32),
        slope=shape((tiles, rows, LANES), f32),
        rect=shape((lru, rows), bf),
        resid=shape((rows, width), f32),
        n2t=shape((width, rows), bf),
        mg=shape((rows, ff), f32),
        mv=shape((rows, ff), f32),
        hidt=shape((ff, rows), bf),
    )
    names = list(saved)
    scratch = dict(
        x=pltpu.VMEM((rows, width), bf),
        n1=pltpu.VMEM((rows, width), bf),
        n1t=pltpu.VMEM((width, rows), bf),
        parts=pltpu.VMEM((8 * 16, lru), f32),
        small=pltpu.VMEM((16, lru), f32),
        pre=pltpu.VMEM((tiles, rows, LANES), f32),
        lin=pltpu.VMEM((tiles, rows + 8, LANES), f32),
        convt=pltpu.VMEM((tiles, LANES, rows), bf),
        decay=pltpu.VMEM((tiles, rows, LANES), f32),
        k2=pltpu.VMEM((tiles, rows, LANES), f32),
        k3=pltpu.VMEM((tiles, rows, LANES), f32),
        k6=pltpu.VMEM((tiles, rows, LANES), f32),
        k7=pltpu.VMEM((tiles, rows, LANES), f32),
        prod=pltpu.VMEM((tiles, rows, LANES), f32),
        total=pltpu.VMEM((tiles, rows, LANES), f32),
        rec=pltpu.VMEM((rows, lru), bf),
        rect=pltpu.VMEM((lru, rows), bf),
        resid=pltpu.VMEM((rows, width), f32),
        n2=pltpu.VMEM((rows, width), bf),
        n2t=pltpu.VMEM((width, rows), bf),
        hidden=pltpu.VMEM((rows, ff), bf),
        ends=pltpu.VMEM((8, 2, tiles, LANES), f32),
        gsend=pltpu.SemaphoreType.DMA((count, len(SENT))),
        grecv=pltpu.SemaphoreType.DMA((count, len(GOT))),
        gown=pltpu.SemaphoreType.DMA((count, 2)),
        esend=pltpu.SemaphoreType.DMA((7,)),
        erecv=pltpu.SemaphoreType.DMA((7,)),
        hsend=pltpu.SemaphoreType.DMA(()),
        hrecv=pltpu.SemaphoreType.DMA(()),
        load=pltpu.SemaphoreType.DMA((2,)),
        keep=pltpu.SemaphoreType.DMA((len(names),)),
    )
    keys = list(scratch)
    R = 128

    def kernel(lengths_ref, tokens_ref, *refs):
        ins, outs = refs[:count], refs[count : 2 * count]
        out = named(names, refs[2 * count : 2 * count + len(names)])
        bounce = refs[-count:]
        v = named(keys, refs[2 * count + len(names) : -count])
        gelu_w, input_w, gates_w, output_w, mgate_w, mvalue_w, mdown_w = outs[1:]
        place = Place()
        gather = Gather(place, ins, outs, kinds, v.gsend, v.grecv, v.gown, bounce)
        ends = Ends(place, v.ends, (v.esend, v.erecv), False)
        z, seq = place.z, place.seq
        meet([(z, (seq + d) % 8) for d in range(1, 8)])
        kept = []

        def keep(src, dst):
            cp = pltpu.make_async_copy(src, dst, v.keep.at[len(kept)])
            cp.start()
            kept.append(cp)

        load = pltpu.make_async_copy(tokens_ref, v.x, v.load.at[0])
        load.start()
        for i in range(4):
            gather.start(i)
        load.wait()
        gather.relay(0, ("X", "Y"))
        gather.start(4)
        gather.relay(0, ("D1", "D2"))
        gather.arrive(0)
        load = pltpu.make_async_copy(outs[0], v.parts, v.load.at[1])
        load.start()
        gather.relay(1, ("X", "Y"))
        load.wait()
        small = v.small
        total = v.parts[0:16, :]
        for k in range(1, 8):
            total = total + v.parts[16 * k : 16 * (k + 1), :]
        small[...] = total
        keep(v.small, out.small)

        def norm_one(at):
            x = wide(v.x[at, :])
            scale = lax.rsqrt(jnp.mean(x * x, axis=-1, keepdims=True) + epsilon)
            v.n1[at, :] = low(x * scale * small[8:9, :width])

        rows_loop(rows, norm_one, 64)
        gather.relay(2, ("X", "Y"))
        gather.start(5)
        gather.relay(1, ("D1", "D2"))

        def turn(src, dst, at):
            dst[at, :] = src[:, at].T

        @pl.loop(0, width // 256)
        def _(k):
            turn(v.n1, v.n1t, pl.ds(pl.multiple_of(k * 256, 256), 256))

        keep(v.n1t, out.n1t)
        gather.relay(3, ("X", "Y"))
        gather.relay(2, ("D1", "D2"))
        gather.arrive(1)

        def project(weight, dst, first):
            def body(w):
                t = pl.program_id(0)
                both = dot(v.n1[...], w[...])
                dst[2 * t, pl.ds(first, rows), :] = both[:, :LANES]
                dst[2 * t + 1, pl.ds(first, rows), :] = both[:, LANES:]

            pltpu.emit_pipeline(body, grid=(tiles // 2,), in_specs=[pl.BlockSpec((width, 2 * LANES), lambda t: (0, t))])(weight)

        project(gelu_w, v.pre, 0)
        gather.relay(4, ("X", "Y"))
        gather.start(6)
        gather.relay(3, ("D1", "D2"))
        gather.arrive(2)
        project(input_w, v.lin, 8)

        def halo():
            return pltpu.make_async_remote_copy(
                src_ref=v.lin.at[:, pl.ds(rows, 8)], dst_ref=v.lin.at[:, pl.ds(0, 8)], send_sem=v.hsend, recv_sem=v.hrecv,
                device_id=(z, (seq + 1) % 8), device_id_type=MESH,
            )

        @pl.when(seq < 7)
        def _():
            halo().start()

        gather.relay(5, ("X", "Y"))
        gather.relay(4, ("D1", "D2"))
        gather.start(7)
        gather.arrive(3)

        @pl.when(seq == 0)
        def _():
            v.lin[:, 0:8, :] = jnp.zeros((tiles, 8, LANES), f32)

        @pl.when(seq > 0)
        def _():
            halo().wait_recv()

        keep(v.lin, out.lin)

        def gates(w):
            h = pl.program_id(0)
            lane = pl.ds(pl.multiple_of(h * LANES, LANES), LANES)
            taps = [small[k : k + 1, lane] for k in range(4)]
            cb, rb, ib, dp = [small[k : k + 1, lane] for k in range(4, 8)]
            rate = -cfactor * softplus_minus(dp)
            for r in range(0, rows, R):
                acc = cb + taps[0] * v.lin[h, 8 + r : 8 + r + R, :]
                for k in range(1, 4):
                    acc = acc + taps[k] * v.lin[h, 8 + r - k : 8 + r - k + R, :]
                cl = low(acc)
                v.convt[h, :, r : r + R] = cl.T
                both = dot(cl, w[...])
                rg = sigmoid(both[:, :LANES] + rb)
                ig = sigmoid(both[:, LANES:] + ib)
                log_decay = rate * rg
                decay = jnp.exp(log_decay)
                mult = jnp.sqrt(minus_expm1(2.0 * log_decay, log_decay))
                cv = wide(cl)
                through = mult * ig
                at = slice(r, r + R)
                v.prod[h, at, :] = decay
                v.decay[h, at, :] = decay
                v.total[h, at, :] = through * cv
                v.k3[h, at, :] = through
                v.k2[h, at, :] = through * cv * (1.0 - ig)
                v.k6[h, at, :] = ig * cv * (decay * decay) / mult
                v.k7[h, at, :] = rg

        pltpu.emit_pipeline(gates, grid=(tiles,), in_specs=[pl.BlockSpec((LANES, 2 * LANES), lambda h: (h, 0))])(gates_w)
        for src, dst in ((v.convt, out.convt), (v.decay, out.decay), (v.k2, out.k2), (v.k3, out.k3)):
            keep(src, dst)
        gather.relay(6, ("X", "Y"))
        gather.relay(5, ("D1", "D2"))
        tails = strided_scan(v.prod, v.total, v.prod, v.total, False, rows, lambda: None)
        before, whole = segment_ends(tails, False)
        ends.tell(whole)
        gather.relay(7, ("X", "Y"))
        gather.relay(6, ("D1", "D2"))
        carry = ends.joined()
        span = rows // 8
        for c in range(tiles):
            into = before[c][0] * carry[c : c + 1, :] + before[c][1]
            v.parts[8 * c : 8 * c + 8, 0:LANES] = into

        @pl.loop(0, tiles)
        def _(c):
            lane = pl.ds(pl.multiple_of(c * LANES, LANES), LANES)
            into = v.parts[pl.ds(pl.multiple_of(c * 8, 8), 8), 0:LANES]
            rate = -cfactor * softplus_minus(small[7:8, lane])
            first = lax.broadcasted_iota(jnp.int32, (span, LANES), 0) == 0
            for s in range(8):
                at = slice(s * span, (s + 1) * span)
                state = v.total[c, at, :] + v.prod[c, at, :] * into[s : s + 1, :]
                before_it = jnp.where(first, into[s : s + 1, :], pltpu.roll(state, 1, axis=0))
                rg = v.k7[c, at, :]
                k7 = (before_it * v.decay[c, at, :] - v.k6[c, at, :]) * rg
                v.k7[c, at, :] = k7
                v.k6[c, at, :] = k7 * rate * (1.0 - rg)
                value, slope = gelu_parts(v.pre[c, at, :])
                v.rec[at, lane] = low(state * value)
                v.pre[c, at, :] = value
                v.total[c, at, :] = state * slope
            v.rect[lane, :] = v.rec[:, lane].T

        for src, dst in ((v.k6, out.k6), (v.k7, out.k7), (v.pre, out.pre), (v.total, out.slope)):
            keep(src, dst)
        keep(v.rect, out.rect)
        gather.arrive(4)

        def back_to_width(w):
            t = pl.program_id(0)
            at = pl.ds(pl.multiple_of(t * 256, 256), 256)
            v.resid[:, at] = wide(v.x[:, at]) + dot(v.rec[...], w[...])

        pltpu.emit_pipeline(back_to_width, grid=(width // 256,), in_specs=[pl.BlockSpec((lru, 256), lambda t: (0, t))])(output_w)
        keep(v.resid, out.resid)
        def norm_two(at):
            x = v.resid[at, :]
            scale = lax.rsqrt(jnp.mean(x * x, axis=-1, keepdims=True) + epsilon)
            v.n2[at, :] = low(x * scale * small[9:10, :width])

        rows_loop(rows, norm_two, 64)

        @pl.loop(0, width // 256)
        def _(k):
            turn(v.n2, v.n2t, pl.ds(pl.multiple_of(k * 256, 256), 256))

        keep(v.n2t, out.n2t)
        gather.arrive(5)
        gather.arrive(6)

        def mlp(wg, wv, mg, mv, hidt):
            t = pl.program_id(0)
            at = pl.ds(pl.multiple_of(t * 256, 256), 256)
            mg[...] = dot(v.n2[...], wg[...])
            mv[...] = dot(v.n2[...], wv[...])

            def act(rs):
                value, slope = gelu_parts(mg[rs, :])
                linear = mv[rs, :]
                v.hidden[rs, at] = low(value * linear)
                mg[rs, :] = value
                mv[rs, :] = linear * slope

            rows_loop(rows, act, 64)
            hidt[...] = v.hidden[:, at].T

        wide_tile = pl.BlockSpec((width, 256), lambda t: (0, t))
        pltpu.emit_pipeline(
            mlp,
            grid=(ff // 256,),
            in_specs=[wide_tile, wide_tile],
            out_specs=[pl.BlockSpec((rows, 256), lambda t: (0, t))] * 2 + [pl.BlockSpec((256, rows), lambda t: (t, 0))],
        )(mgate_w, mvalue_w, out.mg, out.mv, out.hidt)
        gather.relay(7, ("D1", "D2"))
        gather.arrive(7)
        valid_rows = lengths_ref[z] - seq * rows

        def down(w, mixed):
            t = pl.program_id(0)
            at = pl.ds(pl.multiple_of(t * 256, 256), 256)
            valid = (lax.broadcasted_iota(jnp.int32, (rows, 256), 0) < valid_rows).astype(f32)
            mixed[...] = low((v.resid[:, at] + dot(v.hidden[...], w[...])) * valid)

        pltpu.emit_pipeline(
            down,
            grid=(width // 256,),
            in_specs=[pl.BlockSpec((ff, 256), lambda t: (0, t))],
            out_specs=[pl.BlockSpec((rows, 256), lambda t: (0, t))],
        )(mdown_w, out.mixed)
        for cp in kept:
            cp.wait()
        for i in range(count):
            gather.drain(i)
        ends.drain()

        @pl.when(seq < 7)
        def _():
            halo().wait_send()

    result = pl.pallas_call(
        kernel,
        out_shape=wholes + [saved[name] for name in names],
        in_specs=[pl.BlockSpec(memory_space=pltpu.SMEM), HBM] + [HBM] * count,
        out_specs=[HBM] * (count + len(names)),
        scratch_shapes=[scratch[key] for key in keys] + [pltpu.VMEM(s.shape, s.dtype) for s in shards],
        compiler_params=pltpu.CompilerParams(collective_id=1, has_side_effects=True, vmem_limit_bytes=60 << 20),
        name="forward",
    )(lengths, tokens, *shards)
    return result[:count], named(names, result[count:])

def slot_scratch(rows, columns):
    n, h = rows // 8, columns // 2
    bf = jnp.bfloat16
    return dict(
        ab=pltpu.VMEM((2, 4, n, h), bf),
        fr=pltpu.VMEM((2, 2, n, h), bf),
        se=pltpu.VMEM((2, n, h), bf),
        zo=pltpu.VMEM((2, n, h), bf),
        zp=pltpu.VMEM((n, h), bf),
        res=pltpu.VMEM((2, n, h), bf),
    )


PUMPS = (
    (),
    (),
    (),
    (),
    (),
    (),
    ((6, 0, 0),),
    ((6, 0, 1),),
    (),
    (),
    (),
    (),
    (),
    ((6, 1, 0),),
    ((6, 2, 1),),
    (),
    (),
    (),
    ((0, 0, 0), (0, 0, 1),),
    (),
    (),
    (),
    (),
    (),
    ((0, 1, 0), (6, 2, 0), (0, 2, 1),),
    (),
    (),
    ((1, 0, 1),),
    ((1, 0, 0), (6, 1, 1),),
    (),
    (),
    (),
    ((2, 0, 1), (1, 1, 0),),
    ((0, 2, 0), (6, 3, 0), (2, 0, 0),),
    (),
    (),
    ((3, 0, 1),),
    ((1, 2, 1),),
    ((2, 1, 0), (6, 3, 1), (0, 1, 1), (3, 0, 0),),
    ((0, 3, 0),),
    ((6, 4, 0),),
    ((1, 2, 0), (2, 2, 1),),
    ((4, 0, 1),),
    ((6, 4, 1),),
    ((4, 0, 0), (1, 1, 1), (0, 3, 1),),
    ((3, 1, 0), (2, 2, 0), (1, 3, 0),),
    ((3, 2, 1), (6, 6, 0), (6, 6, 1), (0, 4, 0),),
    (),
    (),
    ((2, 1, 1), (1, 3, 1), (0, 6, 0), (0, 4, 1), (0, 6, 1), (4, 1, 0), (3, 2, 0), (2, 3, 0),),
    ((1, 4, 0), (1, 6, 0),),
    ((2, 3, 1), (6, 5, 0), (1, 4, 1), (1, 6, 1),),
    ((6, 5, 1),),
    ((4, 2, 1), (3, 1, 1),),
    ((2, 4, 0), (2, 6, 0), (3, 3, 0), (2, 4, 1), (2, 6, 1), (0, 5, 0), (4, 2, 0), (0, 5, 1), (3, 3, 1), (4, 1, 1), (1, 5, 0), (1, 5, 1), (4, 3, 0), (3, 4, 0), (3, 6, 0), (2, 5, 0), (3, 4, 1), (3, 6, 1), (4, 3, 1), (2, 5, 1), (4, 4, 0), (3, 5, 0), (4, 6, 0), (4, 4, 1), (3, 5, 1), (4, 6, 1), (4, 5, 0), (4, 5, 1), (5, 0, 0), (5, 0, 1), (5, 1, 0), (5, 2, 0), (5, 2, 1), (5, 3, 0), (5, 1, 1), (5, 4, 0), (5, 6, 0), (5, 3, 1), (5, 5, 0), (5, 4, 1), (5, 6, 1), (5, 5, 1),),
)


def backward_call(lengths, tokens, cotangent, weights, saved):
    rows, width = tokens.shape
    gelu_full, input_full, gates_full, output_full, mgate_full, mvalue_full, mdown_full = weights
    lru, ff = gelu_full.shape[1], mgate_full.shape[1]
    tiles = lru // LANES
    wide_tile = 2 * LANES
    f32, bf = jnp.float32, jnp.bfloat16
    shape = jax.ShapeDtypeStruct
    DOWN, MGATE, MVALUE, OUTPUT, GELU, INPUT, GATES = range(7)
    full = [mdown_full, mgate_full, mvalue_full, output_full, gelu_full, input_full, gates_full]
    extents = [w.shape for w in full]
    count = len(full)
    split = lambda v: v.reshape(4, 2, v.shape[0] // 8, v.shape[1])
    inputs = dict(
        tokens=tokens, cot=cotangent, gelu_w=gelu_full, input_w=input_full, gates_w=gates_full, output_w=output_full, mgate_w=mgate_full,
        mvalue_w=mvalue_full, mdown_w=mdown_full, small=saved.small, n1t=split(saved.n1t), pre=saved.pre, lin=saved.lin,
        convt=saved.convt, decay=saved.decay, k6=saved.k6, k2=saved.k2, k3=saved.k3, k7=saved.k7, slope=saved.slope,
        rect=split(saved.rect), resid=saved.resid, n2t=split(saved.n2t), mg=saved.mg, mv=saved.mv, hidt=split(saved.hidt),
    )
    slot_keys = list(slot_scratch(8, 256))
    most = max(4 * (r // 8) * (c // 2) // wide_tile for r, c in extents)
    passes = 13
    scratch = dict(
        go=pltpu.VMEM((rows, width), bf),
        gm=pltpu.VMEM((rows, width), bf),
        gn=pltpu.VMEM((rows, width), f32),
        n1t=pltpu.VMEM((4, 2, width // 8, rows), bf),
        n2t=pltpu.VMEM((4, 2, width // 8, rows), bf),
        rect=pltpu.VMEM((4, 2, lru // 8, rows), bf),
        small=pltpu.VMEM((16, lru), f32),
        part=pltpu.VMEM((16, lru), f32),
        gain=pltpu.VMEM((8, width), f32),
        into=pltpu.VMEM((tiles, 8, LANES), f32),
        halo=pltpu.VMEM((tiles, 8, LANES), f32),
        edge=pltpu.VMEM((tiles, 8, LANES), f32),
        stage=pltpu.VMEM((2, most, wide_tile), bf),
        landed=pltpu.VMEM((2, most, wide_tile), bf),
        gstage=pltpu.VMEM((4, 2, lru // 8, wide_tile), bf),
        ends=pltpu.VMEM((8, 2, tiles, LANES), f32),
        sslots=pltpu.VMEM((2, 5, 16, lru), f32),
        psend=pltpu.SemaphoreType.DMA((passes,)),
        precv=pltpu.SemaphoreType.DMA((passes,)),
        rsend=pltpu.SemaphoreType.DMA((count, 14)),
        rrecv=pltpu.SemaphoreType.DMA((count, 14)),
        esend=pltpu.SemaphoreType.DMA((7,)),
        erecv=pltpu.SemaphoreType.DMA((7,)),
        hsend=pltpu.SemaphoreType.DMA(()),
        hrecv=pltpu.SemaphoreType.DMA(()),
        ssend=pltpu.SemaphoreType.DMA((5,)),
        srecv=pltpu.SemaphoreType.DMA((5,)),
        load=pltpu.SemaphoreType.DMA((8,)),
        keep=pltpu.SemaphoreType.DMA((count + 1, 2)),
        credit=pltpu.SemaphoreType.REGULAR,
    )
    keys = list(scratch)
    outs = dict(tokens_grad=shape((rows, width), f32), small_sum=shape((16, lru), f32))
    out_keys = list(outs)
    sums = [shape((r // 8, c), bf) for r, c in extents]

    def kernel(lengths_ref, *refs):
        refs = list(refs)

        def take(k):
            got = refs[:k]
            del refs[:k]
            return got

        w = named(inputs, take(len(inputs)))
        out = named(out_keys, take(len(out_keys)))
        sum_refs = take(count)
        v = named(keys, take(len(keys)))
        slots = []
        for i, (r, c) in enumerate(extents):
            s = named(slot_keys, take(len(slot_keys)))
            s.n, s.h, s.tiles = r // 8, c // 2, c // 2 // wide_tile
            slots.append(s)
        place = Place()
        z, seq, core = place.z, place.seq, place.core
        red = Reduce(place, slots, (v.rsend, v.rrecv))
        ends = Ends(place, v.ends, (v.esend, v.erecv), True)
        tot = Small(place, v.part, v.sslots, (v.ssend, v.srecv))
        small, part = v.small, v.part
        kept = []

        def load(src, dst, k):
            cp = pltpu.make_async_copy(src, dst, v.load.at[k])
            cp.start()
            return cp

        first_loads = [load(w.cot, v.go, 0)]
        loads = [load(w.small, v.small, 1), load(w.n2t, v.n2t, 2), load(w.rect, v.rect, 3), load(w.n1t, v.n1t, 4)]

        def arrived(i, h):
            red.arrive(i, h)
            s = slots[i]
            cp = pltpu.make_async_copy(s.res.at[h], sum_refs[i].at[:, pl.ds(side(i, h) * s.h, s.h)], v.keep.at[i, h])

            @pl.when(red.outer)
            def _():
                cp.start()

        def totalled(i, h):
            s = slots[i]
            return pltpu.make_async_copy(s.res.at[h], sum_refs[i].at[:, pl.ds(side(i, h) * s.h, s.h)], v.keep.at[i, h])

        def add_peer(i, h):
            red.add_peer(i, h)
            cp = totalled(i, h)

            @pl.when(red.makes(h))
            def _():
                cp.start()

        def pass_on(i, h):
            red.pass_on(i, h)
            cp = totalled(i, h)

            @pl.when(red.helps(h))
            def _():
                cp.start()

        steps = (red.add_first, red.add_second, red.add_outer, add_peer, pass_on, arrived, red.start_first)
        turn = [0]

        def serve(spot):
            for step, i, h in PUMPS[spot]:
                steps[step](i, h)

        def pump():
            serve(turn[0])
            turn[0] += 1

        def pumps_at(*grid_steps):
            spots = list(enumerate(grid_steps, turn[0]))
            turn[0] += len(spots)

            def at_step():
                for spot, grid_step in spots:
                    if PUMPS[spot]:
                        pl.when(pl.program_id(0) == grid_step)(lambda spot=spot: serve(spot))

            return at_step

        def to_sib(k, used):
            return pltpu.make_async_remote_copy(
                src_ref=v.stage.at[k % 2, pl.ds(0, used)], dst_ref=v.landed.at[k % 2, pl.ds(0, used)], send_sem=v.psend.at[k],
                recv_sem=v.precv.at[k], device_id=place.sib, device_id_type=MESH,
            )

        sent = {}

        def send_blocks(k, used):
            if k >= 2:
                pl.semaphore_wait(v.credit, 1)
            sent[k] = used
            to_sib(k, used).start()

        def free_stage(k):
            if k >= 2:
                to_sib(k - 2, sent[k - 2]).wait_send()

        def give_credit(k):
            if k + 2 < passes:
                pl.semaphore_signal(v.credit, inc=1, device_id=place.sib, device_id_type=MESH)

        def side(i, h):
            return 1 - h if i == MVALUE else h

        def blocks(s):
            group = max(1, 512 // s.n)
            return [(j, group) for j in range(0, 4, group)]

        def for_sib(k, i, h, left, right):
            pump()
            s = slots[i]
            free_stage(k)

            @pl.loop(0, s.tiles)
            def _(t):
                r = right[:, pl.ds(pl.multiple_of((side(i, h) * s.tiles + t) * wide_tile, wide_tile), wide_tile)]
                for j, group in blocks(s):
                    value = dot(left[j : j + group, 1 - core].reshape(group * s.n, rows), r)
                    at = pl.ds(pl.multiple_of(t * 4 * s.n + j * s.n, s.n), group * s.n)
                    v.stage[k % 2, at, :] = low(value)

            send_blocks(k, 4 * s.n * s.tiles)

        def for_us(k, i, h, left, right):
            pump()
            s = slots[i]
            to_sib(k, sent[k]).wait_recv()

            @pl.loop(0, s.tiles)
            def _(t):
                r = right[:, pl.ds(pl.multiple_of((side(i, h) * s.tiles + t) * wide_tile, wide_tile), wide_tile)]
                for j, group in blocks(s):
                    value = dot(left[j : j + group, core].reshape(group * s.n, rows), r)
                    at = pl.ds(pl.multiple_of(t * 4 * s.n + j * s.n, s.n), group * s.n)
                    both = low(value + wide(v.landed[k % 2, at, :]))
                    lane = pl.ds(pl.multiple_of(t * wide_tile, wide_tile), wide_tile)
                    s.ab[h, j : j + group, :, lane] = both.reshape(group, s.n, wide_tile)

            give_credit(k)

        def eight(value):
            return value.reshape(value.shape[0] // 8, 8, value.shape[1]).sum(axis=0)

        def norm_back(x, grad, gain, add):
            scale = lax.rsqrt(jnp.mean(x * x, axis=-1, keepdims=True) + epsilon)
            v.gain[...] += eight(grad * x * scale)
            scaled = grad * gain
            m = jnp.mean(scaled * x, axis=-1, keepdims=True)
            return add + scale * (scaled - x * (scale * scale * m))

        def mlp_half(gmg, gmv, half):
            pump()
            steps_half = ff // wide_tile // 2
            inside = pumps_at(steps_half // 3, 2 * steps_half // 3)

            def body(md, value, slope):
                inside()
                t = pl.program_id(0) + half * steps_half
                at = pl.ds(pl.multiple_of(t * wide_tile, wide_tile), wide_tile)
                gh = dot_t(v.go[...], md[...])
                gmg[:, at] = low(gh * slope[...])
                gmv[:, at] = low(gh * value[...])

            across = pl.BlockSpec((rows, wide_tile), lambda t: (0, t + half * steps_half))
            pltpu.emit_pipeline(
                body, grid=(steps_half,), in_specs=[pl.BlockSpec((wide_tile, width), lambda t: (t + half * steps_half, 0)), across, across]
            )(w.mdown_w, w.mg, w.mv)

        def mlp_norm_half(gmg, gmv, half):
            pump()

            inside = pumps_at(1)

            def body(wg, wv):
                inside()
                t = pl.program_id(0) + 2 * half
                at = pl.ds(pl.multiple_of(t * wide_tile, wide_tile), wide_tile)
                v.gn[:, at] = dot_t(gmg[...], wg[...]) + dot_t(gmv[...], wv[...])

            pltpu.emit_pipeline(body, grid=(2,), in_specs=[pl.BlockSpec((wide_tile, ff), lambda t: (t + 2 * half, 0))] * 2)(
                w.mgate_w, w.mvalue_w
            )

        def mlp_phase(gmg, gmv):
            def head(hidt):
                down_loads = load(w.hidt, hidt, 5)
                meet([(z, (seq + d) % 8) for d in range(1, 8)] + [((z + d) % 4, seq) for d in range(1, 4)])
                first_loads[0].wait()
                valid_rows = lengths_ref[z] - seq * rows

                def mask(at):
                    here = lax.broadcasted_iota(jnp.int32, (64, width), 0) + at.start < valid_rows
                    v.go[at, :] = low(jnp.where(here, wide(v.go[at, :]), 0.0))

                rows_loop(rows, mask, 64)
                part[...] = jnp.zeros_like(part)
                down_loads.wait()
                for_sib(0, DOWN, 0, hidt, v.go)
                for_sib(1, DOWN, 1, hidt, v.go)
                mlp_half(gmg, gmv, 0)
                for_us(0, DOWN, 0, hidt, v.go)
                for_us(1, DOWN, 1, hidt, v.go)

            pl.run_scoped(head, pltpu.VMEM((4, 2, ff // 8, rows), bf))
            for cp in loads:
                cp.wait()
            for_sib(2, MGATE, 0, v.n2t, gmg)
            for_sib(3, MVALUE, 1, v.n2t, gmv)
            mlp_half(gmg, gmv, 1)
            for_us(2, MGATE, 0, v.n2t, gmg)
            for_us(3, MVALUE, 1, v.n2t, gmv)
            for_sib(4, MGATE, 1, v.n2t, gmg)
            for_sib(5, MVALUE, 0, v.n2t, gmv)
            mlp_norm_half(gmg, gmv, 0)
            for_us(4, MGATE, 1, v.n2t, gmg)
            for_us(5, MVALUE, 0, v.n2t, gmv)
            mlp_norm_half(gmg, gmv, 1)

        pl.run_scoped(mlp_phase, pltpu.VMEM((rows, ff), bf), pltpu.VMEM((rows, ff), bf))
        pump()
        v.gain[...] = jnp.zeros_like(v.gain)

        inside = pumps_at(rows // 128)

        def norm_two(resid, inside=inside):
            inside()
            at = pl.ds(pl.multiple_of(pl.program_id(0) * 64, 64), 64)
            value = norm_back(resid[...], v.gn[at, :], small[9:10, :width], wide(v.go[at, :]))
            v.gn[at, :] = value
            v.gm[at, :] = low(value)

        pltpu.emit_pipeline(norm_two, grid=(rows // 64,), in_specs=[pl.BlockSpec((64, width), lambda t: (t, 0))])(w.resid)
        part[9:10, :width] = v.gain[...].sum(axis=0, keepdims=True)
        tokens_load = load(w.tokens, v.go, 6)

        def branch_phase(adj, prod, gg, gl, gri):
            decay_load = load(w.decay, prod, 7)
            for_sib(6, OUTPUT, 0, v.rect, v.gm)
            for_sib(7, OUTPUT, 1, v.rect, v.gm)
            pump()

            inside = pumps_at(tiles // 6, tiles // 3)

            def into_branch(wo, value, slope, inside=inside):
                inside()
                t = pl.program_id(0)
                gr = dot_t(v.gm[...], wo[...])
                for q in range(2):
                    c = 2 * t + q
                    grad = gr[:, q * LANES : (q + 1) * LANES]
                    adj[c, pl.ds(0, rows), :] = grad * value[q]
                    gg[:, pl.ds(pl.multiple_of(c * LANES, LANES), LANES)] = low(grad * slope[q])

            pair = pl.BlockSpec((2, rows, LANES), lambda t: (t, 0, 0))
            pltpu.emit_pipeline(
                into_branch, grid=(tiles // 2,), in_specs=[pl.BlockSpec((wide_tile, width), lambda t: (t, 0)), pair, pair]
            )(w.output_w, w.pre, w.slope)
            for_us(6, OUTPUT, 0, v.rect, v.gm)
            for_us(7, OUTPUT, 1, v.rect, v.gm)
            pump()
            decay_load.wait()
            tails = strided_scan(prod, adj, prod, adj, True, rows, pump)
            before, whole = segment_ends(tails, True)
            ends.tell(whole)
            for c in range(tiles):
                v.into[c] = before[c][1]
                v.edge[c] = before[c][0]
            for_sib(8, GELU, 0, v.n1t, gg)
            for_sib(9, GELU, 1, v.n1t, gg)
            pump()
            carry = ends.joined()
            for c in range(tiles):
                v.into[c] = v.into[c] + v.edge[c] * carry[c : c + 1, :]
            span = rows // 8

            inside = pumps_at(tiles // 4, tiles // 2, 3 * tiles // 4)

            def through_gates(k6, k2, k3, k7, convt, wg, inside=inside):
                inside()
                c = pl.program_id(0)
                lane = pl.ds(pl.multiple_of(c * LANES, LANES), LANES)
                sums = [jnp.zeros((8, LANES), f32) for _ in range(3)]
                for k in range(8):
                    at = slice(k * span, (k + 1) * span)
                    here = adj[c, at, :] + prod[c, at, :] * v.into[c, k : k + 1, :]
                    grad_r = here * k6[at, :]
                    grad_i = here * k2[at, :]
                    adj[c, at, :] = here * k3[at, :]
                    gri[at, :LANES] = low(grad_r)
                    gri[at, LANES:] = low(grad_i)
                    for q, value in enumerate((here * k7[at, :], grad_r, grad_i)):
                        sums[q] = sums[q] + eight(value)
                part[7:8, lane] = sums[0].sum(axis=0, keepdims=True) * (cfactor * sigmoid(-small[7:8, lane]))
                part[5:6, lane] = sums[1].sum(axis=0, keepdims=True)
                part[6:7, lane] = sums[2].sum(axis=0, keepdims=True)
                product = low(dot(convt[...], gri[...]))
                for q in range(2):
                    unit = 2 * c + q
                    block = unit // 3
                    at = pl.ds(pl.multiple_of((unit % 3) * 64, 64), 64)
                    v.gstage[block // 2, block % 2, at, :] = product[64 * q : 64 * (q + 1), :]
                grad_conv = adj[c, pl.ds(0, rows), :] + dot_t(gri[...], wg[...])
                adj[c, pl.ds(0, rows), :] = grad_conv
                part[4:5, lane] = eight(grad_conv).sum(axis=0, keepdims=True)

            one = pl.BlockSpec((None, rows, LANES), lambda t: (t, 0, 0))
            pltpu.emit_pipeline(
                through_gates,
                grid=(tiles,),
                in_specs=[one] * 4
                + [pl.BlockSpec((None, LANES, rows), lambda t: (t, 0, 0)), pl.BlockSpec((LANES, wide_tile), lambda t: (t, 0))],
            )(w.k6, w.k2, w.k3, w.k7, w.convt, w.gates_w)

            def halo():
                return pltpu.make_async_remote_copy(
                    src_ref=v.edge, dst_ref=v.halo, send_sem=v.hsend, recv_sem=v.hrecv, device_id=(z, (seq + 7) % 8), device_id_type=MESH
                )

            v.edge[...] = adj[:, 0:8, :]

            @pl.when(seq > 0)
            def _():
                halo().start()

            for_us(8, GELU, 0, v.n1t, gg)
            pump()
            s = slots[GATES]
            free_stage(10)
            for j in range(4):

                def copy_block(at, j=j):
                    v.stage[0, pl.ds(pl.multiple_of(j * s.n + at.start, 16), 16), :] = v.gstage[j, 1 - core, at, :]

                rows_loop(s.n, copy_block)
            send_blocks(10, 4 * s.n)
            for_us(9, GELU, 1, v.n1t, gg)
            pump()

            @pl.when(seq == 7)
            def _():
                adj[:, pl.ds(rows, 8), :] = jnp.zeros((tiles, 8, LANES), f32)

            @pl.when(seq < 7)
            def _():
                halo().wait_recv()
                adj[:, pl.ds(rows, 8), :] = v.halo[...]

            inside = pumps_at(tiles // 3, 2 * tiles // 3)

            def through_conv(lin, inside=inside):
                inside()
                c = pl.program_id(0)
                lane = pl.ds(pl.multiple_of(c * LANES, LANES), LANES)
                taps = [small[k : k + 1, lane] for k in range(4)]
                sums = [jnp.zeros((8, LANES), f32) for _ in range(4)]
                for r in range(0, rows, 128):
                    here = adj[c, r : r + 128, :]
                    acc = taps[0] * here
                    for k in range(4):
                        sums[k] = sums[k] + eight(here * lin[8 + r - k : 8 + r - k + 128, :])
                        if k:
                            acc = acc + taps[k] * adj[c, r + k : r + k + 128, :]
                    gl[r : r + 128, lane] = low(acc)
                for k in range(4):
                    part[k : k + 1, lane] = sums[k].sum(axis=0, keepdims=True)

            pltpu.emit_pipeline(
                through_conv, grid=(tiles,), in_specs=[pl.BlockSpec((None, rows + 8, LANES), lambda t: (t, 0, 0))]
            )(w.lin)
            pump()
            to_sib(10, sent[10]).wait_recv()
            for j in range(4):

                def fold(at, j=j):
                    came = v.landed[0, pl.ds(pl.multiple_of(j * s.n + at.start, 16), 16), :]
                    both = low(wide(v.gstage[j, core, at, :]) + wide(came))
                    s.ab[0, j, at, :] = both[:, : s.h]
                    s.ab[1, j, at, :] = both[:, s.h :]

                rows_loop(s.n, fold)
            give_credit(10)
            for_sib(11, INPUT, 0, v.n1t, gl)
            for_sib(12, INPUT, 1, v.n1t, gl)
            pump()

            inside = pumps_at(width // wide_tile // 2)

            def into_norm(wi, wg, inside=inside):
                inside()
                t = pl.program_id(0)
                value = dot_t(gl[...], wi[...]) + dot_t(gg[...], wg[...])
                adj[2 * t, pl.ds(0, rows), :] = value[:, :LANES]
                adj[2 * t + 1, pl.ds(0, rows), :] = value[:, LANES:]

            pltpu.emit_pipeline(into_norm, grid=(width // wide_tile,), in_specs=[pl.BlockSpec((wide_tile, lru), lambda t: (t, 0))] * 2)(
                w.input_w, w.gelu_w
            )
            for_us(11, INPUT, 0, v.n1t, gl)
            for_us(12, INPUT, 1, v.n1t, gl)
            pump()
            v.gain[...] = jnp.zeros_like(v.gain)
            tokens_load.wait()

            def norm_one(at):
                grad = jnp.concatenate([adj[c, at, :] for c in range(width // LANES)], axis=1)
                v.gn[at, :] = norm_back(wide(v.go[at, :]), grad, small[8:9, :width], v.gn[at, :])

            rows_loop(rows // 2, norm_one, 64)
            pump()
            rows_loop(rows, norm_one, 64, rows // 2)
            part[8:9, :width] = v.gain[...].sum(axis=0, keepdims=True)

        pl.run_scoped(
            branch_phase,
            pltpu.VMEM((tiles, rows + 8, LANES), f32),
            pltpu.VMEM((tiles, rows, LANES), f32),
            pltpu.VMEM((rows, lru), bf),
            pltpu.VMEM((rows, lru), bf),
            pltpu.VMEM((rows, wide_tile), bf),
        )
        tot.begin()
        cp = pltpu.make_async_copy(v.gn, out.tokens_grad, v.keep.at[count, 0])
        cp.start()
        kept.append(cp)
        last = PUMPS[turn[0]]
        for k, (step, i, h) in enumerate(last):
            steps[step](i, h)
            if k % 4 == 3 and k < 20:
                tot.step(k // 4)
        cp = pltpu.make_async_copy(part, out.small_sum, v.keep.at[count, 1])
        cp.start()
        kept.append(cp)
        for i in range(count):
            for h in range(2):
                kept.append(totalled(i, h))
        for cp in kept:
            cp.wait()
        for i in range(count):
            red.drain(i)
        for k in (passes - 2, passes - 1):
            to_sib(k, sent[k]).wait_send()
        tot.drain()
        ends.drain()

        @pl.when(seq > 0)
        def _():
            pltpu.make_async_remote_copy(
                src_ref=v.edge, dst_ref=v.halo, send_sem=v.hsend, recv_sem=v.hrecv, device_id=(z, (seq + 7) % 8), device_id_type=MESH
            ).wait_send()

    slot_list = [value for r, c in extents for value in slot_scratch(r, c).values()]
    result = pl.pallas_call(
        kernel,
        out_shape=list(outs.values()) + sums,
        in_specs=[pl.BlockSpec(memory_space=pltpu.SMEM)] + [HBM] * len(inputs),
        out_specs=[HBM] * (len(outs) + count),
        scratch_shapes=list(scratch.values()) + slot_list,
        compiler_params=pltpu.CompilerParams(collective_id=2, has_side_effects=True, vmem_limit_bytes=62 << 20),
        name="backward",
    )(lengths, *inputs.values())
    return result[0], result[1], result[len(outs) :]


def local(
    tokens,
    lengths,
    mixer_gain,
    gelu_weight,
    input_weight,
    conv_taps,
    conv_bias,
    rgate_weight,
    rgate_bias,
    igate_weight,
    igate_bias,
    decay_param,
    output_weight,
    mlp_gain,
    mlp_gate,
    mlp_value,
    mlp_down,
    cotangent,
):
    count = tokens.shape[0]
    width_lru = input_weight.shape[1]
    block = rgate_weight.shape[1]
    heads = width_lru // block
    taps_count = conv_taps.shape[1]
    rim = taps_count - 1
    seq_count = lax.axis_size("seq")
    slot_length = count * seq_count
    first_row = (lax.axis_index("grp") * seq_count + lax.axis_index("seq")) * count
    global_row = first_row + jnp.arange(count, dtype=jnp.int32)
    position = global_row % slot_length
    slot_of = global_row // slot_length
    slot_ids = jnp.arange(lengths.shape[0], dtype=jnp.int32)
    slot_len = jnp.sum(
        jnp.where(slot_of[:, None] == slot_ids[None, :], lengths[None, :], 0), axis=1
    )
    valid = (position < slot_len).astype(jnp.float32)[:, None]
    starts = (position > 0).astype(jnp.float32)[:, None]
    lag_masks = [(position >= lag).astype(jnp.float32)[:, None] for lag in range(taps_count)]
    zeros_lru = jnp.zeros((width_lru,), jnp.float32)
    ones_lru = jnp.ones((width_lru,), jnp.float32)
    (
        gain_one,
        gelu_full,
        input_full,
        taps_full,
        cbias_full,
        rgate_full,
        rbias_full,
        igate_full,
        ibias_full,
        decay_full,
        output_full,
        gain_two,
        mgate_full,
        mvalue_full,
        mdown_full,
    ) = (
        lax.all_gather(mixer_gain, "seq", axis=0, tiled=True),
        lax.all_gather(gelu_weight, "seq", axis=0, tiled=True),
        lax.all_gather(input_weight, "seq", axis=0, tiled=True),
        lax.all_gather(conv_taps, "seq", axis=0, tiled=True),
        lax.all_gather(conv_bias, "seq", axis=0, tiled=True),
        lax.all_gather(rgate_weight, "seq", axis=0, tiled=True),
        lax.all_gather(rgate_bias, "seq", axis=0, tiled=True),
        lax.all_gather(igate_weight, "seq", axis=0, tiled=True),
        lax.all_gather(igate_bias, "seq", axis=0, tiled=True),
        lax.all_gather(decay_param, "seq", axis=0, tiled=True),
        lax.all_gather(output_weight, "seq", axis=0, tiled=True),
        lax.all_gather(mlp_gain, "seq", axis=0, tiled=True),
        lax.all_gather(mlp_gate, "seq", axis=0, tiled=True),
        lax.all_gather(mlp_value, "seq", axis=0, tiled=True),
        lax.all_gather(mlp_down, "seq", axis=0, tiled=True),
    )
    inputs = tokens.astype(jnp.float32)
    normed_one, norm_one_back = jax.vjp(rms_norm, inputs, gain_one.astype(jnp.float32))
    normed_one = normed_one.astype(jnp.bfloat16)
    gate_pre = matmul(normed_one, gelu_full)
    gate_act, gate_back = jax.vjp(gelu_tanh, gate_pre)
    linear = matmul(normed_one, input_full)
    rim_in = passed_along(linear[count - rim :], "seq", 1)
    extended = jnp.concatenate([rim_in, linear], axis=0)
    taps_fwd = taps_full.astype(jnp.float32)
    conv = cbias_full.astype(jnp.float32) + taps_fwd[:, 0] * linear
    for lag in range(1, taps_count):
        conv = conv + taps_fwd[:, lag] * (extended[rim - lag : rim - lag + count] * lag_masks[lag])
    conv_low = conv.astype(jnp.bfloat16)
    conv_value = conv_low.astype(jnp.float32)
    rgate_pre = block_apply(conv_low, rgate_full, heads) + rbias_full.astype(jnp.float32)
    igate_pre = block_apply(conv_low, igate_full, heads) + ibias_full.astype(jnp.float32)
    (decay, inject), gates_back = jax.vjp(
        recurrence_gates, rgate_pre, igate_pre, conv_value, decay_full.astype(jnp.float32)
    )
    decay_used = decay * starts
    cum_decay, state_zero = lax.associative_scan(chain_combine, (decay_used, inject), axis=0)
    scanned = carried_in(
        (cum_decay[-1], state_zero[-1]), "seq", chain_combine, (ones_lru, zeros_lru), False
    )
    carry_in = scanned[1]
    state = state_zero + cum_decay * carry_in
    mixed_rec = (state * gate_act).astype(jnp.bfloat16)
    resid = inputs + matmul(mixed_rec, output_full)
    normed_two, norm_two_back = jax.vjp(rms_norm, resid, gain_two.astype(jnp.float32))
    normed_two = normed_two.astype(jnp.bfloat16)
    mgate_pre = matmul(normed_two, mgate_full)
    mvalue_pre = matmul(normed_two, mvalue_full)
    mgate_act, mgate_back = jax.vjp(gelu_tanh, mgate_pre)
    hidden = (mgate_act * mvalue_pre).astype(jnp.bfloat16)
    mixed = ((resid + matmul(hidden, mdown_full)) * valid).astype(jnp.bfloat16)
    (
        gain_one,
        gelu_full,
        input_full,
        taps_full,
        cbias_full,
        rgate_full,
        rbias_full,
        igate_full,
        ibias_full,
        decay_full,
        output_full,
        gain_two,
        mgate_full,
        mvalue_full,
        mdown_full,
    ) = (
        lax.all_gather(mixer_gain, "seq", axis=0, tiled=True),
        lax.all_gather(gelu_weight, "seq", axis=0, tiled=True),
        lax.all_gather(input_weight, "seq", axis=0, tiled=True),
        lax.all_gather(conv_taps, "seq", axis=0, tiled=True),
        lax.all_gather(conv_bias, "seq", axis=0, tiled=True),
        lax.all_gather(rgate_weight, "seq", axis=0, tiled=True),
        lax.all_gather(rgate_bias, "seq", axis=0, tiled=True),
        lax.all_gather(igate_weight, "seq", axis=0, tiled=True),
        lax.all_gather(igate_bias, "seq", axis=0, tiled=True),
        lax.all_gather(decay_param, "seq", axis=0, tiled=True),
        lax.all_gather(output_weight, "seq", axis=0, tiled=True),
        lax.all_gather(mlp_gain, "seq", axis=0, tiled=True),
        lax.all_gather(mlp_gate, "seq", axis=0, tiled=True),
        lax.all_gather(mlp_value, "seq", axis=0, tiled=True),
        lax.all_gather(mlp_down, "seq", axis=0, tiled=True),
    )
    taps_back = taps_full.astype(jnp.float32)
    grad_out = cotangent.astype(jnp.float32) * valid
    grad_out_low = grad_out.astype(jnp.bfloat16)
    down_grad = inner_rows(hidden, grad_out_low)
    grad_hidden = outer_cols(grad_out_low, mdown_full)
    grad_mgate = mgate_back(grad_hidden * mvalue_pre)[0].astype(jnp.bfloat16)
    grad_mvalue = (grad_hidden * mgate_act).astype(jnp.bfloat16)
    mgate_grad = inner_rows(normed_two, grad_mgate)
    mvalue_grad = inner_rows(normed_two, grad_mvalue)
    grad_ntwo = outer_cols(grad_mgate, mgate_full) + outer_cols(grad_mvalue, mvalue_full)
    grad_resid_norm, gain_two_grad = norm_two_back(grad_ntwo)
    grad_resid = grad_out + grad_resid_norm
    grad_mix = grad_resid.astype(jnp.bfloat16)
    output_grad = inner_rows(mixed_rec, grad_mix)
    grad_rec = outer_cols(grad_mix, output_full)
    grad_state = grad_rec * gate_act
    grad_gate = gate_back(grad_rec * state)[0].astype(jnp.bfloat16)
    decay_next = jnp.concatenate([decay_used[1:], jnp.ones((1, width_lru), jnp.float32)], axis=0)
    rev_prod, rev_adjoint = lax.associative_scan(
        chain_combine, (jnp.flip(decay_next, 0), jnp.flip(grad_state, 0)), axis=0
    )
    tail_prod = jnp.flip(rev_prod, 0)
    adjoint_zero = jnp.flip(rev_adjoint, 0)
    summary_decay = decay_used[0] * tail_prod[0]
    summary_adjoint = decay_used[0] * adjoint_zero[0]
    scanned_back = carried_in(
        (summary_decay, summary_adjoint), "seq", chain_combine, (ones_lru, zeros_lru), True
    )
    incoming = scanned_back[1]
    adjoint = adjoint_zero + tail_prod * incoming
    state_prev = jnp.concatenate([carry_in[None, :], state[:-1]], axis=0)
    grad_decay = adjoint * state_prev * starts
    grad_rpre, grad_ipre, grad_direct, decay_grad = gates_back((grad_decay, adjoint))
    rbias_grad = jnp.sum(grad_rpre, axis=0)
    ibias_grad = jnp.sum(grad_ipre, axis=0)
    grad_rlow = grad_rpre.astype(jnp.bfloat16)
    grad_ilow = grad_ipre.astype(jnp.bfloat16)
    rgate_grad = block_grad(conv_low, grad_rlow, heads)
    igate_grad = block_grad(conv_low, grad_ilow, heads)
    grad_conv = (
        grad_direct
        + block_back(grad_rlow, rgate_full, heads)
        + block_back(grad_ilow, igate_full, heads)
    )
    cbias_grad = jnp.sum(grad_conv, axis=0)
    taps_columns = []
    grad_extended = jnp.zeros((count + rim, width_lru), jnp.float32)
    for lag in range(taps_count):
        masked_term = grad_conv * lag_masks[lag]
        taps_columns.append(jnp.sum(masked_term * extended[rim - lag : rim - lag + count], axis=0))
        grad_extended = grad_extended + jnp.pad(
            taps_back[:, lag] * masked_term, ((rim - lag, lag), (0, 0))
        )
    taps_grad = jnp.stack(taps_columns, axis=1)
    rim_back = passed_along(grad_extended[:rim], "seq", -1)
    grad_linear = grad_extended[rim:] + jnp.pad(rim_back, ((count - rim, 0), (0, 0)))
    grad_lin = grad_linear.astype(jnp.bfloat16)
    input_grad = inner_rows(normed_one, grad_lin)
    gelu_grad = inner_rows(normed_one, grad_gate)
    grad_none = outer_cols(grad_lin, input_full) + outer_cols(grad_gate, gelu_full)
    grad_inputs_norm, gain_one_grad = norm_one_back(grad_none)
    tokens_grad = grad_resid + grad_inputs_norm
    partials = (
        gain_one_grad,
        gelu_grad,
        input_grad,
        taps_grad,
        cbias_grad,
        rgate_grad,
        rbias_grad,
        igate_grad,
        ibias_grad,
        decay_grad,
        output_grad,
        gain_two_grad,
        mgate_grad,
        mvalue_grad,
        down_grad,
    )
    summed_seq = (
        lax.psum_scatter(partials[0], "seq", scatter_dimension=0, tiled=True),
        lax.psum_scatter(partials[1], "seq", scatter_dimension=0, tiled=True),
        lax.psum_scatter(partials[2], "seq", scatter_dimension=0, tiled=True),
        lax.psum_scatter(partials[3], "seq", scatter_dimension=0, tiled=True),
        lax.psum_scatter(partials[4], "seq", scatter_dimension=0, tiled=True),
        lax.psum_scatter(partials[5], "seq", scatter_dimension=0, tiled=True),
        lax.psum_scatter(partials[6], "seq", scatter_dimension=0, tiled=True),
        lax.psum_scatter(partials[7], "seq", scatter_dimension=0, tiled=True),
        lax.psum_scatter(partials[8], "seq", scatter_dimension=0, tiled=True),
        lax.psum_scatter(partials[9], "seq", scatter_dimension=0, tiled=True),
        lax.psum_scatter(partials[10], "seq", scatter_dimension=0, tiled=True),
        lax.psum_scatter(partials[11], "seq", scatter_dimension=0, tiled=True),
        lax.psum_scatter(partials[12], "seq", scatter_dimension=0, tiled=True),
        lax.psum_scatter(partials[13], "seq", scatter_dimension=0, tiled=True),
        lax.psum_scatter(partials[14], "seq", scatter_dimension=0, tiled=True),
    )
    totals = lax.psum(tuple(summed_seq), "grp")
    return (
        mixed,
        tokens_grad,
        totals[0],
        totals[1],
        totals[2],
        totals[3],
        totals[4],
        totals[5],
        totals[6],
        totals[7],
        totals[8],
        totals[9],
        totals[10],
        totals[11],
        totals[12],
        totals[13],
        totals[14],
    )


def local_fast(
    tokens,
    lengths,
    mixer_gain,
    gelu_weight,
    input_weight,
    conv_taps,
    conv_bias,
    rgate_weight,
    rgate_bias,
    igate_weight,
    igate_bias,
    decay_param,
    output_weight,
    mlp_gain,
    mlp_gate,
    mlp_value,
    mlp_down,
    cotangent,
):
    block = rgate_weight.shape[1]
    width_lru = input_weight.shape[1]
    lru_rows = jnp.concatenate(
        [conv_taps.T, conv_bias[None], rgate_bias[None], igate_bias[None], decay_param[None]], axis=0
    ).astype(jnp.float32)
    model_rows = jnp.stack([mixer_gain, mlp_gain]).astype(jnp.float32)
    mine = lax.axis_index("seq")
    small = jnp.zeros((16, width_lru), jnp.float32)
    small = lax.dynamic_update_slice(small, lru_rows, (0, mine * lru_rows.shape[1]))
    small = lax.dynamic_update_slice(small, model_rows, (8, mine * model_rows.shape[1]))
    gates = jnp.concatenate([rgate_weight, igate_weight], axis=1)
    weights, saved = forward_call(
        lengths, tokens, [small, gelu_weight, input_weight, gates, output_weight, mlp_gate, mlp_value, mlp_down]
    )
    tokens_grad, small_sum, big = backward_call(lengths, tokens, cotangent, weights[1:], saved)
    down, mgate, mvalue, out_w, gelu_w, input_w, gates = [value.astype(jnp.float32) for value in big]
    lru_own = lax.dynamic_slice(small_sum, (0, mine * conv_bias.shape[0]), (8, conv_bias.shape[0]))
    model_own = lax.dynamic_slice(small_sum, (8, mine * mixer_gain.shape[0]), (2, mixer_gain.shape[0]))
    return (
        saved.mixed,
        tokens_grad,
        model_own[0],
        gelu_w,
        input_w,
        lru_own[:4].T,
        lru_own[4],
        gates[:, :block],
        lru_own[5],
        gates[:, block:],
        lru_own[6],
        lru_own[7],
        out_w,
        model_own[1],
        mgate,
        mvalue,
        down,
    )


def solution(mesh):
    placed = (
        P(("grp", "seq"), None),
        P(),
        P("seq"),
        P("seq", None),
        P("seq", None),
        P("seq", None),
        P("seq"),
        P("seq", None),
        P("seq"),
        P("seq", None),
        P("seq"),
        P("seq"),
        P("seq", None),
        P("seq"),
        P("seq", None),
        P("seq", None),
        P("seq", None),
        P(("grp", "seq"), None),
    )
    fits = mesh.shape["grp"] == 4 and mesh.shape["seq"] == 8
    return jax.shard_map(
        local_fast if fits else local,
        mesh=mesh,
        in_specs=placed,
        out_specs=(
            P(("grp", "seq"), None),
            P(("grp", "seq"), None),
            P("seq"),
            P("seq", None),
            P("seq", None),
            P("seq", None),
            P("seq"),
            P("seq", None),
            P("seq"),
            P("seq", None),
            P("seq"),
            P("seq"),
            P("seq", None),
            P("seq"),
            P("seq", None),
            P("seq", None),
            P("seq", None),
        ),
        check_vma=False,
    )
```

```python
import math
from types import SimpleNamespace

import jax
import jax.numpy as jnp
from jax import lax
from jax.experimental import pallas as pl
from jax.experimental.pallas import tpu as pltpu
from jax.sharding import PartitionSpec as P

epsilon = 1e-06
cfactor = 8.0


def passed_along(value, axis, steps):
    count = lax.axis_size(axis)
    leading, last = (max(0, -steps), min(count, count - steps))
    return lax.ppermute(value, axis, [(source, source + steps) for source in range(leading, last)])


def carried_in(value, axis, join, neutral, backward):
    count, mine = (lax.axis_size(axis), lax.axis_index(axis))
    pieces = jax.tree.map(lambda part: lax.all_gather(part, axis), value)
    if backward:
        pieces = jax.tree.map(lambda part: part[::-1], pieces)
        mine = count - 1 - mine
    so_far = jax.tree.map(
        lambda part, zero: jnp.full_like(part, 0) + jnp.asarray(zero, part.dtype), value, neutral
    )

    def step(position, so_far):
        longer = join(so_far, jax.tree.map(lambda part: part[position], pieces))
        return jax.tree.map(lambda new, old: jnp.where(position < mine, new, old), longer, so_far)

    return lax.fori_loop(0, count - 1, step, so_far)


def rms_norm(rows_in, gain):
    return rows_in * lax.rsqrt(jnp.mean(rows_in * rows_in, axis=-1, keepdims=True) + epsilon) * gain


def gelu_tanh(values):
    return jax.nn.gelu(values, approximate=True)


def matmul(left, right):
    return jnp.dot(left, right, preferred_element_type=jnp.float32)


def inner_rows(left, right):
    return lax.dot_general(
        left, right, (((0,), (0,)), ((), ())), preferred_element_type=jnp.float32
    )


def outer_cols(left, right):
    return lax.dot_general(
        left, right, (((1,), (1,)), ((), ())), preferred_element_type=jnp.float32
    )


def block_apply(values, weight, heads):
    count = values.shape[0]
    width = weight.shape[1]
    parts = values.reshape(count, heads, width)
    blocks = weight.reshape(heads, width, width)
    return jnp.einsum("rhi,hij->rhj", parts, blocks, preferred_element_type=jnp.float32).reshape(
        count, heads * width
    )


def block_back(grads, weight, heads):
    count = grads.shape[0]
    width = weight.shape[1]
    parts = grads.reshape(count, heads, width)
    blocks = weight.reshape(heads, width, width)
    return jnp.einsum("rhj,hij->rhi", parts, blocks, preferred_element_type=jnp.float32).reshape(
        count, heads * width
    )


def block_grad(values, grads, heads):
    count = values.shape[0]
    width = values.shape[1] // heads
    left = values.reshape(count, heads, width)
    right = grads.reshape(count, heads, width)
    return jnp.einsum("rhi,rhj->hij", left, right, preferred_element_type=jnp.float32).reshape(
        heads * width, width
    )


def chain_combine(earlier, later):
    return (earlier[0] * later[0], later[0] * earlier[1] + later[1])


def recurrence_gates(rgate_pre, igate_pre, conv_in, decay_in):
    rgate = jax.nn.sigmoid(rgate_pre)
    igate = jax.nn.sigmoid(igate_pre)
    log_decay = -cfactor * jax.nn.softplus(-decay_in) * rgate
    return (jnp.exp(log_decay), jnp.sqrt(-jnp.expm1(2.0 * log_decay)) * igate * conv_in)


MESH = pl.DeviceIdType.MESH


class Place:
    def __init__(self):
        self.z = lax.axis_index("grp")
        seq = lax.axis_index("seq")
        self.core = seq % 2
        self.x = (seq // 2) % 2
        self.y = seq // 4
        self.seq = seq
        self.sib = (self.z, self.at(self.y, self.x, 1 - self.core))
        self.xnb = (self.z, self.at(self.y, 1 - self.x, self.core))
        self.ynb = (self.z, self.at(1 - self.y, self.x, self.core))

    def at(self, y, x, core):
        return (y * 2 + x) * 2 + core

    def level(self, z):
        return (z, self.seq)


def meet(peers):
    barrier = pltpu.get_barrier_semaphore()
    for peer in peers:
        pl.semaphore_signal(barrier, inc=1, device_id=peer, device_id_type=MESH)
    pl.semaphore_wait(barrier, len(peers))


GOT = ("X", "Y", "D1", "D2", "SO", "SX", "SY", "S1", "S2")
SENT = ("ox", "oy", "os", "fy", "fx", "zX", "zY", "zD1", "zD2", "SX", "SY", "S1", "S2")
OVER_LINKS = GOT[:4]
TO_SIB = dict(zip(OVER_LINKS, GOT[5:]))


class Gather:
    def __init__(self, place, shards, fulls, kinds, send, recv, own, bounce):
        self.p, self.shards, self.fulls, self.bounce, self.kinds = place, shards, fulls, bounce, kinds
        self.send, self.recv, self.own = send, recv, own
        self.znb = place.level(place.z + 1 - 2 * (place.z % 2))

    def fetched(self, i, odd):
        return self.kinds[i] != 2 - odd

    def part(self, i, name):
        p = self.p
        n = self.shards[i].shape[0]
        y, x = p.y, p.x
        if name[-1] == "X":
            x = 1 - x
        elif name[-1] == "Y":
            y = 1 - y
        elif name[-1] in "12":
            x, y = 1 - x, 1 - y
        core = 1 - p.core if name[0] == "S" else p.core
        first = pl.multiple_of(p.at(y, x, core) * n, n)
        if name[-1] == "1":
            return pl.ds(first, n // 2)
        if name[-1] == "2":
            return pl.ds(pl.multiple_of(first + n // 2, n // 2), n // 2)
        return pl.ds(first, n)

    def half(self, i, name, which):
        n = self.shards[i].shape[0]
        return pl.ds(pl.multiple_of(self.part(i, name).start + which * (n // 2), n // 2), n // 2)

    def copy(self, i, how, got, peer, rows, src=None):
        full = self.fulls[i]
        return pltpu.make_async_remote_copy(
            src_ref=full.at[rows] if src is None else src,
            dst_ref=full.at[rows],
            send_sem=self.send.at[i, SENT.index(how)],
            recv_sem=self.recv.at[i, GOT.index(got)],
            device_id=peer,
            device_id_type=MESH,
        )

    def wait(self, i, name):
        self.copy(i, "ox", name, self.p.sib, self.part(i, name)).wait_recv()

    def own_far(self, i):
        p, mine = self.p, self.part(i, "O")
        return [self.copy(i, "ox", "X", p.xnb, mine, self.shards[i]), self.copy(i, "oy", "Y", p.ynb, mine, self.shards[i])]

    def own_near(self, i):
        return self.copy(i, "os", "SO", self.p.sib, self.part(i, "O"), self.shards[i])

    def own_kept(self, i, leg):
        if leg == 0:
            return pltpu.make_async_copy(self.shards[i], self.bounce[i], self.own.at[i, 0])
        return pltpu.make_async_copy(self.bounce[i], self.fulls[i].at[self.part(i, "O")], self.own.at[i, 1])

    def start(self, i, odd):
        if self.fetched(i, odd):
            for c in self.own_far(i):
                c.start()
        self.own_near(i).start()
        self.own_kept(i, 0).start()

    def onward(self, i, name, odd):
        p = self.p
        copies = []
        if self.fetched(i, odd):
            if name == "X":
                copies.append(self.copy(i, "fy", "D1", p.ynb, self.half(i, "X", 0)))
            if name == "Y":
                copies.append(self.copy(i, "fx", "D2", p.xnb, self.half(i, "Y", 1)))
            if self.kinds[i]:
                copies.append(self.copy(i, "z" + name, name, self.znb, self.part(i, name)))
        copies.append(self.copy(i, TO_SIB[name], TO_SIB[name], p.sib, self.part(i, name)))
        return copies

    def relay(self, i, name, odd):
        self.wait(i, name)
        for c in self.onward(i, name, odd):
            c.start()
        if name == "X":
            self.own_kept(i, 0).wait()
            self.own_kept(i, 1).start()

    def arrive(self, i):
        for name in GOT[4:]:
            self.wait(i, name)
        self.own_kept(i, 1).wait()

    def drain(self, i, odd):
        if self.fetched(i, odd):
            for c in self.own_far(i):
                c.wait_send()
        self.own_near(i).wait_send()
        for name in OVER_LINKS:
            for c in self.onward(i, name, odd):
                c.wait_send()


def rows_loop(total, body, step=16, start=0):
    @pl.loop(start // step, total // step)
    def _(k):
        body(pl.ds(pl.multiple_of(k * step, step), step))


def wide(value):
    return value.astype(jnp.float32)

class Reduce:
    def __init__(self, place, slots, sems):
        self.p = place
        self.slots = slots
        self.send, self.recv = sems
        z = place.z
        inner = (z == 1) | (z == 2)
        self.inner = inner
        self.outer = (z == 0) | (z == 3)
        self.peer = place.level(jnp.where(inner, 3 - z, z))
        self.out = place.level(jnp.where(z < 2, 1 - z, 5 - z))
        self.me = 2 * place.y + place.x

    def makes(self, h):
        return self.p.z == 1 + h

    def helps(self, h):
        return self.p.z == 2 - h

    def copy(self, i, tag, src, dst, peer):
        return pltpu.make_async_remote_copy(
            src_ref=src, dst_ref=dst, send_sem=self.send.at[i, tag], recv_sem=self.recv.at[i, tag], device_id=peer, device_id_type=MESH
        )

    def first(self, i, h):
        p, s = self.p, self.slots[i]
        if h == 0:
            return [self.copy(i, q, s.ab.at[0, 2 * q + 1 - p.x], s.fr.at[0, q], p.xnb) for q in range(2)]
        return [self.copy(i, 2 + q, s.ab.at[1, 2 * (1 - p.y) + q], s.fr.at[1, q], p.ynb) for q in range(2)]

    def second(self, i, h):
        p, s = self.p, self.slots[i]
        if h == 0:
            return self.copy(i, 4, s.ab.at[0, 2 * (1 - p.y) + p.x], s.se.at[0], p.ynb)
        return self.copy(i, 5, s.ab.at[1, 2 * p.y + 1 - p.x], s.se.at[1], p.xnb)

    def up(self, i, h):
        s = self.slots[i]
        return self.copy(i, 6 + h, s.ab.at[h, self.me], s.zo.at[h], self.out)

    def across(self, i, h):
        s = self.slots[i]
        return self.copy(i, 8 + h, s.ab.at[h, self.me], s.zp, self.peer)

    def down(self, i, h):
        res = self.slots[i].res.at[h]
        return self.copy(i, 10 + h, res, res, self.out)

    def over(self, i, h):
        res = self.slots[i].res.at[h]
        return self.copy(i, 12 + h, res, res, self.peer)

    def start_first(self, i, h):
        for cp in self.first(i, h):
            cp.start()

    def add_first(self, i, h):
        p, s = self.p, self.slots[i]
        for cp in self.first(i, h):
            cp.wait_recv()
        for q in range(2):
            j = 2 * q + p.x if h == 0 else 2 * p.y + q

            def body(rows, q=q, j=j):
                s.ab[h, j, rows, :] = low(wide(s.ab[h, j, rows, :]) + wide(s.fr[h, q, rows, :]))

            rows_loop(s.n, body)
        self.second(i, h).start()

    def add_second(self, i, h):
        s, me = self.slots[i], self.me
        self.second(i, h).wait_recv()

        def body(rows):
            s.ab[h, me, rows, :] = low(wide(s.ab[h, me, rows, :]) + wide(s.se[h, rows, :]))

        rows_loop(s.n, body)

        @pl.when(self.outer)
        def _():
            self.up(i, h).start()

    def add_outer(self, i, h):
        s, me = self.slots[i], self.me

        @pl.when(self.inner)
        def _():
            self.up(i, h).wait_recv()

            def body(rows):
                s.ab[h, me, rows, :] = low(wide(s.ab[h, me, rows, :]) + wide(s.zo[h, rows, :]))

            rows_loop(s.n, body)

        @pl.when(self.helps(h))
        def _():
            self.across(i, h).start()

    def add_peer(self, i, h):
        s, me = self.slots[i], self.me

        @pl.when(self.makes(h))
        def _():
            self.across(i, h).wait_recv()

            def body(rows):
                s.res[h, rows, :] = low(wide(s.ab[h, me, rows, :]) + wide(s.zp[rows, :]))

            rows_loop(s.n, body)
            self.down(i, h).start()
            self.over(i, h).start()

    def pass_on(self, i, h):
        @pl.when(self.helps(h))
        def _():
            self.over(i, h).wait_recv()
            self.down(i, h).start()

    def arrive(self, i, h):
        @pl.when(self.outer)
        def _():
            self.down(i, h).wait_recv()

    def drain(self, i):
        for h in range(2):

            @pl.when(self.outer)
            def _(h=h):
                self.up(i, h).wait_send()

            @pl.when(self.inner)
            def _(h=h):
                self.down(i, h).wait_send()

            @pl.when(self.makes(h))
            def _(h=h):
                self.over(i, h).wait_send()

            @pl.when(self.helps(h))
            def _(h=h):
                self.across(i, h).wait_send()

            for cp in self.first(i, h) + [self.second(i, h)]:
                cp.wait_send()


class Small:
    def __init__(self, place, total, slots, sems):
        p = place
        self.total, self.slots = total, slots
        self.send, self.recv = sems
        z = p.z
        self.order = [p.sib, p.xnb, p.ynb, p.level(z + 1 - 2 * (z % 2)), p.level((z + 2) % 4)]

    def copy(self, k):
        return pltpu.make_async_remote_copy(
            src_ref=self.slots.at[0, k],
            dst_ref=self.slots.at[1, k],
            send_sem=self.send.at[k],
            recv_sem=self.recv.at[k],
            device_id=self.order[k],
            device_id_type=MESH,
        )

    def begin(self):
        self.slots[0, 0] = self.total[...]
        self.copy(0).start()

    def step(self, k):
        self.copy(k).wait_recv()
        both = self.slots[0, k] + self.slots[1, k]
        if k < 4:
            self.slots[0, k + 1] = both
            self.copy(k + 1).start()
        else:
            self.total[...] = both

    def drain(self):
        for k in range(5):
            self.copy(k).wait_send()

ROOT = math.sqrt(2.0 / math.pi)
CUBE = 0.044715
LANES = 128


def low(value):
    return value.astype(jnp.bfloat16)


def gelu_parts(v):
    square = v * v
    t = jnp.tanh(ROOT * (v + CUBE * v * square))
    half = 0.5 * (1.0 + t)
    return v * half, half + 0.5 * v * (1.0 - t * t) * (ROOT * (1.0 + 3.0 * CUBE * square))


def dot(left, right):
    return jnp.dot(left, right, preferred_element_type=jnp.float32)


def dot_t(left, right):
    return lax.dot_general(left, right, (((1,), (1,)), ((), ())), preferred_element_type=jnp.float32)


def sigmoid(v):
    return 1.0 / (1.0 + jnp.exp(-v))


def minus_expm1(twice, half_of):
    t = jnp.tanh(half_of)
    return -2.0 * t / (1.0 - t)


def softplus_minus(v):
    return jnp.maximum(-v, 0.0) + jnp.log1p(jnp.exp(-jnp.abs(v)))


def strided_scan(decay_ref, value_ref, prod_ref, sum_ref, backward, rows, between):
    tiles, _, lanes = sum_ref.shape
    span = rows // 8

    def step(k, carry):
        prod, total = carry
        t = span - 1 - k if backward else k
        spot = pl.ds(t, 8, stride=span)
        new_prod, new_total = [], []
        for c in range(tiles):
            d, v = decay_ref[c, spot, :], value_ref[c, spot, :]
            if backward:
                seen = total[c] + v
                sum_ref[c, spot, :] = seen
                prod_ref[c, spot, :] = prod[c]
                new_prod.append(prod[c] * d)
                new_total.append(seen * d)
            else:
                new_prod.append(prod[c] * d)
                new_total.append(total[c] * d + v)
                prod_ref[c, spot, :] = new_prod[c]
                sum_ref[c, spot, :] = new_total[c]
        return new_prod, new_total

    ones = [jnp.ones((8, lanes), jnp.float32)] * tiles
    zeros = [jnp.zeros((8, lanes), jnp.float32)] * tiles
    half = lax.fori_loop(0, span // 2, step, (ones, zeros), unroll=2)
    between()
    return lax.fori_loop(span // 2, span, step, half, unroll=2)


def segment_ends(ends, backward):
    before, whole = [], []
    order = range(7, -1, -1) if backward else range(8)
    for prod, total in zip(*ends):
        p = jnp.ones((1, prod.shape[1]), jnp.float32)
        s = jnp.zeros((1, prod.shape[1]), jnp.float32)
        ps, ss = [None] * 8, [None] * 8
        for k in order:
            ps[k], ss[k] = p, s
            d, v = prod[k : k + 1], total[k : k + 1]
            p, s = p * d, s * d + v
        before.append((jnp.concatenate(ps, axis=0), jnp.concatenate(ss, axis=0)))
        whole.append((p, s))
    return before, whole


class Ends:
    def __init__(self, place, slots, sems, backward):
        self.p, self.slots, self.backward = place, slots, backward
        self.send, self.recv = sems

    def copy(self, d):
        to = (self.p.seq + d) % 8
        return pltpu.make_async_remote_copy(
            src_ref=self.slots.at[self.p.seq], dst_ref=self.slots.at[self.p.seq], send_sem=self.send.at[d - 1],
            recv_sem=self.recv.at[d - 1], device_id=(self.p.z, to), device_id_type=MESH,
        )

    def come(self, d):
        src = (self.p.seq + 8 - d) % 8
        return pltpu.make_async_remote_copy(
            src_ref=self.slots.at[src], dst_ref=self.slots.at[src], send_sem=self.send.at[d - 1],
            recv_sem=self.recv.at[d - 1], device_id=(self.p.z, src), device_id_type=MESH,
        )

    def tell(self, whole):
        for c, (prod, total) in enumerate(whole):
            self.slots[self.p.seq, 0, c : c + 1, :] = prod
            self.slots[self.p.seq, 1, c : c + 1, :] = total
        self.share()

    def share(self):
        for d in range(1, 8):
            self.copy(d).start()

    def shared(self):
        for d in range(1, 8):
            self.come(d).wait_recv()

    def joined(self):
        self.shared()
        carry = jnp.zeros(self.slots.shape[2:], jnp.float32)
        for k in range(7, 0, -1) if self.backward else range(7):
            further = self.slots[k, 0] * carry + self.slots[k, 1]
            counts = k > self.p.seq if self.backward else k < self.p.seq
            carry = jnp.where(counts, further, carry)
        return carry

    def drain(self):
        for d in range(1, 8):
            self.copy(d).wait_send()


def named(keys, refs):
    return SimpleNamespace(**dict(zip(keys, refs)))


HBM = pl.BlockSpec(memory_space=pl.ANY)
VMEM = pl.BlockSpec(memory_space=pltpu.VMEM)


KINDS = (0, 1, 0, 0, 2, 1, 0)
FETCHES = (
    (
        ((0, 1),),
        ((0, 0),),
        ((0, 2), (1, 1), (2, 1), (1, 0), (2, 0), (1, 2), (2, 2), (3, 1), (4, 1), (0, 5), (0, 4), (3, 0), (4, 0), (3, 2), (4, 2),),
        (),
        (),
        (),
        ((0, 3),),
        ((1, 4), (1, 5), (2, 5),),
        (),
        (),
        ((1, 3), (2, 3),),
        ((0, 6), (2, 4),),
        ((3, 5), (4, 5),),
        ((3, 3), (4, 3),),
        ((3, 4),),
        (),
        (),
        ((4, 4),),
        (),
        (),
        ((1, 6), (2, 6),),
        (),
        (),
        (),
        (),
        ((3, 6), (4, 6),),
        (),
        (),
        (),
        (),
        (),
        (),
        (),
    ),
    (
        ((0, 0), (0, 1), (0, 4),),
        (),
        ((1, 0), (2, 0), (1, 1), (0, 2), (0, 5), (1, 4), (2, 4), (2, 1), (3, 0), (4, 0), (3, 1), (1, 2), (2, 2),),
        ((4, 1), (0, 3),),
        (),
        ((3, 4), (4, 4), (3, 2), (4, 2),),
        ((0, 6),),
        (),
        ((1, 3), (2, 3),),
        (),
        (),
        ((1, 5),),
        ((1, 6), (2, 6),),
        (),
        ((3, 3), (4, 3),),
        (),
        ((3, 6), (4, 6),),
        ((2, 5),),
        (),
        (),
        (),
        ((3, 5),),
        (),
        (),
        (),
        ((4, 5),),
        (),
        (),
        (),
        (),
        (),
        (),
        (),
    ),
)


def forward_call(lengths, tokens, small_own, shards):
    rows, width = tokens.shape
    lru = shards[0].shape[1]
    ff = shards[4].shape[1]
    tiles = lru // LANES
    kinds = KINDS
    count = len(shards)
    f32, bf = jnp.float32, jnp.bfloat16
    shape = jax.ShapeDtypeStruct
    wholes = [shape((8 * s.shape[0], s.shape[1]), s.dtype) for s in shards]
    saved = dict(
        mixed=shape((rows, width), bf),
        small=shape((16, lru), f32),
        n1t=shape((width, rows), bf),
        pre=shape((tiles, rows, LANES), f32),
        lin=shape((tiles, rows + 8, LANES), f32),
        convt=shape((tiles, LANES, rows), bf),
        decay=shape((tiles, rows, LANES), f32),
        k2=shape((tiles, rows, LANES), f32),
        k3=shape((tiles, rows, LANES), f32),
        k6=shape((tiles, rows, LANES), f32),
        k7=shape((tiles, rows, LANES), f32),
        slope=shape((tiles, rows, LANES), f32),
        rect=shape((lru, rows), bf),
        resid=shape((rows, width), f32),
        n2t=shape((width, rows), bf),
        mg=shape((rows, ff), f32),
        bend=shape((rows, ff), f32),
        mv=shape((rows, ff), f32),
        hidt=shape((ff, rows), bf),
    )
    names = list(saved)
    scratch = dict(
        x=pltpu.VMEM((rows, width), bf),
        n1=pltpu.VMEM((rows, width), bf),
        n1t=pltpu.VMEM((width, rows), bf),
        parts=pltpu.VMEM((8,) + small_own.shape, f32),
        into=pltpu.VMEM((8 * tiles, LANES), f32),
        small=pltpu.VMEM((16, lru), f32),
        pre=pltpu.VMEM((tiles, rows, LANES), f32),
        lin=pltpu.VMEM((tiles, rows + 8, LANES), f32),
        convt=pltpu.VMEM((tiles, LANES, rows), bf),
        decay=pltpu.VMEM((tiles, rows, LANES), f32),
        k2=pltpu.VMEM((tiles, rows, LANES), f32),
        k3=pltpu.VMEM((tiles, rows, LANES), f32),
        k6=pltpu.VMEM((tiles, rows, LANES), f32),
        k7=pltpu.VMEM((tiles, rows, LANES), f32),
        prod=pltpu.VMEM((tiles, rows, LANES), f32),
        total=pltpu.VMEM((tiles, rows, LANES), f32),
        rec=pltpu.VMEM((rows, lru), bf),
        rect=pltpu.VMEM((lru, rows), bf),
        resid=pltpu.VMEM((rows, width), f32),
        n2=pltpu.VMEM((rows, width), bf),
        n2t=pltpu.VMEM((width, rows), bf),
        hidden=pltpu.VMEM((rows, ff), bf),
        ends=pltpu.VMEM((8, 2, tiles, LANES), f32),
        gsend=pltpu.SemaphoreType.DMA((count, len(SENT))),
        grecv=pltpu.SemaphoreType.DMA((count, len(GOT))),
        gown=pltpu.SemaphoreType.DMA((count, 2)),
        esend=pltpu.SemaphoreType.DMA((7,)),
        erecv=pltpu.SemaphoreType.DMA((7,)),
        ssend=pltpu.SemaphoreType.DMA((7,)),
        srecv=pltpu.SemaphoreType.DMA((7,)),
        hsend=pltpu.SemaphoreType.DMA(()),
        hrecv=pltpu.SemaphoreType.DMA(()),
        load=pltpu.SemaphoreType.DMA((2,)),
        keep=pltpu.SemaphoreType.DMA((len(names),)),
    )
    keys = list(scratch)
    R = 128

    def kernel(lengths_ref, tokens_ref, small_ref, *refs):
        ins, outs = refs[:count], refs[count : 2 * count]
        out = named(names, refs[2 * count : 2 * count + len(names)])
        bounce = refs[-count:]
        v = named(keys, refs[2 * count + len(names) : -count])
        gelu_w, input_w, gates_w, output_w, mgate_w, mvalue_w, mdown_w = outs
        place = Place()
        gather = Gather(place, ins, outs, kinds, v.gsend, v.grecv, v.gown, bounce)
        ends = Ends(place, v.ends, (v.esend, v.erecv), False)
        packs = Ends(place, v.parts, (v.ssend, v.srecv), False)
        z, seq = place.z, place.seq
        loads = [
            pltpu.make_async_copy(tokens_ref, v.x, v.load.at[0]),
            pltpu.make_async_copy(small_ref, v.parts.at[seq], v.load.at[1]),
        ]
        for cp in loads:
            cp.start()
        meet([(z, (seq + d) % 8) for d in range(1, 8)] + [gather.znb])
        kept = []

        def keep(src, dst):
            cp = pltpu.make_async_copy(src, dst, v.keep.at[len(kept)])
            cp.start()
            kept.append(cp)

        def by_level(act):
            for odd in range(2):
                pl.when(z % 2 == odd)(lambda odd=odd: act(odd))

        turn_of = [0]

        def serve(spot):
            def act(odd):
                for step, i in FETCHES[odd][spot]:
                    if step == 0:
                        gather.start(i, odd)
                    else:
                        gather.relay(i, OVER_LINKS[step - 1], odd)

            if FETCHES[0][spot] or FETCHES[1][spot]:
                by_level(act)

        def pump():
            serve(turn_of[0])
            turn_of[0] += 1

        def pumps_at(*places):
            spots = list(enumerate(places, turn_of[0]))
            turn_of[0] += len(spots)

            def at_place(here):
                for spot, there in spots:
                    if FETCHES[0][spot] or FETCHES[1][spot]:
                        pl.when(here == there)(lambda spot=spot: serve(spot))

            return at_place

        loads[1].wait()
        packs.share()
        pump()
        packs.shared()
        small = v.small
        lane = lax.broadcasted_iota(jnp.int32, (8, LANES), 1)
        for k in range(4):
            left, right = v.parts[2 * k, 0:8, :], pltpu.roll(v.parts[2 * k + 1, 0:8, :], 64, axis=1)
            first = 3 * k * LANES
            small[0:8, first : first + LANES] = left[:, :LANES]
            small[0:8, first + LANES : first + 2 * LANES] = jnp.where(lane < 64, left[:, LANES:], right[:, :LANES])
            small[0:8, first + 2 * LANES : first + 3 * LANES] = right[:, LANES:]
        for k in range(8):
            small[8:16, k * LANES : (k + 1) * LANES] = v.parts[k, 8:16, :LANES]
        small[8:16, width:] = jnp.zeros((8, lru - width), f32)
        keep(v.small, out.small)
        loads[0].wait()

        def norm_one(at):
            x = wide(v.x[at, :])
            scale = lax.rsqrt(jnp.mean(x * x, axis=-1, keepdims=True) + epsilon)
            v.n1[at, :] = low(x * scale * small[8:9, :width])

        rows_loop(rows, norm_one, 64)
        pump()

        def turn(src, dst, at):
            dst[at, :] = src[:, at].T

        @pl.loop(0, width // 256)
        def _(k):
            turn(v.n1, v.n1t, pl.ds(pl.multiple_of(k * 256, 256), 256))

        keep(v.n1t, out.n1t)

        def project(weight, dst, first):
            inside = pumps_at(tiles // 4)

            def body(w):
                t = pl.program_id(0)
                inside(t)
                both = dot(v.n1[...], w[...])
                dst[2 * t, pl.ds(first, rows), :] = both[:, :LANES]
                dst[2 * t + 1, pl.ds(first, rows), :] = both[:, LANES:]

            pltpu.emit_pipeline(body, grid=(tiles // 2,), in_specs=[pl.BlockSpec((width, 2 * LANES), lambda t: (0, t))])(weight)

        pump()
        gather.arrive(0)
        project(gelu_w, v.pre, 0)
        pump()
        gather.arrive(1)
        project(input_w, v.lin, 8)

        def halo():
            return pltpu.make_async_remote_copy(
                src_ref=v.lin.at[:, pl.ds(rows, 8)], dst_ref=v.lin.at[:, pl.ds(0, 8)], send_sem=v.hsend, recv_sem=v.hrecv,
                device_id=(z, (seq + 1) % 8), device_id_type=MESH,
            )

        @pl.when(seq < 7)
        def _():
            halo().start()

        pump()
        gather.arrive(2)

        @pl.when(seq == 0)
        def _():
            v.lin[:, 0:8, :] = jnp.zeros((tiles, 8, LANES), f32)

        @pl.when(seq > 0)
        def _():
            halo().wait_recv()

        keep(v.lin, out.lin)

        gates_inside = pumps_at(tiles // 3, 2 * tiles // 3)

        def gates(w):
            h = pl.program_id(0)
            gates_inside(h)
            lane = pl.ds(pl.multiple_of(h * LANES, LANES), LANES)
            taps = [small[k : k + 1, lane] for k in range(4)]
            cb, rb, ib, dp = [small[k : k + 1, lane] for k in range(4, 8)]
            rate = -cfactor * softplus_minus(dp)
            for r in range(0, rows, R):
                acc = cb + taps[0] * v.lin[h, 8 + r : 8 + r + R, :]
                for k in range(1, 4):
                    acc = acc + taps[k] * v.lin[h, 8 + r - k : 8 + r - k + R, :]
                cl = low(acc)
                v.convt[h, :, r : r + R] = cl.T
                both = dot(cl, w[...])
                rg = sigmoid(both[:, :LANES] + rb)
                ig = sigmoid(both[:, LANES:] + ib)
                log_decay = rate * rg
                decay = jnp.exp(log_decay)
                mult = jnp.sqrt(minus_expm1(2.0 * log_decay, log_decay))
                cv = wide(cl)
                through = mult * ig
                at = slice(r, r + R)
                v.prod[h, at, :] = decay
                v.decay[h, at, :] = decay
                v.total[h, at, :] = through * cv
                v.k3[h, at, :] = through
                v.k2[h, at, :] = through * cv * (1.0 - ig)
                v.k6[h, at, :] = ig * cv * (decay * decay) / mult
                v.k7[h, at, :] = rg

        pltpu.emit_pipeline(gates, grid=(tiles,), in_specs=[pl.BlockSpec((LANES, 2 * LANES), lambda h: (h, 0))])(gates_w)
        for src, dst in ((v.convt, out.convt), (v.decay, out.decay), (v.k2, out.k2), (v.k3, out.k3)):
            keep(src, dst)
        pump()
        tails = strided_scan(v.prod, v.total, v.prod, v.total, False, rows, pump)
        before, whole = segment_ends(tails, False)
        ends.tell(whole)
        pump()
        carry = ends.joined()
        span = rows // 8
        for c in range(tiles):
            into = before[c][0] * carry[c : c + 1, :] + before[c][1]
            v.into[8 * c : 8 * c + 8, :] = into

        pump()
        state_inside = pumps_at(tiles // 3, 2 * tiles // 3)

        @pl.loop(0, tiles)
        def _(c):
            state_inside(c)
            lane = pl.ds(pl.multiple_of(c * LANES, LANES), LANES)
            into = v.into[pl.ds(pl.multiple_of(c * 8, 8), 8), :]
            rate = -cfactor * softplus_minus(small[7:8, lane])
            first = lax.broadcasted_iota(jnp.int32, (span, LANES), 0) == 0
            for s in range(8):
                at = slice(s * span, (s + 1) * span)
                state = v.total[c, at, :] + v.prod[c, at, :] * into[s : s + 1, :]
                before_it = jnp.where(first, into[s : s + 1, :], pltpu.roll(state, 1, axis=0))
                rg = v.k7[c, at, :]
                k7 = (before_it * v.decay[c, at, :] - v.k6[c, at, :]) * rg
                v.k7[c, at, :] = k7
                v.k6[c, at, :] = k7 * rate * (1.0 - rg)
                value, slope = gelu_parts(v.pre[c, at, :])
                v.rec[at, lane] = low(state * value)
                v.pre[c, at, :] = value
                v.total[c, at, :] = state * slope
            v.rect[lane, :] = v.rec[:, lane].T

        for src, dst in ((v.k6, out.k6), (v.k7, out.k7), (v.pre, out.pre), (v.total, out.slope)):
            keep(src, dst)
        keep(v.rect, out.rect)
        pump()
        gather.arrive(3)
        width_inside = pumps_at(width // 512)

        def back_to_width(w):
            t = pl.program_id(0)
            width_inside(t)
            at = pl.ds(pl.multiple_of(t * 256, 256), 256)
            v.resid[:, at] = wide(v.x[:, at]) + dot(v.rec[...], w[...])

        pltpu.emit_pipeline(back_to_width, grid=(width // 256,), in_specs=[pl.BlockSpec((lru, 256), lambda t: (0, t))])(output_w)
        keep(v.resid, out.resid)
        pump()
        def norm_two(at):
            x = v.resid[at, :]
            scale = lax.rsqrt(jnp.mean(x * x, axis=-1, keepdims=True) + epsilon)
            v.n2[at, :] = low(x * scale * small[9:10, :width])

        rows_loop(rows, norm_two, 64)
        pump()

        @pl.loop(0, width // 256)
        def _(k):
            turn(v.n2, v.n2t, pl.ds(pl.multiple_of(k * 256, 256), 256))

        keep(v.n2t, out.n2t)
        steps = ff // 256
        sixths = [k * steps // 6 for k in range(1, 6)]
        across = pl.BlockSpec((rows, 256), lambda t: (0, t))
        columns = pl.BlockSpec((width, 256), lambda t: (0, t))
        pump()
        gather.arrive(4)
        gate_inside = pumps_at(*sixths)

        def mlp_gate(wg, value, slope):
            gate_inside(pl.program_id(0))
            value[...] = dot(v.n2[...], wg[...])

            def act(rs):
                value[rs, :], slope[rs, :] = gelu_parts(value[rs, :])

            rows_loop(rows, act, 64)

        pltpu.emit_pipeline(mlp_gate, grid=(steps,), in_specs=[columns], out_specs=[across, across])(mgate_w, out.mg, out.bend)
        pump()
        gather.arrive(5)
        value_inside = pumps_at(*sixths)

        def mlp_value(wv, value, slope, mv, hidt):
            t = pl.program_id(0)
            value_inside(t)
            at = pl.ds(pl.multiple_of(t * 256, 256), 256)
            linear = dot(v.n2[...], wv[...])
            mv[...] = linear * slope[...]
            hidden = low(linear * value[...])
            v.hidden[:, at] = hidden
            hidt[...] = hidden.T

        pltpu.emit_pipeline(
            mlp_value,
            grid=(steps,),
            in_specs=[columns, across, across],
            out_specs=[across, pl.BlockSpec((256, rows), lambda t: (t, 0))],
        )(mvalue_w, out.mg, out.bend, out.mv, out.hidt)
        pump()
        gather.arrive(6)
        valid_rows = lengths_ref[z] - seq * rows

        def down(w, mixed):
            t = pl.program_id(0)
            at = pl.ds(pl.multiple_of(t * 256, 256), 256)
            valid = (lax.broadcasted_iota(jnp.int32, (rows, 256), 0) < valid_rows).astype(f32)
            mixed[...] = low((v.resid[:, at] + dot(v.hidden[...], w[...])) * valid)

        pltpu.emit_pipeline(
            down,
            grid=(width // 256,),
            in_specs=[pl.BlockSpec((ff, 256), lambda t: (0, t))],
            out_specs=[pl.BlockSpec((rows, 256), lambda t: (0, t))],
        )(mdown_w, out.mixed)
        for cp in kept:
            cp.wait()
        pump()

        def drain(odd):
            for i in range(count):
                gather.drain(i, odd)

        by_level(drain)
        ends.drain()
        packs.drain()

        @pl.when(seq < 7)
        def _():
            halo().wait_send()

    result = pl.pallas_call(
        kernel,
        out_shape=wholes + [saved[name] for name in names],
        in_specs=[pl.BlockSpec(memory_space=pltpu.SMEM), HBM, HBM] + [HBM] * count,
        out_specs=[HBM] * (count + len(names)),
        scratch_shapes=[scratch[key] for key in keys] + [pltpu.VMEM(s.shape, s.dtype) for s in shards],
        compiler_params=pltpu.CompilerParams(collective_id=1, has_side_effects=True, vmem_limit_bytes=60 << 20),
        name="forward",
    )(lengths, tokens, small_own, *shards)
    return result[:count], named(names, result[count:])

def slot_scratch(rows, columns):
    n, h = rows // 8, columns // 2
    bf = jnp.bfloat16
    return dict(
        ab=pltpu.VMEM((2, 4, n, h), bf),
        fr=pltpu.VMEM((2, 2, n, h), bf),
        se=pltpu.VMEM((2, n, h), bf),
        zo=pltpu.VMEM((2, n, h), bf),
        zp=pltpu.VMEM((n, h), bf),
        res=pltpu.VMEM((2, n, h), bf),
    )


PUMPS = (
    (),
    (),
    (),
    (),
    (),
    (),
    ((6, 0, 0),),
    ((6, 0, 1),),
    (),
    (),
    (),
    (),
    (),
    ((6, 1, 0),),
    ((6, 2, 1),),
    (),
    (),
    (),
    ((0, 0, 0), (0, 0, 1),),
    (),
    (),
    (),
    (),
    (),
    ((0, 1, 0), (6, 2, 0), (0, 2, 1),),
    (),
    (),
    ((1, 0, 1),),
    ((1, 0, 0), (6, 1, 1),),
    (),
    (),
    (),
    ((2, 0, 1), (1, 1, 0),),
    ((0, 2, 0), (6, 3, 0), (2, 0, 0),),
    (),
    (),
    ((3, 0, 1),),
    ((1, 2, 1),),
    ((2, 1, 0), (6, 3, 1), (0, 1, 1), (3, 0, 0),),
    ((0, 3, 0),),
    ((6, 4, 0),),
    ((1, 2, 0), (2, 2, 1),),
    ((4, 0, 1),),
    ((6, 4, 1),),
    ((4, 0, 0), (1, 1, 1), (0, 3, 1),),
    ((3, 1, 0), (2, 2, 0), (1, 3, 0),),
    ((3, 2, 1), (6, 6, 0), (6, 6, 1), (0, 4, 0),),
    (),
    (),
    ((2, 1, 1), (1, 3, 1), (0, 6, 0), (0, 4, 1), (0, 6, 1), (4, 1, 0), (3, 2, 0), (2, 3, 0),),
    ((1, 4, 0), (1, 6, 0),),
    ((2, 3, 1), (6, 5, 0), (1, 4, 1), (1, 6, 1),),
    ((6, 5, 1),),
    ((4, 2, 1), (3, 1, 1),),
    ((2, 4, 0), (2, 6, 0), (3, 3, 0), (2, 4, 1), (2, 6, 1), (0, 5, 0), (4, 2, 0), (0, 5, 1), (3, 3, 1), (4, 1, 1), (1, 5, 0), (1, 5, 1), (4, 3, 0), (3, 4, 0), (3, 6, 0), (2, 5, 0), (3, 4, 1), (3, 6, 1), (4, 3, 1), (2, 5, 1), (4, 4, 0), (3, 5, 0), (4, 6, 0), (4, 4, 1), (3, 5, 1), (4, 6, 1), (4, 5, 0), (4, 5, 1), (5, 0, 0), (5, 0, 1), (5, 1, 0), (5, 2, 0), (5, 2, 1), (5, 3, 0), (5, 1, 1), (5, 4, 0), (5, 6, 0), (5, 3, 1), (5, 5, 0), (5, 4, 1), (5, 6, 1), (5, 5, 1),),
)


def backward_call(lengths, tokens, cotangent, weights, saved):
    rows, width = tokens.shape
    gelu_full, input_full, gates_full, output_full, mgate_full, mvalue_full, mdown_full = weights
    lru, ff = gelu_full.shape[1], mgate_full.shape[1]
    tiles = lru // LANES
    wide_tile = 2 * LANES
    f32, bf = jnp.float32, jnp.bfloat16
    shape = jax.ShapeDtypeStruct
    DOWN, MGATE, MVALUE, OUTPUT, GELU, INPUT, GATES = range(7)
    full = [mdown_full, mgate_full, mvalue_full, output_full, gelu_full, input_full, gates_full]
    extents = [w.shape for w in full]
    count = len(full)
    split = lambda v: v.reshape(4, 2, v.shape[0] // 8, v.shape[1])
    inputs = dict(
        tokens=tokens, cot=cotangent, gelu_w=gelu_full, input_w=input_full, gates_w=gates_full, output_w=output_full, mgate_w=mgate_full,
        mvalue_w=mvalue_full, mdown_w=mdown_full, small=saved.small, n1t=split(saved.n1t), pre=saved.pre, lin=saved.lin,
        convt=saved.convt, decay=saved.decay, k6=saved.k6, k2=saved.k2, k3=saved.k3, k7=saved.k7, slope=saved.slope,
        rect=split(saved.rect), resid=saved.resid, n2t=split(saved.n2t), mg=saved.mg, mv=saved.mv, hidt=split(saved.hidt),
    )
    slot_keys = list(slot_scratch(8, 256))
    most = max(4 * (r // 8) * (c // 2) // wide_tile for r, c in extents)
    passes = 13
    scratch = dict(
        go=pltpu.VMEM((rows, width), bf),
        gm=pltpu.VMEM((rows, width), bf),
        gn=pltpu.VMEM((rows, width), f32),
        n1t=pltpu.VMEM((4, 2, width // 8, rows), bf),
        n2t=pltpu.VMEM((4, 2, width // 8, rows), bf),
        rect=pltpu.VMEM((4, 2, lru // 8, rows), bf),
        small=pltpu.VMEM((16, lru), f32),
        part=pltpu.VMEM((16, lru), f32),
        gain=pltpu.VMEM((8, width), f32),
        into=pltpu.VMEM((tiles, 8, LANES), f32),
        halo=pltpu.VMEM((tiles, 8, LANES), f32),
        edge=pltpu.VMEM((tiles, 8, LANES), f32),
        stage=pltpu.VMEM((2, most, wide_tile), bf),
        landed=pltpu.VMEM((2, most, wide_tile), bf),
        gstage=pltpu.VMEM((4, 2, lru // 8, wide_tile), bf),
        ends=pltpu.VMEM((8, 2, tiles, LANES), f32),
        sslots=pltpu.VMEM((2, 5, 16, lru), f32),
        psend=pltpu.SemaphoreType.DMA((passes,)),
        precv=pltpu.SemaphoreType.DMA((passes,)),
        rsend=pltpu.SemaphoreType.DMA((count, 14)),
        rrecv=pltpu.SemaphoreType.DMA((count, 14)),
        esend=pltpu.SemaphoreType.DMA((7,)),
        erecv=pltpu.SemaphoreType.DMA((7,)),
        hsend=pltpu.SemaphoreType.DMA(()),
        hrecv=pltpu.SemaphoreType.DMA(()),
        ssend=pltpu.SemaphoreType.DMA((5,)),
        srecv=pltpu.SemaphoreType.DMA((5,)),
        load=pltpu.SemaphoreType.DMA((8,)),
        keep=pltpu.SemaphoreType.DMA((count + 1, 2)),
        credit=pltpu.SemaphoreType.REGULAR,
    )
    keys = list(scratch)
    outs = dict(tokens_grad=shape((rows, width), f32), small_sum=shape((16, lru), f32))
    out_keys = list(outs)
    sums = [shape((r // 8, c), bf) for r, c in extents]

    def kernel(lengths_ref, *refs):
        refs = list(refs)

        def take(k):
            got = refs[:k]
            del refs[:k]
            return got

        w = named(inputs, take(len(inputs)))
        out = named(out_keys, take(len(out_keys)))
        sum_refs = take(count)
        v = named(keys, take(len(keys)))
        slots = []
        for i, (r, c) in enumerate(extents):
            s = named(slot_keys, take(len(slot_keys)))
            s.n, s.h, s.tiles = r // 8, c // 2, c // 2 // wide_tile
            slots.append(s)
        place = Place()
        z, seq, core = place.z, place.seq, place.core
        red = Reduce(place, slots, (v.rsend, v.rrecv))
        ends = Ends(place, v.ends, (v.esend, v.erecv), True)
        tot = Small(place, v.part, v.sslots, (v.ssend, v.srecv))
        small, part = v.small, v.part
        kept = []

        def load(src, dst, k):
            cp = pltpu.make_async_copy(src, dst, v.load.at[k])
            cp.start()
            return cp

        first_loads = [load(w.cot, v.go, 0)]
        loads = [load(w.small, v.small, 1), load(w.n2t, v.n2t, 2), load(w.rect, v.rect, 3), load(w.n1t, v.n1t, 4)]

        def arrived(i, h):
            red.arrive(i, h)
            s = slots[i]
            cp = pltpu.make_async_copy(s.res.at[h], sum_refs[i].at[:, pl.ds(side(i, h) * s.h, s.h)], v.keep.at[i, h])

            @pl.when(red.outer)
            def _():
                cp.start()

        def totalled(i, h):
            s = slots[i]
            return pltpu.make_async_copy(s.res.at[h], sum_refs[i].at[:, pl.ds(side(i, h) * s.h, s.h)], v.keep.at[i, h])

        def add_peer(i, h):
            red.add_peer(i, h)
            cp = totalled(i, h)

            @pl.when(red.makes(h))
            def _():
                cp.start()

        def pass_on(i, h):
            red.pass_on(i, h)
            cp = totalled(i, h)

            @pl.when(red.helps(h))
            def _():
                cp.start()

        steps = (red.add_first, red.add_second, red.add_outer, add_peer, pass_on, arrived, red.start_first)
        turn = [0]

        def serve(spot):
            for step, i, h in PUMPS[spot]:
                steps[step](i, h)

        def pump():
            serve(turn[0])
            turn[0] += 1

        def pumps_at(*grid_steps):
            spots = list(enumerate(grid_steps, turn[0]))
            turn[0] += len(spots)

            def at_step():
                for spot, grid_step in spots:
                    if PUMPS[spot]:
                        pl.when(pl.program_id(0) == grid_step)(lambda spot=spot: serve(spot))

            return at_step

        def to_sib(k, used):
            return pltpu.make_async_remote_copy(
                src_ref=v.stage.at[k % 2, pl.ds(0, used)], dst_ref=v.landed.at[k % 2, pl.ds(0, used)], send_sem=v.psend.at[k],
                recv_sem=v.precv.at[k], device_id=place.sib, device_id_type=MESH,
            )

        sent = {}

        def send_blocks(k, used):
            if k >= 2:
                pl.semaphore_wait(v.credit, 1)
            sent[k] = used
            to_sib(k, used).start()

        def free_stage(k):
            if k >= 2:
                to_sib(k - 2, sent[k - 2]).wait_send()

        def give_credit(k):
            if k + 2 < passes:
                pl.semaphore_signal(v.credit, inc=1, device_id=place.sib, device_id_type=MESH)

        def side(i, h):
            return 1 - h if i == MVALUE else h

        def blocks(s):
            group = max(1, 512 // s.n)
            return [(j, group) for j in range(0, 4, group)]

        def for_sib(k, i, h, left, right):
            pump()
            s = slots[i]
            free_stage(k)

            @pl.loop(0, s.tiles)
            def _(t):
                r = right[:, pl.ds(pl.multiple_of((side(i, h) * s.tiles + t) * wide_tile, wide_tile), wide_tile)]
                for j, group in blocks(s):
                    value = dot(left[j : j + group, 1 - core].reshape(group * s.n, rows), r)
                    at = pl.ds(pl.multiple_of(t * 4 * s.n + j * s.n, s.n), group * s.n)
                    v.stage[k % 2, at, :] = low(value)

            send_blocks(k, 4 * s.n * s.tiles)

        def for_us(k, i, h, left, right):
            pump()
            s = slots[i]
            to_sib(k, sent[k]).wait_recv()

            @pl.loop(0, s.tiles)
            def _(t):
                r = right[:, pl.ds(pl.multiple_of((side(i, h) * s.tiles + t) * wide_tile, wide_tile), wide_tile)]
                for j, group in blocks(s):
                    value = dot(left[j : j + group, core].reshape(group * s.n, rows), r)
                    at = pl.ds(pl.multiple_of(t * 4 * s.n + j * s.n, s.n), group * s.n)
                    both = low(value + wide(v.landed[k % 2, at, :]))
                    lane = pl.ds(pl.multiple_of(t * wide_tile, wide_tile), wide_tile)
                    s.ab[h, j : j + group, :, lane] = both.reshape(group, s.n, wide_tile)

            give_credit(k)

        def eight(value):
            return value.reshape(value.shape[0] // 8, 8, value.shape[1]).sum(axis=0)

        def norm_back(x, grad, gain, add):
            scale = lax.rsqrt(jnp.mean(x * x, axis=-1, keepdims=True) + epsilon)
            v.gain[...] += eight(grad * x * scale)
            scaled = grad * gain
            m = jnp.mean(scaled * x, axis=-1, keepdims=True)
            return add + scale * (scaled - x * (scale * scale * m))

        def mlp_half(gmg, gmv, half):
            pump()
            steps_half = ff // wide_tile // 2
            inside = pumps_at(steps_half // 3, 2 * steps_half // 3)

            def body(md, value, slope):
                inside()
                t = pl.program_id(0) + half * steps_half
                at = pl.ds(pl.multiple_of(t * wide_tile, wide_tile), wide_tile)
                gh = dot_t(v.go[...], md[...])
                gmg[:, at] = low(gh * slope[...])
                gmv[:, at] = low(gh * value[...])

            across = pl.BlockSpec((rows, wide_tile), lambda t: (0, t + half * steps_half))
            pltpu.emit_pipeline(
                body, grid=(steps_half,), in_specs=[pl.BlockSpec((wide_tile, width), lambda t: (t + half * steps_half, 0)), across, across]
            )(w.mdown_w, w.mg, w.mv)

        def mlp_norm_half(gmg, gmv, half):
            pump()

            inside = pumps_at(1)

            def body(wg, wv):
                inside()
                t = pl.program_id(0) + 2 * half
                at = pl.ds(pl.multiple_of(t * wide_tile, wide_tile), wide_tile)
                v.gn[:, at] = dot_t(gmg[...], wg[...]) + dot_t(gmv[...], wv[...])

            pltpu.emit_pipeline(body, grid=(2,), in_specs=[pl.BlockSpec((wide_tile, ff), lambda t: (t + 2 * half, 0))] * 2)(
                w.mgate_w, w.mvalue_w
            )

        def mlp_phase(gmg, gmv):
            def head(hidt):
                down_loads = load(w.hidt, hidt, 5)
                meet([(z, (seq + d) % 8) for d in range(1, 8)] + [((z + d) % 4, seq) for d in range(1, 4)])
                first_loads[0].wait()
                valid_rows = lengths_ref[z] - seq * rows

                def mask(at):
                    here = lax.broadcasted_iota(jnp.int32, (64, width), 0) + at.start < valid_rows
                    v.go[at, :] = low(jnp.where(here, wide(v.go[at, :]), 0.0))

                rows_loop(rows, mask, 64)
                part[...] = jnp.zeros_like(part)
                down_loads.wait()
                for_sib(0, DOWN, 0, hidt, v.go)
                for_sib(1, DOWN, 1, hidt, v.go)
                mlp_half(gmg, gmv, 0)
                for_us(0, DOWN, 0, hidt, v.go)
                for_us(1, DOWN, 1, hidt, v.go)

            pl.run_scoped(head, pltpu.VMEM((4, 2, ff // 8, rows), bf))
            for cp in loads:
                cp.wait()
            for_sib(2, MGATE, 0, v.n2t, gmg)
            for_sib(3, MVALUE, 1, v.n2t, gmv)
            mlp_half(gmg, gmv, 1)
            for_us(2, MGATE, 0, v.n2t, gmg)
            for_us(3, MVALUE, 1, v.n2t, gmv)
            for_sib(4, MGATE, 1, v.n2t, gmg)
            for_sib(5, MVALUE, 0, v.n2t, gmv)
            mlp_norm_half(gmg, gmv, 0)
            for_us(4, MGATE, 1, v.n2t, gmg)
            for_us(5, MVALUE, 0, v.n2t, gmv)
            mlp_norm_half(gmg, gmv, 1)

        pl.run_scoped(mlp_phase, pltpu.VMEM((rows, ff), bf), pltpu.VMEM((rows, ff), bf))
        pump()
        v.gain[...] = jnp.zeros_like(v.gain)

        inside = pumps_at(rows // 128)

        def norm_two(resid, inside=inside):
            inside()
            at = pl.ds(pl.multiple_of(pl.program_id(0) * 64, 64), 64)
            value = norm_back(resid[...], v.gn[at, :], small[9:10, :width], wide(v.go[at, :]))
            v.gn[at, :] = value
            v.gm[at, :] = low(value)

        pltpu.emit_pipeline(norm_two, grid=(rows // 64,), in_specs=[pl.BlockSpec((64, width), lambda t: (t, 0))])(w.resid)
        part[9:10, :width] = v.gain[...].sum(axis=0, keepdims=True)
        tokens_load = load(w.tokens, v.go, 6)

        def branch_phase(adj, prod, gg, gl, gri):
            decay_load = load(w.decay, prod, 7)
            for_sib(6, OUTPUT, 0, v.rect, v.gm)
            for_sib(7, OUTPUT, 1, v.rect, v.gm)
            pump()

            inside = pumps_at(tiles // 6, tiles // 3)

            def into_branch(wo, value, slope, inside=inside):
                inside()
                t = pl.program_id(0)
                gr = dot_t(v.gm[...], wo[...])
                for q in range(2):
                    c = 2 * t + q
                    grad = gr[:, q * LANES : (q + 1) * LANES]
                    adj[c, pl.ds(0, rows), :] = grad * value[q]
                    gg[:, pl.ds(pl.multiple_of(c * LANES, LANES), LANES)] = low(grad * slope[q])

            pair = pl.BlockSpec((2, rows, LANES), lambda t: (t, 0, 0))
            pltpu.emit_pipeline(
                into_branch, grid=(tiles // 2,), in_specs=[pl.BlockSpec((wide_tile, width), lambda t: (t, 0)), pair, pair]
            )(w.output_w, w.pre, w.slope)
            for_us(6, OUTPUT, 0, v.rect, v.gm)
            for_us(7, OUTPUT, 1, v.rect, v.gm)
            pump()
            decay_load.wait()
            tails = strided_scan(prod, adj, prod, adj, True, rows, pump)
            before, whole = segment_ends(tails, True)
            ends.tell(whole)
            for c in range(tiles):
                v.into[c] = before[c][1]
                v.edge[c] = before[c][0]
            for_sib(8, GELU, 0, v.n1t, gg)
            for_sib(9, GELU, 1, v.n1t, gg)
            pump()
            carry = ends.joined()
            for c in range(tiles):
                v.into[c] = v.into[c] + v.edge[c] * carry[c : c + 1, :]
            span = rows // 8

            inside = pumps_at(tiles // 4, tiles // 2, 3 * tiles // 4)

            def through_gates(k6, k2, k3, k7, convt, wg, inside=inside):
                inside()
                c = pl.program_id(0)
                lane = pl.ds(pl.multiple_of(c * LANES, LANES), LANES)
                sums = [jnp.zeros((8, LANES), f32) for _ in range(3)]
                for k in range(8):
                    at = slice(k * span, (k + 1) * span)
                    here = adj[c, at, :] + prod[c, at, :] * v.into[c, k : k + 1, :]
                    grad_r = here * k6[at, :]
                    grad_i = here * k2[at, :]
                    adj[c, at, :] = here * k3[at, :]
                    gri[at, :LANES] = low(grad_r)
                    gri[at, LANES:] = low(grad_i)
                    for q, value in enumerate((here * k7[at, :], grad_r, grad_i)):
                        sums[q] = sums[q] + eight(value)
                part[7:8, lane] = sums[0].sum(axis=0, keepdims=True) * (cfactor * sigmoid(-small[7:8, lane]))
                part[5:6, lane] = sums[1].sum(axis=0, keepdims=True)
                part[6:7, lane] = sums[2].sum(axis=0, keepdims=True)
                product = low(dot(convt[...], gri[...]))
                for q in range(2):
                    unit = 2 * c + q
                    block = unit // 3
                    at = pl.ds(pl.multiple_of((unit % 3) * 64, 64), 64)
                    v.gstage[block // 2, block % 2, at, :] = product[64 * q : 64 * (q + 1), :]
                grad_conv = adj[c, pl.ds(0, rows), :] + dot_t(gri[...], wg[...])
                adj[c, pl.ds(0, rows), :] = grad_conv
                part[4:5, lane] = eight(grad_conv).sum(axis=0, keepdims=True)

            one = pl.BlockSpec((None, rows, LANES), lambda t: (t, 0, 0))
            pltpu.emit_pipeline(
                through_gates,
                grid=(tiles,),
                in_specs=[one] * 4
                + [pl.BlockSpec((None, LANES, rows), lambda t: (t, 0, 0)), pl.BlockSpec((LANES, wide_tile), lambda t: (t, 0))],
            )(w.k6, w.k2, w.k3, w.k7, w.convt, w.gates_w)

            def halo():
                return pltpu.make_async_remote_copy(
                    src_ref=v.edge, dst_ref=v.halo, send_sem=v.hsend, recv_sem=v.hrecv, device_id=(z, (seq + 7) % 8), device_id_type=MESH
                )

            v.edge[...] = adj[:, 0:8, :]

            @pl.when(seq > 0)
            def _():
                halo().start()

            for_us(8, GELU, 0, v.n1t, gg)
            pump()
            s = slots[GATES]
            free_stage(10)
            for j in range(4):

                def copy_block(at, j=j):
                    v.stage[0, pl.ds(pl.multiple_of(j * s.n + at.start, 16), 16), :] = v.gstage[j, 1 - core, at, :]

                rows_loop(s.n, copy_block)
            send_blocks(10, 4 * s.n)
            for_us(9, GELU, 1, v.n1t, gg)
            pump()

            @pl.when(seq == 7)
            def _():
                adj[:, pl.ds(rows, 8), :] = jnp.zeros((tiles, 8, LANES), f32)

            @pl.when(seq < 7)
            def _():
                halo().wait_recv()
                adj[:, pl.ds(rows, 8), :] = v.halo[...]

            inside = pumps_at(tiles // 3, 2 * tiles // 3)

            def through_conv(lin, inside=inside):
                inside()
                c = pl.program_id(0)
                lane = pl.ds(pl.multiple_of(c * LANES, LANES), LANES)
                taps = [small[k : k + 1, lane] for k in range(4)]
                sums = [jnp.zeros((8, LANES), f32) for _ in range(4)]
                for r in range(0, rows, 128):
                    here = adj[c, r : r + 128, :]
                    acc = taps[0] * here
                    for k in range(4):
                        sums[k] = sums[k] + eight(here * lin[8 + r - k : 8 + r - k + 128, :])
                        if k:
                            acc = acc + taps[k] * adj[c, r + k : r + k + 128, :]
                    gl[r : r + 128, lane] = low(acc)
                for k in range(4):
                    part[k : k + 1, lane] = sums[k].sum(axis=0, keepdims=True)

            pltpu.emit_pipeline(
                through_conv, grid=(tiles,), in_specs=[pl.BlockSpec((None, rows + 8, LANES), lambda t: (t, 0, 0))]
            )(w.lin)
            pump()
            to_sib(10, sent[10]).wait_recv()
            for j in range(4):

                def fold(at, j=j):
                    came = v.landed[0, pl.ds(pl.multiple_of(j * s.n + at.start, 16), 16), :]
                    both = low(wide(v.gstage[j, core, at, :]) + wide(came))
                    s.ab[0, j, at, :] = both[:, : s.h]
                    s.ab[1, j, at, :] = both[:, s.h :]

                rows_loop(s.n, fold)
            give_credit(10)
            for_sib(11, INPUT, 0, v.n1t, gl)
            for_sib(12, INPUT, 1, v.n1t, gl)
            pump()

            inside = pumps_at(width // wide_tile // 2)

            def into_norm(wi, wg, inside=inside):
                inside()
                t = pl.program_id(0)
                value = dot_t(gl[...], wi[...]) + dot_t(gg[...], wg[...])
                adj[2 * t, pl.ds(0, rows), :] = value[:, :LANES]
                adj[2 * t + 1, pl.ds(0, rows), :] = value[:, LANES:]

            pltpu.emit_pipeline(into_norm, grid=(width // wide_tile,), in_specs=[pl.BlockSpec((wide_tile, lru), lambda t: (t, 0))] * 2)(
                w.input_w, w.gelu_w
            )
            for_us(11, INPUT, 0, v.n1t, gl)
            for_us(12, INPUT, 1, v.n1t, gl)
            pump()
            v.gain[...] = jnp.zeros_like(v.gain)
            tokens_load.wait()

            def norm_one(at):
                grad = jnp.concatenate([adj[c, at, :] for c in range(width // LANES)], axis=1)
                v.gn[at, :] = norm_back(wide(v.go[at, :]), grad, small[8:9, :width], v.gn[at, :])

            rows_loop(rows // 2, norm_one, 64)
            pump()
            rows_loop(rows, norm_one, 64, rows // 2)
            part[8:9, :width] = v.gain[...].sum(axis=0, keepdims=True)

        pl.run_scoped(
            branch_phase,
            pltpu.VMEM((tiles, rows + 8, LANES), f32),
            pltpu.VMEM((tiles, rows, LANES), f32),
            pltpu.VMEM((rows, lru), bf),
            pltpu.VMEM((rows, lru), bf),
            pltpu.VMEM((rows, wide_tile), bf),
        )
        tot.begin()
        cp = pltpu.make_async_copy(v.gn, out.tokens_grad, v.keep.at[count, 0])
        cp.start()
        kept.append(cp)
        last = PUMPS[turn[0]]
        for k, (step, i, h) in enumerate(last):
            steps[step](i, h)
            if k % 4 == 3 and k < 20:
                tot.step(k // 4)
        cp = pltpu.make_async_copy(part, out.small_sum, v.keep.at[count, 1])
        cp.start()
        kept.append(cp)
        for i in range(count):
            for h in range(2):
                kept.append(totalled(i, h))
        for cp in kept:
            cp.wait()
        for i in range(count):
            red.drain(i)
        for k in (passes - 2, passes - 1):
            to_sib(k, sent[k]).wait_send()
        tot.drain()
        ends.drain()

        @pl.when(seq > 0)
        def _():
            pltpu.make_async_remote_copy(
                src_ref=v.edge, dst_ref=v.halo, send_sem=v.hsend, recv_sem=v.hrecv, device_id=(z, (seq + 7) % 8), device_id_type=MESH
            ).wait_send()

    slot_list = [value for r, c in extents for value in slot_scratch(r, c).values()]
    result = pl.pallas_call(
        kernel,
        out_shape=list(outs.values()) + sums,
        in_specs=[pl.BlockSpec(memory_space=pltpu.SMEM)] + [HBM] * len(inputs),
        out_specs=[HBM] * (len(outs) + count),
        scratch_shapes=list(scratch.values()) + slot_list,
        compiler_params=pltpu.CompilerParams(collective_id=2, has_side_effects=True, vmem_limit_bytes=62 << 20),
        name="backward",
    )(lengths, *inputs.values())
    return result[0], result[1], result[len(outs) :]


def local(
    tokens,
    lengths,
    mixer_gain,
    gelu_weight,
    input_weight,
    conv_taps,
    conv_bias,
    rgate_weight,
    rgate_bias,
    igate_weight,
    igate_bias,
    decay_param,
    output_weight,
    mlp_gain,
    mlp_gate,
    mlp_value,
    mlp_down,
    cotangent,
):
    count = tokens.shape[0]
    width_lru = input_weight.shape[1]
    block = rgate_weight.shape[1]
    heads = width_lru // block
    taps_count = conv_taps.shape[1]
    rim = taps_count - 1
    seq_count = lax.axis_size("seq")
    slot_length = count * seq_count
    first_row = (lax.axis_index("grp") * seq_count + lax.axis_index("seq")) * count
    global_row = first_row + jnp.arange(count, dtype=jnp.int32)
    position = global_row % slot_length
    slot_of = global_row // slot_length
    slot_ids = jnp.arange(lengths.shape[0], dtype=jnp.int32)
    slot_len = jnp.sum(
        jnp.where(slot_of[:, None] == slot_ids[None, :], lengths[None, :], 0), axis=1
    )
    valid = (position < slot_len).astype(jnp.float32)[:, None]
    starts = (position > 0).astype(jnp.float32)[:, None]
    lag_masks = [(position >= lag).astype(jnp.float32)[:, None] for lag in range(taps_count)]
    zeros_lru = jnp.zeros((width_lru,), jnp.float32)
    ones_lru = jnp.ones((width_lru,), jnp.float32)
    (
        gain_one,
        gelu_full,
        input_full,
        taps_full,
        cbias_full,
        rgate_full,
        rbias_full,
        igate_full,
        ibias_full,
        decay_full,
        output_full,
        gain_two,
        mgate_full,
        mvalue_full,
        mdown_full,
    ) = (
        lax.all_gather(mixer_gain, "seq", axis=0, tiled=True),
        lax.all_gather(gelu_weight, "seq", axis=0, tiled=True),
        lax.all_gather(input_weight, "seq", axis=0, tiled=True),
        lax.all_gather(conv_taps, "seq", axis=0, tiled=True),
        lax.all_gather(conv_bias, "seq", axis=0, tiled=True),
        lax.all_gather(rgate_weight, "seq", axis=0, tiled=True),
        lax.all_gather(rgate_bias, "seq", axis=0, tiled=True),
        lax.all_gather(igate_weight, "seq", axis=0, tiled=True),
        lax.all_gather(igate_bias, "seq", axis=0, tiled=True),
        lax.all_gather(decay_param, "seq", axis=0, tiled=True),
        lax.all_gather(output_weight, "seq", axis=0, tiled=True),
        lax.all_gather(mlp_gain, "seq", axis=0, tiled=True),
        lax.all_gather(mlp_gate, "seq", axis=0, tiled=True),
        lax.all_gather(mlp_value, "seq", axis=0, tiled=True),
        lax.all_gather(mlp_down, "seq", axis=0, tiled=True),
    )
    inputs = tokens.astype(jnp.float32)
    normed_one, norm_one_back = jax.vjp(rms_norm, inputs, gain_one.astype(jnp.float32))
    normed_one = normed_one.astype(jnp.bfloat16)
    gate_pre = matmul(normed_one, gelu_full)
    gate_act, gate_back = jax.vjp(gelu_tanh, gate_pre)
    linear = matmul(normed_one, input_full)
    rim_in = passed_along(linear[count - rim :], "seq", 1)
    extended = jnp.concatenate([rim_in, linear], axis=0)
    taps_fwd = taps_full.astype(jnp.float32)
    conv = cbias_full.astype(jnp.float32) + taps_fwd[:, 0] * linear
    for lag in range(1, taps_count):
        conv = conv + taps_fwd[:, lag] * (extended[rim - lag : rim - lag + count] * lag_masks[lag])
    conv_low = conv.astype(jnp.bfloat16)
    conv_value = conv_low.astype(jnp.float32)
    rgate_pre = block_apply(conv_low, rgate_full, heads) + rbias_full.astype(jnp.float32)
    igate_pre = block_apply(conv_low, igate_full, heads) + ibias_full.astype(jnp.float32)
    (decay, inject), gates_back = jax.vjp(
        recurrence_gates, rgate_pre, igate_pre, conv_value, decay_full.astype(jnp.float32)
    )
    decay_used = decay * starts
    cum_decay, state_zero = lax.associative_scan(chain_combine, (decay_used, inject), axis=0)
    scanned = carried_in(
        (cum_decay[-1], state_zero[-1]), "seq", chain_combine, (ones_lru, zeros_lru), False
    )
    carry_in = scanned[1]
    state = state_zero + cum_decay * carry_in
    mixed_rec = (state * gate_act).astype(jnp.bfloat16)
    resid = inputs + matmul(mixed_rec, output_full)
    normed_two, norm_two_back = jax.vjp(rms_norm, resid, gain_two.astype(jnp.float32))
    normed_two = normed_two.astype(jnp.bfloat16)
    mgate_pre = matmul(normed_two, mgate_full)
    mvalue_pre = matmul(normed_two, mvalue_full)
    mgate_act, mgate_back = jax.vjp(gelu_tanh, mgate_pre)
    hidden = (mgate_act * mvalue_pre).astype(jnp.bfloat16)
    mixed = ((resid + matmul(hidden, mdown_full)) * valid).astype(jnp.bfloat16)
    (
        gain_one,
        gelu_full,
        input_full,
        taps_full,
        cbias_full,
        rgate_full,
        rbias_full,
        igate_full,
        ibias_full,
        decay_full,
        output_full,
        gain_two,
        mgate_full,
        mvalue_full,
        mdown_full,
    ) = (
        lax.all_gather(mixer_gain, "seq", axis=0, tiled=True),
        lax.all_gather(gelu_weight, "seq", axis=0, tiled=True),
        lax.all_gather(input_weight, "seq", axis=0, tiled=True),
        lax.all_gather(conv_taps, "seq", axis=0, tiled=True),
        lax.all_gather(conv_bias, "seq", axis=0, tiled=True),
        lax.all_gather(rgate_weight, "seq", axis=0, tiled=True),
        lax.all_gather(rgate_bias, "seq", axis=0, tiled=True),
        lax.all_gather(igate_weight, "seq", axis=0, tiled=True),
        lax.all_gather(igate_bias, "seq", axis=0, tiled=True),
        lax.all_gather(decay_param, "seq", axis=0, tiled=True),
        lax.all_gather(output_weight, "seq", axis=0, tiled=True),
        lax.all_gather(mlp_gain, "seq", axis=0, tiled=True),
        lax.all_gather(mlp_gate, "seq", axis=0, tiled=True),
        lax.all_gather(mlp_value, "seq", axis=0, tiled=True),
        lax.all_gather(mlp_down, "seq", axis=0, tiled=True),
    )
    taps_back = taps_full.astype(jnp.float32)
    grad_out = cotangent.astype(jnp.float32) * valid
    grad_out_low = grad_out.astype(jnp.bfloat16)
    down_grad = inner_rows(hidden, grad_out_low)
    grad_hidden = outer_cols(grad_out_low, mdown_full)
    grad_mgate = mgate_back(grad_hidden * mvalue_pre)[0].astype(jnp.bfloat16)
    grad_mvalue = (grad_hidden * mgate_act).astype(jnp.bfloat16)
    mgate_grad = inner_rows(normed_two, grad_mgate)
    mvalue_grad = inner_rows(normed_two, grad_mvalue)
    grad_ntwo = outer_cols(grad_mgate, mgate_full) + outer_cols(grad_mvalue, mvalue_full)
    grad_resid_norm, gain_two_grad = norm_two_back(grad_ntwo)
    grad_resid = grad_out + grad_resid_norm
    grad_mix = grad_resid.astype(jnp.bfloat16)
    output_grad = inner_rows(mixed_rec, grad_mix)
    grad_rec = outer_cols(grad_mix, output_full)
    grad_state = grad_rec * gate_act
    grad_gate = gate_back(grad_rec * state)[0].astype(jnp.bfloat16)
    decay_next = jnp.concatenate([decay_used[1:], jnp.ones((1, width_lru), jnp.float32)], axis=0)
    rev_prod, rev_adjoint = lax.associative_scan(
        chain_combine, (jnp.flip(decay_next, 0), jnp.flip(grad_state, 0)), axis=0
    )
    tail_prod = jnp.flip(rev_prod, 0)
    adjoint_zero = jnp.flip(rev_adjoint, 0)
    summary_decay = decay_used[0] * tail_prod[0]
    summary_adjoint = decay_used[0] * adjoint_zero[0]
    scanned_back = carried_in(
        (summary_decay, summary_adjoint), "seq", chain_combine, (ones_lru, zeros_lru), True
    )
    incoming = scanned_back[1]
    adjoint = adjoint_zero + tail_prod * incoming
    state_prev = jnp.concatenate([carry_in[None, :], state[:-1]], axis=0)
    grad_decay = adjoint * state_prev * starts
    grad_rpre, grad_ipre, grad_direct, decay_grad = gates_back((grad_decay, adjoint))
    rbias_grad = jnp.sum(grad_rpre, axis=0)
    ibias_grad = jnp.sum(grad_ipre, axis=0)
    grad_rlow = grad_rpre.astype(jnp.bfloat16)
    grad_ilow = grad_ipre.astype(jnp.bfloat16)
    rgate_grad = block_grad(conv_low, grad_rlow, heads)
    igate_grad = block_grad(conv_low, grad_ilow, heads)
    grad_conv = (
        grad_direct
        + block_back(grad_rlow, rgate_full, heads)
        + block_back(grad_ilow, igate_full, heads)
    )
    cbias_grad = jnp.sum(grad_conv, axis=0)
    taps_columns = []
    grad_extended = jnp.zeros((count + rim, width_lru), jnp.float32)
    for lag in range(taps_count):
        masked_term = grad_conv * lag_masks[lag]
        taps_columns.append(jnp.sum(masked_term * extended[rim - lag : rim - lag + count], axis=0))
        grad_extended = grad_extended + jnp.pad(
            taps_back[:, lag] * masked_term, ((rim - lag, lag), (0, 0))
        )
    taps_grad = jnp.stack(taps_columns, axis=1)
    rim_back = passed_along(grad_extended[:rim], "seq", -1)
    grad_linear = grad_extended[rim:] + jnp.pad(rim_back, ((count - rim, 0), (0, 0)))
    grad_lin = grad_linear.astype(jnp.bfloat16)
    input_grad = inner_rows(normed_one, grad_lin)
    gelu_grad = inner_rows(normed_one, grad_gate)
    grad_none = outer_cols(grad_lin, input_full) + outer_cols(grad_gate, gelu_full)
    grad_inputs_norm, gain_one_grad = norm_one_back(grad_none)
    tokens_grad = grad_resid + grad_inputs_norm
    partials = (
        gain_one_grad,
        gelu_grad,
        input_grad,
        taps_grad,
        cbias_grad,
        rgate_grad,
        rbias_grad,
        igate_grad,
        ibias_grad,
        decay_grad,
        output_grad,
        gain_two_grad,
        mgate_grad,
        mvalue_grad,
        down_grad,
    )
    summed_seq = (
        lax.psum_scatter(partials[0], "seq", scatter_dimension=0, tiled=True),
        lax.psum_scatter(partials[1], "seq", scatter_dimension=0, tiled=True),
        lax.psum_scatter(partials[2], "seq", scatter_dimension=0, tiled=True),
        lax.psum_scatter(partials[3], "seq", scatter_dimension=0, tiled=True),
        lax.psum_scatter(partials[4], "seq", scatter_dimension=0, tiled=True),
        lax.psum_scatter(partials[5], "seq", scatter_dimension=0, tiled=True),
        lax.psum_scatter(partials[6], "seq", scatter_dimension=0, tiled=True),
        lax.psum_scatter(partials[7], "seq", scatter_dimension=0, tiled=True),
        lax.psum_scatter(partials[8], "seq", scatter_dimension=0, tiled=True),
        lax.psum_scatter(partials[9], "seq", scatter_dimension=0, tiled=True),
        lax.psum_scatter(partials[10], "seq", scatter_dimension=0, tiled=True),
        lax.psum_scatter(partials[11], "seq", scatter_dimension=0, tiled=True),
        lax.psum_scatter(partials[12], "seq", scatter_dimension=0, tiled=True),
        lax.psum_scatter(partials[13], "seq", scatter_dimension=0, tiled=True),
        lax.psum_scatter(partials[14], "seq", scatter_dimension=0, tiled=True),
    )
    totals = lax.psum(tuple(summed_seq), "grp")
    return (
        mixed,
        tokens_grad,
        totals[0],
        totals[1],
        totals[2],
        totals[3],
        totals[4],
        totals[5],
        totals[6],
        totals[7],
        totals[8],
        totals[9],
        totals[10],
        totals[11],
        totals[12],
        totals[13],
        totals[14],
    )


def local_fast(
    tokens,
    lengths,
    mixer_gain,
    gelu_weight,
    input_weight,
    conv_taps,
    conv_bias,
    rgate_weight,
    rgate_bias,
    igate_weight,
    igate_bias,
    decay_param,
    output_weight,
    mlp_gain,
    mlp_gate,
    mlp_value,
    mlp_down,
    cotangent,
):
    block = rgate_weight.shape[1]
    width_lru = input_weight.shape[1]
    lru_rows = jnp.concatenate(
        [conv_taps.T, conv_bias[None], rgate_bias[None], igate_bias[None], decay_param[None]], axis=0
    ).astype(jnp.float32)
    model_rows = jnp.stack([mixer_gain, mlp_gain]).astype(jnp.float32)
    mine = lax.axis_index("seq")
    across = lambda value, columns: jnp.pad(value, ((0, 0), (0, columns - value.shape[1])))
    small = jnp.concatenate([across(lru_rows, 256), across(model_rows, 256), jnp.zeros((6, 256), jnp.float32)], axis=0)
    gates = jnp.concatenate([rgate_weight, igate_weight], axis=1)
    weights, saved = forward_call(
        lengths, tokens, small, [gelu_weight, input_weight, gates, output_weight, mlp_gate, mlp_value, mlp_down]
    )
    tokens_grad, small_sum, big = backward_call(lengths, tokens, cotangent, weights, saved)
    down, mgate, mvalue, out_w, gelu_w, input_w, gates = [value.astype(jnp.float32) for value in big]
    lru_own = lax.dynamic_slice(small_sum, (0, mine * conv_bias.shape[0]), (8, conv_bias.shape[0]))
    model_own = lax.dynamic_slice(small_sum, (8, mine * mixer_gain.shape[0]), (2, mixer_gain.shape[0]))
    return (
        saved.mixed,
        tokens_grad,
        model_own[0],
        gelu_w,
        input_w,
        lru_own[:4].T,
        lru_own[4],
        gates[:, :block],
        lru_own[5],
        gates[:, block:],
        lru_own[6],
        lru_own[7],
        out_w,
        model_own[1],
        mgate,
        mvalue,
        down,
    )


def solution(mesh):
    placed = (
        P(("grp", "seq"), None),
        P(),
        P("seq"),
        P("seq", None),
        P("seq", None),
        P("seq", None),
        P("seq"),
        P("seq", None),
        P("seq"),
        P("seq", None),
        P("seq"),
        P("seq"),
        P("seq", None),
        P("seq"),
        P("seq", None),
        P("seq", None),
        P("seq", None),
        P(("grp", "seq"), None),
    )
    fits = mesh.shape["grp"] == 4 and mesh.shape["seq"] == 8
    return jax.shard_map(
        local_fast if fits else local,
        mesh=mesh,
        in_specs=placed,
        out_specs=(
            P(("grp", "seq"), None),
            P(("grp", "seq"), None),
            P("seq"),
            P("seq", None),
            P("seq", None),
            P("seq", None),
            P("seq"),
            P("seq", None),
            P("seq"),
            P("seq", None),
            P("seq"),
            P("seq"),
            P("seq", None),
            P("seq"),
            P("seq", None),
            P("seq", None),
            P("seq", None),
        ),
        check_vma=False,
    )
```

```python
import math
from types import SimpleNamespace

import jax
import jax.numpy as jnp
from jax import lax
from jax.experimental import pallas as pl
from jax.experimental.pallas import tpu as pltpu
from jax.sharding import PartitionSpec as P

epsilon = 1e-06
cfactor = 8.0


def passed_along(value, axis, steps):
    count = lax.axis_size(axis)
    leading, last = (max(0, -steps), min(count, count - steps))
    return lax.ppermute(value, axis, [(source, source + steps) for source in range(leading, last)])


def carried_in(value, axis, join, neutral, backward):
    count, mine = (lax.axis_size(axis), lax.axis_index(axis))
    pieces = jax.tree.map(lambda part: lax.all_gather(part, axis), value)
    if backward:
        pieces = jax.tree.map(lambda part: part[::-1], pieces)
        mine = count - 1 - mine
    so_far = jax.tree.map(
        lambda part, zero: jnp.full_like(part, 0) + jnp.asarray(zero, part.dtype), value, neutral
    )

    def step(position, so_far):
        longer = join(so_far, jax.tree.map(lambda part: part[position], pieces))
        return jax.tree.map(lambda new, old: jnp.where(position < mine, new, old), longer, so_far)

    return lax.fori_loop(0, count - 1, step, so_far)


def rms_norm(rows_in, gain):
    return rows_in * lax.rsqrt(jnp.mean(rows_in * rows_in, axis=-1, keepdims=True) + epsilon) * gain


def gelu_tanh(values):
    return jax.nn.gelu(values, approximate=True)


def matmul(left, right):
    return jnp.dot(left, right, preferred_element_type=jnp.float32)


def inner_rows(left, right):
    return lax.dot_general(
        left, right, (((0,), (0,)), ((), ())), preferred_element_type=jnp.float32
    )


def outer_cols(left, right):
    return lax.dot_general(
        left, right, (((1,), (1,)), ((), ())), preferred_element_type=jnp.float32
    )


def block_apply(values, weight, heads):
    count = values.shape[0]
    width = weight.shape[1]
    parts = values.reshape(count, heads, width)
    blocks = weight.reshape(heads, width, width)
    return jnp.einsum("rhi,hij->rhj", parts, blocks, preferred_element_type=jnp.float32).reshape(
        count, heads * width
    )


def block_back(grads, weight, heads):
    count = grads.shape[0]
    width = weight.shape[1]
    parts = grads.reshape(count, heads, width)
    blocks = weight.reshape(heads, width, width)
    return jnp.einsum("rhj,hij->rhi", parts, blocks, preferred_element_type=jnp.float32).reshape(
        count, heads * width
    )


def block_grad(values, grads, heads):
    count = values.shape[0]
    width = values.shape[1] // heads
    left = values.reshape(count, heads, width)
    right = grads.reshape(count, heads, width)
    return jnp.einsum("rhi,rhj->hij", left, right, preferred_element_type=jnp.float32).reshape(
        heads * width, width
    )


def chain_combine(earlier, later):
    return (earlier[0] * later[0], later[0] * earlier[1] + later[1])


def recurrence_gates(rgate_pre, igate_pre, conv_in, decay_in):
    rgate = jax.nn.sigmoid(rgate_pre)
    igate = jax.nn.sigmoid(igate_pre)
    log_decay = -cfactor * jax.nn.softplus(-decay_in) * rgate
    return (jnp.exp(log_decay), jnp.sqrt(-jnp.expm1(2.0 * log_decay)) * igate * conv_in)


MESH = pl.DeviceIdType.MESH


class Place:
    def __init__(self):
        self.z = lax.axis_index("grp")
        seq = lax.axis_index("seq")
        self.core = seq % 2
        self.x = (seq // 2) % 2
        self.y = seq // 4
        self.seq = seq
        self.sib = (self.z, self.at(self.y, self.x, 1 - self.core))
        self.xnb = (self.z, self.at(self.y, 1 - self.x, self.core))
        self.ynb = (self.z, self.at(1 - self.y, self.x, self.core))

    def at(self, y, x, core):
        return (y * 2 + x) * 2 + core

    def level(self, z):
        return (z, self.seq)


def greet(peers):
    barrier = pltpu.get_barrier_semaphore()
    for peer in peers:
        pl.semaphore_signal(barrier, inc=1, device_id=peer, device_id_type=MESH)


def met(count):
    pl.semaphore_wait(pltpu.get_barrier_semaphore(), count)


GOT = ("X", "Y", "D1", "D2", "SO", "SX", "SY", "S1", "S2")
SENT = ("ox", "oy", "os", "fy", "fx", "zX", "zY", "zD1", "zD2", "SX", "SY", "S1", "S2")
OVER_LINKS = GOT[:4]
TO_SIB = dict(zip(OVER_LINKS, GOT[5:]))


class Gather:
    def __init__(self, place, shards, fulls, kinds, send, recv, own, bounce):
        self.p, self.shards, self.fulls, self.bounce, self.kinds = place, shards, fulls, bounce, kinds
        self.send, self.recv, self.own = send, recv, own
        self.znb = place.level(place.z + 1 - 2 * (place.z % 2))

    def fetched(self, i, odd):
        return self.kinds[i] != 2 - odd

    def part(self, i, name):
        p = self.p
        n = self.shards[i].shape[0]
        y, x = p.y, p.x
        if name[-1] == "X":
            x = 1 - x
        elif name[-1] == "Y":
            y = 1 - y
        elif name[-1] in "12":
            x, y = 1 - x, 1 - y
        core = 1 - p.core if name[0] == "S" else p.core
        first = pl.multiple_of(p.at(y, x, core) * n, n)
        if name[-1] == "1":
            return pl.ds(first, n // 2)
        if name[-1] == "2":
            return pl.ds(pl.multiple_of(first + n // 2, n // 2), n // 2)
        return pl.ds(first, n)

    def half(self, i, name, which):
        n = self.shards[i].shape[0]
        return pl.ds(pl.multiple_of(self.part(i, name).start + which * (n // 2), n // 2), n // 2)

    def copy(self, i, how, got, peer, rows, src=None):
        full = self.fulls[i]
        return pltpu.make_async_remote_copy(
            src_ref=full.at[rows] if src is None else src,
            dst_ref=full.at[rows],
            send_sem=self.send.at[i, SENT.index(how)],
            recv_sem=self.recv.at[i, GOT.index(got)],
            device_id=peer,
            device_id_type=MESH,
        )

    def wait(self, i, name):
        self.copy(i, "ox", name, self.p.sib, self.part(i, name)).wait_recv()

    def own_far(self, i):
        p, mine = self.p, self.part(i, "O")
        return [self.copy(i, "ox", "X", p.xnb, mine, self.shards[i]), self.copy(i, "oy", "Y", p.ynb, mine, self.shards[i])]

    def own_near(self, i):
        return self.copy(i, "os", "SO", self.p.sib, self.part(i, "O"), self.shards[i])

    def own_kept(self, i, leg):
        if leg == 0:
            return pltpu.make_async_copy(self.shards[i], self.bounce[i], self.own.at[i, 0])
        return pltpu.make_async_copy(self.bounce[i], self.fulls[i].at[self.part(i, "O")], self.own.at[i, 1])

    def start(self, i, odd):
        if self.fetched(i, odd):
            for c in self.own_far(i):
                c.start()
        self.own_near(i).start()
        self.own_kept(i, 0).start()

    def onward(self, i, name, odd):
        p = self.p
        copies = []
        if self.fetched(i, odd):
            if name == "X":
                copies.append(self.copy(i, "fy", "D1", p.ynb, self.half(i, "X", 0)))
            if name == "Y":
                copies.append(self.copy(i, "fx", "D2", p.xnb, self.half(i, "Y", 1)))
            if self.kinds[i]:
                copies.append(self.copy(i, "z" + name, name, self.znb, self.part(i, name)))
        copies.append(self.copy(i, TO_SIB[name], TO_SIB[name], p.sib, self.part(i, name)))
        return copies

    def relay(self, i, name, odd):
        self.wait(i, name)
        for c in self.onward(i, name, odd):
            c.start()
        if name == "X":
            self.own_kept(i, 0).wait()
            self.own_kept(i, 1).start()

    def arrive(self, i):
        for name in GOT[4:]:
            self.wait(i, name)
        self.own_kept(i, 1).wait()

    def drain(self, i, odd):
        if self.fetched(i, odd):
            for c in self.own_far(i):
                c.wait_send()
        self.own_near(i).wait_send()
        for name in OVER_LINKS:
            for c in self.onward(i, name, odd):
                c.wait_send()


def rows_loop(total, body, step=16, start=0):
    @pl.loop(start // step, total // step)
    def _(k):
        body(pl.ds(pl.multiple_of(k * step, step), step))


def wide(value):
    return value.astype(jnp.float32)

class Reduce:
    def __init__(self, place, slots, sems):
        self.p = place
        self.slots = slots
        self.send, self.recv = sems
        z = place.z
        inner = (z == 1) | (z == 2)
        self.inner = inner
        self.outer = (z == 0) | (z == 3)
        self.peer = place.level(jnp.where(inner, 3 - z, z))
        self.out = place.level(jnp.where(z < 2, 1 - z, 5 - z))
        self.me = 2 * place.y + place.x

    def makes(self, h):
        return self.p.z == 1 + h

    def helps(self, h):
        return self.p.z == 2 - h

    def copy(self, i, tag, src, dst, peer):
        return pltpu.make_async_remote_copy(
            src_ref=src, dst_ref=dst, send_sem=self.send.at[i, tag], recv_sem=self.recv.at[i, tag], device_id=peer, device_id_type=MESH
        )

    def first(self, i, h):
        p, s = self.p, self.slots[i]
        if h == 0:
            return [self.copy(i, q, s.ab.at[0, 2 * q + 1 - p.x], s.fr.at[0, q], p.xnb) for q in range(2)]
        return [self.copy(i, 2 + q, s.ab.at[1, 2 * (1 - p.y) + q], s.fr.at[1, q], p.ynb) for q in range(2)]

    def second(self, i, h):
        p, s = self.p, self.slots[i]
        if h == 0:
            return self.copy(i, 4, s.ab.at[0, 2 * (1 - p.y) + p.x], s.se.at[0], p.ynb)
        return self.copy(i, 5, s.ab.at[1, 2 * p.y + 1 - p.x], s.se.at[1], p.xnb)

    def up(self, i, h):
        s = self.slots[i]
        return self.copy(i, 6 + h, s.ab.at[h, self.me], s.zo.at[h], self.out)

    def across(self, i, h):
        s = self.slots[i]
        return self.copy(i, 8 + h, s.ab.at[h, self.me], s.zp, self.peer)

    def down(self, i, h):
        res = self.slots[i].res.at[h]
        return self.copy(i, 10 + h, res, res, self.out)

    def over(self, i, h):
        res = self.slots[i].res.at[h]
        return self.copy(i, 12 + h, res, res, self.peer)

    def start_first(self, i, h):
        for cp in self.first(i, h):
            cp.start()

    def add_first(self, i, h):
        p, s = self.p, self.slots[i]
        for cp in self.first(i, h):
            cp.wait_recv()
        for q in range(2):
            j = 2 * q + p.x if h == 0 else 2 * p.y + q

            def body(rows, q=q, j=j):
                s.ab[h, j, rows, :] = low(wide(s.ab[h, j, rows, :]) + wide(s.fr[h, q, rows, :]))

            rows_loop(s.n, body)
        self.second(i, h).start()

    def add_second(self, i, h):
        s, me = self.slots[i], self.me
        self.second(i, h).wait_recv()

        def body(rows):
            s.ab[h, me, rows, :] = low(wide(s.ab[h, me, rows, :]) + wide(s.se[h, rows, :]))

        rows_loop(s.n, body)

        @pl.when(self.outer)
        def _():
            self.up(i, h).start()

    def add_outer(self, i, h):
        s, me = self.slots[i], self.me

        @pl.when(self.inner)
        def _():
            self.up(i, h).wait_recv()

            def body(rows):
                s.ab[h, me, rows, :] = low(wide(s.ab[h, me, rows, :]) + wide(s.zo[h, rows, :]))

            rows_loop(s.n, body)

        @pl.when(self.helps(h))
        def _():
            self.across(i, h).start()

    def add_peer(self, i, h):
        s, me = self.slots[i], self.me

        @pl.when(self.makes(h))
        def _():
            self.across(i, h).wait_recv()

            def body(rows):
                s.res[h, rows, :] = low(wide(s.ab[h, me, rows, :]) + wide(s.zp[rows, :]))

            rows_loop(s.n, body)
            self.down(i, h).start()
            self.over(i, h).start()

    def pass_on(self, i, h):
        @pl.when(self.helps(h))
        def _():
            self.over(i, h).wait_recv()
            self.down(i, h).start()

    def arrive(self, i, h):
        @pl.when(self.outer)
        def _():
            self.down(i, h).wait_recv()

    def drain(self, i):
        for h in range(2):

            @pl.when(self.outer)
            def _(h=h):
                self.up(i, h).wait_send()

            @pl.when(self.inner)
            def _(h=h):
                self.down(i, h).wait_send()

            @pl.when(self.makes(h))
            def _(h=h):
                self.over(i, h).wait_send()

            @pl.when(self.helps(h))
            def _(h=h):
                self.across(i, h).wait_send()

            for cp in self.first(i, h) + [self.second(i, h)]:
                cp.wait_send()


class Small:
    def __init__(self, place, total, slots, sems):
        p = place
        self.total, self.slots = total, slots
        self.send, self.recv = sems
        z = p.z
        self.order = [p.sib, p.xnb, p.ynb, p.level(z + 1 - 2 * (z % 2)), p.level((z + 2) % 4)]

    def copy(self, k):
        return pltpu.make_async_remote_copy(
            src_ref=self.slots.at[0, k],
            dst_ref=self.slots.at[1, k],
            send_sem=self.send.at[k],
            recv_sem=self.recv.at[k],
            device_id=self.order[k],
            device_id_type=MESH,
        )

    def begin(self):
        self.slots[0, 0] = self.total[...]
        self.copy(0).start()

    def step(self, k):
        self.copy(k).wait_recv()
        both = self.slots[0, k] + self.slots[1, k]
        if k < 4:
            self.slots[0, k + 1] = both
            self.copy(k + 1).start()
        else:
            self.total[...] = both

    def drain(self):
        for k in range(5):
            self.copy(k).wait_send()

ROOT = math.sqrt(2.0 / math.pi)
CUBE = 0.044715
LANES = 128


def low(value):
    return value.astype(jnp.bfloat16)


def gelu_parts(v):
    square = v * v
    t = jnp.tanh(ROOT * (v + CUBE * v * square))
    half = 0.5 * (1.0 + t)
    return v * half, half + 0.5 * v * (1.0 - t * t) * (ROOT * (1.0 + 3.0 * CUBE * square))


def dot(left, right):
    return jnp.dot(left, right, preferred_element_type=jnp.float32)


def dot_t(left, right):
    return lax.dot_general(left, right, (((1,), (1,)), ((), ())), preferred_element_type=jnp.float32)


def sigmoid(v):
    return 1.0 / (1.0 + jnp.exp(-v))


def minus_expm1(twice, half_of):
    t = jnp.tanh(half_of)
    return -2.0 * t / (1.0 - t)


def softplus_minus(v):
    return jnp.maximum(-v, 0.0) + jnp.log1p(jnp.exp(-jnp.abs(v)))


def strided_scan(decay_ref, value_ref, prod_ref, sum_ref, backward, rows, between):
    tiles, _, lanes = sum_ref.shape
    span = rows // 8

    def step(k, carry):
        prod, total = carry
        t = span - 1 - k if backward else k
        spot = pl.ds(t, 8, stride=span)
        new_prod, new_total = [], []
        for c in range(tiles):
            d, v = decay_ref[c, spot, :], value_ref[c, spot, :]
            if backward:
                seen = total[c] + v
                sum_ref[c, spot, :] = seen
                prod_ref[c, spot, :] = prod[c]
                new_prod.append(prod[c] * d)
                new_total.append(seen * d)
            else:
                new_prod.append(prod[c] * d)
                new_total.append(total[c] * d + v)
                prod_ref[c, spot, :] = new_prod[c]
                sum_ref[c, spot, :] = new_total[c]
        return new_prod, new_total

    ones = [jnp.ones((8, lanes), jnp.float32)] * tiles
    zeros = [jnp.zeros((8, lanes), jnp.float32)] * tiles
    half = lax.fori_loop(0, span // 2, step, (ones, zeros), unroll=2)
    between()
    return lax.fori_loop(span // 2, span, step, half, unroll=2)


def segment_ends(ends, backward):
    before, whole = [], []
    order = range(7, -1, -1) if backward else range(8)
    for prod, total in zip(*ends):
        p = jnp.ones((1, prod.shape[1]), jnp.float32)
        s = jnp.zeros((1, prod.shape[1]), jnp.float32)
        ps, ss = [None] * 8, [None] * 8
        for k in order:
            ps[k], ss[k] = p, s
            d, v = prod[k : k + 1], total[k : k + 1]
            p, s = p * d, s * d + v
        before.append((jnp.concatenate(ps, axis=0), jnp.concatenate(ss, axis=0)))
        whole.append((p, s))
    return before, whole


class Ends:
    def __init__(self, place, slots, sems, backward):
        self.p, self.slots, self.backward = place, slots, backward
        self.send, self.recv = sems

    def copy(self, d):
        to = (self.p.seq + d) % 8
        return pltpu.make_async_remote_copy(
            src_ref=self.slots.at[self.p.seq], dst_ref=self.slots.at[self.p.seq], send_sem=self.send.at[d - 1],
            recv_sem=self.recv.at[d - 1], device_id=(self.p.z, to), device_id_type=MESH,
        )

    def come(self, d):
        src = (self.p.seq + 8 - d) % 8
        return pltpu.make_async_remote_copy(
            src_ref=self.slots.at[src], dst_ref=self.slots.at[src], send_sem=self.send.at[d - 1],
            recv_sem=self.recv.at[d - 1], device_id=(self.p.z, src), device_id_type=MESH,
        )

    def tell(self, whole):
        for c, (prod, total) in enumerate(whole):
            self.slots[self.p.seq, 0, c : c + 1, :] = prod
            self.slots[self.p.seq, 1, c : c + 1, :] = total
        self.share()

    def share(self):
        for d in range(1, 8):
            self.copy(d).start()

    def shared(self):
        for d in range(1, 8):
            self.come(d).wait_recv()

    def joined(self):
        self.shared()
        carry = jnp.zeros(self.slots.shape[2:], jnp.float32)
        for k in range(7, 0, -1) if self.backward else range(7):
            further = self.slots[k, 0] * carry + self.slots[k, 1]
            counts = k > self.p.seq if self.backward else k < self.p.seq
            carry = jnp.where(counts, further, carry)
        return carry

    def drain(self):
        for d in range(1, 8):
            self.copy(d).wait_send()


def named(keys, refs):
    return SimpleNamespace(**dict(zip(keys, refs)))


HBM = pl.BlockSpec(memory_space=pl.ANY)
VMEM = pl.BlockSpec(memory_space=pltpu.VMEM)


KINDS = (0, 1, 0, 0, 2, 1, 0)
FETCHES = (
    (
        ((0, 1), (0, 0),),
        ((0, 2),),
        ((1, 1), (2, 1), (1, 0), (2, 0), (1, 2), (2, 2), (3, 1), (4, 1), (0, 5), (0, 4), (3, 0), (4, 0), (3, 2), (4, 2),),
        (),
        (),
        (),
        ((0, 3),),
        ((1, 5), (2, 5),),
        (),
        ((1, 4),),
        ((1, 3), (2, 3),),
        (),
        ((3, 5), (4, 5),),
        ((3, 3), (4, 3), (0, 6),),
        ((2, 4),),
        (),
        ((3, 4),),
        (),
        (),
        ((4, 4), (1, 6), (2, 6),),
        (),
        (),
        (),
        (),
        ((3, 6), (4, 6),),
        (),
        (),
        (),
        (),
        (),
        (),
        (),
        (),
    ),
    (
        ((0, 0), (0, 2), (0, 1),),
        (),
        ((1, 0), (2, 0), (1, 2), (2, 2), (0, 4), (0, 5), (3, 0), (4, 0), (3, 2), (4, 2), (1, 1),),
        (),
        ((2, 1), (0, 3), (3, 1), (1, 4), (2, 4), (4, 1),),
        ((1, 3), (2, 3),),
        (),
        (),
        ((3, 4), (4, 4),),
        ((3, 3), (4, 3), (0, 6),),
        (),
        (),
        ((1, 5),),
        (),
        (),
        ((1, 6), (2, 6),),
        (),
        (),
        ((2, 5),),
        ((3, 6), (4, 6),),
        (),
        (),
        ((3, 5),),
        (),
        (),
        ((4, 5),),
        (),
        (),
        (),
        (),
        (),
        (),
        (),
    ),
)


def forward_call(tokens, small_own, shards):
    rows, width = tokens.shape
    lru = shards[0].shape[1]
    ff = shards[4].shape[1]
    tiles = lru // LANES
    kinds = KINDS
    count = len(shards)
    f32, bf = jnp.float32, jnp.bfloat16
    shape = jax.ShapeDtypeStruct
    wholes = [shape((8 * s.shape[0], s.shape[1]), s.dtype) for s in shards]
    saved = dict(
        hidden=shape((rows, ff), bf),
        small=shape((16, lru), f32),
        n1t=shape((width, rows), bf),
        pre=shape((tiles, rows, LANES), f32),
        lin=shape((tiles, rows + 8, LANES), f32),
        convt=shape((tiles, LANES, rows), bf),
        decay=shape((tiles, rows, LANES), f32),
        k2=shape((tiles, rows, LANES), f32),
        k3=shape((tiles, rows, LANES), f32),
        k6=shape((tiles, rows, LANES), f32),
        k7=shape((tiles, rows, LANES), f32),
        slope=shape((tiles, rows, LANES), f32),
        rect=shape((lru, rows), bf),
        resid=shape((rows, width), f32),
        n2t=shape((width, rows), bf),
        mg=shape((rows, ff), f32),
        bend=shape((rows, ff), f32),
        mv=shape((rows, ff), f32),
        hidt=shape((ff, rows), bf),
    )
    names = list(saved)
    scratch = dict(
        x=pltpu.VMEM((rows, width), bf),
        n1=pltpu.VMEM((rows, width), bf),
        n1t=pltpu.VMEM((width, rows), bf),
        parts=pltpu.VMEM((8,) + small_own.shape, f32),
        into=pltpu.VMEM((8 * tiles, LANES), f32),
        small=pltpu.VMEM((16, lru), f32),
        pre=pltpu.VMEM((tiles, rows, LANES), f32),
        lin=pltpu.VMEM((tiles, rows + 8, LANES), f32),
        convt=pltpu.VMEM((tiles, LANES, rows), bf),
        decay=pltpu.VMEM((tiles, rows, LANES), f32),
        k2=pltpu.VMEM((tiles, rows, LANES), f32),
        k3=pltpu.VMEM((tiles, rows, LANES), f32),
        k6=pltpu.VMEM((tiles, rows, LANES), f32),
        k7=pltpu.VMEM((tiles, rows, LANES), f32),
        prod=pltpu.VMEM((tiles, rows, LANES), f32),
        total=pltpu.VMEM((tiles, rows, LANES), f32),
        rec=pltpu.VMEM((rows, lru), bf),
        rect=pltpu.VMEM((lru, rows), bf),
        resid=pltpu.VMEM((rows, width), f32),
        n2=pltpu.VMEM((rows, width), bf),
        n2t=pltpu.VMEM((width, rows), bf),
        hidden=pltpu.VMEM((rows, ff), bf),
        ends=pltpu.VMEM((8, 2, tiles, LANES), f32),
        gsend=pltpu.SemaphoreType.DMA((count, len(SENT))),
        grecv=pltpu.SemaphoreType.DMA((count, len(GOT))),
        gown=pltpu.SemaphoreType.DMA((count, 2)),
        esend=pltpu.SemaphoreType.DMA((7,)),
        erecv=pltpu.SemaphoreType.DMA((7,)),
        ssend=pltpu.SemaphoreType.DMA((7,)),
        srecv=pltpu.SemaphoreType.DMA((7,)),
        hsend=pltpu.SemaphoreType.DMA(()),
        hrecv=pltpu.SemaphoreType.DMA(()),
        load=pltpu.SemaphoreType.DMA((2,)),
        keep=pltpu.SemaphoreType.DMA((len(names),)),
    )
    keys = list(scratch)
    R = 128

    def kernel(tokens_ref, small_ref, *refs):
        ins, outs = refs[:count], refs[count : 2 * count]
        out = named(names, refs[2 * count : 2 * count + len(names)])
        bounce = refs[-count:]
        v = named(keys, refs[2 * count + len(names) : -count])
        gelu_w, input_w, gates_w, output_w, mgate_w, mvalue_w, mdown_w = outs
        place = Place()
        gather = Gather(place, ins, outs, kinds, v.gsend, v.grecv, v.gown, bounce)
        ends = Ends(place, v.ends, (v.esend, v.erecv), False)
        packs = Ends(place, v.parts, (v.ssend, v.srecv), False)
        z, seq = place.z, place.seq
        loads = [
            pltpu.make_async_copy(tokens_ref, v.x, v.load.at[0]),
            pltpu.make_async_copy(small_ref, v.parts.at[seq], v.load.at[1]),
        ]
        greet([(z, (seq + d) % 8) for d in range(1, 8)] + [gather.znb])
        for cp in loads:
            cp.start()
        kept = []

        def keep(src, dst):
            cp = pltpu.make_async_copy(src, dst, v.keep.at[len(kept)])
            cp.start()
            kept.append(cp)

        def by_level(act):
            for odd in range(2):
                pl.when(z % 2 == odd)(lambda odd=odd: act(odd))

        turn_of = [0]

        def serve(spot):
            def act(odd):
                for step, i in FETCHES[odd][spot]:
                    if step == 0:
                        gather.start(i, odd)
                    else:
                        gather.relay(i, OVER_LINKS[step - 1], odd)

            if FETCHES[0][spot] or FETCHES[1][spot]:
                by_level(act)

        def pump():
            serve(turn_of[0])
            turn_of[0] += 1

        def pumps_at(*places):
            spots = list(enumerate(places, turn_of[0]))
            turn_of[0] += len(spots)

            def at_place(here):
                for spot, there in spots:
                    if FETCHES[0][spot] or FETCHES[1][spot]:
                        pl.when(here == there)(lambda spot=spot: serve(spot))

            return at_place

        loads[1].wait()
        met(8)
        packs.share()
        pump()
        packs.shared()
        small = v.small
        lane = lax.broadcasted_iota(jnp.int32, (8, LANES), 1)
        for k in range(4):
            left, right = v.parts[2 * k, 0:8, :], pltpu.roll(v.parts[2 * k + 1, 0:8, :], 64, axis=1)
            first = 3 * k * LANES
            small[0:8, first : first + LANES] = left[:, :LANES]
            small[0:8, first + LANES : first + 2 * LANES] = jnp.where(lane < 64, left[:, LANES:], right[:, :LANES])
            small[0:8, first + 2 * LANES : first + 3 * LANES] = right[:, LANES:]
        for k in range(8):
            small[8:16, k * LANES : (k + 1) * LANES] = v.parts[k, 8:16, :LANES]
        small[8:16, width:] = jnp.zeros((8, lru - width), f32)
        keep(v.small, out.small)
        loads[0].wait()

        def norm_one(at):
            x = wide(v.x[at, :])
            scale = lax.rsqrt(jnp.mean(x * x, axis=-1, keepdims=True) + epsilon)
            v.n1[at, :] = low(x * scale * small[8:9, :width])

        rows_loop(rows, norm_one, 64)
        pump()

        def turn(src, dst, at):
            dst[at, :] = src[:, at].T

        @pl.loop(0, width // 256)
        def _(k):
            turn(v.n1, v.n1t, pl.ds(pl.multiple_of(k * 256, 256), 256))

        keep(v.n1t, out.n1t)

        def project(weight, dst, first):
            inside = pumps_at(tiles // 4)

            def body(w):
                t = pl.program_id(0)
                inside(t)
                both = dot(v.n1[...], w[...])
                dst[2 * t, pl.ds(first, rows), :] = both[:, :LANES]
                dst[2 * t + 1, pl.ds(first, rows), :] = both[:, LANES:]

            pltpu.emit_pipeline(body, grid=(tiles // 2,), in_specs=[pl.BlockSpec((width, 2 * LANES), lambda t: (0, t))])(weight)

        pump()
        gather.arrive(0)
        project(gelu_w, v.pre, 0)
        pump()
        gather.arrive(1)
        project(input_w, v.lin, 8)

        def halo():
            return pltpu.make_async_remote_copy(
                src_ref=v.lin.at[:, pl.ds(rows, 8)], dst_ref=v.lin.at[:, pl.ds(0, 8)], send_sem=v.hsend, recv_sem=v.hrecv,
                device_id=(z, (seq + 1) % 8), device_id_type=MESH,
            )

        @pl.when(seq < 7)
        def _():
            halo().start()

        pump()
        gather.arrive(2)

        @pl.when(seq == 0)
        def _():
            v.lin[:, 0:8, :] = jnp.zeros((tiles, 8, LANES), f32)

        @pl.when(seq > 0)
        def _():
            halo().wait_recv()

        keep(v.lin, out.lin)

        gates_inside = pumps_at(tiles // 3, 2 * tiles // 3)

        def gates(w):
            h = pl.program_id(0)
            gates_inside(h)
            lane = pl.ds(pl.multiple_of(h * LANES, LANES), LANES)
            taps = [small[k : k + 1, lane] for k in range(4)]
            cb, rb, ib, dp = [small[k : k + 1, lane] for k in range(4, 8)]
            rate = -cfactor * softplus_minus(dp)
            for r in range(0, rows, R):
                acc = cb + taps[0] * v.lin[h, 8 + r : 8 + r + R, :]
                for k in range(1, 4):
                    acc = acc + taps[k] * v.lin[h, 8 + r - k : 8 + r - k + R, :]
                cl = low(acc)
                v.convt[h, :, r : r + R] = cl.T
                both = dot(cl, w[...])
                rg = sigmoid(both[:, :LANES] + rb)
                ig = sigmoid(both[:, LANES:] + ib)
                log_decay = rate * rg
                decay = jnp.exp(log_decay)
                mult = jnp.sqrt(minus_expm1(2.0 * log_decay, log_decay))
                cv = wide(cl)
                through = mult * ig
                at = slice(r, r + R)
                v.prod[h, at, :] = decay
                v.decay[h, at, :] = decay
                v.total[h, at, :] = through * cv
                v.k3[h, at, :] = through
                v.k2[h, at, :] = through * cv * (1.0 - ig)
                v.k6[h, at, :] = ig * cv * (decay * decay) / mult
                v.k7[h, at, :] = rg

        pltpu.emit_pipeline(gates, grid=(tiles,), in_specs=[pl.BlockSpec((LANES, 2 * LANES), lambda h: (h, 0))])(gates_w)
        for src, dst in ((v.convt, out.convt), (v.decay, out.decay), (v.k2, out.k2), (v.k3, out.k3)):
            keep(src, dst)
        pump()
        tails = strided_scan(v.prod, v.total, v.prod, v.total, False, rows, pump)
        before, whole = segment_ends(tails, False)
        ends.tell(whole)
        pump()
        carry = ends.joined()
        span = rows // 8
        for c in range(tiles):
            into = before[c][0] * carry[c : c + 1, :] + before[c][1]
            v.into[8 * c : 8 * c + 8, :] = into

        pump()
        state_inside = pumps_at(tiles // 3, 2 * tiles // 3)

        @pl.loop(0, tiles)
        def _(c):
            state_inside(c)
            lane = pl.ds(pl.multiple_of(c * LANES, LANES), LANES)
            into = v.into[pl.ds(pl.multiple_of(c * 8, 8), 8), :]
            rate = -cfactor * softplus_minus(small[7:8, lane])
            first = lax.broadcasted_iota(jnp.int32, (span, LANES), 0) == 0
            for s in range(8):
                at = slice(s * span, (s + 1) * span)
                state = v.total[c, at, :] + v.prod[c, at, :] * into[s : s + 1, :]
                before_it = jnp.where(first, into[s : s + 1, :], pltpu.roll(state, 1, axis=0))
                rg = v.k7[c, at, :]
                k7 = (before_it * v.decay[c, at, :] - v.k6[c, at, :]) * rg
                v.k7[c, at, :] = k7
                v.k6[c, at, :] = k7 * rate * (1.0 - rg)
                value, slope = gelu_parts(v.pre[c, at, :])
                v.rec[at, lane] = low(state * value)
                v.pre[c, at, :] = value
                v.total[c, at, :] = state * slope
            v.rect[lane, :] = v.rec[:, lane].T

        for src, dst in ((v.k6, out.k6), (v.k7, out.k7), (v.pre, out.pre), (v.total, out.slope)):
            keep(src, dst)
        keep(v.rect, out.rect)
        pump()
        gather.arrive(3)
        width_inside = pumps_at(width // 512)

        def back_to_width(w):
            t = pl.program_id(0)
            width_inside(t)
            at = pl.ds(pl.multiple_of(t * 256, 256), 256)
            v.resid[:, at] = wide(v.x[:, at]) + dot(v.rec[...], w[...])

        pltpu.emit_pipeline(back_to_width, grid=(width // 256,), in_specs=[pl.BlockSpec((lru, 256), lambda t: (0, t))])(output_w)
        keep(v.resid, out.resid)
        pump()
        def norm_two(at):
            x = v.resid[at, :]
            scale = lax.rsqrt(jnp.mean(x * x, axis=-1, keepdims=True) + epsilon)
            v.n2[at, :] = low(x * scale * small[9:10, :width])

        rows_loop(rows, norm_two, 64)
        pump()

        @pl.loop(0, width // 256)
        def _(k):
            turn(v.n2, v.n2t, pl.ds(pl.multiple_of(k * 256, 256), 256))

        keep(v.n2t, out.n2t)
        steps = ff // 256
        sixths = [k * steps // 6 for k in range(1, 6)]
        across = pl.BlockSpec((rows, 256), lambda t: (0, t))
        columns = pl.BlockSpec((width, 256), lambda t: (0, t))
        pump()
        gather.arrive(4)
        gate_inside = pumps_at(*sixths)

        def mlp_gate(wg, value, slope):
            gate_inside(pl.program_id(0))
            value[...] = dot(v.n2[...], wg[...])

            def act(rs):
                value[rs, :], slope[rs, :] = gelu_parts(value[rs, :])

            rows_loop(rows, act, 64)

        pltpu.emit_pipeline(mlp_gate, grid=(steps,), in_specs=[columns], out_specs=[across, across])(mgate_w, out.mg, out.bend)
        pump()
        gather.arrive(5)
        value_inside = pumps_at(*sixths)

        def mlp_value(wv, value, slope, mv, hidt):
            t = pl.program_id(0)
            value_inside(t)
            at = pl.ds(pl.multiple_of(t * 256, 256), 256)
            linear = dot(v.n2[...], wv[...])
            mv[...] = linear * slope[...]
            hidden = low(linear * value[...])
            v.hidden[:, at] = hidden
            hidt[...] = hidden.T

        pltpu.emit_pipeline(
            mlp_value,
            grid=(steps,),
            in_specs=[columns, across, across],
            out_specs=[across, pl.BlockSpec((256, rows), lambda t: (t, 0))],
        )(mvalue_w, out.mg, out.bend, out.mv, out.hidt)
        pump()
        gather.arrive(6)
        keep(v.hidden, out.hidden)
        for cp in kept:
            cp.wait()
        pump()

        def drain(odd):
            for i in range(count):
                gather.drain(i, odd)

        by_level(drain)
        ends.drain()
        packs.drain()

        @pl.when(seq < 7)
        def _():
            halo().wait_send()

    result = pl.pallas_call(
        kernel,
        out_shape=wholes + [saved[name] for name in names],
        in_specs=[HBM] * (2 + count),
        out_specs=[HBM] * (count + len(names)),
        scratch_shapes=[scratch[key] for key in keys] + [pltpu.VMEM(s.shape, s.dtype) for s in shards],
        compiler_params=pltpu.CompilerParams(collective_id=1, has_side_effects=True, vmem_limit_bytes=60 << 20),
        name="forward",
    )(tokens, small_own, *shards)
    return result[:count], named(names, result[count:])

def slot_scratch(n, h):
    bf = jnp.bfloat16
    return dict(
        ab=pltpu.VMEM((2, 4, n, h), bf),
        fr=pltpu.VMEM((2, 2, n, h), bf),
        se=pltpu.VMEM((2, n, h), bf),
        zo=pltpu.VMEM((2, n, h), bf),
        zp=pltpu.VMEM((n, h), bf),
        res=pltpu.VMEM((2, n, h), bf),
    )


PUMPS = (
    (),
    (),
    (),
    (),
    ((6, 0, 0),),
    ((6, 0, 1),),
    (),
    (),
    (),
    (),
    ((6, 1, 0),),
    ((6, 1, 1),),
    (),
    ((0, 0, 0), (0, 0, 1),),
    (),
    (),
    (),
    (),
    ((0, 1, 0), (0, 1, 1),),
    ((6, 2, 0),),
    ((6, 2, 1),),
    ((1, 0, 1), (6, 4, 0),),
    ((1, 0, 0), (6, 4, 1),),
    (),
    (),
    (),
    ((1, 1, 1),),
    ((2, 0, 1), (1, 1, 0),),
    ((2, 0, 0),),
    ((6, 3, 0),),
    ((0, 2, 0), (6, 3, 1), (3, 0, 1), (0, 2, 1), (2, 1, 1),),
    (),
    (),
    ((2, 1, 0), (3, 0, 0),),
    ((4, 0, 1), (6, 5, 0), (6, 5, 1), (0, 4, 0), (0, 4, 1), (3, 1, 1),),
    ((4, 0, 0), (1, 2, 0), (3, 1, 0),),
    ((4, 1, 1), (0, 3, 0),),
    (),
    ((2, 2, 0), (4, 1, 0), (1, 2, 1), (0, 3, 1),),
    (),
    ((3, 2, 0), (2, 2, 1),),
    ((0, 5, 0), (0, 5, 1),),
    (),
    ((4, 2, 0), (1, 4, 1), (1, 4, 0),),
    ((1, 3, 1), (6, 6, 0), (6, 6, 1), (1, 3, 0), (3, 2, 1), (2, 4, 1),),
    ((2, 4, 0), (1, 5, 1), (1, 5, 0), (4, 2, 1), (3, 4, 1),),
    (),
    (),
    ((2, 3, 1), (0, 6, 0), (0, 6, 1), (3, 4, 0), (2, 3, 0),),
    ((4, 4, 1),),
    ((2, 5, 1), (1, 6, 0), (1, 6, 1), (3, 3, 1),),
    ((4, 4, 0), (2, 5, 0), (3, 3, 0),),
    ((6, 7, 0),),
    ((6, 7, 1),),
    ((4, 3, 1), (3, 5, 1), (2, 6, 0),),
    (),
    ((4, 3, 0), (2, 6, 1), (3, 5, 0),),
    ((4, 5, 1), (0, 7, 0), (0, 7, 1),),
    ((6, 10, 0), (6, 10, 1),),
    ((3, 6, 1),),
    ((3, 6, 0),),
    (),
    (),
    ((1, 7, 0), (6, 8, 0), (4, 5, 0), (1, 7, 1), (0, 10, 1),),
    ((0, 10, 0), (6, 8, 1),),
    ((4, 6, 1), (6, 9, 0),),
    ((6, 9, 1),),
    ((4, 6, 0), (1, 10, 0),),
    ((2, 7, 0),),
    ((1, 10, 1), (0, 8, 0),),
    ((2, 7, 1), (2, 10, 0), (0, 8, 1), (2, 10, 1), (0, 9, 0),),
    ((0, 9, 1), (3, 7, 0), (3, 10, 0),),
    ((1, 8, 0), (1, 8, 1), (3, 7, 1), (1, 9, 0), (1, 9, 1), (3, 10, 1),),
    (),
    ((4, 7, 0), (2, 8, 0), (4, 10, 0),),
    ((4, 7, 1), (4, 10, 1), (2, 8, 1), (2, 9, 0),),
    ((2, 9, 1), (3, 8, 0), (3, 9, 0), (3, 8, 1), (3, 9, 1), (4, 8, 0), (4, 8, 1), (4, 9, 0), (4, 9, 1), (5, 0, 0), (5, 0, 1), (5, 1, 0), (5, 1, 1), (5, 2, 0), (5, 2, 1), (5, 4, 0), (5, 4, 1), (5, 3, 0), (5, 3, 1), (5, 5, 0), (5, 5, 1), (5, 6, 0), (5, 6, 1), (5, 7, 0), (5, 10, 0), (5, 7, 1), (5, 10, 1), (5, 8, 0), (5, 9, 0), (5, 8, 1), (5, 9, 1),),
)


def backward_call(lengths, tokens, cotangent, weights, saved):
    rows, width = tokens.shape
    gelu_full, input_full, gates_full, output_full, mgate_full, mvalue_full, mdown_full = weights
    lru, ff = gelu_full.shape[1], mgate_full.shape[1]
    tiles = lru // LANES
    wide_tile = 2 * LANES
    f32, bf = jnp.float32, jnp.bfloat16
    shape = jax.ShapeDtypeStruct
    full = [mdown_full, mgate_full, mvalue_full, output_full, gelu_full, input_full, gates_full]
    cut = lambda k, *shares: [(k, full[k].shape[1] * a // 6, full[k].shape[1] * (b - a) // 6) for a, b in zip((0,) + shares, shares + (6,))]
    pieces = cut(0, 3) + cut(1, 3) + cut(2, 3) + cut(3) + cut(4) + cut(5, 4) + cut(6)
    DOWN, DOWN2, MGATE, MGATE2, MVALUE, MVALUE2, OUTPUT, GELU, INPUT, INPUT2, GATES = range(11)
    extents = [(full[k].shape[0] // 8, columns // 2) for k, _, columns in pieces]
    count = len(pieces)
    split = lambda v: v.reshape(4, 2, v.shape[0] // 8, v.shape[1])
    inputs = dict(
        tokens=tokens, cot=cotangent, gelu_w=gelu_full, input_w=input_full, gates_w=gates_full, output_w=output_full, mgate_w=mgate_full,
        mvalue_w=mvalue_full, mdown_w=mdown_full, small=saved.small, n1t=split(saved.n1t), pre=saved.pre, lin=saved.lin,
        convt=saved.convt, decay=saved.decay, k6=saved.k6, k2=saved.k2, k3=saved.k3, k7=saved.k7, slope=saved.slope,
        rect=split(saved.rect), resid=saved.resid, n2t=split(saved.n2t), mg=saved.mg, mv=saved.mv, hidt=split(saved.hidt), hidden=saved.hidden,
    )
    slot_keys = list(slot_scratch(8, 128))
    most = max(4 * n * h // wide_tile for n, h in extents)
    passes, depth = 2 * count - 1, 4
    scratch = dict(
        go=pltpu.VMEM((rows, width), bf),
        gm=pltpu.VMEM((rows, width), bf),
        gn=pltpu.VMEM((rows, width), f32),
        n1t=pltpu.VMEM((4, 2, width // 8, rows), bf),
        n2t=pltpu.VMEM((4, 2, width // 8, rows), bf),
        rect=pltpu.VMEM((4, 2, lru // 8, rows), bf),
        small=pltpu.VMEM((16, lru), f32),
        part=pltpu.VMEM((16, lru), f32),
        own=pltpu.VMEM((16, wide_tile), f32),
        gain=pltpu.VMEM((8, width), f32),
        into=pltpu.VMEM((tiles, 8, LANES), f32),
        halo=pltpu.VMEM((tiles, 8, LANES), f32),
        edge=pltpu.VMEM((tiles, 8, LANES), f32),
        stage=pltpu.VMEM((depth, most, wide_tile), bf),
        landed=pltpu.VMEM((depth, most, wide_tile), bf),
        gstage=pltpu.VMEM((4, 2, lru // 8, wide_tile), bf),
        ends=pltpu.VMEM((8, 2, tiles, LANES), f32),
        sslots=pltpu.VMEM((2, 5, 16, lru), f32),
        psend=pltpu.SemaphoreType.DMA((passes,)),
        precv=pltpu.SemaphoreType.DMA((passes,)),
        rsend=pltpu.SemaphoreType.DMA((count, 14)),
        rrecv=pltpu.SemaphoreType.DMA((count, 14)),
        esend=pltpu.SemaphoreType.DMA((7,)),
        erecv=pltpu.SemaphoreType.DMA((7,)),
        hsend=pltpu.SemaphoreType.DMA(()),
        hrecv=pltpu.SemaphoreType.DMA(()),
        ssend=pltpu.SemaphoreType.DMA((5,)),
        srecv=pltpu.SemaphoreType.DMA((5,)),
        load=pltpu.SemaphoreType.DMA((8,)),
        keep=pltpu.SemaphoreType.DMA((count + 2, 2)),
        credit=pltpu.SemaphoreType.REGULAR,
    )
    keys = list(scratch)
    outs = dict(mixed=shape((rows, width), bf), tokens_grad=shape((rows, width), f32), small_sum=shape((16, wide_tile), f32))
    out_keys = list(outs)
    sums = [shape((w.shape[0] // 8, w.shape[1]), bf) for w in full]

    def kernel(lengths_ref, *refs):
        refs = list(refs)

        def take(k):
            got = refs[:k]
            del refs[:k]
            return got

        w = named(inputs, take(len(inputs)))
        out = named(out_keys, take(len(out_keys)))
        sum_refs = take(len(full))
        v = named(keys, take(len(keys)))
        slots = []
        for (k, first, _), (n, h) in zip(pieces, extents):
            s = named(slot_keys, take(len(slot_keys)))
            s.n, s.h, s.tiles, s.first, s.sum = n, h, h // wide_tile, first, sum_refs[k]
            slots.append(s)
        place = Place()
        z, seq, core = place.z, place.seq, place.core
        red = Reduce(place, slots, (v.rsend, v.rrecv))
        ends = Ends(place, v.ends, (v.esend, v.erecv), True)
        tot = Small(place, v.part, v.sslots, (v.ssend, v.srecv))
        small, part = v.small, v.part
        kept = []

        def load(src, dst, k):
            cp = pltpu.make_async_copy(src, dst, v.load.at[k])
            cp.start()
            return cp

        greet([(z, (seq + d) % 8) for d in range(1, 8)] + [((z + d) % 4, seq) for d in range(1, 4)])
        first_loads = [load(w.cot, v.go, 0)]
        loads = [load(w.small, v.small, 1), load(w.n2t, v.n2t, 2), load(w.rect, v.rect, 3), load(w.n1t, v.n1t, 4)]

        def arrived(i, h):
            red.arrive(i, h)
            cp = totalled(i, h)

            @pl.when(red.outer)
            def _():
                cp.start()

        def totalled(i, h):
            s = slots[i]
            return pltpu.make_async_copy(s.res.at[h], s.sum.at[:, pl.ds(s.first + h * s.h, s.h)], v.keep.at[i, h])

        def add_peer(i, h):
            red.add_peer(i, h)
            cp = totalled(i, h)

            @pl.when(red.makes(h))
            def _():
                cp.start()

        def pass_on(i, h):
            red.pass_on(i, h)
            cp = totalled(i, h)

            @pl.when(red.helps(h))
            def _():
                cp.start()

        steps = (red.add_first, red.add_second, red.add_outer, add_peer, pass_on, arrived, red.start_first)
        turn = [0]

        def serve(spot):
            for step, i, h in PUMPS[spot]:
                steps[step](i, h)

        def pump():
            serve(turn[0])
            turn[0] += 1

        def pumps_at(*grid_steps):
            spots = list(enumerate(grid_steps, turn[0]))
            turn[0] += len(spots)

            def at_step():
                for spot, grid_step in spots:
                    if PUMPS[spot]:
                        pl.when(pl.program_id(0) == grid_step)(lambda spot=spot: serve(spot))

            return at_step

        sent = []
        pass_of = {}

        def to_sib(k):
            return pltpu.make_async_remote_copy(
                src_ref=v.stage.at[k % depth, pl.ds(0, sent[k])], dst_ref=v.landed.at[k % depth, pl.ds(0, sent[k])],
                send_sem=v.psend.at[k], recv_sem=v.precv.at[k], device_id=place.sib, device_id_type=MESH,
            )

        def next_pass():
            k = len(sent)
            if k >= depth:
                to_sib(k - depth).wait_send()
            return k

        def send_blocks(used):
            k = len(sent)
            sent.append(used)
            if k == 0:
                met(10)
            if k >= depth:
                pl.semaphore_wait(v.credit, 1)
            to_sib(k).start()

        def give_credit(k):
            if k + depth < passes:
                pl.semaphore_signal(v.credit, inc=1, device_id=place.sib, device_id_type=MESH)

        def blocks(s):
            group = max(1, 512 // s.n)
            return [(j, group) for j in range(0, 4, group)]

        def right_tile(s, h, right, t):
            return right[:, pl.ds(pl.multiple_of(s.first + h * s.h + t * wide_tile, wide_tile), wide_tile)]

        def for_sib(i, left, right):
            s = slots[i]
            for h in range(2):
                pump()
                k = next_pass()
                pass_of[i, h] = k

                @pl.loop(0, s.tiles)
                def _(t, h=h, k=k):
                    r = right_tile(s, h, right, t)
                    for j, group in blocks(s):
                        value = dot(left[j : j + group, 1 - core].reshape(group * s.n, rows), r)
                        at = pl.ds(pl.multiple_of(t * 4 * s.n + j * s.n, s.n), group * s.n)
                        v.stage[k % depth, at, :] = low(value)

                send_blocks(4 * s.n * s.tiles)

        def for_us(i, left, right):
            s = slots[i]
            for h in range(2):
                pump()
                k = pass_of[i, h]
                to_sib(k).wait_recv()

                @pl.loop(0, s.tiles)
                def _(t, h=h, k=k):
                    r = right_tile(s, h, right, t)
                    for j, group in blocks(s):
                        value = dot(left[j : j + group, core].reshape(group * s.n, rows), r)
                        at = pl.ds(pl.multiple_of(t * 4 * s.n + j * s.n, s.n), group * s.n)
                        both = low(value + wide(v.landed[k % depth, at, :]))
                        lane = pl.ds(pl.multiple_of(t * wide_tile, wide_tile), wide_tile)
                        s.ab[h, j : j + group, :, lane] = both.reshape(group, s.n, wide_tile)

                give_credit(k)

        def eight(value):
            return value.reshape(value.shape[0] // 8, 8, value.shape[1]).sum(axis=0)

        def norm_back(x, grad, gain, add):
            scale = lax.rsqrt(jnp.mean(x * x, axis=-1, keepdims=True) + epsilon)
            v.gain[...] += eight(grad * x * scale)
            scaled = grad * gain
            m = jnp.mean(scaled * x, axis=-1, keepdims=True)
            return add + scale * (scaled - x * (scale * scale * m))

        def mlp_steps(gmg, gmv, first, count_of, *inner):
            pump()
            inside = pumps_at(*inner)

            def body(md, value, slope):
                inside()
                at = pl.ds(pl.multiple_of((pl.program_id(0) + first) * wide_tile, wide_tile), wide_tile)
                gh = dot_t(v.go[...], md[...])
                gmg[:, at] = low(gh * slope[...])
                gmv[:, at] = low(gh * value[...])

            across = pl.BlockSpec((rows, wide_tile), lambda t: (0, t + first))
            pltpu.emit_pipeline(
                body, grid=(count_of,), in_specs=[pl.BlockSpec((wide_tile, width), lambda t: (t + first, 0)), across, across]
            )(w.mdown_w, w.mg, w.mv)

        def mlp_norm_half(gmg, gmv, half):
            pump()

            inside = pumps_at(1)

            def body(wg, wv):
                inside()
                t = pl.program_id(0) + 2 * half
                at = pl.ds(pl.multiple_of(t * wide_tile, wide_tile), wide_tile)
                v.gn[:, at] = dot_t(gmg[...], wg[...]) + dot_t(gmv[...], wv[...])

            pltpu.emit_pipeline(body, grid=(2,), in_specs=[pl.BlockSpec((wide_tile, ff), lambda t: (t + 2 * half, 0))] * 2)(
                w.mgate_w, w.mvalue_w
            )

        valid_rows = lengths_ref[z] - seq * rows
        third = ff // wide_tile // 6

        def mlp_phase(gmg, gmv):
            def head(hidt):
                down_loads = load(w.hidt, hidt, 5)
                first_loads[0].wait()

                def mask(at):
                    here = lax.broadcasted_iota(jnp.int32, (64, width), 0) + at.start < valid_rows
                    v.go[at, :] = low(jnp.where(here, wide(v.go[at, :]), 0.0))

                rows_loop(rows, mask, 64)
                part[...] = jnp.zeros_like(part)
                down_loads.wait()
                for_sib(DOWN, hidt, v.go)
                mlp_steps(gmg, gmv, 0, third)
                for_us(DOWN, hidt, v.go)
                for_sib(DOWN2, hidt, v.go)
                mlp_steps(gmg, gmv, third, 2 * third, third)
                for_us(DOWN2, hidt, v.go)

            pl.run_scoped(head, pltpu.VMEM((4, 2, ff // 8, rows), bf))
            for cp in loads:
                cp.wait()
            for_sib(MGATE, v.n2t, gmg)
            for_sib(MVALUE, v.n2t, gmv)
            mlp_steps(gmg, gmv, 3 * third, 3 * third, third, 2 * third)
            for_us(MGATE, v.n2t, gmg)
            for_us(MVALUE, v.n2t, gmv)
            for_sib(MGATE2, v.n2t, gmg)
            for_sib(MVALUE2, v.n2t, gmv)
            mlp_norm_half(gmg, gmv, 0)
            for_us(MGATE2, v.n2t, gmg)
            for_us(MVALUE2, v.n2t, gmv)
            mlp_norm_half(gmg, gmv, 1)

        pl.run_scoped(mlp_phase, pltpu.VMEM((rows, ff), bf), pltpu.VMEM((rows, ff), bf))
        pump()
        v.gain[...] = jnp.zeros_like(v.gain)

        inside = pumps_at(rows // 128)

        def norm_two(resid, inside=inside):
            inside()
            at = pl.ds(pl.multiple_of(pl.program_id(0) * 64, 64), 64)
            value = norm_back(resid[...], v.gn[at, :], small[9:10, :width], wide(v.go[at, :]))
            v.gn[at, :] = value
            v.gm[at, :] = low(value)

        pltpu.emit_pipeline(norm_two, grid=(rows // 64,), in_specs=[pl.BlockSpec((64, width), lambda t: (t, 0))])(w.resid)
        part[9:10, :width] = v.gain[...].sum(axis=0, keepdims=True)
        tokens_load = load(w.tokens, v.go, 6)

        def branch_phase(adj, prod, gg, gl, gri):
            decay_load = load(w.decay, prod, 7)
            for_sib(OUTPUT, v.rect, v.gm)
            pump()

            inside = pumps_at(tiles // 6, tiles // 3)

            def into_branch(wo, value, slope, inside=inside):
                inside()
                t = pl.program_id(0)
                gr = dot_t(v.gm[...], wo[...])
                for q in range(2):
                    c = 2 * t + q
                    grad = gr[:, q * LANES : (q + 1) * LANES]
                    adj[c, pl.ds(0, rows), :] = grad * value[q]
                    gg[:, pl.ds(pl.multiple_of(c * LANES, LANES), LANES)] = low(grad * slope[q])

            pair = pl.BlockSpec((2, rows, LANES), lambda t: (t, 0, 0))
            pltpu.emit_pipeline(
                into_branch, grid=(tiles // 2,), in_specs=[pl.BlockSpec((wide_tile, width), lambda t: (t, 0)), pair, pair]
            )(w.output_w, w.pre, w.slope)
            for_us(OUTPUT, v.rect, v.gm)
            pump()
            decay_load.wait()
            tails = strided_scan(prod, adj, prod, adj, True, rows, pump)
            before, whole = segment_ends(tails, True)
            ends.tell(whole)
            for c in range(tiles):
                v.into[c] = before[c][1]
                v.edge[c] = before[c][0]
            for_sib(GELU, v.n1t, gg)
            pump()
            carry = ends.joined()
            for c in range(tiles):
                v.into[c] = v.into[c] + v.edge[c] * carry[c : c + 1, :]
            span = rows // 8

            inside = pumps_at(tiles // 4, tiles // 2, 3 * tiles // 4)

            def through_gates(k6, k2, k3, k7, convt, wg, inside=inside):
                inside()
                c = pl.program_id(0)
                lane = pl.ds(pl.multiple_of(c * LANES, LANES), LANES)
                sums = [jnp.zeros((8, LANES), f32) for _ in range(3)]
                for k in range(8):
                    at = slice(k * span, (k + 1) * span)
                    here = adj[c, at, :] + prod[c, at, :] * v.into[c, k : k + 1, :]
                    grad_r = here * k6[at, :]
                    grad_i = here * k2[at, :]
                    adj[c, at, :] = here * k3[at, :]
                    gri[at, :LANES] = low(grad_r)
                    gri[at, LANES:] = low(grad_i)
                    for q, value in enumerate((here * k7[at, :], grad_r, grad_i)):
                        sums[q] = sums[q] + eight(value)
                part[7:8, lane] = sums[0].sum(axis=0, keepdims=True) * (cfactor * sigmoid(-small[7:8, lane]))
                part[5:6, lane] = sums[1].sum(axis=0, keepdims=True)
                part[6:7, lane] = sums[2].sum(axis=0, keepdims=True)
                product = low(dot(convt[...], gri[...]))
                for q in range(2):
                    unit = 2 * c + q
                    block = unit // 3
                    at = pl.ds(pl.multiple_of((unit % 3) * 64, 64), 64)
                    v.gstage[block // 2, block % 2, at, :] = product[64 * q : 64 * (q + 1), :]
                grad_conv = adj[c, pl.ds(0, rows), :] + dot_t(gri[...], wg[...])
                adj[c, pl.ds(0, rows), :] = grad_conv
                part[4:5, lane] = eight(grad_conv).sum(axis=0, keepdims=True)

            one = pl.BlockSpec((None, rows, LANES), lambda t: (t, 0, 0))
            pltpu.emit_pipeline(
                through_gates,
                grid=(tiles,),
                in_specs=[one] * 4
                + [pl.BlockSpec((None, LANES, rows), lambda t: (t, 0, 0)), pl.BlockSpec((LANES, wide_tile), lambda t: (t, 0))],
            )(w.k6, w.k2, w.k3, w.k7, w.convt, w.gates_w)

            def halo():
                return pltpu.make_async_remote_copy(
                    src_ref=v.edge, dst_ref=v.halo, send_sem=v.hsend, recv_sem=v.hrecv, device_id=(z, (seq + 7) % 8), device_id_type=MESH
                )

            v.edge[...] = adj[:, 0:8, :]

            @pl.when(seq > 0)
            def _():
                halo().start()

            for_us(GELU, v.n1t, gg)
            pump()
            s = slots[GATES]
            gates_pass = next_pass()
            for j in range(4):

                def copy_block(at, j=j):
                    v.stage[gates_pass % depth, pl.ds(pl.multiple_of(j * s.n + at.start, 16), 16), :] = v.gstage[j, 1 - core, at, :]

                rows_loop(s.n, copy_block)
            send_blocks(4 * s.n)
            pump()

            @pl.when(seq == 7)
            def _():
                adj[:, pl.ds(rows, 8), :] = jnp.zeros((tiles, 8, LANES), f32)

            @pl.when(seq < 7)
            def _():
                halo().wait_recv()
                adj[:, pl.ds(rows, 8), :] = v.halo[...]

            inside = pumps_at(tiles // 3, 2 * tiles // 3)

            def through_conv(lin, inside=inside):
                inside()
                c = pl.program_id(0)
                lane = pl.ds(pl.multiple_of(c * LANES, LANES), LANES)
                taps = [small[k : k + 1, lane] for k in range(4)]
                sums = [jnp.zeros((8, LANES), f32) for _ in range(4)]
                for r in range(0, rows, 128):
                    here = adj[c, r : r + 128, :]
                    acc = taps[0] * here
                    for k in range(4):
                        sums[k] = sums[k] + eight(here * lin[8 + r - k : 8 + r - k + 128, :])
                        if k:
                            acc = acc + taps[k] * adj[c, r + k : r + k + 128, :]
                    gl[r : r + 128, lane] = low(acc)
                for k in range(4):
                    part[k : k + 1, lane] = sums[k].sum(axis=0, keepdims=True)

            pltpu.emit_pipeline(
                through_conv, grid=(tiles,), in_specs=[pl.BlockSpec((None, rows + 8, LANES), lambda t: (t, 0, 0))]
            )(w.lin)
            pump()
            to_sib(gates_pass).wait_recv()
            for j in range(4):

                def fold(at, j=j):
                    came = v.landed[gates_pass % depth, pl.ds(pl.multiple_of(j * s.n + at.start, 16), 16), :]
                    both = low(wide(v.gstage[j, core, at, :]) + wide(came))
                    s.ab[0, j, at, :] = both[:, : s.h]
                    s.ab[1, j, at, :] = both[:, s.h :]

                rows_loop(s.n, fold)
            give_credit(gates_pass)
            for_sib(INPUT, v.n1t, gl)
            for_sib(INPUT2, v.n1t, gl)
            for_us(INPUT, v.n1t, gl)
            for_us(INPUT2, v.n1t, gl)
            pump()
            inside = pumps_at(*range(1, width // wide_tile))

            def into_norm(wi, wg, inside=inside):
                inside()
                t = pl.program_id(0)
                value = dot_t(gl[...], wi[...]) + dot_t(gg[...], wg[...])
                adj[2 * t, pl.ds(0, rows), :] = value[:, :LANES]
                adj[2 * t + 1, pl.ds(0, rows), :] = value[:, LANES:]

            pltpu.emit_pipeline(into_norm, grid=(width // wide_tile,), in_specs=[pl.BlockSpec((wide_tile, lru), lambda t: (t, 0))] * 2)(
                w.input_w, w.gelu_w
            )
            pump()
            v.gain[...] = jnp.zeros_like(v.gain)
            tokens_load.wait()

            def norm_one(at):
                grad = jnp.concatenate([adj[c, at, :] for c in range(width // LANES)], axis=1)
                v.gn[at, :] = norm_back(wide(v.go[at, :]), grad, small[8:9, :width], v.gn[at, :])

            rows_loop(rows // 2, norm_one, 64)
            pump()
            rows_loop(rows, norm_one, 64, rows // 2)
            part[8:9, :width] = v.gain[...].sum(axis=0, keepdims=True)

        pl.run_scoped(
            branch_phase,
            pltpu.VMEM((tiles, rows + 8, LANES), f32),
            pltpu.VMEM((tiles, rows, LANES), f32),
            pltpu.VMEM((rows, lru), bf),
            pltpu.VMEM((rows, lru), bf),
            pltpu.VMEM((rows, wide_tile), bf),
        )
        tot.begin()
        cp = pltpu.make_async_copy(v.gn, out.tokens_grad, v.keep.at[count, 0])
        cp.start()
        kept.append(cp)

        def mixed_phase(hidden):
            hidden_load = load(w.hidden, hidden, 7)
            pump()
            inside = pumps_at(*range(1, width // wide_tile))
            hidden_load.wait()

            def body(wd, resid, mixed):
                inside()
                valid = lax.broadcasted_iota(jnp.int32, (rows, wide_tile), 0) < valid_rows
                mixed[...] = low(jnp.where(valid, resid[...] + dot(hidden[...], wd[...]), 0.0))

            across = pl.BlockSpec((rows, wide_tile), lambda t: (0, t))
            pltpu.emit_pipeline(
                body, grid=(width // wide_tile,), in_specs=[pl.BlockSpec((ff, wide_tile), lambda t: (0, t)), across], out_specs=[across]
            )(w.mdown_w, w.resid, out.mixed)

        pl.run_scoped(mixed_phase, pltpu.VMEM((rows, ff), bf))
        summed = 0
        for k, (step, i, h) in enumerate(PUMPS[turn[0]]):
            steps[step](i, h)
            if k % 4 == 3 and summed < 5:
                tot.step(summed)
                summed += 1
        for k in range(summed, 5):
            tot.step(k)
        v.own[0:8, :] = pltpu.roll(part[0:8, :], (8 - seq) % 8 * (lru // 8), axis=1)[:, :wide_tile]
        v.own[8:16, :] = pltpu.roll(part[8:16, :], (lru - seq * (width // 8)) % lru, axis=1)[:, :wide_tile]
        cp = pltpu.make_async_copy(v.own, out.small_sum, v.keep.at[count, 1])
        cp.start()
        kept.append(cp)
        for i in range(count):
            for h in range(2):
                kept.append(totalled(i, h))
        for cp in kept:
            cp.wait()
        for i in range(count):
            red.drain(i)
        for k in range(passes - depth, passes):
            to_sib(k).wait_send()
        tot.drain()
        ends.drain()

        @pl.when(seq > 0)
        def _():
            pltpu.make_async_remote_copy(
                src_ref=v.edge, dst_ref=v.halo, send_sem=v.hsend, recv_sem=v.hrecv, device_id=(z, (seq + 7) % 8), device_id_type=MESH
            ).wait_send()

    slot_list = [value for n, h in extents for value in slot_scratch(n, h).values()]
    result = pl.pallas_call(
        kernel,
        out_shape=list(outs.values()) + sums,
        in_specs=[pl.BlockSpec(memory_space=pltpu.SMEM)] + [HBM] * len(inputs),
        out_specs=[HBM] * (len(outs) + len(full)),
        scratch_shapes=list(scratch.values()) + slot_list,
        compiler_params=pltpu.CompilerParams(collective_id=2, has_side_effects=True, vmem_limit_bytes=62 << 20),
        name="backward",
    )(lengths, *inputs.values())
    return result[: len(outs)], result[len(outs) :]


def finish_call(plain, sums):
    parts = 4
    block = lambda v: pl.BlockSpec((v.shape[0] // parts, v.shape[1]), lambda t: (t, 0))
    half = sums[-1].shape[1] // 2
    ins = list(plain) + list(sums)
    outs = [jax.ShapeDtypeStruct(v.shape, v.dtype) for v in plain] + [jax.ShapeDtypeStruct(v.shape, jnp.float32) for v in sums[:-1]]
    outs += [jax.ShapeDtypeStruct((sums[-1].shape[0], half), jnp.float32)] * 2

    def kernel(*refs):
        src, dst = refs[: len(ins)], refs[len(ins) :]
        for a, b in zip(src[:-1], dst):
            b[...] = a[...].astype(b.dtype)
        dst[-2][...] = wide(src[-1][:, :half])
        dst[-1][...] = wide(src[-1][:, half:])

    return pl.pallas_call(
        kernel,
        grid=(parts,),
        out_shape=outs,
        in_specs=[block(v) for v in ins],
        out_specs=[block(v) for v in outs],
        compiler_params=pltpu.CompilerParams(vmem_limit_bytes=60 << 20),
        name="finish",
    )(*ins)


def local(
    tokens,
    lengths,
    mixer_gain,
    gelu_weight,
    input_weight,
    conv_taps,
    conv_bias,
    rgate_weight,
    rgate_bias,
    igate_weight,
    igate_bias,
    decay_param,
    output_weight,
    mlp_gain,
    mlp_gate,
    mlp_value,
    mlp_down,
    cotangent,
):
    count = tokens.shape[0]
    width_lru = input_weight.shape[1]
    block = rgate_weight.shape[1]
    heads = width_lru // block
    taps_count = conv_taps.shape[1]
    rim = taps_count - 1
    seq_count = lax.axis_size("seq")
    slot_length = count * seq_count
    first_row = (lax.axis_index("grp") * seq_count + lax.axis_index("seq")) * count
    global_row = first_row + jnp.arange(count, dtype=jnp.int32)
    position = global_row % slot_length
    slot_of = global_row // slot_length
    slot_ids = jnp.arange(lengths.shape[0], dtype=jnp.int32)
    slot_len = jnp.sum(
        jnp.where(slot_of[:, None] == slot_ids[None, :], lengths[None, :], 0), axis=1
    )
    valid = (position < slot_len).astype(jnp.float32)[:, None]
    starts = (position > 0).astype(jnp.float32)[:, None]
    lag_masks = [(position >= lag).astype(jnp.float32)[:, None] for lag in range(taps_count)]
    zeros_lru = jnp.zeros((width_lru,), jnp.float32)
    ones_lru = jnp.ones((width_lru,), jnp.float32)
    (
        gain_one,
        gelu_full,
        input_full,
        taps_full,
        cbias_full,
        rgate_full,
        rbias_full,
        igate_full,
        ibias_full,
        decay_full,
        output_full,
        gain_two,
        mgate_full,
        mvalue_full,
        mdown_full,
    ) = (
        lax.all_gather(mixer_gain, "seq", axis=0, tiled=True),
        lax.all_gather(gelu_weight, "seq", axis=0, tiled=True),
        lax.all_gather(input_weight, "seq", axis=0, tiled=True),
        lax.all_gather(conv_taps, "seq", axis=0, tiled=True),
        lax.all_gather(conv_bias, "seq", axis=0, tiled=True),
        lax.all_gather(rgate_weight, "seq", axis=0, tiled=True),
        lax.all_gather(rgate_bias, "seq", axis=0, tiled=True),
        lax.all_gather(igate_weight, "seq", axis=0, tiled=True),
        lax.all_gather(igate_bias, "seq", axis=0, tiled=True),
        lax.all_gather(decay_param, "seq", axis=0, tiled=True),
        lax.all_gather(output_weight, "seq", axis=0, tiled=True),
        lax.all_gather(mlp_gain, "seq", axis=0, tiled=True),
        lax.all_gather(mlp_gate, "seq", axis=0, tiled=True),
        lax.all_gather(mlp_value, "seq", axis=0, tiled=True),
        lax.all_gather(mlp_down, "seq", axis=0, tiled=True),
    )
    inputs = tokens.astype(jnp.float32)
    normed_one, norm_one_back = jax.vjp(rms_norm, inputs, gain_one.astype(jnp.float32))
    normed_one = normed_one.astype(jnp.bfloat16)
    gate_pre = matmul(normed_one, gelu_full)
    gate_act, gate_back = jax.vjp(gelu_tanh, gate_pre)
    linear = matmul(normed_one, input_full)
    rim_in = passed_along(linear[count - rim :], "seq", 1)
    extended = jnp.concatenate([rim_in, linear], axis=0)
    taps_fwd = taps_full.astype(jnp.float32)
    conv = cbias_full.astype(jnp.float32) + taps_fwd[:, 0] * linear
    for lag in range(1, taps_count):
        conv = conv + taps_fwd[:, lag] * (extended[rim - lag : rim - lag + count] * lag_masks[lag])
    conv_low = conv.astype(jnp.bfloat16)
    conv_value = conv_low.astype(jnp.float32)
    rgate_pre = block_apply(conv_low, rgate_full, heads) + rbias_full.astype(jnp.float32)
    igate_pre = block_apply(conv_low, igate_full, heads) + ibias_full.astype(jnp.float32)
    (decay, inject), gates_back = jax.vjp(
        recurrence_gates, rgate_pre, igate_pre, conv_value, decay_full.astype(jnp.float32)
    )
    decay_used = decay * starts
    cum_decay, state_zero = lax.associative_scan(chain_combine, (decay_used, inject), axis=0)
    scanned = carried_in(
        (cum_decay[-1], state_zero[-1]), "seq", chain_combine, (ones_lru, zeros_lru), False
    )
    carry_in = scanned[1]
    state = state_zero + cum_decay * carry_in
    mixed_rec = (state * gate_act).astype(jnp.bfloat16)
    resid = inputs + matmul(mixed_rec, output_full)
    normed_two, norm_two_back = jax.vjp(rms_norm, resid, gain_two.astype(jnp.float32))
    normed_two = normed_two.astype(jnp.bfloat16)
    mgate_pre = matmul(normed_two, mgate_full)
    mvalue_pre = matmul(normed_two, mvalue_full)
    mgate_act, mgate_back = jax.vjp(gelu_tanh, mgate_pre)
    hidden = (mgate_act * mvalue_pre).astype(jnp.bfloat16)
    mixed = ((resid + matmul(hidden, mdown_full)) * valid).astype(jnp.bfloat16)
    (
        gain_one,
        gelu_full,
        input_full,
        taps_full,
        cbias_full,
        rgate_full,
        rbias_full,
        igate_full,
        ibias_full,
        decay_full,
        output_full,
        gain_two,
        mgate_full,
        mvalue_full,
        mdown_full,
    ) = (
        lax.all_gather(mixer_gain, "seq", axis=0, tiled=True),
        lax.all_gather(gelu_weight, "seq", axis=0, tiled=True),
        lax.all_gather(input_weight, "seq", axis=0, tiled=True),
        lax.all_gather(conv_taps, "seq", axis=0, tiled=True),
        lax.all_gather(conv_bias, "seq", axis=0, tiled=True),
        lax.all_gather(rgate_weight, "seq", axis=0, tiled=True),
        lax.all_gather(rgate_bias, "seq", axis=0, tiled=True),
        lax.all_gather(igate_weight, "seq", axis=0, tiled=True),
        lax.all_gather(igate_bias, "seq", axis=0, tiled=True),
        lax.all_gather(decay_param, "seq", axis=0, tiled=True),
        lax.all_gather(output_weight, "seq", axis=0, tiled=True),
        lax.all_gather(mlp_gain, "seq", axis=0, tiled=True),
        lax.all_gather(mlp_gate, "seq", axis=0, tiled=True),
        lax.all_gather(mlp_value, "seq", axis=0, tiled=True),
        lax.all_gather(mlp_down, "seq", axis=0, tiled=True),
    )
    taps_back = taps_full.astype(jnp.float32)
    grad_out = cotangent.astype(jnp.float32) * valid
    grad_out_low = grad_out.astype(jnp.bfloat16)
    down_grad = inner_rows(hidden, grad_out_low)
    grad_hidden = outer_cols(grad_out_low, mdown_full)
    grad_mgate = mgate_back(grad_hidden * mvalue_pre)[0].astype(jnp.bfloat16)
    grad_mvalue = (grad_hidden * mgate_act).astype(jnp.bfloat16)
    mgate_grad = inner_rows(normed_two, grad_mgate)
    mvalue_grad = inner_rows(normed_two, grad_mvalue)
    grad_ntwo = outer_cols(grad_mgate, mgate_full) + outer_cols(grad_mvalue, mvalue_full)
    grad_resid_norm, gain_two_grad = norm_two_back(grad_ntwo)
    grad_resid = grad_out + grad_resid_norm
    grad_mix = grad_resid.astype(jnp.bfloat16)
    output_grad = inner_rows(mixed_rec, grad_mix)
    grad_rec = outer_cols(grad_mix, output_full)
    grad_state = grad_rec * gate_act
    grad_gate = gate_back(grad_rec * state)[0].astype(jnp.bfloat16)
    decay_next = jnp.concatenate([decay_used[1:], jnp.ones((1, width_lru), jnp.float32)], axis=0)
    rev_prod, rev_adjoint = lax.associative_scan(
        chain_combine, (jnp.flip(decay_next, 0), jnp.flip(grad_state, 0)), axis=0
    )
    tail_prod = jnp.flip(rev_prod, 0)
    adjoint_zero = jnp.flip(rev_adjoint, 0)
    summary_decay = decay_used[0] * tail_prod[0]
    summary_adjoint = decay_used[0] * adjoint_zero[0]
    scanned_back = carried_in(
        (summary_decay, summary_adjoint), "seq", chain_combine, (ones_lru, zeros_lru), True
    )
    incoming = scanned_back[1]
    adjoint = adjoint_zero + tail_prod * incoming
    state_prev = jnp.concatenate([carry_in[None, :], state[:-1]], axis=0)
    grad_decay = adjoint * state_prev * starts
    grad_rpre, grad_ipre, grad_direct, decay_grad = gates_back((grad_decay, adjoint))
    rbias_grad = jnp.sum(grad_rpre, axis=0)
    ibias_grad = jnp.sum(grad_ipre, axis=0)
    grad_rlow = grad_rpre.astype(jnp.bfloat16)
    grad_ilow = grad_ipre.astype(jnp.bfloat16)
    rgate_grad = block_grad(conv_low, grad_rlow, heads)
    igate_grad = block_grad(conv_low, grad_ilow, heads)
    grad_conv = (
        grad_direct
        + block_back(grad_rlow, rgate_full, heads)
        + block_back(grad_ilow, igate_full, heads)
    )
    cbias_grad = jnp.sum(grad_conv, axis=0)
    taps_columns = []
    grad_extended = jnp.zeros((count + rim, width_lru), jnp.float32)
    for lag in range(taps_count):
        masked_term = grad_conv * lag_masks[lag]
        taps_columns.append(jnp.sum(masked_term * extended[rim - lag : rim - lag + count], axis=0))
        grad_extended = grad_extended + jnp.pad(
            taps_back[:, lag] * masked_term, ((rim - lag, lag), (0, 0))
        )
    taps_grad = jnp.stack(taps_columns, axis=1)
    rim_back = passed_along(grad_extended[:rim], "seq", -1)
    grad_linear = grad_extended[rim:] + jnp.pad(rim_back, ((count - rim, 0), (0, 0)))
    grad_lin = grad_linear.astype(jnp.bfloat16)
    input_grad = inner_rows(normed_one, grad_lin)
    gelu_grad = inner_rows(normed_one, grad_gate)
    grad_none = outer_cols(grad_lin, input_full) + outer_cols(grad_gate, gelu_full)
    grad_inputs_norm, gain_one_grad = norm_one_back(grad_none)
    tokens_grad = grad_resid + grad_inputs_norm
    partials = (
        gain_one_grad,
        gelu_grad,
        input_grad,
        taps_grad,
        cbias_grad,
        rgate_grad,
        rbias_grad,
        igate_grad,
        ibias_grad,
        decay_grad,
        output_grad,
        gain_two_grad,
        mgate_grad,
        mvalue_grad,
        down_grad,
    )
    summed_seq = (
        lax.psum_scatter(partials[0], "seq", scatter_dimension=0, tiled=True),
        lax.psum_scatter(partials[1], "seq", scatter_dimension=0, tiled=True),
        lax.psum_scatter(partials[2], "seq", scatter_dimension=0, tiled=True),
        lax.psum_scatter(partials[3], "seq", scatter_dimension=0, tiled=True),
        lax.psum_scatter(partials[4], "seq", scatter_dimension=0, tiled=True),
        lax.psum_scatter(partials[5], "seq", scatter_dimension=0, tiled=True),
        lax.psum_scatter(partials[6], "seq", scatter_dimension=0, tiled=True),
        lax.psum_scatter(partials[7], "seq", scatter_dimension=0, tiled=True),
        lax.psum_scatter(partials[8], "seq", scatter_dimension=0, tiled=True),
        lax.psum_scatter(partials[9], "seq", scatter_dimension=0, tiled=True),
        lax.psum_scatter(partials[10], "seq", scatter_dimension=0, tiled=True),
        lax.psum_scatter(partials[11], "seq", scatter_dimension=0, tiled=True),
        lax.psum_scatter(partials[12], "seq", scatter_dimension=0, tiled=True),
        lax.psum_scatter(partials[13], "seq", scatter_dimension=0, tiled=True),
        lax.psum_scatter(partials[14], "seq", scatter_dimension=0, tiled=True),
    )
    totals = lax.psum(tuple(summed_seq), "grp")
    return (
        mixed,
        tokens_grad,
        totals[0],
        totals[1],
        totals[2],
        totals[3],
        totals[4],
        totals[5],
        totals[6],
        totals[7],
        totals[8],
        totals[9],
        totals[10],
        totals[11],
        totals[12],
        totals[13],
        totals[14],
    )


def local_fast(
    tokens,
    lengths,
    mixer_gain,
    gelu_weight,
    input_weight,
    conv_taps,
    conv_bias,
    rgate_weight,
    rgate_bias,
    igate_weight,
    igate_bias,
    decay_param,
    output_weight,
    mlp_gain,
    mlp_gate,
    mlp_value,
    mlp_down,
    cotangent,
):
    lru_rows = jnp.concatenate(
        [conv_taps.T, conv_bias[None], rgate_bias[None], igate_bias[None], decay_param[None]], axis=0
    ).astype(jnp.float32)
    model_rows = jnp.stack([mixer_gain, mlp_gain]).astype(jnp.float32)
    across = lambda value, columns: jnp.pad(value, ((0, 0), (0, columns - value.shape[1])))
    small = jnp.concatenate([across(lru_rows, 256), across(model_rows, 256), jnp.zeros((6, 256), jnp.float32)], axis=0)
    gates = jnp.concatenate([rgate_weight, igate_weight], axis=1)
    weights, saved = forward_call(
        tokens, small, [gelu_weight, input_weight, gates, output_weight, mlp_gate, mlp_value, mlp_down]
    )
    (mixed, tokens_grad, small_sum), sums = backward_call(lengths, tokens, cotangent, weights, saved)
    mixed, tokens_grad, down, mgate, mvalue, out_w, gelu_w, input_w, rgates, igates = finish_call([mixed, tokens_grad], sums)
    lru_own, model_own = small_sum[:8, : conv_bias.shape[0]], small_sum[8:10, : mixer_gain.shape[0]]
    return (
        mixed,
        tokens_grad,
        model_own[0],
        gelu_w,
        input_w,
        lru_own[:4].T,
        lru_own[4],
        rgates,
        lru_own[5],
        igates,
        lru_own[6],
        lru_own[7],
        out_w,
        model_own[1],
        mgate,
        mvalue,
        down,
    )


def solution(mesh):
    placed = (
        P(("grp", "seq"), None),
        P(),
        P("seq"),
        P("seq", None),
        P("seq", None),
        P("seq", None),
        P("seq"),
        P("seq", None),
        P("seq"),
        P("seq", None),
        P("seq"),
        P("seq"),
        P("seq", None),
        P("seq"),
        P("seq", None),
        P("seq", None),
        P("seq", None),
        P(("grp", "seq"), None),
    )
    fits = mesh.shape["grp"] == 4 and mesh.shape["seq"] == 8
    return jax.shard_map(
        local_fast if fits else local,
        mesh=mesh,
        in_specs=placed,
        out_specs=(
            P(("grp", "seq"), None),
            P(("grp", "seq"), None),
            P("seq"),
            P("seq", None),
            P("seq", None),
            P("seq", None),
            P("seq"),
            P("seq", None),
            P("seq"),
            P("seq", None),
            P("seq"),
            P("seq"),
            P("seq", None),
            P("seq"),
            P("seq", None),
            P("seq", None),
            P("seq", None),
        ),
        check_vma=False,
    )
```

```python
import math
from types import SimpleNamespace

import jax
import jax.numpy as jnp
from jax import lax
from jax.experimental import pallas as pl
from jax.experimental.pallas import tpu as pltpu
from jax.sharding import PartitionSpec as P

epsilon = 1e-06
cfactor = 8.0


def passed_along(value, axis, steps):
    count = lax.axis_size(axis)
    leading, last = (max(0, -steps), min(count, count - steps))
    return lax.ppermute(value, axis, [(source, source + steps) for source in range(leading, last)])


def carried_in(value, axis, join, neutral, backward):
    count, mine = (lax.axis_size(axis), lax.axis_index(axis))
    pieces = jax.tree.map(lambda part: lax.all_gather(part, axis), value)
    if backward:
        pieces = jax.tree.map(lambda part: part[::-1], pieces)
        mine = count - 1 - mine
    so_far = jax.tree.map(
        lambda part, zero: jnp.full_like(part, 0) + jnp.asarray(zero, part.dtype), value, neutral
    )

    def step(position, so_far):
        longer = join(so_far, jax.tree.map(lambda part: part[position], pieces))
        return jax.tree.map(lambda new, old: jnp.where(position < mine, new, old), longer, so_far)

    return lax.fori_loop(0, count - 1, step, so_far)


def rms_norm(rows_in, gain):
    return rows_in * lax.rsqrt(jnp.mean(rows_in * rows_in, axis=-1, keepdims=True) + epsilon) * gain


def gelu_tanh(values):
    return jax.nn.gelu(values, approximate=True)


def matmul(left, right):
    return jnp.dot(left, right, preferred_element_type=jnp.float32)


def inner_rows(left, right):
    return lax.dot_general(
        left, right, (((0,), (0,)), ((), ())), preferred_element_type=jnp.float32
    )


def outer_cols(left, right):
    return lax.dot_general(
        left, right, (((1,), (1,)), ((), ())), preferred_element_type=jnp.float32
    )


def block_apply(values, weight, heads):
    count = values.shape[0]
    width = weight.shape[1]
    parts = values.reshape(count, heads, width)
    blocks = weight.reshape(heads, width, width)
    return jnp.einsum("rhi,hij->rhj", parts, blocks, preferred_element_type=jnp.float32).reshape(
        count, heads * width
    )


def block_back(grads, weight, heads):
    count = grads.shape[0]
    width = weight.shape[1]
    parts = grads.reshape(count, heads, width)
    blocks = weight.reshape(heads, width, width)
    return jnp.einsum("rhj,hij->rhi", parts, blocks, preferred_element_type=jnp.float32).reshape(
        count, heads * width
    )


def block_grad(values, grads, heads):
    count = values.shape[0]
    width = values.shape[1] // heads
    left = values.reshape(count, heads, width)
    right = grads.reshape(count, heads, width)
    return jnp.einsum("rhi,rhj->hij", left, right, preferred_element_type=jnp.float32).reshape(
        heads * width, width
    )


def chain_combine(earlier, later):
    return (earlier[0] * later[0], later[0] * earlier[1] + later[1])


def recurrence_gates(rgate_pre, igate_pre, conv_in, decay_in):
    rgate = jax.nn.sigmoid(rgate_pre)
    igate = jax.nn.sigmoid(igate_pre)
    log_decay = -cfactor * jax.nn.softplus(-decay_in) * rgate
    return (jnp.exp(log_decay), jnp.sqrt(-jnp.expm1(2.0 * log_decay)) * igate * conv_in)


MESH = pl.DeviceIdType.MESH


class Place:
    def __init__(self):
        self.z = lax.axis_index("grp")
        seq = lax.axis_index("seq")
        self.core = seq % 2
        self.x = (seq // 2) % 2
        self.y = seq // 4
        self.seq = seq
        self.sib = (self.z, self.at(self.y, self.x, 1 - self.core))
        self.xnb = (self.z, self.at(self.y, 1 - self.x, self.core))
        self.ynb = (self.z, self.at(1 - self.y, self.x, self.core))

    def at(self, y, x, core):
        return (y * 2 + x) * 2 + core

    def level(self, z):
        return (z, self.seq)


def greet(peers):
    barrier = pltpu.get_barrier_semaphore()
    for peer in peers:
        pl.semaphore_signal(barrier, inc=1, device_id=peer, device_id_type=MESH)


def met(count):
    pl.semaphore_wait(pltpu.get_barrier_semaphore(), count)


GOT = ("X", "Y", "D1", "D2", "SO", "SX", "SY", "S1", "S2")
SENT = ("ox", "oy", "os", "fy", "fx", "zX", "zY", "zD1", "zD2", "SX", "SY", "S1", "S2")
OVER_LINKS = GOT[:4]
TO_SIB = dict(zip(OVER_LINKS, GOT[5:]))


class Gather:
    def __init__(self, place, shards, fulls, kinds, send, recv, own, bounce):
        self.p, self.shards, self.fulls, self.bounce, self.kinds = place, shards, fulls, bounce, kinds
        self.send, self.recv, self.own = send, recv, own
        self.held = [shard is buffer for shard, buffer in zip(shards, bounce)]
        self.znb = place.level(place.z + 1 - 2 * (place.z % 2))

    def fetched(self, i, odd):
        return self.kinds[i] != 2 - odd

    def part(self, i, name):
        p = self.p
        n = self.shards[i].shape[0]
        y, x = p.y, p.x
        if name[-1] == "X":
            x = 1 - x
        elif name[-1] == "Y":
            y = 1 - y
        elif name[-1] in "12":
            x, y = 1 - x, 1 - y
        core = 1 - p.core if name[0] == "S" else p.core
        first = pl.multiple_of(p.at(y, x, core) * n, n)
        if name[-1] == "1":
            return pl.ds(first, n // 2)
        if name[-1] == "2":
            return pl.ds(pl.multiple_of(first + n // 2, n // 2), n // 2)
        return pl.ds(first, n)

    def half(self, i, name, which):
        n = self.shards[i].shape[0]
        return pl.ds(pl.multiple_of(self.part(i, name).start + which * (n // 2), n // 2), n // 2)

    def copy(self, i, how, got, peer, rows, src=None):
        full = self.fulls[i]
        return pltpu.make_async_remote_copy(
            src_ref=full.at[rows] if src is None else src,
            dst_ref=full.at[rows],
            send_sem=self.send.at[i, SENT.index(how)],
            recv_sem=self.recv.at[i, GOT.index(got)],
            device_id=peer,
            device_id_type=MESH,
        )

    def wait(self, i, name):
        self.copy(i, "ox", name, self.p.sib, self.part(i, name)).wait_recv()

    def own_far(self, i):
        p, mine = self.p, self.part(i, "O")
        return [self.copy(i, "ox", "X", p.xnb, mine, self.shards[i]), self.copy(i, "oy", "Y", p.ynb, mine, self.shards[i])]

    def own_near(self, i):
        return self.copy(i, "os", "SO", self.p.sib, self.part(i, "O"), self.shards[i])

    def own_kept(self, i, leg):
        if leg == 0:
            return pltpu.make_async_copy(self.shards[i], self.bounce[i], self.own.at[i, 0])
        return pltpu.make_async_copy(self.bounce[i], self.fulls[i].at[self.part(i, "O")], self.own.at[i, 1])

    def start(self, i, odd):
        if self.fetched(i, odd):
            for c in self.own_far(i):
                c.start()
        self.own_near(i).start()
        if not self.held[i]:
            self.own_kept(i, 0).start()

    def onward(self, i, name, odd):
        p = self.p
        copies = []
        if self.fetched(i, odd):
            if name == "X":
                copies.append(self.copy(i, "fy", "D1", p.ynb, self.half(i, "X", 0)))
            if name == "Y":
                copies.append(self.copy(i, "fx", "D2", p.xnb, self.half(i, "Y", 1)))
            if self.kinds[i]:
                copies.append(self.copy(i, "z" + name, name, self.znb, self.part(i, name)))
        copies.append(self.copy(i, TO_SIB[name], TO_SIB[name], p.sib, self.part(i, name)))
        return copies

    def relay(self, i, name, odd):
        self.wait(i, name)
        for c in self.onward(i, name, odd):
            c.start()
        if name == "X":
            if not self.held[i]:
                self.own_kept(i, 0).wait()
            self.own_kept(i, 1).start()

    def arrive(self, i):
        for name in GOT[4:]:
            self.wait(i, name)
        self.own_kept(i, 1).wait()

    def drain(self, i, odd):
        if self.fetched(i, odd):
            for c in self.own_far(i):
                c.wait_send()
        self.own_near(i).wait_send()
        for name in OVER_LINKS:
            for c in self.onward(i, name, odd):
                c.wait_send()


def rows_loop(total, body, step=16, start=0):
    @pl.loop(start // step, total // step)
    def _(k):
        body(pl.ds(pl.multiple_of(k * step, step), step))


def wide(value):
    return value.astype(jnp.float32)

class Reduce:
    def __init__(self, place, slots, sems):
        self.p = place
        self.slots = slots
        self.send, self.recv = sems
        z = place.z
        inner = (z == 1) | (z == 2)
        self.inner = inner
        self.outer = (z == 0) | (z == 3)
        self.peer = place.level(jnp.where(inner, 3 - z, z))
        self.out = place.level(jnp.where(z < 2, 1 - z, 5 - z))
        self.me = 2 * place.y + place.x

    def makes(self, h):
        return self.p.z == 1 + h

    def helps(self, h):
        return self.p.z == 2 - h

    def copy(self, i, tag, src, dst, peer):
        return pltpu.make_async_remote_copy(
            src_ref=src, dst_ref=dst, send_sem=self.send.at[i, tag], recv_sem=self.recv.at[i, tag], device_id=peer, device_id_type=MESH
        )

    def first(self, i, h):
        p, s = self.p, self.slots[i]
        if h == 0:
            return [self.copy(i, q, s.ab.at[0, 2 * q + 1 - p.x], s.fr.at[0, q], p.xnb) for q in range(2)]
        return [self.copy(i, 2 + q, s.ab.at[1, 2 * (1 - p.y) + q], s.fr.at[1, q], p.ynb) for q in range(2)]

    def second(self, i, h):
        p, s = self.p, self.slots[i]
        if h == 0:
            return self.copy(i, 4, s.ab.at[0, 2 * (1 - p.y) + p.x], s.se.at[0], p.ynb)
        return self.copy(i, 5, s.ab.at[1, 2 * p.y + 1 - p.x], s.se.at[1], p.xnb)

    def up(self, i, h):
        s = self.slots[i]
        return self.copy(i, 6 + h, s.ab.at[h, self.me], s.zo.at[h], self.out)

    def across(self, i, h):
        s = self.slots[i]
        return self.copy(i, 8 + h, s.ab.at[h, self.me], s.zp, self.peer)

    def down(self, i, h):
        res = self.slots[i].res.at[h]
        return self.copy(i, 10 + h, res, res, self.out)

    def over(self, i, h):
        res = self.slots[i].res.at[h]
        return self.copy(i, 12 + h, res, res, self.peer)

    def start_first(self, i, h):
        for cp in self.first(i, h):
            cp.start()

    def add_first(self, i, h):
        p, s = self.p, self.slots[i]
        for cp in self.first(i, h):
            cp.wait_recv()
        for q in range(2):
            j = 2 * q + p.x if h == 0 else 2 * p.y + q

            def body(rows, q=q, j=j):
                s.ab[h, j, rows, :] = low(wide(s.ab[h, j, rows, :]) + wide(s.fr[h, q, rows, :]))

            rows_loop(s.n, body)
        self.second(i, h).start()

    def add_second(self, i, h):
        s, me = self.slots[i], self.me
        self.second(i, h).wait_recv()

        def body(rows):
            s.ab[h, me, rows, :] = low(wide(s.ab[h, me, rows, :]) + wide(s.se[h, rows, :]))

        rows_loop(s.n, body)

        @pl.when(self.outer)
        def _():
            self.up(i, h).start()

    def add_outer(self, i, h):
        s, me = self.slots[i], self.me

        @pl.when(self.inner)
        def _():
            self.up(i, h).wait_recv()

            def body(rows):
                s.ab[h, me, rows, :] = low(wide(s.ab[h, me, rows, :]) + wide(s.zo[h, rows, :]))

            rows_loop(s.n, body)

        @pl.when(self.helps(h))
        def _():
            self.across(i, h).start()

    def add_peer(self, i, h):
        s, me = self.slots[i], self.me

        @pl.when(self.makes(h))
        def _():
            self.across(i, h).wait_recv()

            def body(rows):
                s.res[h, rows, :] = low(wide(s.ab[h, me, rows, :]) + wide(s.zp[rows, :]))

            rows_loop(s.n, body)
            self.down(i, h).start()
            self.over(i, h).start()

    def pass_on(self, i, h):
        @pl.when(self.helps(h))
        def _():
            self.over(i, h).wait_recv()
            self.down(i, h).start()

    def arrive(self, i, h):
        @pl.when(self.outer)
        def _():
            self.down(i, h).wait_recv()

    def drain(self, i):
        for h in range(2):

            @pl.when(self.outer)
            def _(h=h):
                self.up(i, h).wait_send()

            @pl.when(self.inner)
            def _(h=h):
                self.down(i, h).wait_send()

            @pl.when(self.makes(h))
            def _(h=h):
                self.over(i, h).wait_send()

            @pl.when(self.helps(h))
            def _(h=h):
                self.across(i, h).wait_send()

            for cp in self.first(i, h) + [self.second(i, h)]:
                cp.wait_send()


class Small:
    def __init__(self, place, total, slots, sems):
        p = place
        self.total, self.slots = total, slots
        self.send, self.recv = sems
        z = p.z
        self.order = [p.sib, p.xnb, p.ynb, p.level(z + 1 - 2 * (z % 2)), p.level((z + 2) % 4)]

    def copy(self, k):
        return pltpu.make_async_remote_copy(
            src_ref=self.slots.at[0, k],
            dst_ref=self.slots.at[1, k],
            send_sem=self.send.at[k],
            recv_sem=self.recv.at[k],
            device_id=self.order[k],
            device_id_type=MESH,
        )

    def begin(self):
        self.slots[0, 0] = self.total[...]
        self.copy(0).start()

    def step(self, k):
        self.copy(k).wait_recv()
        both = self.slots[0, k] + self.slots[1, k]
        if k < 4:
            self.slots[0, k + 1] = both
            self.copy(k + 1).start()
        else:
            self.total[...] = both

    def drain(self):
        for k in range(5):
            self.copy(k).wait_send()

ROOT = math.sqrt(2.0 / math.pi)
CUBE = 0.044715
LANES = 128


def low(value):
    return value.astype(jnp.bfloat16)


def gelu_parts(v):
    square = v * v
    t = jnp.tanh(ROOT * (v + CUBE * v * square))
    half = 0.5 * (1.0 + t)
    return v * half, half + 0.5 * v * (1.0 - t * t) * (ROOT * (1.0 + 3.0 * CUBE * square))


def dot(left, right):
    return jnp.dot(left, right, preferred_element_type=jnp.float32)


def dot_t(left, right):
    return lax.dot_general(left, right, (((1,), (1,)), ((), ())), preferred_element_type=jnp.float32)


def sigmoid(v):
    return 1.0 / (1.0 + jnp.exp(-v))


def minus_expm1(twice, half_of):
    t = jnp.tanh(half_of)
    return -2.0 * t / (1.0 - t)


def softplus_minus(v):
    return jnp.maximum(-v, 0.0) + jnp.log1p(jnp.exp(-jnp.abs(v)))


def interleave(rows, back):
    span = rows // 8
    shape = (8, span, rows) if back else (span, 8, rows)
    major, minor, of = [lax.broadcasted_iota(jnp.int32, shape, d).astype(jnp.float32) for d in range(3)]
    source = minor * (8.0 if back else float(span)) + major
    return low(jnp.where(of == source, 1.0, 0.0)).reshape(rows, rows)


def over_segments(value, tile):
    return (value.reshape(value.shape[0] // 8, 8, value.shape[1]) * tile[None]).reshape(value.shape)


def segment_scan(decay_ref, value_ref, prod_ref, sum_ref, backward, rows, between):
    tiles, _, lanes = sum_ref.shape
    span = rows // 8

    def step(k, carry):
        prod, total = carry
        t = span - 1 - k if backward else k
        spot = pl.ds(pl.multiple_of(t * 8, 8), 8)
        new_prod, new_total = [], []
        for c in range(tiles):
            d, v = decay_ref[c, spot, :], value_ref[c, spot, :]
            if backward:
                seen = total[c] + v
                sum_ref[c, spot, :] = seen
                prod_ref[c, spot, :] = prod[c]
                new_prod.append(prod[c] * d)
                new_total.append(seen * d)
            else:
                new_prod.append(prod[c] * d)
                new_total.append(total[c] * d + v)
                prod_ref[c, spot, :] = new_prod[c]
                sum_ref[c, spot, :] = new_total[c]
        return new_prod, new_total

    ones = [jnp.ones((8, lanes), jnp.float32)] * tiles
    zeros = [jnp.zeros((8, lanes), jnp.float32)] * tiles
    half = lax.fori_loop(0, span // 2, step, (ones, zeros), unroll=2)
    between()
    return lax.fori_loop(span // 2, span, step, half, unroll=2)


def segment_ends(ends, backward):
    before, whole = [], []
    order = range(7, -1, -1) if backward else range(8)
    for prod, total in zip(*ends):
        p = jnp.ones((1, prod.shape[1]), jnp.float32)
        s = jnp.zeros((1, prod.shape[1]), jnp.float32)
        ps, ss = [None] * 8, [None] * 8
        for k in order:
            ps[k], ss[k] = p, s
            d, v = prod[k : k + 1], total[k : k + 1]
            p, s = p * d, s * d + v
        before.append((jnp.concatenate(ps, axis=0), jnp.concatenate(ss, axis=0)))
        whole.append((p, s))
    return before, whole


class Ends:
    def __init__(self, place, slots, sems, backward):
        self.p, self.slots, self.backward = place, slots, backward
        self.send, self.recv = sems

    def copy(self, d):
        to = (self.p.seq + d) % 8
        return pltpu.make_async_remote_copy(
            src_ref=self.slots.at[self.p.seq], dst_ref=self.slots.at[self.p.seq], send_sem=self.send.at[d - 1],
            recv_sem=self.recv.at[d - 1], device_id=(self.p.z, to), device_id_type=MESH,
        )

    def come(self, d):
        src = (self.p.seq + 8 - d) % 8
        return pltpu.make_async_remote_copy(
            src_ref=self.slots.at[src], dst_ref=self.slots.at[src], send_sem=self.send.at[d - 1],
            recv_sem=self.recv.at[d - 1], device_id=(self.p.z, src), device_id_type=MESH,
        )

    def tell(self, whole):
        for c, (prod, total) in enumerate(whole):
            self.slots[self.p.seq, 0, c : c + 1, :] = prod
            self.slots[self.p.seq, 1, c : c + 1, :] = total
        self.share()

    def share(self):
        for d in range(1, 8):
            self.copy(d).start()

    def shared(self):
        for d in range(1, 8):
            self.come(d).wait_recv()

    def joined(self):
        self.shared()
        carry = jnp.zeros(self.slots.shape[2:], jnp.float32)
        for k in range(7, 0, -1) if self.backward else range(7):
            further = self.slots[k, 0] * carry + self.slots[k, 1]
            counts = k > self.p.seq if self.backward else k < self.p.seq
            carry = jnp.where(counts, further, carry)
        return carry

    def drain(self):
        for d in range(1, 8):
            self.copy(d).wait_send()


def named(keys, refs):
    return SimpleNamespace(**dict(zip(keys, refs)))


RIM = 24
HBM = pl.BlockSpec(memory_space=pl.ANY)
VMEM = pl.BlockSpec(memory_space=pltpu.VMEM)


KINDS = (0, 1, 0, 0, 2, 1, 0)
FETCHES = (
    (
        ((0, 1),),
        (),
        ((0, 0), (0, 2), (1, 1), (2, 1), (1, 0), (2, 0), (1, 2), (2, 2), (3, 1), (4, 1), (0, 5), (0, 4), (3, 0), (4, 0), (3, 2), (4, 2),),
        (),
        (),
        (),
        ((0, 3),),
        ((1, 5), (2, 5), (1, 4),),
        (),
        (),
        ((1, 3), (2, 3),),
        ((2, 4), (0, 6),),
        ((3, 5), (4, 5),),
        ((3, 3), (4, 3),),
        ((3, 4),),
        (),
        (),
        ((4, 4),),
        (),
        ((1, 6), (2, 6),),
        (),
        (),
        (),
        (),
        ((3, 6), (4, 6),),
        (),
        (),
        (),
        (),
        (),
        (),
        (),
        (),
    ),
    (
        ((0, 0), (0, 1),),
        (),
        ((0, 4), (1, 0), (2, 0), (1, 1), (0, 2), (0, 5), (1, 4), (2, 4), (2, 1), (3, 0), (4, 0), (3, 1), (1, 2), (2, 2),),
        ((4, 1),),
        ((0, 3),),
        ((3, 4), (4, 4), (3, 2), (4, 2),),
        ((0, 6),),
        (),
        ((1, 3), (2, 3),),
        (),
        (),
        (),
        ((1, 5), (1, 6), (2, 6),),
        (),
        ((3, 3), (4, 3),),
        (),
        ((3, 6), (4, 6),),
        ((2, 5),),
        (),
        (),
        (),
        ((3, 5),),
        (),
        (),
        (),
        ((4, 5),),
        (),
        (),
        (),
        (),
        (),
        (),
        (),
    ),
)


def forward_call(tokens, small_own, gate_weights, shards):
    rows, width = tokens.shape
    lru = shards[0].shape[1]
    ff = shards[3].shape[1]
    own = lambda v: jax.ShapeDtypeStruct(v.shape, v.dtype)
    gates_own = jax.ShapeDtypeStruct((gate_weights[0].shape[0], 2 * LANES), gate_weights[0].dtype)
    inputs = len(gate_weights) + len(shards)
    shapes = [own(v) for v in shards[:2]] + [gates_own] + [own(v) for v in shards[2:]]
    tiles = lru // LANES
    kinds = KINDS
    count = len(shapes)
    f32, bf = jnp.float32, jnp.bfloat16
    shape = jax.ShapeDtypeStruct
    wholes = [shape((8 * s.shape[0], s.shape[1]), s.dtype) for s in shapes]
    saved = dict(
        hidden=shape((rows, ff), bf),
        x=shape((rows, width), bf),
        small=shape((16, lru), f32),
        n1t=shape((width, rows), bf),
        pre=shape((tiles, rows, LANES), f32),
        lin=shape((tiles, rows + RIM, LANES), f32),
        convt=shape((tiles, LANES, rows), bf),
        decay=shape((tiles, rows, LANES), f32),
        k2=shape((tiles, rows, LANES), f32),
        k3=shape((tiles, rows, LANES), f32),
        k6=shape((tiles, rows, LANES), f32),
        k7=shape((tiles, rows, LANES), f32),
        slope=shape((tiles, rows, LANES), f32),
        rect=shape((lru, rows), bf),
        resid=shape((rows, width), f32),
        n2t=shape((width, rows), bf),
        mg=shape((rows, ff), f32),
        bend=shape((rows, ff), f32),
        mv=shape((rows, ff), f32),
        hidt=shape((ff, rows), bf),
    )
    names = list(saved)
    scratch = dict(
        x=pltpu.VMEM((rows, width), bf),
        n1=pltpu.VMEM((rows, width), bf),
        n1t=pltpu.VMEM((width, rows), bf),
        parts=pltpu.VMEM((8,) + small_own.shape, f32),
        into=pltpu.VMEM((tiles, 8, LANES), f32),
        edge=pltpu.VMEM((tiles, 8, LANES), f32),
        halo=pltpu.VMEM((tiles, 8, LANES), f32),
        small=pltpu.VMEM((16, lru), f32),
        pre=pltpu.VMEM((tiles, rows, LANES), f32),
        lin=pltpu.VMEM((tiles, rows + RIM, LANES), f32),
        convt=pltpu.VMEM((tiles, LANES, rows), bf),
        decay=pltpu.VMEM((tiles, rows, LANES), f32),
        k2=pltpu.VMEM((tiles, rows, LANES), f32),
        k3=pltpu.VMEM((tiles, rows, LANES), f32),
        k6=pltpu.VMEM((tiles, rows, LANES), f32),
        k7=pltpu.VMEM((tiles, rows, LANES), f32),
        prod=pltpu.VMEM((tiles, rows, LANES), f32),
        total=pltpu.VMEM((tiles, rows, LANES), f32),
        rec=pltpu.VMEM((rows, lru), bf),
        rect=pltpu.VMEM((lru, rows), bf),
        resid=pltpu.VMEM((rows, width), f32),
        n2=pltpu.VMEM((rows, width), bf),
        n2t=pltpu.VMEM((width, rows), bf),
        hidden=pltpu.VMEM((rows, ff), bf),
        ends=pltpu.VMEM((8, 2, tiles, LANES), f32),
        gsend=pltpu.SemaphoreType.DMA((count, len(SENT))),
        grecv=pltpu.SemaphoreType.DMA((count, len(GOT))),
        gown=pltpu.SemaphoreType.DMA((count, 2)),
        esend=pltpu.SemaphoreType.DMA((7,)),
        erecv=pltpu.SemaphoreType.DMA((7,)),
        ssend=pltpu.SemaphoreType.DMA((7,)),
        srecv=pltpu.SemaphoreType.DMA((7,)),
        hsend=pltpu.SemaphoreType.DMA(()),
        hrecv=pltpu.SemaphoreType.DMA(()),
        load=pltpu.SemaphoreType.DMA((4,)),
        keep=pltpu.SemaphoreType.DMA((len(names),)),
    )
    keys = list(scratch)
    R = 128

    def kernel(tokens_ref, small_ref, *refs):
        pair, given, refs = refs[:2], refs[2:inputs], refs[inputs:]
        outs, bounce = refs[:count], refs[-count:]
        ins = list(given[:2]) + [bounce[2]] + list(given[2:])
        out = named(names, refs[count : count + len(names)])
        v = named(keys, refs[count + len(names) : -count])
        gelu_w, input_w, gates_w, output_w, mgate_w, mvalue_w, mdown_w = outs
        place = Place()
        gather = Gather(place, ins, outs, kinds, v.gsend, v.grecv, v.gown, bounce)
        ends = Ends(place, v.ends, (v.esend, v.erecv), False)
        packs = Ends(place, v.parts, (v.ssend, v.srecv), False)
        z, seq = place.z, place.seq
        loads = [
            pltpu.make_async_copy(tokens_ref, v.n2, v.load.at[0]),
            pltpu.make_async_copy(small_ref, v.parts.at[seq], v.load.at[1]),
        ] + [pltpu.make_async_copy(pair[k], bounce[2].at[:, pl.ds(k * LANES, LANES)], v.load.at[2 + k]) for k in range(2)]
        greet([(z, (seq + d) % 8) for d in range(1, 8)] + [gather.znb])
        for cp in loads:
            cp.start()
        kept = []

        def keep(src, dst):
            cp = pltpu.make_async_copy(src, dst, v.keep.at[len(kept)])
            cp.start()
            kept.append(cp)

        def by_level(act):
            for odd in range(2):
                pl.when(z % 2 == odd)(lambda odd=odd: act(odd))

        turn_of = [0]

        def serve(spot):
            def act(odd):
                for step, i in FETCHES[odd][spot]:
                    if step == 0:
                        gather.start(i, odd)
                    else:
                        gather.relay(i, OVER_LINKS[step - 1], odd)

            if FETCHES[0][spot] or FETCHES[1][spot]:
                by_level(act)

        def pump():
            serve(turn_of[0])
            turn_of[0] += 1

        def pumps_at(*places):
            spots = list(enumerate(places, turn_of[0]))
            turn_of[0] += len(spots)

            def at_place(here):
                for spot, there in spots:
                    if FETCHES[0][spot] or FETCHES[1][spot]:
                        pl.when(here == there)(lambda spot=spot: serve(spot))

            return at_place

        for cp in loads[1:]:
            cp.wait()
        met(8)
        packs.share()
        pump()
        loads[0].wait()
        v.x[...] = low(dot(interleave(rows, False), v.n2[...]))
        packs.shared()
        small = v.small
        lane = lax.broadcasted_iota(jnp.int32, (8, LANES), 1)
        for k in range(4):
            left, right = v.parts[2 * k, 0:8, :], pltpu.roll(v.parts[2 * k + 1, 0:8, :], 64, axis=1)
            first = 3 * k * LANES
            small[0:8, first : first + LANES] = left[:, :LANES]
            small[0:8, first + LANES : first + 2 * LANES] = jnp.where(lane < 64, left[:, LANES:], right[:, :LANES])
            small[0:8, first + 2 * LANES : first + 3 * LANES] = right[:, LANES:]
        for k in range(8):
            small[8:16, k * LANES : (k + 1) * LANES] = v.parts[k, 8:16, :LANES]
        small[8:16, width:] = jnp.zeros((8, lru - width), f32)
        keep(v.small, out.small)
        keep(v.x, out.x)

        def norm_one(at):
            x = wide(v.x[at, :])
            scale = lax.rsqrt(jnp.mean(x * x, axis=-1, keepdims=True) + epsilon)
            v.n1[at, :] = low(x * scale * small[8:9, :width])

        rows_loop(rows, norm_one, 64)
        pump()

        def turn(src, dst, at):
            dst[at, :] = src[:, at].T

        @pl.loop(0, width // 256)
        def _(k):
            turn(v.n1, v.n1t, pl.ds(pl.multiple_of(k * 256, 256), 256))

        keep(v.n1t, out.n1t)

        def project(weight, dst, first):
            inside = pumps_at(tiles // 4)

            def body(w):
                t = pl.program_id(0)
                inside(t)
                both = dot(v.n1[...], w[...])
                dst[2 * t, pl.ds(first, rows), :] = both[:, :LANES]
                dst[2 * t + 1, pl.ds(first, rows), :] = both[:, LANES:]

            pltpu.emit_pipeline(body, grid=(tiles // 2,), in_specs=[pl.BlockSpec((width, 2 * LANES), lambda t: (0, t))])(weight)

        pump()
        gather.arrive(0)
        project(gelu_w, v.pre, 0)
        pump()
        gather.arrive(1)
        project(input_w, v.lin, RIM)

        def halo():
            return pltpu.make_async_remote_copy(
                src_ref=v.edge, dst_ref=v.halo, send_sem=v.hsend, recv_sem=v.hrecv, device_id=(z, (seq + 1) % 8), device_id_type=MESH
            )

        for k in range(3):
            v.edge[:, k : k + 1, :] = v.lin[:, RIM + rows - 8 * k - 1 : RIM + rows - 8 * k, :]

        @pl.when(seq < 7)
        def _():
            halo().start()

        pump()
        gather.arrive(2)

        @pl.when(seq == 0)
        def _():
            v.halo[...] = jnp.zeros((tiles, 8, LANES), f32)

        @pl.when(seq > 0)
        def _():
            halo().wait_recv()

        lowest = lax.broadcasted_iota(jnp.int32, (8, LANES), 0) == 0

        @pl.loop(0, tiles)
        def _(c):
            for k in range(3):
                tile = pltpu.roll(v.lin[c, RIM + rows - 8 * (k + 1) : RIM + rows - 8 * k, :], 1, axis=0)
                v.lin[c, RIM - 8 * (k + 1) : RIM - 8 * k, :] = jnp.where(lowest, v.halo[c, k : k + 1, :], tile)

        keep(v.lin, out.lin)

        gates_inside = pumps_at(tiles // 3, 2 * tiles // 3)

        def gates(w):
            h = pl.program_id(0)
            gates_inside(h)
            lane = pl.ds(pl.multiple_of(h * LANES, LANES), LANES)
            taps = [small[k : k + 1, lane] for k in range(4)]
            cb, rb, ib, dp = [small[k : k + 1, lane] for k in range(4, 8)]
            rate = -cfactor * softplus_minus(dp)
            for r in range(0, rows, R):
                acc = cb + taps[0] * v.lin[h, RIM + r : RIM + r + R, :]
                for k in range(1, 4):
                    acc = acc + taps[k] * v.lin[h, RIM + r - 8 * k : RIM + r - 8 * k + R, :]
                cl = low(acc)
                v.convt[h, :, r : r + R] = cl.T
                both = dot(cl, w[...])
                rg = sigmoid(both[:, :LANES] + rb)
                ig = sigmoid(both[:, LANES:] + ib)
                log_decay = rate * rg
                decay = jnp.exp(log_decay)
                mult = jnp.sqrt(minus_expm1(2.0 * log_decay, log_decay))
                cv = wide(cl)
                through = mult * ig
                at = slice(r, r + R)
                v.prod[h, at, :] = decay
                v.decay[h, at, :] = decay
                v.total[h, at, :] = through * cv
                v.k3[h, at, :] = through
                v.k2[h, at, :] = through * cv * (1.0 - ig)
                v.k6[h, at, :] = ig * cv * (decay * decay) / mult
                v.k7[h, at, :] = rg

        pltpu.emit_pipeline(gates, grid=(tiles,), in_specs=[pl.BlockSpec((LANES, 2 * LANES), lambda h: (h, 0))])(gates_w)
        for src, dst in ((v.convt, out.convt), (v.decay, out.decay), (v.k2, out.k2), (v.k3, out.k3)):
            keep(src, dst)
        pump()
        tails = segment_scan(v.prod, v.total, v.prod, v.total, False, rows, pump)
        before, whole = segment_ends(tails, False)
        ends.tell(whole)
        pump()
        carry = ends.joined()
        span = rows // 8
        for c in range(tiles):
            into = before[c][0] * carry[c : c + 1, :] + before[c][1]
            v.into[c] = into

        pump()
        state_inside = pumps_at(tiles // 3, 2 * tiles // 3)

        @pl.loop(0, tiles)
        def _(c):
            state_inside(c)
            lane = pl.ds(pl.multiple_of(c * LANES, LANES), LANES)
            into = v.into[c]
            rate = -cfactor * softplus_minus(small[7:8, lane])
            last = into
            for s in range(8):
                at = slice(s * span, (s + 1) * span)
                state = v.total[c, at, :] + over_segments(v.prod[c, at, :], into)
                before_it = jnp.concatenate([last, state[:-8]], axis=0)
                last = state[-8:]
                rg = v.k7[c, at, :]
                k7 = (before_it * v.decay[c, at, :] - v.k6[c, at, :]) * rg
                v.k7[c, at, :] = k7
                v.k6[c, at, :] = k7 * rate * (1.0 - rg)
                value, slope = gelu_parts(v.pre[c, at, :])
                v.rec[at, lane] = low(state * value)
                v.pre[c, at, :] = value
                v.total[c, at, :] = state * slope
            v.rect[lane, :] = v.rec[:, lane].T

        for src, dst in ((v.k6, out.k6), (v.k7, out.k7), (v.pre, out.pre), (v.total, out.slope)):
            keep(src, dst)
        keep(v.rect, out.rect)
        pump()
        gather.arrive(3)
        width_inside = pumps_at(width // 512)

        def back_to_width(w):
            t = pl.program_id(0)
            width_inside(t)
            at = pl.ds(pl.multiple_of(t * 256, 256), 256)
            v.resid[:, at] = wide(v.x[:, at]) + dot(v.rec[...], w[...])

        pltpu.emit_pipeline(back_to_width, grid=(width // 256,), in_specs=[pl.BlockSpec((lru, 256), lambda t: (0, t))])(output_w)
        keep(v.resid, out.resid)
        pump()
        def norm_two(at):
            x = v.resid[at, :]
            scale = lax.rsqrt(jnp.mean(x * x, axis=-1, keepdims=True) + epsilon)
            v.n2[at, :] = low(x * scale * small[9:10, :width])

        rows_loop(rows, norm_two, 64)
        pump()

        @pl.loop(0, width // 256)
        def _(k):
            turn(v.n2, v.n2t, pl.ds(pl.multiple_of(k * 256, 256), 256))

        keep(v.n2t, out.n2t)
        steps = ff // 256
        sixths = [k * steps // 6 for k in range(1, 6)]
        across = pl.BlockSpec((rows, 256), lambda t: (0, t))
        columns = pl.BlockSpec((width, 256), lambda t: (0, t))
        pump()
        gather.arrive(4)
        gate_inside = pumps_at(*sixths)

        def mlp_gate(wg, value, slope):
            gate_inside(pl.program_id(0))
            value[...] = dot(v.n2[...], wg[...])

            def act(rs):
                value[rs, :], slope[rs, :] = gelu_parts(value[rs, :])

            rows_loop(rows, act, 64)

        pltpu.emit_pipeline(mlp_gate, grid=(steps,), in_specs=[columns], out_specs=[across, across])(mgate_w, out.mg, out.bend)
        pump()
        gather.arrive(5)
        value_inside = pumps_at(*sixths)

        def mlp_value(wv, value, slope, mv, hidt):
            t = pl.program_id(0)
            value_inside(t)
            at = pl.ds(pl.multiple_of(t * 256, 256), 256)
            linear = dot(v.n2[...], wv[...])
            mv[...] = linear * slope[...]
            hidden = low(linear * value[...])
            v.hidden[:, at] = hidden
            hidt[...] = hidden.T

        pltpu.emit_pipeline(
            mlp_value,
            grid=(steps,),
            in_specs=[columns, across, across],
            out_specs=[across, pl.BlockSpec((256, rows), lambda t: (t, 0))],
        )(mvalue_w, out.mg, out.bend, out.mv, out.hidt)
        pump()
        gather.arrive(6)
        keep(v.hidden, out.hidden)
        for cp in kept:
            cp.wait()
        pump()

        def drain(odd):
            for i in range(count):
                gather.drain(i, odd)

        by_level(drain)
        ends.drain()
        packs.drain()

        @pl.when(seq < 7)
        def _():
            halo().wait_send()

    result = pl.pallas_call(
        kernel,
        out_shape=wholes + [saved[name] for name in names],
        in_specs=[HBM] * (2 + inputs),
        out_specs=[HBM] * (count + len(names)),
        scratch_shapes=[scratch[key] for key in keys] + [pltpu.VMEM(s.shape, s.dtype) for s in shapes],
        compiler_params=pltpu.CompilerParams(collective_id=1, has_side_effects=True, vmem_limit_bytes=60 << 20),
        name="forward",
    )(tokens, small_own, *gate_weights, *shards)
    return result[:count], named(names, result[count:])

def slot_scratch(n, h):
    bf = jnp.bfloat16
    return dict(
        ab=pltpu.VMEM((2, 4, n, h), bf),
        fr=pltpu.VMEM((2, 2, n, h), bf),
        se=pltpu.VMEM((2, n, h), bf),
        zo=pltpu.VMEM((2, n, h), bf),
        zp=pltpu.VMEM((n, h), bf),
        res=pltpu.VMEM((2, n, h), bf),
    )


PUMPS = (
    (),
    (),
    (),
    (),
    ((6, 0, 0),),
    ((6, 0, 1),),
    (),
    (),
    (),
    (),
    ((6, 1, 0),),
    ((6, 1, 1),),
    (),
    (),
    (),
    ((0, 0, 0), (0, 0, 1),),
    (),
    (),
    (),
    ((6, 2, 0),),
    ((0, 1, 0), (6, 2, 1), (0, 1, 1),),
    ((6, 4, 0),),
    ((6, 4, 1),),
    (),
    ((1, 0, 1),),
    ((1, 0, 0),),
    (),
    (),
    ((2, 0, 1), (1, 1, 0),),
    ((0, 2, 0),),
    (),
    ((6, 5, 0),),
    ((2, 0, 0),),
    ((3, 0, 1), (6, 5, 1), (1, 1, 1), (0, 2, 1), (2, 1, 0),),
    ((3, 0, 0),),
    ((2, 1, 1), (0, 4, 0), (4, 0, 1), (0, 4, 1),),
    ((4, 0, 0), (1, 2, 0), (3, 1, 0),),
    (),
    ((6, 3, 0),),
    ((3, 1, 1), (6, 3, 1), (0, 5, 0),),
    ((2, 2, 0), (1, 2, 1), (4, 1, 0), (0, 5, 1),),
    ((1, 4, 1), (1, 4, 0), (4, 1, 1),),
    (),
    ((2, 2, 1), (3, 2, 0),),
    (),
    (),
    ((2, 4, 1), (6, 6, 0), (0, 3, 0), (0, 3, 1), (3, 2, 1),),
    (),
    ((2, 4, 0), (6, 6, 1), (1, 5, 1), (1, 5, 0), (4, 2, 0),),
    (),
    ((1, 3, 0), (3, 4, 1), (4, 2, 1),),
    ((2, 5, 1), (3, 4, 0), (0, 6, 0),),
    ((6, 7, 0),),
    ((2, 5, 0), (6, 7, 1), (1, 3, 1), (4, 4, 1), (0, 6, 1),),
    ((3, 5, 1),),
    ((2, 3, 0), (1, 6, 0),),
    ((3, 5, 0), (4, 4, 0), (2, 3, 1),),
    ((0, 7, 0), (4, 5, 1),),
    ((6, 10, 0), (6, 10, 1),),
    ((2, 6, 0),),
    ((1, 6, 1), (4, 5, 0), (0, 7, 1), (3, 3, 0), (0, 10, 0),),
    (),
    (),
    ((6, 8, 0),),
    ((1, 7, 0), (6, 8, 1), (3, 3, 1), (3, 6, 0), (1, 10, 0), (0, 10, 1),),
    ((2, 6, 1), (6, 9, 0),),
    ((1, 7, 1), (6, 9, 1),),
    ((4, 3, 0),),
    ((2, 7, 0), (2, 10, 0), (4, 3, 1),),
    ((4, 6, 0), (0, 8, 1), (1, 10, 1), (0, 8, 0),),
    ((2, 7, 1), (2, 10, 1), (3, 6, 1), (3, 7, 0), (3, 10, 0), (0, 9, 1), (0, 9, 0), (1, 8, 1), (1, 8, 0),),
    (),
    ((3, 7, 1), (3, 10, 1), (1, 9, 1), (1, 9, 0), (4, 6, 1),),
    ((2, 8, 1),),
    ((2, 8, 0), (4, 7, 0), (4, 10, 0), (2, 9, 1), (4, 7, 1), (4, 10, 1), (2, 9, 0),),
    ((3, 8, 1), (3, 9, 1), (3, 8, 0),),
    ((3, 9, 0), (4, 8, 1), (4, 8, 0), (4, 9, 1), (4, 9, 0), (5, 0, 0), (5, 0, 1), (5, 1, 0), (5, 1, 1), (5, 2, 0), (5, 2, 1), (5, 4, 0), (5, 4, 1), (5, 5, 0), (5, 5, 1), (5, 3, 0), (5, 6, 0), (5, 3, 1), (5, 7, 0), (5, 10, 0), (5, 6, 1), (5, 7, 1), (5, 10, 1), (5, 8, 0), (5, 9, 0), (5, 8, 1), (5, 9, 1),),
)


def backward_call(lengths, cotangent, weights, saved):
    rows, width = cotangent.shape
    gelu_full, input_full, gates_full, output_full, mgate_full, mvalue_full, mdown_full = weights
    lru, ff = gelu_full.shape[1], mgate_full.shape[1]
    tiles = lru // LANES
    wide_tile = 2 * LANES
    f32, bf = jnp.float32, jnp.bfloat16
    shape = jax.ShapeDtypeStruct
    full = [mdown_full, mgate_full, mvalue_full, output_full, gelu_full, input_full, gates_full]
    cut = lambda k, *shares: [(k, full[k].shape[1] * a // 6, full[k].shape[1] * (b - a) // 6) for a, b in zip((0,) + shares, shares + (6,))]
    pieces = cut(0, 3) + cut(1, 3) + cut(2, 3) + cut(3) + cut(4) + cut(5, 4) + cut(6)
    DOWN, DOWN2, MGATE, MGATE2, MVALUE, MVALUE2, OUTPUT, GELU, INPUT, INPUT2, GATES = range(11)
    extents = [(full[k].shape[0] // 8, columns // 2) for k, _, columns in pieces]
    count = len(pieces)
    split = lambda v: v.reshape(4, 2, v.shape[0] // 8, v.shape[1])
    inputs = dict(
        x=saved.x, cot=cotangent, gelu_w=gelu_full, input_w=input_full, gates_w=gates_full, output_w=output_full, mgate_w=mgate_full,
        mvalue_w=mvalue_full, mdown_w=mdown_full, small=saved.small, n1t=split(saved.n1t), pre=saved.pre, lin=saved.lin,
        convt=saved.convt, decay=saved.decay, k6=saved.k6, k2=saved.k2, k3=saved.k3, k7=saved.k7, slope=saved.slope,
        rect=split(saved.rect), resid=saved.resid, n2t=split(saved.n2t), mg=saved.mg, mv=saved.mv, hidt=split(saved.hidt), hidden=saved.hidden,
    )
    slot_keys = list(slot_scratch(8, 128))
    most = max(4 * n * h // wide_tile for n, h in extents)
    passes, depth = 2 * count - 1, 4
    scratch = dict(
        go=pltpu.VMEM((rows, width), bf),
        gm=pltpu.VMEM((rows, width), bf),
        gn=pltpu.VMEM((rows, width), f32),
        normt=pltpu.VMEM((4, 2, width // 8, rows), bf),
        rect=pltpu.VMEM((4, 2, lru // 8, rows), bf),
        small=pltpu.VMEM((16, lru), f32),
        part=pltpu.VMEM((16, lru), f32),
        own=pltpu.VMEM((16, wide_tile), f32),
        gain=pltpu.VMEM((8, width), f32),
        into=pltpu.VMEM((tiles, 8, LANES), f32),
        halo=pltpu.VMEM((tiles, 8, LANES), f32),
        edge=pltpu.VMEM((tiles, 8, LANES), f32),
        stage=pltpu.VMEM((depth, most, wide_tile), bf),
        landed=pltpu.VMEM((depth, most, wide_tile), bf),
        gstage=pltpu.VMEM((4, 2, lru // 8, wide_tile), bf),
        ends=pltpu.VMEM((8, 2, tiles, LANES), f32),
        sslots=pltpu.VMEM((2, 5, 16, lru), f32),
        psend=pltpu.SemaphoreType.DMA((passes,)),
        precv=pltpu.SemaphoreType.DMA((passes,)),
        rsend=pltpu.SemaphoreType.DMA((count, 14)),
        rrecv=pltpu.SemaphoreType.DMA((count, 14)),
        esend=pltpu.SemaphoreType.DMA((7,)),
        erecv=pltpu.SemaphoreType.DMA((7,)),
        hsend=pltpu.SemaphoreType.DMA(()),
        hrecv=pltpu.SemaphoreType.DMA(()),
        ssend=pltpu.SemaphoreType.DMA((5,)),
        srecv=pltpu.SemaphoreType.DMA((5,)),
        load=pltpu.SemaphoreType.DMA((8,)),
        keep=pltpu.SemaphoreType.DMA((count + 2, 2)),
        credit=pltpu.SemaphoreType.REGULAR,
    )
    keys = list(scratch)
    outs = dict(mixed=shape((rows, width), bf), tokens_grad=shape((rows, width), f32), small_sum=shape((16, wide_tile), f32))
    out_keys = list(outs)
    sums = [shape((w.shape[0] // 8, w.shape[1]), bf) for w in full]

    def kernel(lengths_ref, *refs):
        refs = list(refs)

        def take(k):
            got = refs[:k]
            del refs[:k]
            return got

        w = named(inputs, take(len(inputs)))
        out = named(out_keys, take(len(out_keys)))
        sum_refs = take(len(full))
        v = named(keys, take(len(keys)))
        slots = []
        for (k, first, _), (n, h) in zip(pieces, extents):
            s = named(slot_keys, take(len(slot_keys)))
            s.n, s.h, s.tiles, s.first, s.sum = n, h, h // wide_tile, first, sum_refs[k]
            slots.append(s)
        place = Place()
        z, seq, core = place.z, place.seq, place.core
        red = Reduce(place, slots, (v.rsend, v.rrecv))
        ends = Ends(place, v.ends, (v.esend, v.erecv), True)
        tot = Small(place, v.part, v.sslots, (v.ssend, v.srecv))
        small, part = v.small, v.part
        kept = []

        def load(src, dst, k):
            cp = pltpu.make_async_copy(src, dst, v.load.at[k])
            cp.start()
            return cp

        greet([(z, (seq + d) % 8) for d in range(1, 8)] + [((z + d) % 4, seq) for d in range(1, 4)])
        first_loads = [load(w.cot, v.gm, 0)]
        loads = [load(w.small, v.small, 1), load(w.n2t, v.normt, 2), load(w.rect, v.rect, 3)]

        def arrived(i, h):
            red.arrive(i, h)
            cp = totalled(i, h)

            @pl.when(red.outer)
            def _():
                cp.start()

        def totalled(i, h):
            s = slots[i]
            return pltpu.make_async_copy(s.res.at[h], s.sum.at[:, pl.ds(s.first + h * s.h, s.h)], v.keep.at[i, h])

        def add_peer(i, h):
            red.add_peer(i, h)
            cp = totalled(i, h)

            @pl.when(red.makes(h))
            def _():
                cp.start()

        def pass_on(i, h):
            red.pass_on(i, h)
            cp = totalled(i, h)

            @pl.when(red.helps(h))
            def _():
                cp.start()

        steps = (red.add_first, red.add_second, red.add_outer, add_peer, pass_on, arrived, red.start_first)
        turn = [0]

        def serve(spot):
            for step, i, h in PUMPS[spot]:
                steps[step](i, h)

        def pump():
            serve(turn[0])
            turn[0] += 1

        def pumps_at(*grid_steps):
            spots = list(enumerate(grid_steps, turn[0]))
            turn[0] += len(spots)

            def at_step():
                for spot, grid_step in spots:
                    if PUMPS[spot]:
                        pl.when(pl.program_id(0) == grid_step)(lambda spot=spot: serve(spot))

            return at_step

        sent = []
        pass_of = {}

        def to_sib(k):
            return pltpu.make_async_remote_copy(
                src_ref=v.stage.at[k % depth, pl.ds(0, sent[k])], dst_ref=v.landed.at[k % depth, pl.ds(0, sent[k])],
                send_sem=v.psend.at[k], recv_sem=v.precv.at[k], device_id=place.sib, device_id_type=MESH,
            )

        def next_pass():
            k = len(sent)
            if k >= depth:
                to_sib(k - depth).wait_send()
            return k

        def send_blocks(used):
            k = len(sent)
            sent.append(used)
            if k == 0:
                met(10)
            if k >= depth:
                pl.semaphore_wait(v.credit, 1)
            to_sib(k).start()

        def give_credit(k):
            if k + depth < passes:
                pl.semaphore_signal(v.credit, inc=1, device_id=place.sib, device_id_type=MESH)

        def blocks(s):
            group = max(1, 512 // s.n)
            return [(j, group) for j in range(0, 4, group)]

        def right_tile(s, h, right, t):
            return right[:, pl.ds(pl.multiple_of(s.first + h * s.h + t * wide_tile, wide_tile), wide_tile)]

        def for_sib(i, left, right):
            s = slots[i]
            for h in range(2):
                pump()
                k = next_pass()
                pass_of[i, h] = k

                @pl.loop(0, s.tiles)
                def _(t, h=h, k=k):
                    r = right_tile(s, h, right, t)
                    for j, group in blocks(s):
                        value = dot(left[j : j + group, 1 - core].reshape(group * s.n, rows), r)
                        at = pl.ds(pl.multiple_of(t * 4 * s.n + j * s.n, s.n), group * s.n)
                        v.stage[k % depth, at, :] = low(value)

                send_blocks(4 * s.n * s.tiles)

        def for_us(i, left, right):
            s = slots[i]
            for h in range(2):
                pump()
                k = pass_of[i, h]
                to_sib(k).wait_recv()

                @pl.loop(0, s.tiles)
                def _(t, h=h, k=k):
                    r = right_tile(s, h, right, t)
                    for j, group in blocks(s):
                        value = dot(left[j : j + group, core].reshape(group * s.n, rows), r)
                        at = pl.ds(pl.multiple_of(t * 4 * s.n + j * s.n, s.n), group * s.n)
                        both = low(value + wide(v.landed[k % depth, at, :]))
                        lane = pl.ds(pl.multiple_of(t * wide_tile, wide_tile), wide_tile)
                        s.ab[h, j : j + group, :, lane] = both.reshape(group, s.n, wide_tile)

                give_credit(k)

        def eight(value):
            return value.reshape(value.shape[0] // 8, 8, value.shape[1]).sum(axis=0)

        def norm_back(x, grad, gain, add):
            scale = lax.rsqrt(jnp.mean(x * x, axis=-1, keepdims=True) + epsilon)
            v.gain[...] += eight(grad * x * scale)
            scaled = grad * gain
            m = jnp.mean(scaled * x, axis=-1, keepdims=True)
            return add + scale * (scaled - x * (scale * scale * m))

        def mlp_steps(gmg, gmv, first, count_of, *inner):
            pump()
            inside = pumps_at(*inner)

            def body(md, value, slope):
                inside()
                at = pl.ds(pl.multiple_of((pl.program_id(0) + first) * wide_tile, wide_tile), wide_tile)
                gh = dot_t(v.go[...], md[...])
                gmg[:, at] = low(gh * slope[...])
                gmv[:, at] = low(gh * value[...])

            across = pl.BlockSpec((rows, wide_tile), lambda t: (0, t + first))
            pltpu.emit_pipeline(
                body, grid=(count_of,), in_specs=[pl.BlockSpec((wide_tile, width), lambda t: (t + first, 0)), across, across]
            )(w.mdown_w, w.mg, w.mv)

        def mlp_norm_half(gmg, gmv, half):
            pump()

            inside = pumps_at(1)

            def body(wg, wv):
                inside()
                t = pl.program_id(0) + 2 * half
                at = pl.ds(pl.multiple_of(t * wide_tile, wide_tile), wide_tile)
                v.gn[:, at] = dot_t(gmg[...], wg[...]) + dot_t(gmv[...], wv[...])

            pltpu.emit_pipeline(body, grid=(2,), in_specs=[pl.BlockSpec((wide_tile, ff), lambda t: (t + 2 * half, 0))] * 2)(
                w.mgate_w, w.mvalue_w
            )

        valid_rows = lengths_ref[z] - seq * rows
        third = ff // wide_tile // 6

        def mlp_phase(gmg, gmv):
            def head(hidt):
                down_loads = load(w.hidt, hidt, 5)
                first_loads[0].wait()

                here = lax.broadcasted_iota(jnp.int32, (rows, width), 0) < valid_rows
                v.gm[...] = low(jnp.where(here, wide(v.gm[...]), 0.0))
                v.go[...] = low(dot(interleave(rows, False), v.gm[...]))
                part[...] = jnp.zeros_like(part)
                down_loads.wait()
                for_sib(DOWN, hidt, v.go)
                mlp_steps(gmg, gmv, 0, third)
                for_us(DOWN, hidt, v.go)
                for_sib(DOWN2, hidt, v.go)
                mlp_steps(gmg, gmv, third, 2 * third, third)
                for_us(DOWN2, hidt, v.go)

            pl.run_scoped(head, pltpu.VMEM((4, 2, ff // 8, rows), bf))
            for cp in loads:
                cp.wait()
            for_sib(MGATE, v.normt, gmg)
            for_sib(MVALUE, v.normt, gmv)
            mlp_steps(gmg, gmv, 3 * third, 3 * third, third, 2 * third)
            for_us(MGATE, v.normt, gmg)
            for_us(MVALUE, v.normt, gmv)
            for_sib(MGATE2, v.normt, gmg)
            for_sib(MVALUE2, v.normt, gmv)
            mlp_norm_half(gmg, gmv, 0)
            for_us(MGATE2, v.normt, gmg)
            for_us(MVALUE2, v.normt, gmv)
            mlp_norm_half(gmg, gmv, 1)

        pl.run_scoped(mlp_phase, pltpu.VMEM((rows, ff), bf), pltpu.VMEM((rows, ff), bf))
        pump()
        v.gain[...] = jnp.zeros_like(v.gain)

        inside = pumps_at(rows // 128)

        def norm_two(resid, inside=inside):
            inside()
            at = pl.ds(pl.multiple_of(pl.program_id(0) * 64, 64), 64)
            value = norm_back(resid[...], v.gn[at, :], small[9:10, :width], wide(v.go[at, :]))
            v.gn[at, :] = value
            v.gm[at, :] = low(value)

        pltpu.emit_pipeline(norm_two, grid=(rows // 64,), in_specs=[pl.BlockSpec((64, width), lambda t: (t, 0))])(w.resid)
        part[9:10, :width] = v.gain[...].sum(axis=0, keepdims=True)
        tokens_load = load(w.x, v.go, 6)

        norm_load = load(w.n1t, v.normt, 4)

        def branch_phase(adj, prod, gg, gl, gri):
            decay_load = load(w.decay, prod, 7)
            for_sib(OUTPUT, v.rect, v.gm)
            pump()

            inside = pumps_at(tiles // 6, tiles // 3)

            def into_branch(wo, value, slope, inside=inside):
                inside()
                t = pl.program_id(0)
                gr = dot_t(v.gm[...], wo[...])
                for q in range(2):
                    c = 2 * t + q
                    grad = gr[:, q * LANES : (q + 1) * LANES]
                    adj[c, pl.ds(0, rows), :] = grad * value[q]
                    gg[:, pl.ds(pl.multiple_of(c * LANES, LANES), LANES)] = low(grad * slope[q])

            pair = pl.BlockSpec((2, rows, LANES), lambda t: (t, 0, 0))
            pltpu.emit_pipeline(
                into_branch, grid=(tiles // 2,), in_specs=[pl.BlockSpec((wide_tile, width), lambda t: (t, 0)), pair, pair]
            )(w.output_w, w.pre, w.slope)
            for_us(OUTPUT, v.rect, v.gm)
            pump()
            decay_load.wait()
            tails = segment_scan(prod, adj, prod, adj, True, rows, pump)
            before, whole = segment_ends(tails, True)
            ends.tell(whole)
            for c in range(tiles):
                v.into[c] = before[c][1]
                v.edge[c] = before[c][0]
            norm_load.wait()
            for_sib(GELU, v.normt, gg)
            pump()
            carry = ends.joined()
            for c in range(tiles):
                v.into[c] = v.into[c] + v.edge[c] * carry[c : c + 1, :]
            span = rows // 8

            inside = pumps_at(tiles // 4, tiles // 2, 3 * tiles // 4)

            def through_gates(k6, k2, k3, k7, convt, wg, inside=inside):
                inside()
                c = pl.program_id(0)
                lane = pl.ds(pl.multiple_of(c * LANES, LANES), LANES)
                sums = [jnp.zeros((8, LANES), f32) for _ in range(3)]
                for k in range(8):
                    at = slice(k * span, (k + 1) * span)
                    here = adj[c, at, :] + over_segments(prod[c, at, :], v.into[c])
                    grad_r = here * k6[at, :]
                    grad_i = here * k2[at, :]
                    adj[c, at, :] = here * k3[at, :]
                    gri[at, :LANES] = low(grad_r)
                    gri[at, LANES:] = low(grad_i)
                    for q, value in enumerate((here * k7[at, :], grad_r, grad_i)):
                        sums[q] = sums[q] + eight(value)
                part[7:8, lane] = sums[0].sum(axis=0, keepdims=True) * (cfactor * sigmoid(-small[7:8, lane]))
                part[5:6, lane] = sums[1].sum(axis=0, keepdims=True)
                part[6:7, lane] = sums[2].sum(axis=0, keepdims=True)
                product = low(dot(convt[...], gri[...]))
                for q in range(2):
                    unit = 2 * c + q
                    block = unit // 3
                    at = pl.ds(pl.multiple_of((unit % 3) * 64, 64), 64)
                    v.gstage[block // 2, block % 2, at, :] = product[64 * q : 64 * (q + 1), :]
                grad_conv = adj[c, pl.ds(0, rows), :] + dot_t(gri[...], wg[...])
                adj[c, pl.ds(0, rows), :] = grad_conv
                part[4:5, lane] = eight(grad_conv).sum(axis=0, keepdims=True)

            one = pl.BlockSpec((None, rows, LANES), lambda t: (t, 0, 0))
            pltpu.emit_pipeline(
                through_gates,
                grid=(tiles,),
                in_specs=[one] * 4
                + [pl.BlockSpec((None, LANES, rows), lambda t: (t, 0, 0)), pl.BlockSpec((LANES, wide_tile), lambda t: (t, 0))],
            )(w.k6, w.k2, w.k3, w.k7, w.convt, w.gates_w)

            def halo():
                return pltpu.make_async_remote_copy(
                    src_ref=v.edge, dst_ref=v.halo, send_sem=v.hsend, recv_sem=v.hrecv, device_id=(z, (seq + 7) % 8), device_id_type=MESH
                )

            for k in range(3):
                v.edge[:, k : k + 1, :] = adj[:, 8 * k : 8 * k + 1, :]

            @pl.when(seq > 0)
            def _():
                halo().start()

            for_us(GELU, v.normt, gg)
            pump()
            s = slots[GATES]
            gates_pass = next_pass()
            for j in range(4):

                def copy_block(at, j=j):
                    v.stage[gates_pass % depth, pl.ds(pl.multiple_of(j * s.n + at.start, 16), 16), :] = v.gstage[j, 1 - core, at, :]

                rows_loop(s.n, copy_block)
            send_blocks(4 * s.n)
            pump()

            @pl.when(seq == 7)
            def _():
                v.halo[...] = jnp.zeros((tiles, 8, LANES), f32)

            @pl.when(seq < 7)
            def _():
                halo().wait_recv()

            highest = lax.broadcasted_iota(jnp.int32, (8, LANES), 0) == 7

            @pl.loop(0, tiles)
            def _(c):
                for k in range(3):
                    tile = adj[c, 8 * k + 1 : 8 * k + 9, :]
                    adj[c, rows + 8 * k : rows + 8 * (k + 1), :] = jnp.where(highest, v.halo[c, k : k + 1, :], tile)

            inside = pumps_at(tiles // 3, 2 * tiles // 3)

            def through_conv(lin, inside=inside):
                inside()
                c = pl.program_id(0)
                lane = pl.ds(pl.multiple_of(c * LANES, LANES), LANES)
                taps = [small[k : k + 1, lane] for k in range(4)]
                sums = [jnp.zeros((8, LANES), f32) for _ in range(4)]
                for r in range(0, rows, 128):
                    here = adj[c, r : r + 128, :]
                    acc = taps[0] * here
                    for k in range(4):
                        sums[k] = sums[k] + eight(here * lin[RIM + r - 8 * k : RIM + r - 8 * k + 128, :])
                        if k:
                            acc = acc + taps[k] * adj[c, r + 8 * k : r + 8 * k + 128, :]
                    gl[r : r + 128, lane] = low(acc)
                for k in range(4):
                    part[k : k + 1, lane] = sums[k].sum(axis=0, keepdims=True)

            pltpu.emit_pipeline(
                through_conv, grid=(tiles,), in_specs=[pl.BlockSpec((None, rows + RIM, LANES), lambda t: (t, 0, 0))]
            )(w.lin)
            pump()
            to_sib(gates_pass).wait_recv()
            for j in range(4):

                def fold(at, j=j):
                    came = v.landed[gates_pass % depth, pl.ds(pl.multiple_of(j * s.n + at.start, 16), 16), :]
                    both = low(wide(v.gstage[j, core, at, :]) + wide(came))
                    s.ab[0, j, at, :] = both[:, : s.h]
                    s.ab[1, j, at, :] = both[:, s.h :]

                rows_loop(s.n, fold)
            give_credit(gates_pass)
            for_sib(INPUT, v.normt, gl)
            for_sib(INPUT2, v.normt, gl)
            for_us(INPUT, v.normt, gl)
            for_us(INPUT2, v.normt, gl)
            pump()
            inside = pumps_at(*range(1, width // wide_tile))

            def into_norm(wi, wg, inside=inside):
                inside()
                t = pl.program_id(0)
                value = dot_t(gl[...], wi[...]) + dot_t(gg[...], wg[...])
                adj[2 * t, pl.ds(0, rows), :] = value[:, :LANES]
                adj[2 * t + 1, pl.ds(0, rows), :] = value[:, LANES:]

            pltpu.emit_pipeline(into_norm, grid=(width // wide_tile,), in_specs=[pl.BlockSpec((wide_tile, lru), lambda t: (t, 0))] * 2)(
                w.input_w, w.gelu_w
            )
            pump()
            v.gain[...] = jnp.zeros_like(v.gain)
            tokens_load.wait()

            def norm_one(at):
                grad = jnp.concatenate([adj[c, at, :] for c in range(width // LANES)], axis=1)
                v.gn[at, :] = norm_back(wide(v.go[at, :]), grad, small[8:9, :width], v.gn[at, :])

            rows_loop(rows // 2, norm_one, 64)
            pump()
            rows_loop(rows, norm_one, 64, rows // 2)
            part[8:9, :width] = v.gain[...].sum(axis=0, keepdims=True)

        pl.run_scoped(
            branch_phase,
            pltpu.VMEM((tiles, rows + RIM, LANES), f32),
            pltpu.VMEM((tiles, rows, LANES), f32),
            pltpu.VMEM((rows, lru), bf),
            pltpu.VMEM((rows, lru), bf),
            pltpu.VMEM((rows, wide_tile), bf),
        )
        tot.begin()

        def tokens_out():
            return pltpu.make_async_copy(v.gn, out.tokens_grad, v.keep.at[count, 0])

        def last_phase(hidden, order):
            hidden_load = load(w.hidden, hidden, 7)
            order[...] = interleave(rows, True)

            @pl.loop(0, width // wide_tile)
            def _(t):
                at = pl.ds(pl.multiple_of(t * wide_tile, wide_tile), wide_tile)
                value = v.gn[:, at]
                high = low(value)
                rest = value - wide(high)
                middle = low(rest)
                lowest = low(rest - wide(middle))
                v.gn[:, at] = (dot(order[...], high) + dot(order[...], middle)) + dot(order[...], lowest)

            tokens_out().start()
            pump()
            inside = pumps_at(*range(1, width // wide_tile))
            hidden_load.wait()

            def body(wd, resid, mixed):
                inside()
                value = dot(order[...], low(resid[...] + dot(hidden[...], wd[...])))
                here = lax.broadcasted_iota(jnp.int32, (rows, wide_tile), 0) < valid_rows
                mixed[...] = low(jnp.where(here, value, 0.0))

            across = pl.BlockSpec((rows, wide_tile), lambda t: (0, t))
            pltpu.emit_pipeline(
                body, grid=(width // wide_tile,), in_specs=[pl.BlockSpec((ff, wide_tile), lambda t: (0, t)), across], out_specs=[across]
            )(w.mdown_w, w.resid, out.mixed)

        kept.append(tokens_out())
        pl.run_scoped(last_phase, pltpu.VMEM((rows, ff), bf), pltpu.VMEM((rows, rows), bf))
        summed = 0
        for k, (step, i, h) in enumerate(PUMPS[turn[0]]):
            steps[step](i, h)
            if k % 4 == 3 and summed < 5:
                tot.step(summed)
                summed += 1
        for k in range(summed, 5):
            tot.step(k)
        v.own[0:8, :] = pltpu.roll(part[0:8, :], (8 - seq) % 8 * (lru // 8), axis=1)[:, :wide_tile]
        v.own[8:16, :] = pltpu.roll(part[8:16, :], (lru - seq * (width // 8)) % lru, axis=1)[:, :wide_tile]
        cp = pltpu.make_async_copy(v.own, out.small_sum, v.keep.at[count, 1])
        cp.start()
        kept.append(cp)
        for i in range(count):
            for h in range(2):
                kept.append(totalled(i, h))
        for cp in kept:
            cp.wait()
        for i in range(count):
            red.drain(i)
        for k in range(passes - depth, passes):
            to_sib(k).wait_send()
        tot.drain()
        ends.drain()

        @pl.when(seq > 0)
        def _():
            pltpu.make_async_remote_copy(
                src_ref=v.edge, dst_ref=v.halo, send_sem=v.hsend, recv_sem=v.hrecv, device_id=(z, (seq + 7) % 8), device_id_type=MESH
            ).wait_send()

    slot_list = [value for n, h in extents for value in slot_scratch(n, h).values()]
    result = pl.pallas_call(
        kernel,
        out_shape=list(outs.values()) + sums,
        in_specs=[pl.BlockSpec(memory_space=pltpu.SMEM)] + [HBM] * len(inputs),
        out_specs=[HBM] * (len(outs) + len(full)),
        scratch_shapes=list(scratch.values()) + slot_list,
        compiler_params=pltpu.CompilerParams(collective_id=2, has_side_effects=True, vmem_limit_bytes=62 << 20),
        name="backward",
    )(lengths, *inputs.values())
    return result[: len(outs)], result[len(outs) :]


def finish_call(plain, sums):
    parts = 4
    block = lambda v: pl.BlockSpec((v.shape[0] // parts, v.shape[1]), lambda t: (t, 0))
    half = sums[-1].shape[1] // 2
    ins = list(plain) + list(sums)
    outs = [jax.ShapeDtypeStruct(v.shape, v.dtype) for v in plain] + [jax.ShapeDtypeStruct(v.shape, jnp.float32) for v in sums[:-1]]
    outs += [jax.ShapeDtypeStruct((sums[-1].shape[0], half), jnp.float32)] * 2

    def kernel(*refs):
        src, dst = refs[: len(ins)], refs[len(ins) :]
        for a, b in zip(src[:-1], dst):
            b[...] = a[...].astype(b.dtype)
        dst[-2][...] = wide(src[-1][:, :half])
        dst[-1][...] = wide(src[-1][:, half:])

    return pl.pallas_call(
        kernel,
        grid=(parts,),
        out_shape=outs,
        in_specs=[block(v) for v in ins],
        out_specs=[block(v) for v in outs],
        compiler_params=pltpu.CompilerParams(vmem_limit_bytes=60 << 20),
        name="finish",
    )(*ins)


def local(
    tokens,
    lengths,
    mixer_gain,
    gelu_weight,
    input_weight,
    conv_taps,
    conv_bias,
    rgate_weight,
    rgate_bias,
    igate_weight,
    igate_bias,
    decay_param,
    output_weight,
    mlp_gain,
    mlp_gate,
    mlp_value,
    mlp_down,
    cotangent,
):
    count = tokens.shape[0]
    width_lru = input_weight.shape[1]
    block = rgate_weight.shape[1]
    heads = width_lru // block
    taps_count = conv_taps.shape[1]
    rim = taps_count - 1
    seq_count = lax.axis_size("seq")
    slot_length = count * seq_count
    first_row = (lax.axis_index("grp") * seq_count + lax.axis_index("seq")) * count
    global_row = first_row + jnp.arange(count, dtype=jnp.int32)
    position = global_row % slot_length
    slot_of = global_row // slot_length
    slot_ids = jnp.arange(lengths.shape[0], dtype=jnp.int32)
    slot_len = jnp.sum(
        jnp.where(slot_of[:, None] == slot_ids[None, :], lengths[None, :], 0), axis=1
    )
    valid = (position < slot_len).astype(jnp.float32)[:, None]
    starts = (position > 0).astype(jnp.float32)[:, None]
    lag_masks = [(position >= lag).astype(jnp.float32)[:, None] for lag in range(taps_count)]
    zeros_lru = jnp.zeros((width_lru,), jnp.float32)
    ones_lru = jnp.ones((width_lru,), jnp.float32)
    (
        gain_one,
        gelu_full,
        input_full,
        taps_full,
        cbias_full,
        rgate_full,
        rbias_full,
        igate_full,
        ibias_full,
        decay_full,
        output_full,
        gain_two,
        mgate_full,
        mvalue_full,
        mdown_full,
    ) = (
        lax.all_gather(mixer_gain, "seq", axis=0, tiled=True),
        lax.all_gather(gelu_weight, "seq", axis=0, tiled=True),
        lax.all_gather(input_weight, "seq", axis=0, tiled=True),
        lax.all_gather(conv_taps, "seq", axis=0, tiled=True),
        lax.all_gather(conv_bias, "seq", axis=0, tiled=True),
        lax.all_gather(rgate_weight, "seq", axis=0, tiled=True),
        lax.all_gather(rgate_bias, "seq", axis=0, tiled=True),
        lax.all_gather(igate_weight, "seq", axis=0, tiled=True),
        lax.all_gather(igate_bias, "seq", axis=0, tiled=True),
        lax.all_gather(decay_param, "seq", axis=0, tiled=True),
        lax.all_gather(output_weight, "seq", axis=0, tiled=True),
        lax.all_gather(mlp_gain, "seq", axis=0, tiled=True),
        lax.all_gather(mlp_gate, "seq", axis=0, tiled=True),
        lax.all_gather(mlp_value, "seq", axis=0, tiled=True),
        lax.all_gather(mlp_down, "seq", axis=0, tiled=True),
    )
    inputs = tokens.astype(jnp.float32)
    normed_one, norm_one_back = jax.vjp(rms_norm, inputs, gain_one.astype(jnp.float32))
    normed_one = normed_one.astype(jnp.bfloat16)
    gate_pre = matmul(normed_one, gelu_full)
    gate_act, gate_back = jax.vjp(gelu_tanh, gate_pre)
    linear = matmul(normed_one, input_full)
    rim_in = passed_along(linear[count - rim :], "seq", 1)
    extended = jnp.concatenate([rim_in, linear], axis=0)
    taps_fwd = taps_full.astype(jnp.float32)
    conv = cbias_full.astype(jnp.float32) + taps_fwd[:, 0] * linear
    for lag in range(1, taps_count):
        conv = conv + taps_fwd[:, lag] * (extended[rim - lag : rim - lag + count] * lag_masks[lag])
    conv_low = conv.astype(jnp.bfloat16)
    conv_value = conv_low.astype(jnp.float32)
    rgate_pre = block_apply(conv_low, rgate_full, heads) + rbias_full.astype(jnp.float32)
    igate_pre = block_apply(conv_low, igate_full, heads) + ibias_full.astype(jnp.float32)
    (decay, inject), gates_back = jax.vjp(
        recurrence_gates, rgate_pre, igate_pre, conv_value, decay_full.astype(jnp.float32)
    )
    decay_used = decay * starts
    cum_decay, state_zero = lax.associative_scan(chain_combine, (decay_used, inject), axis=0)
    scanned = carried_in(
        (cum_decay[-1], state_zero[-1]), "seq", chain_combine, (ones_lru, zeros_lru), False
    )
    carry_in = scanned[1]
    state = state_zero + cum_decay * carry_in
    mixed_rec = (state * gate_act).astype(jnp.bfloat16)
    resid = inputs + matmul(mixed_rec, output_full)
    normed_two, norm_two_back = jax.vjp(rms_norm, resid, gain_two.astype(jnp.float32))
    normed_two = normed_two.astype(jnp.bfloat16)
    mgate_pre = matmul(normed_two, mgate_full)
    mvalue_pre = matmul(normed_two, mvalue_full)
    mgate_act, mgate_back = jax.vjp(gelu_tanh, mgate_pre)
    hidden = (mgate_act * mvalue_pre).astype(jnp.bfloat16)
    mixed = ((resid + matmul(hidden, mdown_full)) * valid).astype(jnp.bfloat16)
    (
        gain_one,
        gelu_full,
        input_full,
        taps_full,
        cbias_full,
        rgate_full,
        rbias_full,
        igate_full,
        ibias_full,
        decay_full,
        output_full,
        gain_two,
        mgate_full,
        mvalue_full,
        mdown_full,
    ) = (
        lax.all_gather(mixer_gain, "seq", axis=0, tiled=True),
        lax.all_gather(gelu_weight, "seq", axis=0, tiled=True),
        lax.all_gather(input_weight, "seq", axis=0, tiled=True),
        lax.all_gather(conv_taps, "seq", axis=0, tiled=True),
        lax.all_gather(conv_bias, "seq", axis=0, tiled=True),
        lax.all_gather(rgate_weight, "seq", axis=0, tiled=True),
        lax.all_gather(rgate_bias, "seq", axis=0, tiled=True),
        lax.all_gather(igate_weight, "seq", axis=0, tiled=True),
        lax.all_gather(igate_bias, "seq", axis=0, tiled=True),
        lax.all_gather(decay_param, "seq", axis=0, tiled=True),
        lax.all_gather(output_weight, "seq", axis=0, tiled=True),
        lax.all_gather(mlp_gain, "seq", axis=0, tiled=True),
        lax.all_gather(mlp_gate, "seq", axis=0, tiled=True),
        lax.all_gather(mlp_value, "seq", axis=0, tiled=True),
        lax.all_gather(mlp_down, "seq", axis=0, tiled=True),
    )
    taps_back = taps_full.astype(jnp.float32)
    grad_out = cotangent.astype(jnp.float32) * valid
    grad_out_low = grad_out.astype(jnp.bfloat16)
    down_grad = inner_rows(hidden, grad_out_low)
    grad_hidden = outer_cols(grad_out_low, mdown_full)
    grad_mgate = mgate_back(grad_hidden * mvalue_pre)[0].astype(jnp.bfloat16)
    grad_mvalue = (grad_hidden * mgate_act).astype(jnp.bfloat16)
    mgate_grad = inner_rows(normed_two, grad_mgate)
    mvalue_grad = inner_rows(normed_two, grad_mvalue)
    grad_ntwo = outer_cols(grad_mgate, mgate_full) + outer_cols(grad_mvalue, mvalue_full)
    grad_resid_norm, gain_two_grad = norm_two_back(grad_ntwo)
    grad_resid = grad_out + grad_resid_norm
    grad_mix = grad_resid.astype(jnp.bfloat16)
    output_grad = inner_rows(mixed_rec, grad_mix)
    grad_rec = outer_cols(grad_mix, output_full)
    grad_state = grad_rec * gate_act
    grad_gate = gate_back(grad_rec * state)[0].astype(jnp.bfloat16)
    decay_next = jnp.concatenate([decay_used[1:], jnp.ones((1, width_lru), jnp.float32)], axis=0)
    rev_prod, rev_adjoint = lax.associative_scan(
        chain_combine, (jnp.flip(decay_next, 0), jnp.flip(grad_state, 0)), axis=0
    )
    tail_prod = jnp.flip(rev_prod, 0)
    adjoint_zero = jnp.flip(rev_adjoint, 0)
    summary_decay = decay_used[0] * tail_prod[0]
    summary_adjoint = decay_used[0] * adjoint_zero[0]
    scanned_back = carried_in(
        (summary_decay, summary_adjoint), "seq", chain_combine, (ones_lru, zeros_lru), True
    )
    incoming = scanned_back[1]
    adjoint = adjoint_zero + tail_prod * incoming
    state_prev = jnp.concatenate([carry_in[None, :], state[:-1]], axis=0)
    grad_decay = adjoint * state_prev * starts
    grad_rpre, grad_ipre, grad_direct, decay_grad = gates_back((grad_decay, adjoint))
    rbias_grad = jnp.sum(grad_rpre, axis=0)
    ibias_grad = jnp.sum(grad_ipre, axis=0)
    grad_rlow = grad_rpre.astype(jnp.bfloat16)
    grad_ilow = grad_ipre.astype(jnp.bfloat16)
    rgate_grad = block_grad(conv_low, grad_rlow, heads)
    igate_grad = block_grad(conv_low, grad_ilow, heads)
    grad_conv = (
        grad_direct
        + block_back(grad_rlow, rgate_full, heads)
        + block_back(grad_ilow, igate_full, heads)
    )
    cbias_grad = jnp.sum(grad_conv, axis=0)
    taps_columns = []
    grad_extended = jnp.zeros((count + rim, width_lru), jnp.float32)
    for lag in range(taps_count):
        masked_term = grad_conv * lag_masks[lag]
        taps_columns.append(jnp.sum(masked_term * extended[rim - lag : rim - lag + count], axis=0))
        grad_extended = grad_extended + jnp.pad(
            taps_back[:, lag] * masked_term, ((rim - lag, lag), (0, 0))
        )
    taps_grad = jnp.stack(taps_columns, axis=1)
    rim_back = passed_along(grad_extended[:rim], "seq", -1)
    grad_linear = grad_extended[rim:] + jnp.pad(rim_back, ((count - rim, 0), (0, 0)))
    grad_lin = grad_linear.astype(jnp.bfloat16)
    input_grad = inner_rows(normed_one, grad_lin)
    gelu_grad = inner_rows(normed_one, grad_gate)
    grad_none = outer_cols(grad_lin, input_full) + outer_cols(grad_gate, gelu_full)
    grad_inputs_norm, gain_one_grad = norm_one_back(grad_none)
    tokens_grad = grad_resid + grad_inputs_norm
    partials = (
        gain_one_grad,
        gelu_grad,
        input_grad,
        taps_grad,
        cbias_grad,
        rgate_grad,
        rbias_grad,
        igate_grad,
        ibias_grad,
        decay_grad,
        output_grad,
        gain_two_grad,
        mgate_grad,
        mvalue_grad,
        down_grad,
    )
    summed_seq = (
        lax.psum_scatter(partials[0], "seq", scatter_dimension=0, tiled=True),
        lax.psum_scatter(partials[1], "seq", scatter_dimension=0, tiled=True),
        lax.psum_scatter(partials[2], "seq", scatter_dimension=0, tiled=True),
        lax.psum_scatter(partials[3], "seq", scatter_dimension=0, tiled=True),
        lax.psum_scatter(partials[4], "seq", scatter_dimension=0, tiled=True),
        lax.psum_scatter(partials[5], "seq", scatter_dimension=0, tiled=True),
        lax.psum_scatter(partials[6], "seq", scatter_dimension=0, tiled=True),
        lax.psum_scatter(partials[7], "seq", scatter_dimension=0, tiled=True),
        lax.psum_scatter(partials[8], "seq", scatter_dimension=0, tiled=True),
        lax.psum_scatter(partials[9], "seq", scatter_dimension=0, tiled=True),
        lax.psum_scatter(partials[10], "seq", scatter_dimension=0, tiled=True),
        lax.psum_scatter(partials[11], "seq", scatter_dimension=0, tiled=True),
        lax.psum_scatter(partials[12], "seq", scatter_dimension=0, tiled=True),
        lax.psum_scatter(partials[13], "seq", scatter_dimension=0, tiled=True),
        lax.psum_scatter(partials[14], "seq", scatter_dimension=0, tiled=True),
    )
    totals = lax.psum(tuple(summed_seq), "grp")
    return (
        mixed,
        tokens_grad,
        totals[0],
        totals[1],
        totals[2],
        totals[3],
        totals[4],
        totals[5],
        totals[6],
        totals[7],
        totals[8],
        totals[9],
        totals[10],
        totals[11],
        totals[12],
        totals[13],
        totals[14],
    )


def local_fast(
    tokens,
    lengths,
    mixer_gain,
    gelu_weight,
    input_weight,
    conv_taps,
    conv_bias,
    rgate_weight,
    rgate_bias,
    igate_weight,
    igate_bias,
    decay_param,
    output_weight,
    mlp_gain,
    mlp_gate,
    mlp_value,
    mlp_down,
    cotangent,
):
    lru_rows = jnp.concatenate(
        [conv_taps.T, conv_bias[None], rgate_bias[None], igate_bias[None], decay_param[None]], axis=0
    ).astype(jnp.float32)
    model_rows = jnp.stack([mixer_gain, mlp_gain]).astype(jnp.float32)
    across = lambda value, columns: jnp.pad(value, ((0, 0), (0, columns - value.shape[1])))
    small = jnp.concatenate([across(lru_rows, 256), across(model_rows, 256), jnp.zeros((6, 256), jnp.float32)], axis=0)
    weights, saved = forward_call(
        tokens, small, [rgate_weight, igate_weight], [gelu_weight, input_weight, output_weight, mlp_gate, mlp_value, mlp_down]
    )
    (mixed, tokens_grad, small_sum), sums = backward_call(lengths, cotangent, weights, saved)
    mixed, tokens_grad, down, mgate, mvalue, out_w, gelu_w, input_w, rgates, igates = finish_call([mixed, tokens_grad], sums)
    lru_own, model_own = small_sum[:8, : conv_bias.shape[0]], small_sum[8:10, : mixer_gain.shape[0]]
    return (
        mixed,
        tokens_grad,
        model_own[0],
        gelu_w,
        input_w,
        lru_own[:4].T,
        lru_own[4],
        rgates,
        lru_own[5],
        igates,
        lru_own[6],
        lru_own[7],
        out_w,
        model_own[1],
        mgate,
        mvalue,
        down,
    )


def solution(mesh):
    placed = (
        P(("grp", "seq"), None),
        P(),
        P("seq"),
        P("seq", None),
        P("seq", None),
        P("seq", None),
        P("seq"),
        P("seq", None),
        P("seq"),
        P("seq", None),
        P("seq"),
        P("seq"),
        P("seq", None),
        P("seq"),
        P("seq", None),
        P("seq", None),
        P("seq", None),
        P(("grp", "seq"), None),
    )
    fits = mesh.shape["grp"] == 4 and mesh.shape["seq"] == 8
    return jax.shard_map(
        local_fast if fits else local,
        mesh=mesh,
        in_specs=placed,
        out_specs=(
            P(("grp", "seq"), None),
            P(("grp", "seq"), None),
            P("seq"),
            P("seq", None),
            P("seq", None),
            P("seq", None),
            P("seq"),
            P("seq", None),
            P("seq"),
            P("seq", None),
            P("seq"),
            P("seq"),
            P("seq", None),
            P("seq"),
            P("seq", None),
            P("seq", None),
            P("seq", None),
        ),
        check_vma=False,
    )
```
